32 devices in a mesh: dp: 2 (over x), ctx: 4 (over y, core), tp: 4 (over z).
Axes of the slice: x: 2, y: 2, z: 4, core: 2. Of those that a mesh axis runs over, the one named last changes fastest.
Arguments:
- block_in: bfloat16 [2, 4096, 768], P('dp', 'ctx'), may hold values from -6 to 6
- out_grad: bfloat16 [2, 4096, 768], P('dp', 'ctx'), may hold values from -6 to 6
- parents: int32 [2, 16], P('dp'), may hold values from -1 to 7, as said below
- mixer_gain: float32 [768], replicated, may hold values from 0.5 to 1.5
- mixer_shift: float32 [768], replicated, may hold values from -1.75 to 1.75
- in_proj: bfloat16 [768, 3, 768], P('dp', None, 'tp'), may hold values from -0.21875 to 0.21875
- in_bias: float32 [3, 768], P(None, 'tp'), may hold values from -3 to 3
- short_weight: float32 [3, 3, 768], P(None, None, 'tp'), may hold values from -3.5 to 3.5
- short_bias: float32 [3, 768], P(None, 'tp'), may hold values from -1.75 to 1.75
- filter_one: float32 [33, 64], replicated, may hold values from -1 to 1
- filter_one_bias: float32 [64], replicated, may hold values from -6 to 6
- filter_two: float32 [64, 64], replicated, may hold values from -0.75 to 0.75
- filter_two_bias: float32 [64], replicated, may hold values from -6 to 6
- filter_freq: float32 [64], replicated, may hold values from 1.5 to 2
- filter_out: bfloat16 [64, 768], P('dp', 'tp'), may hold values from -0.1875 to 0.1875
- skip_gain: float32 [768], P('tp'), may hold values from -6 to 6
- out_proj: bfloat16 [768, 768], P('tp', 'dp'), may hold values from -0.21875 to 0.21875
- out_bias: float32 [768], replicated, may hold values from -1.75 to 1.75
- feed_gain: float32 [768], replicated, may hold values from 0.5 to 1.5
- feed_shift: float32 [768], replicated, may hold values from -1.75 to 1.75
- feed_up: bfloat16 [768, 3072], P('dp', 'tp'), may hold values from -0.21875 to 0.21875
- feed_up_bias: float32 [3072], P('tp'), may hold values from -1.75 to 1.75
- feed_down: bfloat16 [3072, 768], P('tp', 'dp'), may hold values from -0.109375 to 0.109375
- feed_down_bias: float32 [768], replicated, may hold values from -1.75 to 1.75
Outputs:
- block_out: float32 [2, 4096, 768], P('dp', 'ctx')
- grad_block_in: float32 [2, 4096, 768], P('dp', 'ctx')
- grad_mixer_gain: float32 [768], replicated
- grad_mixer_shift: float32 [768], replicated
- grad_in_proj: float32 [768, 3, 768], P('dp', None, 'tp')
- grad_in_bias: float32 [3, 768], P(None, 'tp')
- grad_short_weight: float32 [3, 3, 768], P(None, None, 'tp')
- grad_short_bias: float32 [3, 768], P(None, 'tp')
- grad_filter_one: float32 [33, 64], replicated
- grad_filter_one_bias: float32 [64], replicated
- grad_filter_two: float32 [64, 64], replicated
- grad_filter_two_bias: float32 [64], replicated
- grad_filter_freq: float32 [64], replicated
- grad_filter_out: float32 [64, 768], P('dp', 'tp')
- grad_skip_gain: float32 [768], P('tp')
- grad_out_proj: float32 [768, 768], P('tp', 'dp')
- grad_out_bias: float32 [768], replicated
- grad_feed_gain: float32 [768], replicated
- grad_feed_shift: float32 [768], replicated
- grad_feed_up: float32 [768, 3072], P('dp', 'tp')
- grad_feed_up_bias: float32 [3072], P('tp')
- grad_feed_down: float32 [3072, 768], P('tp', 'dp')
- grad_feed_down_bias: float32 [768], replicated
The draws below stay inside these ranges and needn't reach their ends.
Inputs may be any that keep to these rules, and one draw needn't show every extreme that they name: `parents`: blocks 0 to 3 form the trunk, block i having parent i - 1 (block 0 is the root, parent -1). Each of the next 4 blocks has a parent among trunk blocks 1 to 3. Each of the last 8 blocks has a parent among those 4 branch blocks; the last block's parent is block 7.
All inputs are finite; a program needn't handle non-finite values.
Results may differ from the reference program's by a relative error of at most 0.009.
Values may be sent and summed in bfloat16 or wider, within the bound.
A program may use at most 128 MiB of HBM per device.

```python
import math
import jax
import jax.numpy as jnp
from jax import lax

D = 768
FF = 3072
FH = 64
EMB = 33
KW = 3
SEG = 256
TRUNK = 4
BRANCHES = 4
NB = 16
DEPTH = 6
TREES = 2
TREE_TOK = 4096


def draw_parents(key, part):
    first_key, second_key = jax.random.split(jax.random.fold_in(key, 17))
    trunk_part = jnp.broadcast_to(jnp.arange(TRUNK, dtype=jnp.int32) - 1, (TREES, TRUNK))
    branch_part = jax.random.randint(first_key, (TREES, BRANCHES), 1, TRUNK, dtype=jnp.int32)
    leaf_part = TRUNK + jax.random.randint(second_key, (TREES, 2 * BRANCHES - 1), 0, BRANCHES, dtype=jnp.int32)
    last_part = jnp.full((TREES, 1), TRUNK + BRANCHES - 1, dtype=jnp.int32)
    return jnp.concatenate([trunk_part, branch_part, leaf_part, last_part], axis=1).astype(jnp.int32)


def block_scale(key, shape, cuts, least, high):
    def one(dim, parts):
        steps = jax.random.uniform(jax.random.fold_in(jax.random.fold_in(key, 6), dim), (parts,), jnp.float32, least / len(cuts), high / len(cuts))
        return jnp.repeat(jnp.exp(steps), shape[dim] // parts).reshape((-1,) + (1,) * (len(shape) - dim - 1))

    loudness = one(*cuts[0])
    for cut in cuts[1:]:
        loudness = loudness * one(*cut)
    return loudness


def noise(own_key, shape, deviation, reach, shards=(), held_as=jnp.bfloat16):
    level = block_scale(own_key, shape, shards, -0.22, 0.18) if shards else 1.0
    drawn = jax.random.normal(own_key, shape, jnp.float32) * deviation * level
    return jnp.minimum(jnp.maximum(drawn, -reach), reach).astype(held_as)


def setup_inputs(seed: int = 0) -> dict:
    keys = jax.random.split(jax.random.key(seed), 25)
    block_in = noise(keys[0], (TREES, TREE_TOK, D), 1.0, 6.0, ((0, 2), (1, 4)))
    out_grad = noise(keys[1], (TREES, TREE_TOK, D), 1.0, 6.0, ((0, 2), (1, 4)))
    parents = draw_parents(jax.random.fold_in(keys[24], 71), 0)
    mixer_gain = jnp.clip(1.0 + 0.1 * jax.random.normal(keys[3], (D,), jnp.float32), 0.5, 1.5)
    mixer_shift = noise(keys[4], (D,), 0.3, 1.75, (), jnp.float32)
    in_proj = noise(keys[5], (D, 3, D), D ** -0.5, 0.21875, ((0, 2), (2, 4)))
    in_bias = noise(keys[6], (3, D), 0.5, 3.0, ((1, 4),), jnp.float32)
    short_weight = noise(keys[7], (3, KW, D), KW ** -0.5, 3.5, ((2, 4),), jnp.float32)
    short_bias = noise(keys[8], (3, D), 0.3, 1.75, ((1, 4),), jnp.float32)
    filter_one = jnp.clip(jax.random.uniform(keys[9], (EMB, FH), jnp.float32, -1.0, 1.0), -1.0, 1.0)
    filter_one_bias = noise(keys[10], (FH,), 1.0, 6.0, (), jnp.float32)
    filter_two = jnp.clip(jax.random.uniform(keys[11], (FH, FH), jnp.float32, -0.75, 0.75), -0.75, 0.75)
    filter_two_bias = noise(keys[12], (FH,), 1.0, 6.0, (), jnp.float32)
    filter_freq = jnp.clip(jnp.exp(jax.random.uniform(keys[13], (FH,), jnp.float32, math.log(1.5), math.log(2.0))), 1.5, 2.0)
    filter_out = noise(keys[14], (FH, D), (FH * 16) ** -0.5, 0.1875, ((0, 2), (1, 4)))
    skip_gain = noise(keys[15], (D,), 1.0, 6.0, ((0, 4),), jnp.float32)
    out_proj = noise(keys[16], (D, D), D ** -0.5, 0.21875, ((0, 4), (1, 2)))
    out_bias = noise(keys[17], (D,), 0.3, 1.75, (), jnp.float32)
    feed_gain = jnp.clip(1.0 + 0.1 * jax.random.normal(keys[18], (D,), jnp.float32), 0.5, 1.5)
    feed_shift = noise(keys[19], (D,), 0.3, 1.75, (), jnp.float32)
    feed_up = noise(keys[20], (D, FF), D ** -0.5, 0.21875, ((0, 2), (1, 4)))
    feed_up_bias = noise(keys[21], (FF,), 0.3, 1.75, ((0, 4),), jnp.float32)
    feed_down = noise(keys[22], (FF, D), FF ** -0.5, 0.109375, ((0, 4), (1, 2)))
    feed_down_bias = noise(keys[23], (D,), 0.3, 1.75, (), jnp.float32)
    return {"block_in": block_in, "out_grad": out_grad, "parents": parents, "mixer_gain": mixer_gain, "mixer_shift": mixer_shift, "in_proj": in_proj, "in_bias": in_bias, "short_weight": short_weight, "short_bias": short_bias, "filter_one": filter_one, "filter_one_bias": filter_one_bias, "filter_two": filter_two, "filter_two_bias": filter_two_bias, "filter_freq": filter_freq, "filter_out": filter_out, "skip_gain": skip_gain, "out_proj": out_proj, "out_bias": out_bias, "feed_gain": feed_gain, "feed_shift": feed_shift, "feed_up": feed_up, "feed_up_bias": feed_up_bias, "feed_down": feed_down, "feed_down_bias": feed_down_bias}


EXACT = lax.Precision.HIGHEST
EPSILON = 1e-05
SLOW_RATE = -math.log(0.01) / 1.5
FAST_RATE = -math.log(0.01) / 0.3
SHIFT_FLOOR = 0.05

@jax.custom_vjp
def low(v):
    return lax.optimization_barrier(v.astype(jnp.bfloat16)).astype(jnp.float32)

@jax.custom_vjp
def low_back(v):
    return v

def low_keep(v):
    return (low(v), None)

def low_pass(kept, grad):
    return (grad,)

def back_keep(v):
    return (v, None)

def back_low(kept, grad):
    return (low(grad),)
low.defvjp(low_keep, low_pass)
low_back.defvjp(back_keep, back_low)

def layer_norm(inputs, gain, shift):
    mean_value = lax.optimization_barrier(jnp.mean(inputs, axis=-1, keepdims=True))
    centered = inputs - mean_value
    variance = lax.optimization_barrier(jnp.mean(centered * centered, axis=-1, keepdims=True))
    return centered * lax.rsqrt(variance + EPSILON) * gain + shift

def gelu_exact(values):
    return jax.nn.gelu(values, approximate=False)

def implicit_filter(first_weight, first_bias, second_weight, second_bias, frequency, last_weight, length, channel_first, width_all):
    positions = jnp.arange(length, dtype=jnp.float32)
    time_pos = positions / (length - 1)
    bands = (first_weight.shape[0] - 1) // 2
    band_freq = jnp.linspace(0.0001, bands - 1, bands, dtype=jnp.float32)
    angles = 2.0 * math.pi / length * positions
    phases = angles[:, None] * band_freq[None, :]
    embedding = jnp.concatenate([time_pos[:, None], jnp.cos(phases), -jnp.sin(phases)], axis=1)
    hidden = jnp.sin(frequency * (jnp.dot(embedding, first_weight, precision=EXACT) + first_bias))
    hidden = jnp.sin(frequency * (jnp.dot(hidden, second_weight, precision=EXACT) + second_bias))
    raw_taps = jnp.dot(hidden, last_weight, precision=EXACT)
    channel_ids = (channel_first + jnp.arange(last_weight.shape[1])).astype(jnp.float32)
    decay_rate = SLOW_RATE + (FAST_RATE - SLOW_RATE) * channel_ids / (width_all - 1)
    envelope = jnp.exp(-time_pos[:, None] * decay_rate[None, :])
    return raw_taps * (envelope + SHIFT_FLOOR)

def tree_tables(parent_row):
    block_count = parent_row.shape[0]
    block_ids = jnp.arange(block_count, dtype=jnp.int32)
    parent_map = (parent_row[:, None] == block_ids[None, :]).astype(jnp.float32)
    identity = jnp.eye(block_count, dtype=jnp.float32)

    def extend(unused_step, current):
        return identity + jnp.dot(parent_map, current, precision=EXACT)
    ancestor = lax.fori_loop(0, block_count, extend, identity)
    depths = lax.optimization_barrier(jnp.sum(ancestor, axis=1))
    return (parent_map, ancestor, depths[:, None] - depths[None, :])

def short_conv(parent_tail, projected, weight, shift):
    extended = jnp.concatenate([parent_tail, projected], axis=1)
    return weight[:, 0] * extended[:, :-2] + weight[:, 1] * extended[:, 1:-1] + weight[:, 2] * extended[:, 2:] + shift

def filter_spectra(filter_taps):
    padded = jnp.concatenate([jnp.zeros((SEG, filter_taps.shape[1]), filter_taps.dtype), filter_taps], axis=0)
    keep_mask = (jnp.arange(2 * SEG) != SEG)[:, None]
    spectra_list = []
    for distance in range(DEPTH):
        window = padded[distance * SEG:(distance + 2) * SEG]
        circular = jnp.where(keep_mask, jnp.concatenate([window[SEG:], window[:SEG]], axis=0), 0.0)
        spectra_list.append(jnp.fft.rfft(circular, axis=0))
    return jnp.stack(spectra_list)

def tree_forward(tree_params, spectra, inputs, parent_row):
    mixer_gain, mixer_shift, in_proj, in_bias, short_weight, short_bias, skip_gain, out_proj, out_bias, feed_gain, feed_shift, feed_up, feed_up_bias, feed_down, feed_down_bias = tree_params
    mixer_normed = low(layer_norm(inputs, mixer_gain, mixer_shift))
    projected = jnp.dot(mixer_normed, in_proj.reshape(D, 3 * D), precision=EXACT).reshape(-1, 3, D) + in_bias
    projected = low_back(projected).reshape(NB, SEG, 3, D)
    parent_map, ancestor, depth_gap = tree_tables(parent_row)
    parent_tail = jnp.einsum('sb,bkgc->skgc', parent_map, projected[:, SEG - 2:], precision=EXACT)
    mixed_in = short_conv(parent_tail, projected, short_weight, short_bias)
    carried = low(mixed_in[:, :, 2] * mixed_in[:, :, 1])
    source_spec = jnp.fft.rfft(carried, n=2 * SEG, axis=1)
    total_spec = jnp.zeros_like(source_spec)
    for distance in range(DEPTH):
        selector = (ancestor * (depth_gap == distance)).astype(source_spec.dtype)
        total_spec = total_spec + spectra[distance] * jnp.einsum('sa,afc->sfc', selector, source_spec)
    long_out = low_back(jnp.fft.irfft(total_spec, n=2 * SEG, axis=1)[:, :SEG])
    convolved = long_out + skip_gain * carried
    gated = low(convolved * mixed_in[:, :, 0]).reshape(-1, D)
    mixer_out = low_back(jnp.dot(gated, out_proj, precision=EXACT) + out_bias)
    residual = inputs + mixer_out
    feed_normed = low(layer_norm(residual, feed_gain, feed_shift))
    pre_act = low_back(jnp.dot(feed_normed, feed_up, precision=EXACT) + feed_up_bias)
    hidden_act = low(gelu_exact(pre_act))
    return residual + jnp.dot(hidden_act, feed_down, precision=EXACT) + feed_down_bias

def to_wide(array_in):
    return array_in.astype(jnp.float32)

def reference(block_in, out_grad, parents, mixer_gain, mixer_shift, in_proj, in_bias, short_weight, short_bias, filter_one, filter_one_bias, filter_two, filter_two_bias, filter_freq, filter_out, skip_gain, out_proj, out_bias, feed_gain, feed_shift, feed_up, feed_up_bias, feed_down, feed_down_bias):
    params = (mixer_gain, mixer_shift, to_wide(in_proj), in_bias, short_weight, short_bias, filter_one, filter_one_bias, filter_two, filter_two_bias, filter_freq, to_wide(filter_out), skip_gain, to_wide(out_proj), out_bias, feed_gain, feed_shift, to_wide(feed_up), feed_up_bias, to_wide(feed_down), feed_down_bias)

    def forward(inputs, weights):
        filter_taps = implicit_filter(weights[6], weights[7], weights[8], weights[9], weights[10], weights[11], DEPTH * SEG, 0, D)
        spectra = filter_spectra(filter_taps)
        tree_params = (weights[0], weights[1], weights[2], weights[3], weights[4], weights[5], weights[12], weights[13], weights[14], weights[15], weights[16], weights[17], weights[18], weights[19], weights[20])

        def one_tree(pair):
            return tree_forward(tree_params, spectra, pair[0], pair[1])
        return lax.map(jax.checkpoint(one_tree), (inputs, parents))
    result, pullback = jax.vjp(forward, to_wide(block_in), params)
    grad_inputs, grads = pullback(to_wide(out_grad))
    return (result, grad_inputs, grads[0], grads[1], grads[2], grads[3], grads[4], grads[5], grads[6], grads[7], grads[8], grads[9], grads[10], grads[11], grads[12], grads[13], grads[14], grads[15], grads[16], grads[17], grads[18], grads[19], grads[20])
```

```python
import functools
import math

import jax
import jax.numpy as jnp
import numpy as np
from jax import lax
from jax.experimental import pallas as pl
from jax.experimental.pallas import tpu as pltpu
from jax.sharding import PartitionSpec as P

SEG = 256
DEPTH = 6
HEADS = 8
EXACT = lax.Precision.HIGHEST
EPSILON = 1e-05
SLOW_RATE = -math.log(0.01) / 1.5
FAST_RATE = -math.log(0.01) / 0.3
SHIFT_FLOOR = 0.05
F32 = jnp.float32
BF16 = jnp.bfloat16
MESH = pl.DeviceIdType.MESH
VM = pl.BlockSpec(memory_space=pltpu.VMEM)
SM = pl.BlockSpec(memory_space=pltpu.SMEM)
LIMIT = 60 << 20


def sds(shape, dtype):
    return jax.ShapeDtypeStruct(shape, dtype)


def call(kernel, out_shape, in_specs, scratch=(), collective=None, flops=0, traffic=0):
    many = isinstance(out_shape, (tuple, list))
    return pl.pallas_call(
        kernel,
        out_shape=out_shape,
        in_specs=in_specs,
        out_specs=tuple(VM for _ in out_shape) if many else VM,
        scratch_shapes=list(scratch),
        compiler_params=pltpu.CompilerParams(
            vmem_limit_bytes=LIMIT,
            collective_id=collective,
            has_side_effects=collective is not None,
        ),
        cost_estimate=pl.CostEstimate(flops=flops, bytes_accessed=traffic, transcendentals=0),
    )


def spectral_constants(block_len):
    freq = np.arange(block_len)[:, None]
    place = np.arange(block_len)[None, :]
    angle = ((2 * freq + 1) * place % (4 * block_len)) * (2.0 * math.pi / (4 * block_len))
    table = np.concatenate([np.cos(angle), -np.sin(angle)], axis=0).astype(np.float32)
    high = table.astype(jnp.bfloat16)
    low = (table - high.astype(np.float32)).astype(jnp.bfloat16)
    sign = np.where(np.arange(block_len) % 2 == 0, 1.0, -1.0).astype(np.float32)[:, None]
    return high, low, np.ascontiguousarray(high.T), np.ascontiguousarray(low.T), sign


def implicit_filter(w1, b1, w2, b2, frequency, last_weight, length, channel_first, width_all):
    positions = jnp.arange(length, dtype=F32)
    time_pos = positions / (length - 1)
    bands = (w1.shape[0] - 1) // 2
    band_freq = jnp.linspace(0.0001, bands - 1, bands, dtype=F32)
    angles = 2.0 * math.pi / length * positions
    phases = angles[:, None] * band_freq[None, :]
    embedding = jnp.concatenate([time_pos[:, None], jnp.cos(phases), -jnp.sin(phases)], axis=1)
    hidden = jnp.sin(frequency * (jnp.dot(embedding, w1, precision=EXACT) + b1))
    hidden = jnp.sin(frequency * (jnp.dot(hidden, w2, precision=EXACT) + b2))
    raw_taps = jnp.dot(hidden, last_weight, precision=EXACT)
    channel_ids = (channel_first + jnp.arange(last_weight.shape[1])).astype(F32)
    decay_rate = SLOW_RATE + (FAST_RATE - SLOW_RATE) * channel_ids / (width_all - 1)
    envelope = jnp.exp(-time_pos[:, None] * decay_rate[None, :])
    return raw_taps * (envelope + SHIFT_FLOOR)


def normalize(values):
    mean_value = jnp.mean(values, axis=-1, keepdims=True)
    centered = values - mean_value
    variance = jnp.mean(centered * centered, axis=-1, keepdims=True)
    scale = lax.rsqrt(variance + EPSILON)
    return centered * scale, scale


def split(values):
    high = values.astype(BF16)
    return high, (values - high.astype(F32)).astype(BF16)


def mm(lhs, rhs):
    return jnp.dot(lhs, rhs, preferred_element_type=F32)


def mm_nt(lhs, rhs):
    return lax.dot_general(lhs, rhs, (((1,), (1,)), ((), ())), preferred_element_type=F32)


def mm_tn(lhs, rhs):
    return lax.dot_general(lhs, rhs, (((0,), (0,)), ((), ())), preferred_element_type=F32)


def mm_split(high, low, values):
    v_high, v_low = split(values)
    return mm(high, v_high) + (mm(low, v_high) + mm(high, v_low))


def mix_in_kernel(
    x_ref, xt_ref, pick_ref, w_ref, bias_ref, gain_ref, shift_ref, sw_ref, sb_ref,
    low_ref, proj_ref, head_ref, mixed_ref, carried_ref, ext_ref,
):
    gain, shift = gain_ref[...], shift_ref[...]
    tails = normalize(xt_ref[...].astype(F32))[0] * gain + shift
    tails = tails.astype(BF16)
    tail_proj = [mm(tails, w_ref[g]) + bias_ref[g : g + 1] for g in range(3)]
    blocks = x_ref.shape[0] // SEG

    def one(s, unused):
        rows = pl.ds(pl.multiple_of(s * SEG, SEG), SEG)
        low = (normalize(x_ref[rows].astype(F32))[0] * gain + shift).astype(BF16)
        low_ref[rows] = low
        out = []
        for g in range(3):
            projected = mm(low, w_ref[g]) + bias_ref[g : g + 1]
            proj_ref[g, rows] = projected
            head = jnp.dot(pick_ref[s], tail_proj[g], precision=EXACT, preferred_element_type=F32)
            head_ref[g, s] = head
            ext_ref[g, 0:HEADS] = head
            ext_ref[g, HEADS : HEADS + SEG] = projected
            mixed = (
                sw_ref[3 * g : 3 * g + 1] * ext_ref[g, HEADS - 2 : HEADS - 2 + SEG]
                + sw_ref[3 * g + 1 : 3 * g + 2] * ext_ref[g, HEADS - 1 : HEADS - 1 + SEG]
                + sw_ref[3 * g + 2 : 3 * g + 3] * projected
                + sb_ref[g : g + 1]
            )
            mixed_ref[g, rows] = mixed
            out.append(mixed)
        carried_ref[rows] = (out[2] * out[1]).astype(BF16)
        return unused

    lax.fori_loop(0, blocks, one, 0)


FT = 64


def conv_fwd_kernel(
    idx_ref, own_ref, trunk_ref, branch_ref, taps_ref, gate_ref, skip_ref,
    fh_ref, fl_ref, th_ref, tl_ref, sign_ref,
    conv_ref, gated_ref, spec_ref, filt_ref, acc_ref,
):
    blocks = own_ref.shape[0]
    fh, fl, th, tl = fh_ref[...], fl_ref[...], th_ref[...], tl_ref[...]

    def source(j, unused):
        for base, ref in ((0, own_ref), (4, trunk_ref), (8, branch_ref)):
            part = ref[j]
            out = mm(fh, part) + mm(fl, part)
            spec_ref[base + j, 0] = out[:SEG]
            spec_ref[base + j, 1] = out[SEG:]
        return unused

    lax.fori_loop(0, blocks, source, 0)
    sign = sign_ref[...]
    last = None
    for j in range(DEPTH):
        part = taps_ref[j * SEG : (j + 1) * SEG]
        out = mm_split(fh, fl, part)
        re, im = out[:SEG], out[SEG:]
        if last is None:
            filt_ref[j, 0] = re
            filt_ref[j, 1] = im
        else:
            filt_ref[j, 0] = re - sign * last[1]
            filt_ref[j, 1] = im + sign * (last[0] - last[2])
        last = (re, im, part[0:1])
    filt_ref[DEPTH] = jnp.zeros(filt_ref.shape[1:], F32)

    def dest(s, unused):
        pairs = [(0, s), (idx_ref[s, 4], 8 + idx_ref[s, 5])] + [(idx_ref[s, a], 4 + a) for a in range(4)]
        for t in range(SEG // FT):
            rows = slice(t * FT, (t + 1) * FT)
            re = im = None
            for h, x in pairs:
                hr, hi = filt_ref[h, 0, rows], filt_ref[h, 1, rows]
                xr, xi = spec_ref[x, 0, rows], spec_ref[x, 1, rows]
                pr, pi = hr * xr - hi * xi, hr * xi + hi * xr
                re, im = (pr, pi) if re is None else (re + pr, im + pi)
            acc_ref[rows] = re
            acc_ref[SEG + t * FT : SEG + (t + 1) * FT] = im
        long_out = mm_split(th, tl, acc_ref[...]) * (1.0 / SEG)
        place = pl.ds(pl.multiple_of(s * SEG, SEG), SEG)
        convolved = long_out + skip_ref[...] * own_ref[s].astype(F32)
        conv_ref[place] = convolved
        gated_ref[place] = (convolved * gate_ref[place]).astype(BF16)
        return unused

    lax.fori_loop(0, blocks, dest, 0)


def conv_bwd_kernel(
    idx_ref, back_ref, leaf_ref, dlong_ref, dall_ref, dconv_ref, spec_ref, filt_ref, skip_ref,
    fh_ref, fl_ref, th_ref, tl_ref, sign_ref,
    dcar_ref, dtaps_ref, yspec_ref, dfilt_ref, acc_ref, sum_ref,
):
    blocks = dlong_ref.shape[0]
    fh, fl, th, tl = fh_ref[...], fl_ref[...], th_ref[...], tl_ref[...]
    scale = 1.0 / SEG

    def transform(j, unused):
        for base, ref, off in ((0, dlong_ref, 0), (4, dall_ref, 0), (8, dall_ref, 4)):
            part = ref[off + j]
            out = (mm(fh, part) + mm(fl, part)) * scale
            yspec_ref[base + j, 0] = out[:SEG]
            yspec_ref[base + j, 1] = out[SEG:]
        total = leaf_ref[j, 0] * dall_ref[8].astype(F32)
        for leaf in range(1, 8):
            total = total + leaf_ref[j, leaf] * dall_ref[8 + leaf].astype(F32)
        out = mm_split(fh, fl, total) * scale
        yspec_ref[12 + j, 0] = out[:SEG]
        yspec_ref[12 + j, 1] = out[SEG:]
        return unused

    lax.fori_loop(0, blocks, transform, 0)

    def source(s, unused):
        pairs = [(0, s)] + [(back_ref[s, k], 4 + k) for k in range(12)]
        for t in range(SEG // FT):
            rows = slice(t * FT, (t + 1) * FT)
            re = im = None
            for h, y in pairs:
                hr, hi = filt_ref[h, 0, rows], filt_ref[h, 1, rows]
                yr, yi = yspec_ref[y, 0, rows], yspec_ref[y, 1, rows]
                pr, pi = hr * yr + hi * yi, hr * yi - hi * yr
                re, im = (pr, pi) if re is None else (re + pr, im + pi)
            acc_ref[rows] = re
            acc_ref[SEG + t * FT : SEG + (t + 1) * FT] = im
        place = pl.ds(pl.multiple_of(s * SEG, SEG), SEG)
        dcar_ref[place] = mm_split(th, tl, acc_ref[...]) + skip_ref[...] * dconv_ref[place]
        return unused

    lax.fori_loop(0, blocks, source, 0)
    dfilt_ref[...] = jnp.zeros(dfilt_ref.shape, F32)

    def filters(s, unused):
        pairs = [(0, s), (idx_ref[s, 4], 8 + idx_ref[s, 5])] + [(idx_ref[s, a], 4 + a) for a in range(4)]
        for t in range(SEG // FT):
            rows = slice(t * FT, (t + 1) * FT)
            yr, yi = yspec_ref[s, 0, rows], yspec_ref[s, 1, rows]
            for h, x in pairs:
                xr, xi = spec_ref[x, 0, rows], spec_ref[x, 1, rows]
                dfilt_ref[h, 0, rows] += xr * yr + xi * yi
                dfilt_ref[h, 1, rows] += xr * yi - xi * yr
        return unused

    lax.fori_loop(0, blocks, filters, 0)
    sign = sign_ref[...]
    first_row = lax.broadcasted_iota(jnp.int32, (SEG, 1), 0) == 0
    for j in range(DEPTH):
        re, im = dfilt_ref[j, 0], dfilt_ref[j, 1]
        fix = None
        if j + 1 < DEPTH:
            nr, ni = dfilt_ref[j + 1, 0], dfilt_ref[j + 1, 1]
            re = re + sign * ni
            im = im - sign * nr
            fix = jnp.sum(sign * ni, axis=0, keepdims=True)
        acc_ref[0:SEG] = re
        acc_ref[SEG : 2 * SEG] = im
        taps = mm_split(th, tl, acc_ref[...])
        if fix is not None:
            taps = jnp.where(first_row, taps - fix, taps)
        dtaps_ref[j * SEG : (j + 1) * SEG] = taps


def feed_kernel(
    gated_ref, out_ref, x_ref, g_ref, ob_ref, gain_ref, shift_ref, up_ref, ub_ref, down_ref,
    resid_ref, dpart_ref, npart_ref, gdown_ref, gup_ref, gdb_ref, gub_ref,
):
    groups = gated_ref.shape[0]
    gdown_ref[...] = jnp.zeros(gdown_ref.shape, F32)
    gup_ref[...] = jnp.zeros(gup_ref.shape, F32)
    gdb_ref[...] = jnp.zeros(gdb_ref.shape, F32)
    gub_ref[...] = jnp.zeros(gub_ref.shape, F32)

    def one(s, unused):
        rows = pl.ds(pl.multiple_of(s * SEG, SEG), SEG)
        residual = x_ref[rows].astype(F32)
        mixed = mm(gated_ref[0, rows], out_ref[0])
        for z in range(1, groups):
            mixed = mixed + mm(gated_ref[z, rows], out_ref[z])
        residual = residual + mixed + ob_ref[...]
        resid_ref[rows] = residual
        low = (normalize(residual)[0] * gain_ref[...] + shift_ref[...]).astype(BF16)
        pre = mm(low, up_ref[...]) + ub_ref[...]
        cdf = 0.5 * (1.0 + lax.erf(pre * math.sqrt(0.5)))
        hidden = (pre * cdf).astype(BF16)
        slope = cdf + pre * (jnp.exp(-0.5 * pre * pre) * (1.0 / math.sqrt(2.0 * math.pi)))
        dpart_ref[rows] = mm(hidden, down_ref[...]).astype(BF16)
        grad = g_ref[rows]
        d_pre = (mm_nt(grad, down_ref[...]) * slope).astype(BF16)
        npart_ref[rows] = mm_nt(d_pre, up_ref[...]).astype(BF16)
        gdown_ref[...] += mm_tn(hidden, grad)
        gup_ref[...] += mm_tn(low, d_pre)
        gdb_ref[...] += jnp.sum(grad.astype(F32), axis=0, keepdims=True)
        gub_ref[...] += jnp.sum(d_pre.astype(F32), axis=0, keepdims=True)
        return unused

    lax.fori_loop(0, x_ref.shape[0] // SEG, one, 0)


def feed_back_kernel(
    resid_ref, dn_ref, g_ref, gain_ref, out_ref, gated_ref, mixed_ref, conv_ref, carried_ref,
    dres_ref, dconv_ref, dlong_ref, dzero_ref, gout_ref, gob_ref, ggain_ref, gshift_ref, gskip_ref,
):
    for ref in (gout_ref, gob_ref, ggain_ref, gshift_ref, gskip_ref):
        ref[...] = jnp.zeros(ref.shape, F32)

    def one(s, unused):
        rows = pl.ds(pl.multiple_of(s * SEG, SEG), SEG)
        xhat, scale = normalize(resid_ref[rows])
        dn = dn_ref[rows].astype(F32)
        e = dn * gain_ref[...]
        d_res = g_ref[rows].astype(F32) + scale * (
            e - jnp.mean(e, axis=-1, keepdims=True) - xhat * jnp.mean(e * xhat, axis=-1, keepdims=True)
        )
        dres_ref[rows] = d_res
        ggain_ref[...] += jnp.sum(dn * xhat, axis=0, keepdims=True)
        gshift_ref[...] += jnp.sum(dn, axis=0, keepdims=True)
        d_mix = d_res.astype(BF16)
        gob_ref[...] += jnp.sum(d_mix.astype(F32), axis=0, keepdims=True)
        gout_ref[...] += mm_tn(gated_ref[rows], d_mix)
        d_gated = mm_nt(d_mix, out_ref[...])
        d_conv = d_gated * mixed_ref[rows]
        dconv_ref[rows] = d_conv
        dlong_ref[rows] = d_conv.astype(BF16)
        dzero_ref[rows] = d_gated * conv_ref[rows]
        gskip_ref[...] += jnp.sum(d_conv * carried_ref[rows].astype(F32), axis=0, keepdims=True)
        return unused

    lax.fori_loop(0, g_ref.shape[0] // SEG, one, 0)


def mix_back_kernel(
    dzero_ref, dcar_ref, mixed_ref, proj_ref, head_ref, heads_ref, pick_ref, sw_ref, low_ref, w_ref,
    part_ref, gin_ref, gib_ref, gsw_ref, gsb_ref, ext_ref, dm_ref,
):
    for ref in (gin_ref, gib_ref, gsw_ref, gsb_ref):
        ref[...] = jnp.zeros(ref.shape, F32)

    def one(s, unused):
        rows = pl.ds(pl.multiple_of(s * SEG, SEG), SEG)
        part = None
        for g in range(3):
            if g == 0:
                dm = dzero_ref[rows]
            else:
                dm = dcar_ref[rows] * mixed_ref[3 - g, rows]
            ext_ref[0:HEADS] = head_ref[g, s]
            ext_ref[HEADS : HEADS + SEG] = proj_ref[g, rows]
            for k in range(3):
                piece = ext_ref[HEADS - 2 + k : HEADS - 2 + k + SEG]
                gsw_ref[3 * g + k : 3 * g + k + 1] += jnp.sum(piece * dm, axis=0, keepdims=True)
            gsb_ref[g : g + 1] += jnp.sum(dm, axis=0, keepdims=True)
            child = jnp.dot(pick_ref[s], heads_ref[g], precision=EXACT, preferred_element_type=F32)
            dm_ref[0:SEG] = dm
            dm_ref[SEG : SEG + HEADS] = child
            dp = (
                sw_ref[3 * g + 2 : 3 * g + 3] * dm
                + sw_ref[3 * g + 1 : 3 * g + 2] * dm_ref[1 : 1 + SEG]
                + sw_ref[3 * g : 3 * g + 1] * dm_ref[2 : 2 + SEG]
            ).astype(BF16)
            gib_ref[g : g + 1] += jnp.sum(dp.astype(F32), axis=0, keepdims=True)
            gin_ref[g] += mm_tn(low_ref[rows], dp)
            term = mm_nt(dp, w_ref[g])
            part = term if part is None else part + term
        part_ref[rows] = part.astype(BF16)
        return unused

    lax.fori_loop(0, low_ref.shape[0] // SEG, one, 0)


def norm_back_kernel(x_ref, dn_ref, dres_ref, gain_ref, gin_ref, ggain_ref, gshift_ref):
    ggain_ref[...] = jnp.zeros(ggain_ref.shape, F32)
    gshift_ref[...] = jnp.zeros(gshift_ref.shape, F32)

    def one(s, unused):
        rows = pl.ds(pl.multiple_of(s * SEG, SEG), SEG)
        xhat, scale = normalize(x_ref[rows].astype(F32))
        dn = dn_ref[rows].astype(F32)
        e = dn * gain_ref[...]
        gin_ref[rows] = dres_ref[rows] + scale * (
            e - jnp.mean(e, axis=-1, keepdims=True) - xhat * jnp.mean(e * xhat, axis=-1, keepdims=True)
        )
        ggain_ref[...] += jnp.sum(dn * xhat, axis=0, keepdims=True)
        gshift_ref[...] += jnp.sum(dn, axis=0, keepdims=True)
        return unused

    lax.fori_loop(0, x_ref.shape[0] // SEG, one, 0)


def spot(**changes):
    base = {name: lax.axis_index(name) for name in ("dp", "ctx", "tp")}
    base.update(changes)
    return (base["dp"], base["ctx"], base["tp"])


def remote(src, dst, send, recv, where):
    return pltpu.make_async_remote_copy(
        src_ref=src, dst_ref=dst, send_sem=send, recv_sem=recv, device_id=where, device_id_type=MESH
    )


def greet(partners):
    barrier = pltpu.get_barrier_semaphore()
    for where in partners:
        pl.semaphore_signal(barrier, inc=1, device_id=where, device_id_type=MESH)
    pl.semaphore_wait(barrier, len(partners))


CHUNK = 64


def chain_sum_kernel(part_ref, out_ref, end_ref, mid_ref, send_ref, acc_ref, s_end, r_end, s_mid, r_mid, s_out, r_out, s_cross, r_cross, s_fwd):
    tp = lax.axis_index("tp")
    inner = jnp.logical_and(tp > 0, tp < 3)
    pairs = part_ref.shape[0] // (2 * CHUNK)
    side = jnp.where(tp < 2, 0, 1)
    mate = spot(tp=jnp.where(inner, jnp.where(side == 0, 0, 3), jnp.where(side == 0, 1, 2)))
    cross = spot(tp=3 - tp)
    barrier = pltpu.get_barrier_semaphore()
    pl.semaphore_signal(barrier, inc=1, device_id=mate, device_id_type=MESH)
    pl.semaphore_signal(barrier, inc=1, device_id=cross, device_id_type=MESH)
    pl.semaphore_wait(barrier, 2)

    def rows(c):
        return pl.ds(pl.multiple_of(c * CHUNK, CHUNK), CHUNK)

    def to_mid(c):
        return remote(part_ref.at[rows(c)], end_ref.at[rows(c)], s_end.at[c], r_end.at[c], mate)

    def to_cross(c):
        return remote(send_ref.at[rows(c)], mid_ref.at[rows(c)], s_mid.at[c], r_mid.at[c], cross)

    def final_end(c):
        return remote(out_ref.at[rows(c)], out_ref.at[rows(c)], s_out.at[c], r_out.at[c], mate)

    def final_cross(c):
        return remote(out_ref.at[rows(c)], out_ref.at[rows(c)], s_cross.at[c], r_cross.at[c], cross)

    @pl.when(jnp.logical_not(inner))
    def _():
        for c in range(2 * pairs):
            to_mid(c).start()
        for c in range(2 * pairs):
            final_end(c).wait_recv()
        for c in range(2 * pairs):
            to_mid(c).wait_send()

    lag = 2

    @pl.when(inner)
    def _():
        for k in range(pairs + 2 * lag):
            if k < pairs:
                mine, other = 2 * k + side, 2 * k + 1 - side
                to_mid(2 * k).wait_recv()
                to_mid(2 * k + 1).wait_recv()
                send_ref[rows(other)] = (
                    part_ref[rows(other)].astype(F32) + end_ref[rows(other)].astype(F32)
                ).astype(BF16)
                to_cross(other).start()
            j = k - lag
            if 0 <= j < pairs:
                mine = 2 * j + side
                to_cross(mine).wait_recv()
                out_ref[rows(mine)] = (
                    part_ref[rows(mine)].astype(F32)
                    + end_ref[rows(mine)].astype(F32)
                    + mid_ref[rows(mine)].astype(F32)
                ).astype(BF16)
                final_cross(mine).start()
                final_end(mine).start()
            j = k - 2 * lag
            if 0 <= j < pairs:
                other = 2 * j + 1 - side
                final_cross(other).wait_recv()
                final_end(other).start()
        for j in range(pairs):
            mine, other = 2 * j + side, 2 * j + 1 - side
            to_cross(other).wait_send()
            final_cross(mine).wait_send()
            final_end(mine).wait_send()
            final_end(other).wait_send()


def chain_sum(part, collective):
    rows, width = part.shape
    count = rows // CHUNK
    return call(
        chain_sum_kernel,
        sds((rows, width), BF16),
        [VM],
        [
            pltpu.VMEM((rows, width), BF16),
            pltpu.VMEM((rows, width), BF16),
            pltpu.VMEM((rows, width), BF16),
            pltpu.VMEM((8, 128), F32),
        ]
        + [pltpu.SemaphoreType.DMA((count,)) for _ in range(8)]
        + [pltpu.SemaphoreType.DMA((1,))],
        collective,
        traffic=rows * width * 8,
    )(part)


def line_gather_kernel(x_ref, out_ref, local_sem, send_sem, recv_sem):
    tp = lax.axis_index("tp")
    count = out_ref.shape[0]
    greet([spot(tp=lax.rem(tp + i, count)) for i in range(1, count)])
    copies = [
        remote(x_ref, out_ref.at[tp], send_sem.at[i], recv_sem.at[tp], spot(tp=lax.rem(tp + i, count)))
        for i in range(1, count)
    ]
    for copy in copies:
        copy.start()
    own = pltpu.make_async_copy(x_ref, out_ref.at[tp], local_sem)
    own.start()
    for i in range(1, count):
        source = lax.rem(tp + i, count)
        remote(x_ref, out_ref.at[source], send_sem.at[0], recv_sem.at[source], spot()).wait_recv()
    for copy in copies:
        copy.wait_send()
    own.wait()


def line_gather(x, count, collective):
    return call(
        line_gather_kernel,
        sds((count,) + x.shape, x.dtype),
        [VM],
        [pltpu.SemaphoreType.DMA, pltpu.SemaphoreType.DMA((count,)), pltpu.SemaphoreType.DMA((count,))],
        collective,
        traffic=x.size * 2 * count,
    )(x)


def pieces_of(half):
    return max(p for p in (1, 2, 3, 4) if half % (16 * p) == 0)


def matrix_sum_kernel(g_ref, out_ref, core_ref, keep_ref, part_ref, y_ref, y_own, s_core, r_core, s_dp, r_dp, s_y, r_y, s_back, r_back):
    dp, ctx = lax.axis_index("dp"), lax.axis_index("ctx")
    owners = g_ref.shape[0]
    half = g_ref.shape[1] // 2
    pieces = pieces_of(half)
    rows = half // pieces
    low = lax.rem(ctx, 2)
    mate = spot(ctx=ctx + 1 - 2 * low)
    across = spot(ctx=lax.rem(ctx + 2, 4))
    peers = [spot(dp=lax.rem(dp + i, owners)) for i in range(1, owners)]
    greet([mate, across] + peers)
    mine, other = low * half, (1 - low) * half

    def at(base, p):
        return pl.ds(pl.multiple_of(base + p * rows, 16), rows)

    def core_copy(o, p):
        return remote(g_ref.at[o, at(other, p)], core_ref.at[o, at(0, p)], s_core.at[o, p], r_core.at[o, p], mate)

    def dp_copy(i, p):
        o = lax.rem(dp + i, owners)
        return remote(keep_ref.at[o, at(0, p)], part_ref.at[dp, at(0, p)], s_dp.at[o, p], r_dp.at[dp, p], peers[i - 1])

    def y_copy(p):
        return remote(y_own.at[at(0, p)], y_ref.at[at(0, p)], s_y.at[p], r_y.at[p], across)

    def back_copy(p):
        return remote(out_ref.at[at(mine, p)], out_ref.at[at(mine, p)], s_back.at[p], r_back.at[p], mate)

    for p in range(pieces):
        for o in range(owners):
            core_copy(o, p).start()
    for p in range(pieces):
        for o in range(owners):
            core_copy(o, p).wait_recv()
            keep_ref[o, at(0, p)] = (
                g_ref[o, at(mine, p)].astype(F32) + core_ref[o, at(0, p)].astype(F32)
            ).astype(BF16)
        for i in range(1, owners):
            dp_copy(i, p).start()
    for p in range(pieces):
        total = keep_ref[dp, at(0, p)].astype(F32)
        for i in range(1, owners):
            source = lax.rem(dp + i, owners)
            remote(keep_ref.at[0, at(0, p)], part_ref.at[source, at(0, p)], s_dp.at[0, p], r_dp.at[source, p], mate).wait_recv()
            total = total + part_ref[source, at(0, p)].astype(F32)
        y_own[at(0, p)] = total.astype(BF16)
        y_copy(p).start()
    for p in range(pieces):
        y_copy(p).wait_recv()
        out_ref[at(mine, p)] = y_own[at(0, p)].astype(F32) + y_ref[at(0, p)].astype(F32)
        back_copy(p).start()
    for p in range(pieces):
        for o in range(owners):
            core_copy(o, p).wait_send()
        for i in range(1, owners):
            dp_copy(i, p).wait_send()
        y_copy(p).wait_send()
        back_copy(p).wait_send()
        remote(out_ref.at[at(other, p)], out_ref.at[at(other, p)], s_back.at[p], r_back.at[p], mate).wait_recv()


def matrix_sum(grads, collective):
    owners, rows, width = grads.shape
    half = rows // 2
    pieces = pieces_of(half)
    return call(
        matrix_sum_kernel,
        sds((rows, width), F32),
        [VM],
        [
            pltpu.VMEM((owners, half, width), BF16),
            pltpu.VMEM((owners, half, width), BF16),
            pltpu.VMEM((owners, half, width), BF16),
            pltpu.VMEM((half, width), BF16),
            pltpu.VMEM((half, width), BF16),
            pltpu.SemaphoreType.DMA((owners, pieces)),
            pltpu.SemaphoreType.DMA((owners, pieces)),
            pltpu.SemaphoreType.DMA((owners, pieces)),
            pltpu.SemaphoreType.DMA((owners, pieces)),
            pltpu.SemaphoreType.DMA((pieces,)),
            pltpu.SemaphoreType.DMA((pieces,)),
            pltpu.SemaphoreType.DMA((pieces,)),
            pltpu.SemaphoreType.DMA((pieces,)),
        ],
        collective,
        traffic=grads.size * 8,
    )(grads)


def tree_tables(parent_row):
    block_count = parent_row.shape[0]
    ids = jnp.arange(block_count, dtype=jnp.int32)
    parent_map = (parent_row[:, None] == ids[None, :]).astype(jnp.int32)
    ancestor = jnp.eye(block_count, dtype=jnp.int32)
    for _ in range(DEPTH - 1):
        ancestor = jnp.eye(block_count, dtype=jnp.int32) + jnp.sum(
            parent_map[:, :, None] * ancestor[None, :, :], axis=1
        )
    depths = jnp.sum(ancestor, axis=1)
    gap = depths[:, None] - depths[None, :]
    return parent_map, ancestor, gap


def body(
    block_in, out_grad, parents, mixer_gain, mixer_shift, in_proj, in_bias, short_weight, short_bias,
    filter_one, filter_one_bias, filter_two, filter_two_bias, filter_freq, filter_out, skip_gain,
    out_proj, out_bias, feed_gain, feed_shift, feed_up, feed_up_bias, feed_down, feed_down_bias,
):
    x = block_in[0]
    g = out_grad[0]
    total_rows, width = x.shape
    channels = skip_gain.shape[0]
    blocks = total_rows // SEG
    hidden = feed_up.shape[1]
    tp_count = lax.axis_size("tp")
    tp_index = lax.axis_index("tp")
    owners = lax.axis_size("dp")
    first = lax.axis_index("ctx") * blocks
    all_blocks = parents.shape[1]

    in_all = jnp.transpose(lax.all_gather(in_proj, "dp", axis=0, tiled=True), (1, 0, 2))
    tails = lax.all_gather(x.reshape(blocks, SEG, width)[:, SEG - 2 :], "ctx", axis=0, tiled=True)
    tails = tails.reshape(2 * all_blocks, width)
    out_own = lax.all_gather(out_proj, "dp", axis=1, tiled=True)
    out_all = lax.all_gather(out_own, "tp", axis=0)
    up_all = lax.all_gather(feed_up, "dp", axis=0, tiled=True)
    down_all = lax.all_gather(feed_down, "dp", axis=1, tiled=True)
    last_all = lax.all_gather(filter_out, "dp", axis=0, tiled=True)

    parent_map, ancestor, gap = tree_tables(parents[0])
    none = DEPTH

    def local(table, axis=0):
        return lax.dynamic_slice_in_dim(table, first, blocks, axis)

    hop = jnp.where(ancestor > 0, gap, none)
    own_ids = first + jnp.arange(blocks)
    to_trunk = jnp.where(own_ids[:, None] == jnp.arange(4)[None, :], none, local(hop)[:, :4])
    own_parent = local(parent_map)
    is_leaf = own_ids >= 8
    branch_of = jnp.sum(own_parent[:, 4:8] * jnp.arange(4), axis=1)
    fwd_idx = jnp.concatenate(
        [to_trunk, jnp.where(is_leaf, 1, none)[:, None], branch_of[:, None], jnp.zeros((blocks, 2), jnp.int32)],
        axis=1,
    ).astype(jnp.int32)
    down_hop = local(hop, 1)
    not_self = jnp.arange(8)[:, None] != own_ids[None, :]
    near = jnp.where(not_self, down_hop[:8], none).T
    branch_reach = down_hop[4:8].T
    far = jnp.where(branch_reach < none, branch_reach + 1, none)
    back_idx = jnp.concatenate([near, far], axis=1).astype(jnp.int32)
    leaf_sel = parent_map[8:16, 4:8].T.astype(F32)

    row_id = jnp.arange(HEADS)
    tail_id = jnp.arange(2 * all_blocks)
    own_par = local(parents[0])
    pick = (
        (tail_id[None, None, :] == (2 * own_par[:, None] + row_id[None, :] - (HEADS - 2))[:, :, None])
        & (row_id[None, :, None] >= HEADS - 2)
        & (own_par[:, None, None] >= 0)
    ).astype(F32)
    child_of = parents[0][tail_id // 2]
    pick_child = (
        (child_of[None, None, :] == own_ids[:, None, None])
        & ((tail_id % 2)[None, None, :] == row_id[None, :, None])
    ).astype(F32)

    def make_taps(w1, b1, w2, b2, frequency, last_weight):
        return implicit_filter(
            w1, b1, w2, b2, frequency, last_weight, DEPTH * SEG, tp_index * channels, channels * tp_count
        )

    filter_taps, taps_back = jax.vjp(
        make_taps, filter_one, filter_one_bias, filter_two, filter_two_bias, filter_freq, last_all.astype(F32)
    )

    row = lambda v: v.reshape(1, -1)
    sw = short_weight.reshape(9, channels)
    low, proj, head, mixed, carried = call(
        mix_in_kernel,
        (
            sds((total_rows, width), BF16),
            sds((3, total_rows, channels), F32),
            sds((3, blocks, HEADS, channels), F32),
            sds((3, total_rows, channels), F32),
            sds((total_rows, channels), BF16),
        ),
        [VM] * 9,
        [pltpu.VMEM((3, HEADS + SEG, channels), F32)],
    )(x, tails, pick, in_all, in_bias, row(mixer_gain), row(mixer_shift), sw, short_bias)

    carried_b = carried.reshape(blocks, SEG, channels)
    incoming = lax.all_gather(carried_b, "ctx", axis=0, tiled=True)
    fh, fl, th, tl, sign = (jnp.asarray(t) for t in spectral_constants(SEG))
    skip = row(skip_gain)
    conv, gated, spec, filt = call(
        conv_fwd_kernel,
        (
            sds((total_rows, channels), F32),
            sds((total_rows, channels), BF16),
            sds((12, 2, SEG, channels), F32),
            sds((DEPTH + 1, 2, SEG, channels), F32),
        ),
        [SM] + [VM] * 11,
        [pltpu.VMEM((2 * SEG, channels), F32)],
    )(fwd_idx, carried_b, incoming[:4], incoming[4:8], filter_taps, mixed[0], skip, fh, fl, th, tl, sign)

    gated_all = line_gather(gated, tp_count, 1)
    residual, down_part, norm_part, grad_down, grad_up, grad_down_bias, grad_up_bias = call(
        feed_kernel,
        (
            sds((total_rows, width), F32),
            sds((total_rows, width), BF16),
            sds((total_rows, width), BF16),
            sds((hidden, width), F32),
            sds((width, hidden), F32),
            sds((1, width), F32),
            sds((1, hidden), F32),
        ),
        [VM] * 10,
    )(
        gated_all, out_all, x, g, row(out_bias), row(feed_gain), row(feed_shift), up_all, row(feed_up_bias), down_all
    )
    norm_sum = chain_sum(norm_part, 2)
    d_res, d_conv, d_long, d_zero, grad_out, grad_out_bias, grad_feed_gain, grad_feed_shift, grad_skip = call(
        feed_back_kernel,
        (
            sds((total_rows, width), F32),
            sds((total_rows, channels), F32),
            sds((total_rows, channels), BF16),
            sds((total_rows, channels), F32),
            sds((channels, width), F32),
            sds((1, width), F32),
            sds((1, width), F32),
            sds((1, width), F32),
            sds((1, channels), F32),
        ),
        [VM] * 9,
    )(residual, norm_sum, g, row(feed_gain), out_own, gated, mixed[0], conv, carried)

    d_long_b = d_long.reshape(blocks, SEG, channels)
    d_all = lax.all_gather(d_long_b, "ctx", axis=0, tiled=True)
    d_car, d_taps = call(
        conv_bwd_kernel,
        (sds((total_rows, channels), F32), sds((DEPTH * SEG, channels), F32)),
        [SM, SM, SM] + [VM] * 11,
        [
            pltpu.VMEM((16, 2, SEG, channels), F32),
            pltpu.VMEM((DEPTH + 1, 2, SEG, channels), F32),
            pltpu.VMEM((2 * SEG, channels), F32),
            pltpu.VMEM((8, 128), F32),
        ],
    )(fwd_idx, back_idx, leaf_sel, d_long_b, d_all, d_conv, spec, filt, skip, fh, fl, th, tl, sign)

    def top(v):
        return v.reshape(blocks, SEG, channels)[:, :2]

    heads = jnp.stack([top(d_zero), top(d_car) * top(mixed[2]), top(d_car) * top(mixed[1])], axis=1)
    heads = lax.all_gather(heads, "ctx", axis=0, tiled=True)
    heads = jnp.transpose(heads, (1, 0, 2, 3)).reshape(3, 2 * all_blocks, channels)
    proj_part, grad_in, grad_in_bias, grad_sw, grad_sb = call(
        mix_back_kernel,
        (
            sds((total_rows, width), BF16),
            sds((3, width, channels), F32),
            sds((3, channels), F32),
            sds((9, channels), F32),
            sds((3, channels), F32),
        ),
        [VM] * 10,
        [pltpu.VMEM((HEADS + SEG, channels), F32), pltpu.VMEM((HEADS + SEG, channels), F32)],
    )(d_zero, d_car, mixed, proj, head, heads, pick_child, sw, low, in_all)
    proj_sum = chain_sum(proj_part, 3)
    grad_x, grad_mixer_gain, grad_mixer_shift = call(
        norm_back_kernel,
        (sds((total_rows, width), F32), sds((1, width), F32), sds((1, width), F32)),
        [VM] * 4,
    )(x, proj_sum, d_res, row(mixer_gain))
    result = residual + chain_sum(down_part, 4).astype(F32) + feed_down_bias

    def share_rows(v):
        return v.reshape(owners, -1, 2 * width // 4)

    def share_cols(v):
        return jnp.transpose(v.reshape(v.shape[0], owners, -1), (1, 0, 2)).reshape(owners, -1, 2 * width // 4)

    packed = jnp.concatenate(
        [
            share_rows(jnp.transpose(grad_in, (1, 0, 2))).astype(BF16),
            share_cols(grad_out).astype(BF16),
            share_rows(grad_up).astype(BF16),
            share_cols(grad_down).astype(BF16),
        ],
        axis=1,
    )
    summed = matrix_sum(packed, 5)
    sizes = [width * 3 * channels, channels * width, width * hidden, hidden * width]
    marks = np.cumsum([0] + [s // owners // (2 * width // 4) for s in sizes])
    parts = [summed[marks[i] : marks[i + 1]] for i in range(4)]
    own_in = parts[0].reshape(width // owners, 3, channels)
    own_out = parts[1].reshape(channels, width // owners)
    own_up = parts[2].reshape(width // owners, hidden)
    own_down = parts[3].reshape(hidden, width // owners)

    g1, g1b, g2, g2b, gfreq, glast = taps_back(d_taps)
    glast = lax.psum_scatter(lax.psum(glast, "ctx"), "dp", scatter_dimension=0, tiled=True)
    share = 1.0 / tp_count
    vec = lax.psum(
        (grad_in_bias, grad_sw, grad_sb, grad_skip, grad_up_bias, grad_mixer_gain, grad_mixer_shift,
         grad_feed_gain, grad_feed_shift, grad_out_bias, grad_down_bias),
        ("dp", "ctx"),
    )
    g1, g1b, g2, g2b, gfreq = lax.psum((g1, g1b, g2, g2b, gfreq), ("dp", "ctx", "tp"))
    flat = lambda v: v.reshape(-1)
    return (
        result[None], grad_x[None], flat(vec[5]), flat(vec[6]), own_in, vec[0], vec[1].reshape(3, 3, channels),
        vec[2], g1, g1b, g2, g2b, gfreq, glast, flat(vec[3]), own_out, flat(vec[9]), flat(vec[7]), flat(vec[8]),
        own_up, flat(vec[4]), own_down, flat(vec[10]),
    )


def solution(mesh):
    in_specs = (
        P("dp", "ctx", None), P("dp", "ctx", None), P("dp", None), P(), P(), P("dp", None, "tp"), P(None, "tp"),
        P(None, None, "tp"), P(None, "tp"), P(), P(), P(), P(), P(), P("dp", "tp"), P("tp"), P("tp", "dp"), P(),
        P(), P(), P("dp", "tp"), P("tp"), P("tp", "dp"), P(),
    )
    out_specs = (
        P("dp", "ctx", None), P("dp", "ctx", None), P(), P(), P("dp", None, "tp"), P(None, "tp"),
        P(None, None, "tp"), P(None, "tp"), P(), P(), P(), P(), P(), P("dp", "tp"), P("tp"), P("tp", "dp"), P(),
        P(), P(), P("dp", "tp"), P("tp"), P("tp", "dp"), P(),
    )
    return jax.shard_map(body, mesh=mesh, in_specs=in_specs, out_specs=out_specs, check_vma=False)
```

```python
import functools
import math

import jax
import jax.numpy as jnp
import numpy as np
from jax import lax
from jax.experimental import pallas as pl
from jax.experimental.pallas import tpu as pltpu
from jax.sharding import PartitionSpec as P

SEG = 256
DEPTH = 6
HEADS = 8
EXACT = lax.Precision.HIGHEST
EPSILON = 1e-05
SLOW_RATE = -math.log(0.01) / 1.5
FAST_RATE = -math.log(0.01) / 0.3
SHIFT_FLOOR = 0.05
F32 = jnp.float32
BF16 = jnp.bfloat16
MESH = pl.DeviceIdType.MESH
VM = pl.BlockSpec(memory_space=pltpu.VMEM)
SM = pl.BlockSpec(memory_space=pltpu.SMEM)
LIMIT = 60 << 20


def sds(shape, dtype):
    return jax.ShapeDtypeStruct(shape, dtype)


HB = pl.BlockSpec(memory_space=pl.ANY)


def call(kernel, out_shape, in_specs, scratch=(), collective=None, flops=0, traffic=0, out_specs=None):
    many = isinstance(out_shape, (tuple, list))
    return pl.pallas_call(
        kernel,
        out_shape=out_shape,
        in_specs=in_specs,
        out_specs=out_specs or (tuple(VM for _ in out_shape) if many else VM),
        scratch_shapes=list(scratch),
        compiler_params=pltpu.CompilerParams(
            vmem_limit_bytes=LIMIT,
            collective_id=collective,
            has_side_effects=collective is not None,
        ),
        cost_estimate=pl.CostEstimate(flops=flops, bytes_accessed=traffic, transcendentals=0),
    )


def spectral_constants(block_len):
    freq = np.arange(block_len)[:, None]
    place = np.arange(block_len)[None, :]
    angle = ((2 * freq + 1) * place % (4 * block_len)) * (2.0 * math.pi / (4 * block_len))
    table = np.concatenate([np.cos(angle), -np.sin(angle)], axis=0).astype(np.float32)
    high = table.astype(jnp.bfloat16)
    low = (table - high.astype(np.float32)).astype(jnp.bfloat16)
    sign = np.where(np.arange(block_len) % 2 == 0, 1.0, -1.0).astype(np.float32)[:, None]
    return high, low, np.ascontiguousarray(high.T), np.ascontiguousarray(low.T), sign


def normalize(values):
    mean_value = jnp.mean(values, axis=-1, keepdims=True)
    centered = values - mean_value
    variance = jnp.mean(centered * centered, axis=-1, keepdims=True)
    scale = lax.rsqrt(variance + EPSILON)
    return centered * scale, scale


def split(values):
    high = values.astype(BF16)
    return high, (values - high.astype(F32)).astype(BF16)


def mm(lhs, rhs):
    return jnp.dot(lhs, rhs, preferred_element_type=F32)


def mm_nt(lhs, rhs):
    return lax.dot_general(lhs, rhs, (((1,), (1,)), ((), ())), preferred_element_type=F32)


def mm_tn(lhs, rhs):
    return lax.dot_general(lhs, rhs, (((0,), (0,)), ((), ())), preferred_element_type=F32)


def mm_split(high, low, values):
    v_high, v_low = split(values)
    return mm(high, v_high) + (mm(low, v_high) + mm(high, v_low))


def mix_in_kernel(
    x_ref, xt_ref, pick_ref, w_ref, bias_ref, gain_ref, shift_ref, sw_ref, sb_ref,
    low_ref, proj_ref, head_ref, mixed_ref, carried_ref, ext_ref,
):
    gain, shift = gain_ref[...], shift_ref[...]
    tails = normalize(xt_ref[...].astype(F32))[0] * gain + shift
    tails = tails.astype(BF16)
    tail_proj = [mm(tails, w_ref[g]) + bias_ref[g : g + 1] for g in range(3)]
    blocks = x_ref.shape[0] // SEG

    def one(s, unused):
        rows = pl.ds(pl.multiple_of(s * SEG, SEG), SEG)
        low = (normalize(x_ref[rows].astype(F32))[0] * gain + shift).astype(BF16)
        low_ref[rows] = low
        out = []
        for g in range(3):
            projected = mm(low, w_ref[g]) + bias_ref[g : g + 1]
            proj_ref[g, rows] = projected
            head = jnp.dot(pick_ref[s], tail_proj[g], precision=EXACT, preferred_element_type=F32)
            head_ref[g, s] = head
            ext_ref[g, 0:HEADS] = head
            ext_ref[g, HEADS : HEADS + SEG] = projected
            mixed = (
                sw_ref[3 * g : 3 * g + 1] * ext_ref[g, HEADS - 2 : HEADS - 2 + SEG]
                + sw_ref[3 * g + 1 : 3 * g + 2] * ext_ref[g, HEADS - 1 : HEADS - 1 + SEG]
                + sw_ref[3 * g + 2 : 3 * g + 3] * projected
                + sb_ref[g : g + 1]
            )
            mixed_ref[g, rows] = mixed
            out.append(mixed)
        carried_ref[rows] = (out[2] * out[1]).astype(BF16)
        return unused

    lax.fori_loop(0, blocks, one, 0)


FT = 64


def lineage(par_ref, block):
    out = []
    current = block
    for _ in range(DEPTH - 1):
        parent = par_ref[0, jnp.maximum(current, 0)]
        current = jnp.where(current >= 0, parent, -1)
        out.append(current)
    return out


def blend(dst, terms, rows, conj):
    re = im = None
    for a, b in terms:
        ar, ai = a[0, rows], a[1, rows]
        br, bi = b[0, rows], b[1, rows]
        if conj:
            pr, pi = ar * br + ai * bi, ar * bi - ai * br
        else:
            pr, pi = ar * br - ai * bi, ar * bi + ai * br
        re, im = (pr, pi) if re is None else (re + pr, im + pi)
    dst[0, rows] = re
    dst[1, rows] = im


def blend_all(dst, terms, conj):
    for t in range(SEG // FT):
        blend(dst, terms, slice(t * FT, (t + 1) * FT), conj)


def unpack_spectrum(th, tl, ref):
    high_re, low_re = split(ref[0])
    high_im, low_im = split(ref[1])
    a, b = slice(0, SEG), slice(SEG, 2 * SEG)
    return (
        mm(th[:, a], high_re) + mm(th[:, b], high_im)
        + (mm(tl[:, a], high_re) + mm(tl[:, b], high_im))
        + (mm(th[:, a], low_re) + mm(th[:, b], low_im))
    )


def filter_kernel(ft_ref, w1_ref, w2_ref, last_ref, freq_ref, net_ref, taps_ref):
    units, channels = last_ref.shape
    length = ft_ref.shape[1]
    tp = lax.axis_index("tp")
    width = channels * lax.axis_size("tp")
    exact = dict(precision=EXACT, preferred_element_type=F32)
    freq = freq_ref[...]
    pad = net_ref.shape[1] - units
    ones = jnp.where(lax.broadcasted_iota(jnp.int32, (pad, length), 0) == 0, 1.0, 0.0)
    net_ref[...] = jnp.zeros(net_ref.shape, F32)
    pre = jnp.dot(w1_ref[...], ft_ref[...], **exact)
    net_ref[0, 0:units] = pre
    net_ref[1, 0:units] = jnp.cos(freq * pre)
    net_ref[2, 0:units] = jnp.sin(freq * pre)
    net_ref[2, units:] = ones
    pre = jnp.dot(w2_ref[...], net_ref[2], **exact)
    net_ref[3, 0:units] = pre
    net_ref[4, 0:units] = jnp.cos(freq * pre)
    second = jnp.sin(freq * pre)
    net_ref[5, 0:units] = second
    raw = lax.dot_general(second, last_ref[...], (((0,), (0,)), ((), ())), **exact)
    time_pos = lax.broadcasted_iota(jnp.int32, (length, 1), 0).astype(F32) * (1.0 / (length - 1))
    channel = (lax.broadcasted_iota(jnp.int32, (1, channels), 1) + tp * channels).astype(F32)
    rate = SLOW_RATE + (FAST_RATE - SLOW_RATE) * channel * (1.0 / (width - 1))
    taps_ref[...] = raw * (jnp.exp(-time_pos * rate) + SHIFT_FLOOR)


def conv_fwd_kernel(
    par_ref, own_ref, all_ref, taps_ref, gate_ref, skip_ref,
    fh_ref, fl_ref, th_ref, tl_ref, sign_ref,
    conv_ref, gated_ref, spec_ref, filt_ref, acc_ref,
):
    blocks = own_ref.shape[0]
    ctx = lax.axis_index("ctx")
    fh, fl, th, tl = fh_ref[...], fl_ref[...], th_ref, tl_ref

    def source(j, unused):
        for base, ref, off in ((0, all_ref, 0), (4, all_ref, 4), (8, own_ref, 0)):
            part = ref[off + j]
            out = mm(fh, part) + mm(fl, part)
            spec_ref[base + j, 0] = out[:SEG]
            spec_ref[base + j, 1] = out[SEG:]
        return unused

    lax.fori_loop(0, blocks, source, 0)
    spec_ref[12] = jnp.zeros(spec_ref.shape[1:], F32)
    sign = sign_ref[...]
    last = None
    for j in range(DEPTH):
        part = taps_ref[j * SEG : (j + 1) * SEG]
        out = mm_split(fh, fl, part)
        re, im = out[:SEG], out[SEG:]
        if last is None:
            filt_ref[j, 0] = re
            filt_ref[j, 1] = im
        else:
            filt_ref[j, 0] = re - sign * last[1]
            filt_ref[j, 1] = im + sign * (last[0] - last[2])
        last = (re, im, part[0:1])

    def dest(s, unused):
        above = lineage(par_ref, ctx * blocks + s)
        places = [8 + s] + [jnp.where(a >= 0, a, 12) for a in above]
        blend_all(acc_ref, [(filt_ref.at[d], spec_ref.at[places[d]]) for d in range(DEPTH)], False)
        long_out = unpack_spectrum(th, tl, acc_ref) * (1.0 / SEG)
        place = pl.ds(pl.multiple_of(s * SEG, SEG), SEG)
        convolved = long_out + skip_ref[...] * own_ref[s].astype(F32)
        conv_ref[place] = convolved
        gated_ref[place] = (convolved * gate_ref[place]).astype(BF16)
        return unused

    lax.fori_loop(0, blocks, dest, 0)


def filter_features(length, bands, rows):
    positions = np.arange(length)
    time_pos = positions / (length - 1)
    freq = np.linspace(0.0001, bands - 1, bands)
    phases = (2.0 * math.pi / length * positions)[None, :] * freq[:, None]
    table = np.zeros((rows, length), np.float32)
    table[0] = time_pos
    table[1 : bands + 1] = np.cos(phases)
    table[bands + 1 : 2 * bands + 1] = -np.sin(phases)
    table[2 * bands + 1] = 1.0
    return table


def spot(**changes):
    base = {name: lax.axis_index(name) for name in ("dp", "ctx", "tp")}
    base.update(changes)
    return (base["dp"], base["ctx"], base["tp"])


def remote(src, dst, send, recv, where):
    return pltpu.make_async_remote_copy(
        src_ref=src, dst_ref=dst, send_sem=send, recv_sem=recv, device_id=where, device_id_type=MESH
    )


def greet(partners):
    barrier = pltpu.get_barrier_semaphore()
    for where in partners:
        pl.semaphore_signal(barrier, inc=1, device_id=where, device_id_type=MESH)
    pl.semaphore_wait(barrier, len(partners))


CHUNK = 32
PER = SEG // (2 * CHUNK)
LAG = 2


def chunk(c):
    return pl.ds(pl.multiple_of(c * CHUNK, CHUNK), CHUNK)


class LineSum:
    scratch_count = 11

    @staticmethod
    def scratch(rows, width):
        count = rows // CHUNK
        return [
            pltpu.VMEM((rows, width), BF16),
            pltpu.VMEM((rows // 2, width), BF16),
            pltpu.VMEM((rows // 2, width), BF16),
        ] + [pltpu.SemaphoreType.DMA((count,)) for _ in range(8)]

    def __init__(self, part, total, scratch):
        self.part, self.total = part, total
        self.end, self.mid, self.out = scratch[:3]
        self.sems = scratch[3:]
        self.pairs = part.shape[0] // (2 * CHUNK)
        tp = lax.axis_index("tp")
        self.inner = jnp.logical_and(tp > 0, tp < 3)
        self.outer = jnp.logical_not(self.inner)
        self.side = jnp.where(tp < 2, 0, 1)
        near = jnp.where(self.side == 0, 0, 3)
        far = jnp.where(self.side == 0, 1, 2)
        self.mate = spot(tp=jnp.where(self.inner, near, far))
        self.cross = spot(tp=3 - tp)

    def to_mid(self, c):
        return remote(self.part.at[chunk(c)], self.end.at[chunk(c)], self.sems[0].at[c], self.sems[1].at[c], self.mate)

    def to_cross(self, k):
        return remote(self.out.at[chunk(k)], self.mid.at[chunk(k)], self.sems[2].at[k], self.sems[3].at[k], self.cross)

    def final_end(self, c):
        at = self.total.at[chunk(c)]
        return remote(at, at, self.sems[4].at[c], self.sems[5].at[c], self.mate)

    def final_cross(self, c):
        at = self.total.at[chunk(c)]
        return remote(at, at, self.sems[6].at[c], self.sems[7].at[c], self.cross)

    def send_block(self, s):
        @pl.when(self.outer)
        def _():
            def one(i, unused):
                self.to_mid(s * 2 * PER + i).start()
                return unused

            lax.fori_loop(0, 2 * PER, one, 0)

    def step(self, k):
        pairs, side = self.pairs, self.side

        @pl.when(k < pairs)
        def _():
            other = 2 * k + 1 - side
            self.to_mid(2 * k).wait_recv()
            self.to_mid(2 * k + 1).wait_recv()
            self.out[chunk(k)] = (
                self.part[chunk(other)].astype(F32) + self.end[chunk(other)].astype(F32)
            ).astype(BF16)
            self.to_cross(k).start()

        j = k - LAG

        @pl.when(jnp.logical_and(j >= 0, j < pairs))
        def _():
            mine = 2 * j + side
            self.to_cross(j).wait_recv()
            self.total[chunk(mine)] = (
                self.part[chunk(mine)].astype(F32)
                + self.end[chunk(mine)].astype(F32)
                + self.mid[chunk(j)].astype(F32)
            ).astype(BF16)
            self.final_cross(mine).start()
            self.final_end(mine).start()

        i = k - 2 * LAG

        @pl.when(jnp.logical_and(i >= 0, i < pairs))
        def _():
            other = 2 * i + 1 - side
            self.final_cross(other).wait_recv()
            self.final_end(other).start()

    def steps(self, first, last):
        @pl.when(self.inner)
        def _():
            def one(k, unused):
                self.step(k)
                return unused

            lax.fori_loop(first, last, one, 0)

    def wait_block(self, s):
        @pl.when(self.outer)
        def _():
            def one(i, unused):
                self.final_end(s * 2 * PER + i).wait_recv()
                return unused

            lax.fori_loop(0, 2 * PER, one, 0)

    def drain(self):
        @pl.when(self.outer)
        def _():
            def one(c, unused):
                self.to_mid(c).wait_send()
                return unused

            lax.fori_loop(0, 2 * self.pairs, one, 0)

        @pl.when(self.inner)
        def _():
            def one(k, unused):
                mine, other = 2 * k + self.side, 2 * k + 1 - self.side
                self.to_cross(k).wait_send()
                self.final_cross(mine).wait_send()
                self.final_end(mine).wait_send()
                self.final_end(other).wait_send()
                return unused

            lax.fori_loop(0, self.pairs, one, 0)


def signal_all(partners):
    barrier = pltpu.get_barrier_semaphore()
    for where in partners:
        pl.semaphore_signal(barrier, inc=1, device_id=where, device_id_type=MESH)
    return barrier, len(partners)


def store_shares(stage_ref, tile, rows_per_tile, value):
    owners = stage_ref.shape[1]
    piece = stage_ref.shape[2]
    first = tile * rows_per_tile // piece
    for q in range(rows_per_tile // piece):
        owner, half = divmod(first + q, 2)
        stage_ref[half, owner] = value[q * piece : (q + 1) * piece].astype(BF16)


def feed_kernel(
    gated_ref, out_ref, x_ref, g_ref, ob_ref, gain_ref, shift_ref, up_ref, ub_ref, down_ref,
    mixed_ref, conv_ref, carried_ref,
    resid_ref, dpart_ref, dres_ref, dconv_ref, dzero_ref, dall_ref, gup_ref, gdown_ref, gout_ref,
    small_ref, gskip_ref,
    low_ref, hidden_ref, dpre_ref, npart_ref, nsum_ref, dmix_ref, own_ref, s_long, r_long, *line,
):
    groups = gated_ref.shape[0]
    width = x_ref.shape[1]
    blocks = x_ref.shape[0] // SEG
    tp, ctx = lax.axis_index("tp"), lax.axis_index("ctx")
    chain = LineSum(npart_ref, nsum_ref, line)
    barrier, count = signal_all([chain.mate, chain.cross] + [spot(ctx=lax.rem(ctx + i, 4)) for i in range(1, 4)])
    small_ref[...] = jnp.zeros(small_ref.shape, F32)
    gskip_ref[...] = jnp.zeros(gskip_ref.shape, F32)

    def core(s, unused):
        rows = pl.ds(pl.multiple_of(s * SEG, SEG), SEG)
        mixed = mm_nt(gated_ref[0, rows], out_ref[0])
        for z in range(1, groups):
            mixed = mixed + mm_nt(gated_ref[z, rows], out_ref[z])
        residual = x_ref[rows].astype(F32) + mixed + ob_ref[...]
        resid_ref[rows] = residual
        low = (normalize(residual)[0] * gain_ref[...] + shift_ref[...]).astype(BF16)
        low_ref[rows] = low
        pre = mm(low, up_ref[...]) + ub_ref[...]
        cdf = 0.5 * (1.0 + lax.erf(pre * math.sqrt(0.5)))
        hidden_ref[rows] = (pre * cdf).astype(BF16)
        slope = cdf + pre * (jnp.exp(-0.5 * pre * pre) * (1.0 / math.sqrt(2.0 * math.pi)))
        grad = g_ref[rows]
        d_pre = (mm(grad, down_ref[...]) * slope).astype(BF16)
        dpre_ref[rows] = d_pre
        npart_ref[rows] = mm_nt(d_pre, up_ref[...]).astype(BF16)
        small_ref[0:1] += jnp.sum(grad.astype(F32), axis=0, keepdims=True)
        small_ref[6:7] += jnp.sum(d_pre.astype(F32), axis=0, keepdims=True)

        @pl.when(s == 0)
        def _():
            pl.semaphore_wait(barrier, count)

        chain.send_block(s)
        return unused

    lax.fori_loop(0, blocks, core, 0)
    chain.steps(0, PER)

    def down(s, unused):
        rows = pl.ds(pl.multiple_of(s * SEG, SEG), SEG)
        dpart_ref[rows] = mm_nt(hidden_ref[rows], down_ref[...]).astype(BF16)
        return unused

    lax.fori_loop(0, blocks, down, 0)
    half = width // 2
    for t in range(2):
        columns = slice(t * half, (t + 1) * half)
        store_shares(gup_ref, t, half, mm_tn(low_ref[:, columns], dpre_ref[...]))
        store_shares(gdown_ref, t, half, mm_tn(g_ref[:, columns], hidden_ref[...]))

    def to_ctx(s, other):
        return remote(own_ref.at[s], dall_ref.at[ctx * blocks + s], s_long.at[other, s], r_long.at[ctx, s], spot(ctx=other))

    def back(s, unused):
        chain.steps((s + 1) * PER, (s + 2) * PER)
        chain.wait_block(s)
        rows = pl.ds(pl.multiple_of(s * SEG, SEG), SEG)
        xhat, scale = normalize(resid_ref[rows])
        dn = nsum_ref[rows].astype(F32)
        e = dn * gain_ref[...]
        d_res = g_ref[rows].astype(F32) + scale * (
            e - jnp.mean(e, axis=-1, keepdims=True) - xhat * jnp.mean(e * xhat, axis=-1, keepdims=True)
        )
        dres_ref[rows] = d_res
        small_ref[2:3] += jnp.sum(dn * xhat, axis=0, keepdims=True)
        small_ref[3:4] += jnp.sum(dn, axis=0, keepdims=True)
        d_mix = d_res.astype(BF16)
        dmix_ref[rows] = d_mix
        small_ref[1:2] += jnp.sum(d_mix.astype(F32), axis=0, keepdims=True)
        d_gated = mm(d_mix, out_ref[tp])
        d_conv = d_gated * mixed_ref[rows]
        dconv_ref[rows] = d_conv
        own_ref[s] = d_conv.astype(BF16)
        for other in range(3):
            @pl.when(other < ctx)
            def _():
                to_ctx(s, other).start()

        dzero_ref[rows] = d_gated * conv_ref[rows]
        gskip_ref[...] += jnp.sum(d_conv * carried_ref[rows].astype(F32), axis=0, keepdims=True)
        return unused

    lax.fori_loop(0, blocks, back, 0)
    for s in range(blocks):
        dall_ref[ctx * blocks + s] = own_ref[s]
    for t in range(2):
        columns = slice(t * half, (t + 1) * half)
        store_shares(gout_ref, t, half, mm_tn(dmix_ref[:, columns], gated_ref[tp]))
    chain.drain()
    for other in range(4):
        @pl.when(other < ctx)
        def _():
            for s in range(blocks):
                to_ctx(s, other).wait_send()

        @pl.when(other > ctx)
        def _():
            for s in range(blocks):
                at = dall_ref.at[other * blocks + s]
                remote(at, at, s_long.at[other, s], r_long.at[other, s], chain.mate).wait_recv()


def line_sum_kernel(part_ref, total_ref, *line):
    chain = LineSum(part_ref, total_ref, line)
    barrier, count = signal_all([chain.mate, chain.cross])
    pl.semaphore_wait(barrier, count)
    blocks = part_ref.shape[0] // SEG

    def send(s, unused):
        chain.send_block(s)
        return unused

    def wait(s, unused):
        chain.wait_block(s)
        return unused

    lax.fori_loop(0, blocks, send, 0)
    chain.steps(0, chain.pairs + 2 * LAG)
    lax.fori_loop(0, blocks, wait, 0)
    chain.drain()


def chain_sum(part, collective):
    rows, width = part.shape
    return call(line_sum_kernel, sds((rows, width), BF16), [VM], LineSum.scratch(rows, width), collective,
                traffic=rows * width * 8)(part)


def line_gather_kernel(x_ref, out_ref, local_sem, send_sem, recv_sem):
    tp = lax.axis_index("tp")
    count = out_ref.shape[0]
    greet([spot(tp=lax.rem(tp + i, count)) for i in range(1, count)])
    copies = [
        remote(x_ref, out_ref.at[tp], send_sem.at[i], recv_sem.at[tp], spot(tp=lax.rem(tp + i, count)))
        for i in range(1, count)
    ]
    for copy in copies:
        copy.start()
    own = pltpu.make_async_copy(x_ref, out_ref.at[tp], local_sem)
    own.start()
    for i in range(1, count):
        source = lax.rem(tp + i, count)
        remote(x_ref, out_ref.at[source], send_sem.at[0], recv_sem.at[source], spot()).wait_recv()
    for copy in copies:
        copy.wait_send()
    own.wait()


def line_gather(x, count, collective):
    return call(
        line_gather_kernel,
        sds((count,) + x.shape, x.dtype),
        [VM],
        [pltpu.SemaphoreType.DMA, pltpu.SemaphoreType.DMA((count,)), pltpu.SemaphoreType.DMA((count,))],
        collective,
        traffic=x.size * 2 * count,
    )(x)


class OwnerSum:
    scratch_count = 17

    @staticmethod
    def scratch(owners, shape):
        many = max(owners - 1, 1)
        return [
            pltpu.VMEM((owners,) + shape, BF16),
            pltpu.VMEM((owners,) + shape, BF16),
            pltpu.VMEM((many,) + shape, BF16),
            pltpu.VMEM(shape, BF16),
            pltpu.VMEM(shape, BF16),
            pltpu.SemaphoreType.DMA,
            pltpu.SemaphoreType.DMA,
            pltpu.SemaphoreType.DMA,
            pltpu.SemaphoreType.DMA((many,)),
            pltpu.SemaphoreType.DMA((many,)),
            pltpu.SemaphoreType.DMA,
            pltpu.SemaphoreType.DMA,
            pltpu.SemaphoreType.DMA,
            pltpu.SemaphoreType.DMA,
        ]

    def __init__(self, stage, out, scratch):
        self.stage, self.result = stage, out
        self.recv, self.keep, self.parts, self.y_own, self.y_in = scratch[:5]
        self.sems = scratch[5:]
        self.owners = stage.shape[1]
        self.dp, ctx = lax.axis_index("dp"), lax.axis_index("ctx")
        self.low = lax.rem(ctx, 2)
        self.mate = spot(ctx=ctx + 1 - 2 * self.low)
        self.across = spot(ctx=lax.rem(ctx + 2, 4))

    def load(self):
        return pltpu.make_async_copy(self.stage.at[self.low], self.keep, self.sems[0])

    def to_mate(self):
        return remote(self.stage.at[1 - self.low], self.recv, self.sems[1], self.sems[2], self.mate)

    def to_owner(self, i):
        owner = lax.rem(self.dp + i, self.owners)
        return remote(
            self.keep.at[owner], self.parts.at[self.owners - 1 - i], self.sems[3].at[i - 1],
            self.sems[4].at[self.owners - 1 - i], spot(dp=owner),
        )

    def from_owner(self, i):
        return remote(self.parts.at[i - 1], self.parts.at[i - 1], self.sems[3].at[i - 1], self.sems[4].at[i - 1], self.mate)

    def to_across(self):
        return remote(self.y_own, self.y_in, self.sems[5], self.sems[6], self.across)

    def to_back(self):
        at = self.result.at[self.low]
        return remote(at, at, self.sems[7], self.sems[8], self.mate)

    def begin(self):
        self.to_mate().start()
        self.load().start()

    def pair(self):
        self.load().wait()
        self.to_mate().wait_recv()
        for o in range(self.owners):
            self.keep[o] = (self.keep[o].astype(F32) + self.recv[o].astype(F32)).astype(BF16)
        for i in range(1, self.owners):
            self.to_owner(i).start()

    def own(self):
        total = self.keep[self.dp].astype(F32)
        for i in range(1, self.owners):
            self.from_owner(i).wait_recv()
            total = total + self.parts[i - 1].astype(F32)
        self.y_own[...] = total.astype(BF16)
        self.to_across().start()

    def cross(self):
        self.to_across().wait_recv()
        self.result[self.low] = self.y_own[...].astype(F32) + self.y_in[...].astype(F32)
        self.to_back().start()

    def finish(self):
        self.to_mate().wait_send()
        for i in range(1, self.owners):
            self.to_owner(i).wait_send()
        self.to_across().wait_send()
        self.to_back().wait_send()
        at = self.result.at[1 - self.low]
        remote(at, at, self.sems[7], self.sems[8], self.mate).wait_recv()


class SmallSum:
    @staticmethod
    def scratch(count, shape):
        return [
            pltpu.VMEM((count,) + shape, F32),
            pltpu.SemaphoreType.DMA((count,)),
            pltpu.SemaphoreType.DMA((count,)),
        ]

    def __init__(self, axis, scratch):
        self.axis = axis
        self.slots, self.send, self.recv = scratch
        self.count = self.slots.shape[0]
        self.me = lax.axis_index(axis)

    def copy(self, i):
        at = self.slots.at[self.me]
        other = lax.rem(self.me + i, self.count)
        return remote(at, at, self.send.at[i], self.recv.at[self.me], spot(**{self.axis: other}))

    def start(self, value):
        self.slots[self.me] = value
        for i in range(1, self.count):
            self.copy(i).start()

    def total(self):
        for i in range(1, self.count):
            other = lax.rem(self.me + i, self.count)
            at = self.slots.at[other]
            remote(at, at, self.send.at[i], self.recv.at[other], spot(**{self.axis: lax.rem(self.me + i, self.count)})).wait_recv()
        out = self.slots[0]
        for i in range(1, self.count):
            out = out + self.slots[i]
        return out

    def finish(self):
        for i in range(1, self.count):
            self.copy(i).wait_send()


def back_kernel(
    par_ref, dall_ref, dconv_ref, dzero_ref, mixed_ref, low_ref, w_ref, x_ref, dpart_ref,
    fh_ref, fl_ref, th_ref, tl_ref, sign_ref, sw_ref, skip_ref, mgain_ref, fbias_ref,
    ft_ref, w2_ref, last_ref, freq_ref, small_ref, gskip_ref,
    resid_hbm, dres_hbm, proj_hbm, head_hbm, spec_hbm, filt_hbm, net_hbm, sup_hbm, sdown_hbm, sout_hbm,
    result_hbm, gradx_hbm, oup_ref, odown_ref, oout_ref, oin_ref, va_ref, vd_ref, vl_ref, vf_ref,
    yown_ref, dcar_ref, dtaps_ref, stage_in, ppart_ref, dsum_ref, psum_ref, hd_ref, s_hd, r_hd, local, *rest,
):
    width = x_ref.shape[1]
    channels = dconv_ref.shape[1]
    total_rows = x_ref.shape[0]
    blocks = total_rows // SEG
    owners = sup_hbm.shape[1]
    ctx, tp, dp = lax.axis_index("ctx"), lax.axis_index("tp"), lax.axis_index("dp")
    rest = list(rest)

    def take(n):
        out = rest[:n]
        del rest[:n]
        return out

    down = LineSum(dpart_ref, dsum_ref, take(11))
    proj = LineSum(ppart_ref, psum_ref, take(11))
    early = [OwnerSum(s, o, take(14)) for s, o in ((sup_hbm, oup_ref), (sdown_hbm, odown_ref), (sout_hbm, oout_ref))]
    late = OwnerSum(stage_in, oin_ref, take(14))
    a_ctx, a_dp = SmallSum("ctx", take(3)), SmallSum("dp", take(3))
    d_ctx, d_dp, d_tp = SmallSum("ctx", take(3)), SmallSum("dp", take(3)), SmallSum("tp", take(3))
    l_ctx, l_dp = SmallSum("ctx", take(3)), SmallSum("dp", take(3))
    f_ctx, f_dp, f_tp = SmallSum("ctx", take(3)), SmallSum("dp", take(3)), SmallSum("tp", take(3))

    partners = [spot(tp=lax.rem(tp + i, 4)) for i in range(1, 4)]
    partners += [spot(ctx=lax.rem(ctx + i, 4)) for i in range(1, 4)]
    partners += [spot(dp=lax.rem(dp + i, owners)) for i in range(1, owners)]
    barrier, count = signal_all(partners)
    pl.semaphore_wait(barrier, count)
    for s in range(blocks):
        down.send_block(s)
    for job in early:
        job.begin()
    fh, fl, th, tl = fh_ref[...], fl_ref[...], th_ref, tl_ref
    scale = 1.0 / SEG

    def put(dst, value):
        dst[0] = value[:SEG] * scale
        dst[1] = value[SEG:] * scale

    def conv_inputs(filt_ref, more_ref, acc_ref):
        load = pltpu.make_async_copy(filt_hbm, filt_ref, local.at[0])
        load.start()

        def transform(s, unused):
            part = dall_ref[ctx * blocks + s]
            put(yown_ref.at[s], mm(fh, part) + mm(fl, part))
            return unused

        lax.fori_loop(0, blocks, transform, 0)
        load.wait()

        def leaf_sum(match):
            total = None
            for leaf in range(8, 16):
                term = jnp.where(match(leaf), 1.0, 0.0) * dall_ref[leaf].astype(F32)
                total = term if total is None else total + term
            return total

        def from_leaf(b):
            return lambda leaf: par_ref[0, leaf] == b

        def finish(s, terms):
            blend_all(acc_ref, terms, True)
            place = pl.ds(pl.multiple_of(s * SEG, SEG), SEG)
            dcar_ref[place] = unpack_spectrum(th, tl, acc_ref) + skip_ref[...] * dconv_ref[place]

        @pl.when(ctx == 0)
        def _():
            def gather(k, unused):
                p = k + 1
                total = None
                for b in range(4, 8):
                    term = jnp.where(par_ref[0, b] == p, 1.0, 0.0) * dall_ref[b].astype(F32)
                    total = term if total is None else total + term
                put(more_ref.at[k], mm_split(fh, fl, total))
                total = leaf_sum(lambda leaf: par_ref[0, par_ref[0, leaf]] == p)
                put(more_ref.at[3 + k], mm_split(fh, fl, total))
                return unused

            lax.fori_loop(0, 3, gather, 0)
            for a in range(4):
                terms = [(filt_ref.at[s - a], yown_ref.at[s]) for s in range(a, 4)]
                for p in range(max(a, 1), 4):
                    terms.append((filt_ref.at[p - a + 1], more_ref.at[p - 1]))
                    terms.append((filt_ref.at[p - a + 2], more_ref.at[p + 2]))
                finish(a, terms)

        @pl.when(ctx == 1)
        def _():
            def one(b, unused):
                put(more_ref.at[0], mm_split(fh, fl, leaf_sum(from_leaf(b + 4))))
                finish(b, [(filt_ref.at[0], yown_ref.at[b]), (filt_ref.at[1], more_ref.at[0])])
                return unused

            lax.fori_loop(0, 4, one, 0)

        @pl.when(ctx > 1)
        def _():
            def one(b, unused):
                finish(b, [(filt_ref.at[0], yown_ref.at[b])])
                return unused

            lax.fori_loop(0, 4, one, 0)

    pl.run_scoped(
        conv_inputs,
        pltpu.VMEM((DEPTH, 2, SEG, channels), F32),
        pltpu.VMEM((6, 2, SEG, channels), F32),
        pltpu.VMEM((2, SEG, channels), F32),
    )

    def to_ctx(i):
        at = hd_ref.at[pl.ds(ctx * blocks, blocks)]
        return remote(at, at, s_hd.at[i], r_hd.at[ctx], spot(ctx=lax.rem(ctx + i, 4)))

    for s in range(blocks):
        top = slice(s * SEG, s * SEG + HEADS)
        d_car = dcar_ref[top]
        rows = [dzero_ref[top], d_car * mixed_ref[1, top], d_car * mixed_ref[0, top]]
        for g in range(3):
            hd_ref[ctx * blocks + s, 2 * g : 2 * g + 2] = rows[g][0:2]
        hd_ref[ctx * blocks + s, 6:8] = jnp.zeros((2, channels), F32)
    for i in range(1, 4):
        to_ctx(i).start()
    down.steps(0, 3)
    for job in early:
        job.pair()

    def conv_filters(spec_ref, dfilt_ref):
        load = pltpu.make_async_copy(spec_hbm, spec_ref, local.at[0])
        load.start()
        load.wait()

        @pl.when(ctx == 0)
        def _():
            for d in range(4):
                blend_all(dfilt_ref.at[d], [(spec_ref.at[8 + s - d], yown_ref.at[s]) for s in range(d, 4)], True)
            dfilt_ref[4:6] = jnp.zeros((2, 2, SEG, channels), F32)

        @pl.when(ctx > 0)
        def _():
            places = []
            for s in range(blocks):
                above = lineage(par_ref, ctx * blocks + s)
                places.append([8 + s] + [jnp.where(a >= 0, a, 12) for a in above])
            for d in range(DEPTH):
                terms = [(spec_ref.at[places[s][d]], yown_ref.at[s]) for s in range(blocks)]
                blend_all(dfilt_ref.at[d], terms, True)

        down.steps(3, 6)
        sign = sign_ref[...]
        first_row = lax.broadcasted_iota(jnp.int32, (SEG, 1), 0) == 0
        for j in range(DEPTH):
            fix = None
            if j + 1 < DEPTH:
                nr, ni = dfilt_ref[j + 1, 0], dfilt_ref[j + 1, 1]
                fix = jnp.sum(sign * ni, axis=0, keepdims=True)
                dfilt_ref[j, 0] = dfilt_ref[j, 0] + sign * ni
                dfilt_ref[j, 1] = dfilt_ref[j, 1] - sign * nr
            taps = unpack_spectrum(th, tl, dfilt_ref.at[j])
            if fix is not None:
                taps = jnp.where(first_row, taps - fix, taps)
            dtaps_ref[j * SEG : (j + 1) * SEG] = taps

    pl.run_scoped(
        conv_filters,
        pltpu.VMEM((13, 2, SEG, channels), F32),
        pltpu.VMEM((DEPTH, 2, SEG, channels), F32),
    )
    down.steps(6, 9)

    va_ref[...] = jnp.zeros(va_ref.shape, F32)
    vd_ref[...] = small_ref[...]
    va_ref[15:16] = gskip_ref[...]
    for i in range(1, 4):
        other = lax.rem(ctx + i, 4)
        at = hd_ref.at[pl.ds(other * blocks, blocks)]
        remote(at, at, s_hd.at[i], r_hd.at[other], spot(ctx=other)).wait_recv()

    def mix_back(dp_ref, ext_ref, dm_ref, pin_ref, hin_ref):
        load_heads = pltpu.make_async_copy(head_hbm, hin_ref, local.at[1])
        load_heads.start()

        def fetch(s):
            rows = pl.ds(pl.multiple_of(s * SEG, SEG), SEG)
            return pltpu.make_async_copy(proj_hbm.at[:, rows], pin_ref.at[lax.rem(s, 2)], local.at[2 + lax.rem(s, 2)])

        fetch(0).start()
        load_heads.wait()

        def one(s, unused):
            rows = pl.ds(pl.multiple_of(s * SEG, SEG), SEG)
            slot = lax.rem(s, 2)
            fetch(s).wait()

            @pl.when(s + 1 < blocks)
            def _():
                fetch(s + 1).start()

            mine = ctx * blocks + s
            child = None
            for b in range(1, 16):
                term = jnp.where(par_ref[0, b] == mine, 1.0, 0.0) * hd_ref[b]
                child = term if child is None else child + term
            part = None
            for g in range(3):
                if g == 0:
                    dm = dzero_ref[rows]
                else:
                    dm = dcar_ref[rows] * mixed_ref[2 - g, rows]
                ext_ref[0:HEADS] = hin_ref[g, s]
                ext_ref[HEADS : HEADS + SEG] = pin_ref[slot, g]
                for k in range(3):
                    piece = ext_ref[HEADS - 2 + k : HEADS - 2 + k + SEG]
                    va_ref[3 * g + k : 3 * g + k + 1] += jnp.sum(piece * dm, axis=0, keepdims=True)
                va_ref[12 + g : 13 + g] += jnp.sum(dm, axis=0, keepdims=True)
                dm_ref[0:SEG] = dm
                dm_ref[SEG : SEG + 2] = child[2 * g : 2 * g + 2]
                d_proj = (
                    sw_ref[3 * g + 2 : 3 * g + 3] * dm
                    + sw_ref[3 * g + 1 : 3 * g + 2] * dm_ref[1 : 1 + SEG]
                    + sw_ref[3 * g : 3 * g + 1] * dm_ref[2 : 2 + SEG]
                ).astype(BF16)
                dp_ref[g, rows] = d_proj
                va_ref[9 + g : 10 + g] += jnp.sum(d_proj.astype(F32), axis=0, keepdims=True)
                term = mm_nt(d_proj, w_ref[g])
                part = term if part is None else part + term
            ppart_ref[rows] = part.astype(BF16)
            proj.send_block(s)
            xhat = normalize(x_ref[rows].astype(F32))[0]
            vd_ref[4:5] += jnp.sum(part * xhat, axis=0, keepdims=True)
            vd_ref[5:6] += jnp.sum(part, axis=0, keepdims=True)
            down.steps(9 + s, 10 + s)
            return unused

        lax.fori_loop(0, blocks, one, 0)
        half = width // 2
        piece = stage_in.shape[3]
        for t in range(2):
            columns = slice(t * half, (t + 1) * half)
            for g in range(3):
                value = mm_tn(low_ref[:, columns], dp_ref[g])
                first = t * half // piece
                for q in range(half // piece):
                    owner, side = divmod(first + q, 2)
                    stage_in[side, owner, g] = value[q * piece : (q + 1) * piece].astype(BF16)

    pl.run_scoped(
        mix_back,
        pltpu.VMEM((3, total_rows, channels), BF16),
        pltpu.VMEM((HEADS + SEG, channels), F32),
        pltpu.VMEM((HEADS + SEG, channels), F32),
        pltpu.VMEM((2, 3, SEG, channels), F32),
        pltpu.VMEM((3, blocks, HEADS, channels), F32),
    )
    late.begin()
    for job in early:
        job.own()
    down.steps(13, 15)

    def filter_back(net_ref):
        load = pltpu.make_async_copy(net_hbm, net_ref, local.at[1])
        load.start()
        time_pos = lax.broadcasted_iota(jnp.int32, (DEPTH * SEG, 1), 0).astype(F32) * (1.0 / (DEPTH * SEG - 1))
        channel = (lax.broadcasted_iota(jnp.int32, (1, channels), 1) + tp * channels).astype(F32)
        rate = SLOW_RATE + (FAST_RATE - SLOW_RATE) * channel * (1.0 / (width - 1))
        d_raw = dtaps_ref[...] * (jnp.exp(-time_pos * rate) + SHIFT_FLOOR)
        load.wait()
        exact = dict(precision=EXACT, preferred_element_type=F32)
        nt = (((1,), (1,)), ((), ()))
        units = last_ref.shape[0]
        freq = freq_ref[...]
        l_ctx.start(jnp.dot(net_ref[5, 0:units], d_raw, **exact))
        d_two = lax.dot_general(last_ref[...], d_raw, nt, **exact)
        s_two = d_two * net_ref[4, 0:units]
        p_two = s_two * freq
        g_two = lax.dot_general(p_two, net_ref[2], nt, **exact)
        d_one = lax.dot_general(w2_ref[...], p_two, (((0,), (0,)), ((), ())), **exact)[0:units]
        s_one = d_one * net_ref[1, 0:units]
        p_one = s_one * freq
        g_one = lax.dot_general(p_one, ft_ref[...], nt, **exact)
        g_freq = jnp.sum(s_one * net_ref[0, 0:units] + s_two * net_ref[3, 0:units], axis=1, keepdims=True)
        vf_ref[...] = jnp.zeros(vf_ref.shape, F32)
        vf_ref[0, :, 0 : g_one.shape[1]] = g_one
        vf_ref[1, :, 0 : g_two.shape[1]] = g_two
        vf_ref[2, :, 0:1] = g_freq
        f_ctx.start(vf_ref[...])

    pl.run_scoped(filter_back, pltpu.VMEM(net_hbm.shape, F32))
    a_ctx.start(va_ref[...])
    d_ctx.start(vd_ref[...])
    late.pair()
    down.steps(15, 17)
    for job in early:
        job.cross()
    for one, two in ((a_ctx, a_dp), (d_ctx, d_dp), (l_ctx, l_dp), (f_ctx, f_dp)):
        two.start(one.total())
    down.steps(17, 20)
    late.own()

    def results(in_ref, out_ref):
        def fetch(src, s):
            rows = pl.ds(pl.multiple_of(s * SEG, SEG), SEG)
            return pltpu.make_async_copy(src.at[rows], in_ref.at[lax.rem(s, 2)], local.at[lax.rem(s, 2)])

        def flush(dst, s):
            rows = pl.ds(pl.multiple_of(s * SEG, SEG), SEG)
            return pltpu.make_async_copy(out_ref.at[s], dst.at[rows], local.at[4 + s])

        fetch(resid_hbm, 0).start()

        def one(s, unused):
            rows = pl.ds(pl.multiple_of(s * SEG, SEG), SEG)
            fetch(resid_hbm, s).wait()

            @pl.when(s + 1 < blocks)
            def _():
                fetch(resid_hbm, s + 1).start()

            proj.steps(s, s + 1)
            down.wait_block(s)
            out_ref[s] = in_ref[lax.rem(s, 2)] + dsum_ref[rows].astype(F32) + fbias_ref[...]
            flush(result_hbm, s).start()
            return unused

        lax.fori_loop(0, blocks, one, 0)
        va_ref[...] = a_dp.total()
        vl_ref[...] = l_dp.total()
        sums = d_dp.total()
        vd_ref[...] = sums
        d_tp.start(sums)
        f_tp.start(f_dp.total())
        fetch(dres_hbm, 0).start()

        def two(s, unused):
            rows = pl.ds(pl.multiple_of(s * SEG, SEG), SEG)
            fetch(dres_hbm, s).wait()

            @pl.when(s + 1 < blocks)
            def _():
                fetch(dres_hbm, s + 1).start()

            xhat, spread = normalize(x_ref[rows].astype(F32))
            proj.steps((s + 1) * PER, (s + 2) * PER)
            proj.wait_block(s)
            e = psum_ref[rows].astype(F32) * mgain_ref[...]
            flush(result_hbm, s).wait()
            out_ref[s] = in_ref[lax.rem(s, 2)] + spread * (
                e - jnp.mean(e, axis=-1, keepdims=True) - xhat * jnp.mean(e * xhat, axis=-1, keepdims=True)
            )
            flush(gradx_hbm, s).start()

            @pl.when(s == 0)
            def _():
                late.cross()

            return unused

        lax.fori_loop(0, blocks, two, 0)
        for s in range(blocks):
            flush(gradx_hbm, s).wait()

    pl.run_scoped(
        results,
        pltpu.VMEM((2, SEG, width), F32),
        pltpu.VMEM((blocks, SEG, width), F32),
    )
    vd_ref[4:6] = d_tp.total()[4:6]
    vf_ref[...] = f_tp.total()
    for job in (a_ctx, a_dp, d_ctx, d_dp, d_tp, l_ctx, l_dp, f_ctx, f_dp, f_tp):
        job.finish()
    for job in early + [late]:
        job.finish()
    for i in range(1, 4):
        to_ctx(i).wait_send()
    down.drain()
    proj.drain()


def body(
    block_in, out_grad, parents, mixer_gain, mixer_shift, in_proj, in_bias, short_weight, short_bias,
    filter_one, filter_one_bias, filter_two, filter_two_bias, filter_freq, filter_out, skip_gain,
    out_proj, out_bias, feed_gain, feed_shift, feed_up, feed_up_bias, feed_down, feed_down_bias,
):
    x = block_in[0]
    g = out_grad[0]
    total_rows, width = x.shape
    channels = skip_gain.shape[0]
    blocks = total_rows // SEG
    hidden = feed_up.shape[1]
    tp_count = lax.axis_size("tp")
    tp_index = lax.axis_index("tp")
    owners = lax.axis_size("dp")
    first = lax.axis_index("ctx") * blocks
    all_blocks = parents.shape[1]

    in_all = jnp.transpose(lax.all_gather(in_proj, "dp", axis=0, tiled=True), (1, 0, 2))
    tails = lax.all_gather(x.reshape(blocks, SEG, width)[:, SEG - 2 :], "ctx", axis=0, tiled=True)
    tails = tails.reshape(2 * all_blocks, width)
    out_own = lax.all_gather(out_proj.T, "dp", axis=0, tiled=True)
    out_all = lax.all_gather(out_own, "tp", axis=0)
    up_all = lax.all_gather(feed_up, "dp", axis=0, tiled=True)
    down_all = lax.all_gather(feed_down.T, "dp", axis=0, tiled=True)
    last_all = lax.all_gather(filter_out, "dp", axis=0, tiled=True)

    own_par = lax.dynamic_slice_in_dim(parents[0], first, blocks, 0)
    row_id = jnp.arange(HEADS)
    tail_id = jnp.arange(2 * all_blocks)
    pick = (
        (tail_id[None, None, :] == (2 * own_par[:, None] + row_id[None, :] - (HEADS - 2))[:, :, None])
        & (row_id[None, :, None] >= HEADS - 2)
        & (own_par[:, None, None] >= 0)
    ).astype(F32)
    units, features = filter_one.shape[1], filter_one.shape[0]
    feat_rows = 40
    ft = jnp.asarray(filter_features(DEPTH * SEG, (features - 1) // 2, feat_rows))
    w1 = jnp.concatenate(
        [filter_one.T, filter_one_bias[:, None], jnp.zeros((units, feat_rows - features - 1), F32)], axis=1
    )
    w2 = jnp.concatenate([filter_two.T, filter_two_bias[:, None], jnp.zeros((units, 7), F32)], axis=1)
    last = last_all.astype(F32)
    freq = filter_freq[:, None]
    net, filter_taps = call(
        filter_kernel,
        (sds((6, units + 8, DEPTH * SEG), F32), sds((DEPTH * SEG, channels), F32)),
        [VM] * 5,
    )(ft, w1, w2, last, freq)

    row = lambda v: v.reshape(1, -1)
    sw = short_weight.reshape(9, channels)
    low, proj, head, mixed, carried = call(
        mix_in_kernel,
        (
            sds((total_rows, width), BF16),
            sds((3, total_rows, channels), F32),
            sds((3, blocks, HEADS, channels), F32),
            sds((3, total_rows, channels), F32),
            sds((total_rows, channels), BF16),
        ),
        [VM] * 9,
        [pltpu.VMEM((3, HEADS + SEG, channels), F32)],
    )(x, tails, pick, in_all, in_bias, row(mixer_gain), row(mixer_shift), sw, short_bias)

    carried_b = carried.reshape(blocks, SEG, channels)
    incoming = lax.all_gather(carried_b, "ctx", axis=0, tiled=True)
    fh, fl, th, tl, sign = (jnp.asarray(t) for t in spectral_constants(SEG))
    skip = row(skip_gain)
    conv, gated, spec, filt = call(
        conv_fwd_kernel,
        (
            sds((total_rows, channels), F32),
            sds((total_rows, channels), BF16),
            sds((13, 2, SEG, channels), F32),
            sds((DEPTH, 2, SEG, channels), F32),
        ),
        [SM] + [VM] * 10,
        [pltpu.VMEM((2, SEG, channels), F32)],
    )(parents, carried_b, incoming, filter_taps, mixed[0], skip, fh, fl, th, tl, sign)

    gated_all = line_gather(gated, tp_count, 1)
    piece = width // owners // 2
    (residual, down_part, d_res, d_conv, d_zero, d_all, stage_up, stage_down, stage_out,
     small, grad_skip) = call(
        feed_kernel,
        (
            sds((total_rows, width), F32),
            sds((total_rows, width), BF16),
            sds((total_rows, width), F32),
            sds((total_rows, channels), F32),
            sds((total_rows, channels), F32),
            sds((all_blocks, SEG, channels), BF16),
            sds((2, owners, piece, hidden), BF16),
            sds((2, owners, piece, hidden), BF16),
            sds((2, owners, piece, channels), BF16),
            sds((8, width), F32),
            sds((1, channels), F32),
        ),
        [VM] * 13,
        [
            pltpu.VMEM((total_rows, width), BF16),
            pltpu.VMEM((total_rows, hidden), BF16),
            pltpu.VMEM((total_rows, hidden), BF16),
            pltpu.VMEM((total_rows, width), BF16),
            pltpu.VMEM((total_rows, width), BF16),
            pltpu.VMEM((total_rows, width), BF16),
            pltpu.VMEM((blocks, SEG, channels), BF16),
            pltpu.SemaphoreType.DMA((4, blocks)),
            pltpu.SemaphoreType.DMA((4, blocks)),
        ]
        + LineSum.scratch(total_rows, width),
        2,
    )(
        gated_all, out_all, x, g, row(out_bias), row(feed_gain), row(feed_shift), up_all, row(feed_up_bias), down_all,
        mixed[0], conv, carried,
    )
    flat_shapes = [(piece, hidden), (piece, hidden), (piece, channels), (3, piece, channels)]
    scratch = [
        pltpu.VMEM((blocks, 2, SEG, channels), F32),
        pltpu.VMEM((total_rows, channels), F32),
        pltpu.VMEM((DEPTH * SEG, channels), F32),
        pltpu.VMEM((2, owners, 3, piece, channels), BF16),
        pltpu.VMEM((total_rows, width), BF16),
        pltpu.VMEM((total_rows, width), BF16),
        pltpu.VMEM((total_rows, width), BF16),
        pltpu.VMEM((all_blocks, HEADS, channels), F32),
        pltpu.SemaphoreType.DMA((4,)),
        pltpu.SemaphoreType.DMA((4,)),
        pltpu.SemaphoreType.DMA((8,)),
    ]
    scratch += LineSum.scratch(total_rows, width) * 2
    for shape in flat_shapes:
        scratch += OwnerSum.scratch(owners, shape)
    for shape, axes in (
        ((16, channels), 2), ((8, width), 3), ((units, channels), 2), ((3, units, 128), 3),
    ):
        for count in (4, owners, tp_count)[:axes]:
            scratch += SmallSum.scratch(count, shape)
    result, grad_x, own_up, own_down, own_out, own_in, va, vd, vl, vf = call(
        back_kernel,
        (
            sds((total_rows, width), F32),
            sds((total_rows, width), F32),
            sds((2, piece, hidden), F32),
            sds((2, piece, hidden), F32),
            sds((2, piece, channels), F32),
            sds((2, 3, piece, channels), F32),
            sds((16, channels), F32),
            sds((8, width), F32),
            sds((units, channels), F32),
            sds((3, units, 128), F32),
        ),
        [SM] + [VM] * 23 + [HB] * 10,
        scratch,
        3,
        out_specs=(HB, HB) + (VM,) * 8,
    )(
        parents, d_all, d_conv, d_zero, mixed[1:], low, in_all, x, down_part, fh, fl, th, tl, sign, sw, skip,
        row(mixer_gain), row(feed_down_bias), ft, w2, last, freq, small, grad_skip,
        residual, d_res, proj, head, spec, filt, net, stage_up, stage_down, stage_out,
    )
    dp_index = lax.axis_index("dp")
    own_last = lax.dynamic_slice_in_dim(vl, dp_index * (units // owners), units // owners, 0)
    return (
        result[None], grad_x[None], vd[4], vd[5],
        jnp.transpose(own_in, (0, 2, 1, 3)).reshape(width // owners, 3, channels),
        va[9:12], va[0:9].reshape(3, 3, channels), va[12:15],
        vf[0, :, :features].T, vf[0, :, features], vf[1, :, :units].T, vf[1, :, units], vf[2, :, 0],
        own_last, va[15], own_out.reshape(width // owners, channels).T, vd[1], vd[2], vd[3],
        own_up.reshape(width // owners, hidden), vd[6], own_down.reshape(width // owners, hidden).T, vd[0],
    )


def solution(mesh):
    in_specs = (
        P("dp", "ctx", None), P("dp", "ctx", None), P("dp", None), P(), P(), P("dp", None, "tp"), P(None, "tp"),
        P(None, None, "tp"), P(None, "tp"), P(), P(), P(), P(), P(), P("dp", "tp"), P("tp"), P("tp", "dp"), P(),
        P(), P(), P("dp", "tp"), P("tp"), P("tp", "dp"), P(),
    )
    out_specs = (
        P("dp", "ctx", None), P("dp", "ctx", None), P(), P(), P("dp", None, "tp"), P(None, "tp"),
        P(None, None, "tp"), P(None, "tp"), P(), P(), P(), P(), P(), P("dp", "tp"), P("tp"), P("tp", "dp"), P(),
        P(), P(), P("dp", "tp"), P("tp"), P("tp", "dp"), P(),
    )
    return jax.shard_map(body, mesh=mesh, in_specs=in_specs, out_specs=out_specs, check_vma=False)
```

```python
import functools
import math

import jax
import jax.numpy as jnp
import numpy as np
from jax import lax
from jax.experimental import pallas as pl
from jax.experimental.pallas import tpu as pltpu
from jax.sharding import PartitionSpec as P

SEG = 256
DEPTH = 6
HEADS = 8
EXACT = lax.Precision.HIGHEST
EPSILON = 1e-05
SLOW_RATE = -math.log(0.01) / 1.5
FAST_RATE = -math.log(0.01) / 0.3
SHIFT_FLOOR = 0.05
F32 = jnp.float32
BF16 = jnp.bfloat16
MESH = pl.DeviceIdType.MESH
VM = pl.BlockSpec(memory_space=pltpu.VMEM)
SM = pl.BlockSpec(memory_space=pltpu.SMEM)
LIMIT = 60 << 20


def sds(shape, dtype):
    return jax.ShapeDtypeStruct(shape, dtype)


HB = pl.BlockSpec(memory_space=pl.ANY)


def call(kernel, out_shape, in_specs, scratch=(), collective=None, flops=0, traffic=0, out_specs=None):
    many = isinstance(out_shape, (tuple, list))
    return pl.pallas_call(
        kernel,
        out_shape=out_shape,
        in_specs=in_specs,
        out_specs=out_specs or (tuple(VM for _ in out_shape) if many else VM),
        scratch_shapes=list(scratch),
        compiler_params=pltpu.CompilerParams(
            vmem_limit_bytes=LIMIT,
            collective_id=collective,
            has_side_effects=collective is not None,
        ),
        cost_estimate=pl.CostEstimate(flops=flops, bytes_accessed=traffic, transcendentals=0),
    )


def spectral_constants(block_len):
    freq = np.arange(block_len)[:, None]
    place = np.arange(block_len)[None, :]
    angle = ((2 * freq + 1) * place % (4 * block_len)) * (2.0 * math.pi / (4 * block_len))
    table = np.concatenate([np.cos(angle), -np.sin(angle)], axis=0).astype(np.float32)
    high = table.astype(jnp.bfloat16)
    low = (table - high.astype(np.float32)).astype(jnp.bfloat16)
    sign = np.where(np.arange(block_len) % 2 == 0, 1.0, -1.0).astype(np.float32)[:, None]
    return high, low, np.ascontiguousarray(high.T), np.ascontiguousarray(low.T), sign


def normalize(values):
    mean_value = jnp.mean(values, axis=-1, keepdims=True)
    centered = values - mean_value
    variance = jnp.mean(centered * centered, axis=-1, keepdims=True)
    scale = lax.rsqrt(variance + EPSILON)
    return centered * scale, scale


def split(values):
    high = values.astype(BF16)
    return high, (values - high.astype(F32)).astype(BF16)


def mm(lhs, rhs):
    return jnp.dot(lhs, rhs, preferred_element_type=F32)


def mm_nt(lhs, rhs):
    return lax.dot_general(lhs, rhs, (((1,), (1,)), ((), ())), preferred_element_type=F32)


def mm_tn(lhs, rhs):
    return lax.dot_general(lhs, rhs, (((0,), (0,)), ((), ())), preferred_element_type=F32)


def mm_split(high, low, values):
    v_high, v_low = split(values)
    return mm(high, v_high) + (mm(low, v_high) + mm(high, v_low))


FT = 32


def lineage(par_ref, block):
    out = []
    current = block
    for _ in range(DEPTH - 1):
        parent = par_ref[0, jnp.maximum(current, 0)]
        current = jnp.where(current >= 0, parent, -1)
        out.append(current)
    return out


def blend_all(dst, terms, conj):
    def tile(t, unused):
        rows = pl.ds(pl.multiple_of(t * FT, FT), FT)
        re = im = None
        for a, b in terms:
            ar, ai = a[0, rows], a[1, rows]
            br, bi = b[0, rows], b[1, rows]
            if conj:
                pr, pi = ar * br + ai * bi, ar * bi - ai * br
            else:
                pr, pi = ar * br - ai * bi, ar * bi + ai * br
            re, im = (pr, pi) if re is None else (re + pr, im + pi)
        dst[0, rows] = re
        dst[1, rows] = im
        return unused

    lax.fori_loop(0, SEG // FT, tile, 0)


def unpack_spectrum(th, tl, ref):
    high_re, low_re = split(ref[0])
    high_im, low_im = split(ref[1])
    a, b = slice(0, SEG), slice(SEG, 2 * SEG)
    return (
        mm(th[:, a], high_re) + mm(th[:, b], high_im)
        + (mm(tl[:, a], high_re) + mm(tl[:, b], high_im))
        + (mm(th[:, a], low_re) + mm(th[:, b], low_im))
    )


def filter_features(length, bands, rows):
    positions = np.arange(length)
    time_pos = positions / (length - 1)
    freq = np.linspace(0.0001, bands - 1, bands)
    phases = (2.0 * math.pi / length * positions)[None, :] * freq[:, None]
    table = np.zeros((rows, length), np.float32)
    table[0] = time_pos
    table[1 : bands + 1] = np.cos(phases)
    table[bands + 1 : 2 * bands + 1] = -np.sin(phases)
    table[2 * bands + 1] = 1.0
    return table


def spot(**changes):
    base = {name: lax.axis_index(name) for name in ("dp", "ctx", "tp")}
    base.update(changes)
    return (base["dp"], base["ctx"], base["tp"])


def remote(src, dst, send, recv, where):
    return pltpu.make_async_remote_copy(
        src_ref=src, dst_ref=dst, send_sem=send, recv_sem=recv, device_id=where, device_id_type=MESH
    )


def greet(partners):
    barrier = pltpu.get_barrier_semaphore()
    for where in partners:
        pl.semaphore_signal(barrier, inc=1, device_id=where, device_id_type=MESH)
    pl.semaphore_wait(barrier, len(partners))


CHUNK = 32
PER = SEG // (2 * CHUNK)
LAG = 2


def chunk(c):
    return pl.ds(pl.multiple_of(c * CHUNK, CHUNK), CHUNK)


class LineSum:
    scratch_count = 11

    @staticmethod
    def scratch(rows, width):
        count = rows // CHUNK
        return [
            pltpu.VMEM((rows, width), BF16),
            pltpu.VMEM((rows // 2, width), BF16),
            pltpu.VMEM((rows // 2, width), BF16),
        ] + [pltpu.SemaphoreType.DMA((count,)) for _ in range(8)]

    def __init__(self, part, total, scratch):
        self.part, self.total = part, total
        self.end, self.mid, self.out = scratch[:3]
        self.sems = scratch[3:]
        self.pairs = part.shape[0] // (2 * CHUNK)
        tp = lax.axis_index("tp")
        self.inner = jnp.logical_and(tp > 0, tp < 3)
        self.outer = jnp.logical_not(self.inner)
        self.side = jnp.where(tp < 2, 0, 1)
        near = jnp.where(self.side == 0, 0, 3)
        far = jnp.where(self.side == 0, 1, 2)
        self.mate = spot(tp=jnp.where(self.inner, near, far))
        self.cross = spot(tp=3 - tp)

    def to_mid(self, c):
        return remote(self.part.at[chunk(c)], self.end.at[chunk(c)], self.sems[0].at[c], self.sems[1].at[c], self.mate)

    def to_cross(self, k):
        return remote(self.out.at[chunk(k)], self.mid.at[chunk(k)], self.sems[2].at[k], self.sems[3].at[k], self.cross)

    def final_end(self, c):
        at = self.total.at[chunk(c)]
        return remote(at, at, self.sems[4].at[c], self.sems[5].at[c], self.mate)

    def final_cross(self, c):
        at = self.total.at[chunk(c)]
        return remote(at, at, self.sems[6].at[c], self.sems[7].at[c], self.cross)

    def send_block(self, s):
        @pl.when(self.outer)
        def _():
            def one(i, unused):
                self.to_mid(s * 2 * PER + i).start()
                return unused

            lax.fori_loop(0, 2 * PER, one, 0)

    def step(self, k):
        pairs, side = self.pairs, self.side

        @pl.when(k < pairs)
        def _():
            other = 2 * k + 1 - side
            self.to_mid(2 * k).wait_recv()
            self.to_mid(2 * k + 1).wait_recv()
            self.out[chunk(k)] = (
                self.part[chunk(other)].astype(F32) + self.end[chunk(other)].astype(F32)
            ).astype(BF16)
            self.to_cross(k).start()

        j = k - LAG

        @pl.when(jnp.logical_and(j >= 0, j < pairs))
        def _():
            mine = 2 * j + side
            self.to_cross(j).wait_recv()
            self.total[chunk(mine)] = (
                self.part[chunk(mine)].astype(F32)
                + self.end[chunk(mine)].astype(F32)
                + self.mid[chunk(j)].astype(F32)
            ).astype(BF16)
            self.final_cross(mine).start()
            self.final_end(mine).start()

        i = k - 2 * LAG

        @pl.when(jnp.logical_and(i >= 0, i < pairs))
        def _():
            other = 2 * i + 1 - side
            self.final_cross(other).wait_recv()
            self.final_end(other).start()

    def steps(self, first, last):
        @pl.when(self.inner)
        def _():
            def one(k, unused):
                self.step(k)
                return unused

            lax.fori_loop(first, last, one, 0)

    def wait_block(self, s):
        @pl.when(self.outer)
        def _():
            def one(i, unused):
                self.final_end(s * 2 * PER + i).wait_recv()
                return unused

            lax.fori_loop(0, 2 * PER, one, 0)

    def drain(self):
        @pl.when(self.outer)
        def _():
            def one(c, unused):
                self.to_mid(c).wait_send()
                return unused

            lax.fori_loop(0, 2 * self.pairs, one, 0)

        @pl.when(self.inner)
        def _():
            def one(k, unused):
                mine, other = 2 * k + self.side, 2 * k + 1 - self.side
                self.to_cross(k).wait_send()
                self.final_cross(mine).wait_send()
                self.final_end(mine).wait_send()
                self.final_end(other).wait_send()
                return unused

            lax.fori_loop(0, self.pairs, one, 0)


def signal_all(partners):
    barrier = pltpu.get_barrier_semaphore()
    for where in partners:
        pl.semaphore_signal(barrier, inc=1, device_id=where, device_id_type=MESH)
    return barrier, len(partners)


def store_columns(stage, half, value):
    owners, share = stage.shape[1], stage.shape[-1]
    for o in range(owners):
        stage[half, o] = value[:, o * share : (o + 1) * share].astype(BF16)


def store_rows(stage, first, value):
    size = stage.shape[2]
    for q in range(value.shape[0] // size):
        owner, half = divmod(first // size + q, 2)
        stage[half, owner] = value[q * size : (q + 1) * size].astype(BF16)


def feed_kernel(
    gated_ref, out_in, x_ref, g_ref, ob_ref, gain_ref, shift_ref, up_ref, ub_ref, down_in,
    mixed_ref, conv_ref, carried_ref,
    resid_ref, dpart_ref, dres_ref, dconv_ref, dzero_ref, dall_ref, gup_ref, gdown_ref, gout_ref,
    small_ref, gskip_ref,
    low_ref, hidden_ref, dpre_ref, npart_ref, nsum_ref, dmix_ref, own_ref, gall_ref, out_ref, down_ref,
    s_gate, r_gate, s_long, r_long, *line,
):
    groups, owners = out_in.shape[:2]
    width = x_ref.shape[1]
    blocks = x_ref.shape[0] // SEG
    share = width // owners
    tp, ctx = lax.axis_index("tp"), lax.axis_index("ctx")
    chain = LineSum(npart_ref, nsum_ref, line)
    barrier, count = signal_all(
        [spot(tp=lax.rem(tp + i, groups)) for i in range(1, groups)]
        + [spot(ctx=lax.rem(ctx + i, 4)) for i in range(1, 4)]
    )

    def gate_copy(s, i):
        rows = pl.ds(pl.multiple_of(s * SEG, SEG), SEG)
        return remote(
            gated_ref.at[rows], gall_ref.at[tp, rows], s_gate.at[i, s], r_gate.at[tp, s],
            spot(tp=lax.rem(tp + i, groups)),
        )

    gall_ref[tp] = gated_ref[...]
    pl.semaphore_wait(barrier, count)
    for s in range(blocks):
        for i in range(1, groups):
            gate_copy(s, i).start()
    for o in range(owners):
        columns = slice(o * share, (o + 1) * share)
        down_ref[:, columns] = down_in[o]
        for z in range(groups):
            out_ref[z, :, columns] = out_in[z, o]
    ob, gain, shift = (ref[...].reshape(1, -1) for ref in (ob_ref, gain_ref, shift_ref))
    ub = ub_ref[...].reshape(1, -1)
    small_ref[...] = jnp.zeros(small_ref.shape, F32)
    gskip_ref[...] = jnp.zeros(gskip_ref.shape, F32)

    def core(s, unused):
        rows = pl.ds(pl.multiple_of(s * SEG, SEG), SEG)
        for i in range(1, groups):
            source = lax.rem(tp + i, groups)
            at = gall_ref.at[source, rows]
            remote(at, at, s_gate.at[i, s], r_gate.at[source, s], chain.mate).wait_recv()
        mixed = mm(gall_ref[0, rows], out_ref[0])
        for z in range(1, groups):
            mixed = mixed + mm(gall_ref[z, rows], out_ref[z])
        residual = x_ref[rows].astype(F32) + mixed + ob
        resid_ref[rows] = residual
        low = (normalize(residual)[0] * gain + shift).astype(BF16)
        low_ref[rows] = low
        pre = mm(low, up_ref[...]) + ub
        cdf = 0.5 * (1.0 + lax.erf(pre * math.sqrt(0.5)))
        hidden_ref[rows] = (pre * cdf).astype(BF16)
        slope = cdf + pre * (jnp.exp(-0.5 * pre * pre) * (1.0 / math.sqrt(2.0 * math.pi)))
        grad = g_ref[rows]
        d_pre = (mm_nt(grad, down_ref[...]) * slope).astype(BF16)
        dpre_ref[rows] = d_pre
        npart_ref[rows] = mm_nt(d_pre, up_ref[...]).astype(BF16)
        small_ref[0:1] += jnp.sum(grad.astype(F32), axis=0, keepdims=True)
        small_ref[6:7] += jnp.sum(d_pre.astype(F32), axis=0, keepdims=True)
        chain.send_block(s)
        return unused

    lax.fori_loop(0, blocks, core, 0)
    chain.steps(0, PER)

    def down(s, unused):
        rows = pl.ds(pl.multiple_of(s * SEG, SEG), SEG)
        dpart_ref[rows] = mm(hidden_ref[rows], down_ref[...]).astype(BF16)
        return unused

    lax.fori_loop(0, blocks, down, 0)
    for t in range(2):
        part = slice(t * width // 2, (t + 1) * width // 2)
        store_rows(gup_ref, t * width // 2, mm_tn(low_ref[:, part], dpre_ref[...]))
        units = hidden_ref.shape[1] // 2
        store_columns(gdown_ref, t, mm_tn(hidden_ref[:, t * units : (t + 1) * units], g_ref[...]))

    def to_ctx(s, other):
        return remote(own_ref.at[s], dall_ref.at[ctx * blocks + s], s_long.at[other, s], r_long.at[ctx, s], spot(ctx=other))

    def back(s, unused):
        chain.steps((s + 1) * PER, (s + 2) * PER)
        chain.wait_block(s)
        rows = pl.ds(pl.multiple_of(s * SEG, SEG), SEG)
        xhat, scale = normalize(resid_ref[rows])
        dn = nsum_ref[rows].astype(F32)
        e = dn * gain
        d_res = g_ref[rows].astype(F32) + scale * (
            e - jnp.mean(e, axis=-1, keepdims=True) - xhat * jnp.mean(e * xhat, axis=-1, keepdims=True)
        )
        dres_ref[rows] = d_res
        small_ref[2:3] += jnp.sum(dn * xhat, axis=0, keepdims=True)
        small_ref[3:4] += jnp.sum(dn, axis=0, keepdims=True)
        d_mix = d_res.astype(BF16)
        dmix_ref[rows] = d_mix
        small_ref[1:2] += jnp.sum(d_mix.astype(F32), axis=0, keepdims=True)
        d_gated = mm_nt(d_mix, out_ref[tp])
        d_conv = d_gated * mixed_ref[rows]
        dconv_ref[rows] = d_conv
        own_ref[s] = d_conv.astype(BF16)
        for other in range(3):
            @pl.when(other < ctx)
            def _():
                to_ctx(s, other).start()

        dzero_ref[rows] = d_gated * conv_ref[rows]
        gskip_ref[...] += jnp.sum(d_conv * carried_ref[rows].astype(F32), axis=0, keepdims=True)
        return unused

    lax.fori_loop(0, blocks, back, 0)
    for s in range(blocks):
        dall_ref[ctx * blocks + s] = own_ref[s]
    value = mm_tn(gated_ref[...], dmix_ref[...])
    for t in range(2):
        store_columns(gout_ref, t, value[t * gout_ref.shape[2] : (t + 1) * gout_ref.shape[2]])
    for s in range(blocks):
        for i in range(1, groups):
            gate_copy(s, i).wait_send()
    chain.drain()
    for other in range(4):
        @pl.when(other < ctx)
        def _():
            for s in range(blocks):
                to_ctx(s, other).wait_send()

        @pl.when(other > ctx)
        def _():
            for s in range(blocks):
                at = dall_ref.at[other * blocks + s]
                remote(at, at, s_long.at[other, s], r_long.at[other, s], chain.mate).wait_recv()


def extend_weights(ref, weight, bias):
    rows = weight.shape[0]
    ref[...] = jnp.zeros(ref.shape, F32)
    ref[0:rows] = weight[...]
    ref[rows : rows + 1] = bias[...].reshape(1, -1)


def decay(length, channels, tp, width):
    time_pos = lax.broadcasted_iota(jnp.int32, (length, 1), 0).astype(F32) * (1.0 / (length - 1))
    channel = (lax.broadcasted_iota(jnp.int32, (1, channels), 1) + tp * channels).astype(F32)
    rate = SLOW_RATE + (FAST_RATE - SLOW_RATE) * channel * (1.0 / (width - 1))
    return jnp.exp(-time_pos * rate) + SHIFT_FLOOR


EXACT_DOT = dict(precision=EXACT, preferred_element_type=F32)
TN = (((0,), (0,)), ((), ()))
NT = (((1,), (1,)), ((), ()))


def front_kernel(
    par_ref, x_ref, win_ref, last_ref, out_in, up_in, down_in, ft_ref, f1_ref, f1b_ref, f2_ref, f2b_ref, freq_ref,
    gain_ref, shift_ref, ib_ref, sw_ref, sb_ref, skip_ref, fh_ref, fl_ref, th_ref, tl_ref, sign_ref,
    low_hbm, proj_hbm, head_hbm, mixed_hbm, spec_hbm, filt_hbm, net_hbm, in_hbm, out_hbm, up_hbm, down_hbm,
    lasts_ref, gate_ref, conv_ref, gated_ref, carried_ref,
    w_ref, low_ref, proj_ref, head_ref, mixed_ref, spec_ref, filt_ref, net_ref, taps_ref, shared_ref,
    xt_ref, tail_ref, ext_ref, w1_ref, w2_ref, acc_ref, lastb_ref, wb_ref,
    s_in, r_in, s_last, r_last, s_out, r_out, s_up, r_up, s_down, r_down, s_xt, r_xt, s_car, r_car, s_fwd, local,
):
    total_rows, width = x_ref.shape
    channels = ib_ref.shape[1]
    blocks = total_rows // SEG
    tp, ctx, dp = lax.axis_index("tp"), lax.axis_index("ctx"), lax.axis_index("dp")
    owners, lines = out_hbm.shape[1], out_hbm.shape[0]
    share = win_ref.shape[2]
    last_share = last_ref.shape[0]
    up_share = up_in.shape[0]

    def cell(i):
        flat = lax.rem(tp * owners + dp + i, owners * lines)
        return flat // owners, lax.rem(flat, owners)

    def owner(i):
        return lax.rem(dp + i, owners)

    def ctx_at(i):
        return lax.rem(ctx + i, 4)

    partners = [spot(ctx=ctx_at(i)) for i in range(1, 4)]
    for i in range(1, owners * lines):
        line, own = cell(i)
        partners.append(spot(tp=line, dp=own))
    barrier, count = signal_all(partners)

    def rows_of(ref, who, size):
        return ref.at[pl.ds(pl.multiple_of(who * size, size), size)]

    def send_in(i):
        return remote(win_ref, wb_ref.at[dp], s_in.at[i], r_in.at[dp], spot(dp=owner(i)))

    def send_last(i):
        return remote(last_ref, lastb_ref.at[dp], s_last.at[i], r_last.at[dp], spot(dp=owner(i)))

    def send_xt(i):
        at = xt_ref.at[ctx]
        return remote(at, at, s_xt.at[i], r_xt.at[ctx], spot(ctx=ctx_at(i)))

    for s in range(blocks):
        tail = x_ref[s * SEG + SEG - 16 : s * SEG + SEG].astype(F32)
        xt_ref[ctx, 2 * s : 2 * s + 2] = tail[14:16]
    pl.semaphore_wait(barrier, count)
    for i in range(1, owners):
        send_in(i).start()
        send_last(i).start()
    for i in range(1, 4):
        send_xt(i).start()
    wb_ref[dp] = win_ref[...]
    lastb_ref[dp] = last_ref[...]

    gain, shift = gain_ref[...].reshape(1, -1), shift_ref[...].reshape(1, -1)

    def norm(s, unused):
        rows = pl.ds(pl.multiple_of(s * SEG, SEG), SEG)
        low_ref[rows] = (normalize(x_ref[rows].astype(F32))[0] * gain + shift).astype(BF16)
        return unused

    lax.fori_loop(0, blocks, norm, 0)
    saves = [pltpu.make_async_copy(low_ref, low_hbm, local.at[1])]
    saves[-1].start()

    units = f1_ref.shape[1]
    length = ft_ref.shape[1]
    extend_weights(w1_ref, f1_ref, f1b_ref)
    extend_weights(w2_ref, f2_ref, f2b_ref)
    freq = freq_ref[...].reshape(1, -1)
    net_ref[...] = jnp.zeros(net_ref.shape, F32)
    angle = lax.dot_general(w1_ref[...] * freq, ft_ref[...], TN, **EXACT_DOT)
    net_ref[0, 0:units] = jnp.cos(angle)
    net_ref[1, 0:units] = jnp.sin(angle)
    pad = net_ref.shape[1] - units
    net_ref[1, units:] = jnp.where(lax.broadcasted_iota(jnp.int32, (pad, length), 0) == 0, 1.0, 0.0)
    angle = lax.dot_general(w2_ref[...] * freq, net_ref[1], TN, **EXACT_DOT)
    net_ref[2, 0:units] = jnp.cos(angle)
    second = jnp.sin(angle)
    net_ref[3, 0:units] = second
    saves.append(pltpu.make_async_copy(net_ref, net_hbm, local.at[2]))
    saves[-1].start()
    for i in range(1, owners):
        at = lastb_ref.at[owner(i)]
        remote(at, at, s_last.at[i], r_last.at[owner(i)], spot(dp=owner(i))).wait_recv()
    for o in range(owners):
        lasts_ref[o * last_share : (o + 1) * last_share] = lastb_ref[o].astype(F32)
    raw = lax.dot_general(second, lasts_ref[...], TN, **EXACT_DOT)
    taps_ref[...] = raw * decay(length, channels, tp, channels * lines)
    fh, fl, th, tl = fh_ref[...], fl_ref[...], th_ref, tl_ref
    sign = sign_ref[...]
    for j in range(DEPTH):
        part = taps_ref[j * SEG : (j + 1) * SEG]
        out = mm_split(fh, fl, part)
        re, im = out[:SEG], out[SEG:]
        filt_ref[j, 0] = re
        filt_ref[j, 1] = im
    for j in range(DEPTH - 1, 0, -1):
        first = taps_ref[(j - 1) * SEG : (j - 1) * SEG + 1]
        filt_ref[j, 0] = filt_ref[j, 0] - sign * filt_ref[j - 1, 1]
        filt_ref[j, 1] = filt_ref[j, 1] + sign * (filt_ref[j - 1, 0] - first)
    saves.append(pltpu.make_async_copy(filt_ref, filt_hbm, local.at[3]))
    saves[-1].start()

    for i in range(1, owners):
        at = wb_ref.at[owner(i)]
        remote(at, at, s_in.at[i], r_in.at[owner(i)], spot(dp=owner(i))).wait_recv()
    for o in range(owners):
        w_ref[:, :, o * share : (o + 1) * share] = wb_ref[o]
    saves.append(pltpu.make_async_copy(w_ref, in_hbm, local.at[4]))
    saves[-1].start()

    def send_out(i):
        line, own = cell(i)
        return remote(out_in, out_hbm.at[tp, dp], s_out.at[i], r_out.at[tp, dp], spot(tp=line, dp=own))

    def send_up(i):
        return remote(up_in, rows_of(up_hbm, dp, up_share), s_up.at[i], r_up.at[dp], spot(dp=owner(i)))

    def send_down(i):
        return remote(down_in, down_hbm.at[dp], s_down.at[i], r_down.at[dp], spot(dp=owner(i)))

    for i in range(1, owners * lines):
        send_out(i).start()
    for i in range(1, owners):
        send_up(i).start()
        send_down(i).start()
    for k, (src, dst) in enumerate(
        ((out_in, out_hbm.at[tp, dp]), (up_in, rows_of(up_hbm, dp, up_share)), (down_in, down_hbm.at[dp]))
    ):
        saves.append(pltpu.make_async_copy(src, dst, local.at[5 + k]))
        saves[-1].start()

    for i in range(1, 4):
        at = xt_ref.at[ctx_at(i)]
        remote(at, at, s_xt.at[i], r_xt.at[ctx_at(i)], spot(ctx=ctx_at(i))).wait_recv()
    tail_ref[...] = jnp.zeros(tail_ref.shape, F32)
    for half in range(2):
        tails = (normalize(xt_ref[half])[0] * gain + shift).astype(BF16)
        for g in range(3):
            value = mm_nt(tails, w_ref[g]) + ib_ref[g : g + 1]
            for s in range(4):
                tail_ref[g, 4 * half + s, 6:8] = value[2 * s : 2 * s + 2]

    def share_block(s, other):
        return remote(
            carried_ref.at[pl.ds(pl.multiple_of(s * SEG, SEG), SEG)], shared_ref.at[4 * ctx + s],
            s_car.at[other, s], r_car.at[ctx, s], spot(ctx=other),
        )

    def forward_block(s, group):
        at = shared_ref.at[4 * group + s]
        return remote(at, at, s_fwd.at[s], r_car.at[group, s], spot(ctx=5 - ctx))

    def mix(s, unused):
        rows = pl.ds(pl.multiple_of(s * SEG, SEG), SEG)
        parent = par_ref[0, ctx * blocks + s]
        slot = jnp.where(parent >= 0, parent, 8)
        out = []
        for g in range(3):
            projected = mm_nt(low_ref[rows], w_ref[g]) + ib_ref[g : g + 1]
            proj_ref[g, rows] = projected
            head = tail_ref[g, slot]
            head_ref[g, s] = head
            ext_ref[g, 0:HEADS] = head
            ext_ref[g, HEADS : HEADS + SEG] = projected
            mixed = (
                sw_ref[g, 0:1] * ext_ref[g, HEADS - 2 : HEADS - 2 + SEG]
                + sw_ref[g, 1:2] * ext_ref[g, HEADS - 1 : HEADS - 1 + SEG]
                + sw_ref[g, 2:3] * projected
                + sb_ref[g : g + 1]
            )
            if g == 0:
                gate_ref[rows] = mixed
            else:
                mixed_ref[g - 1, rows] = mixed
            out.append(mixed)
        carried = (out[2] * out[1]).astype(BF16)
        carried_ref[rows] = carried

        @pl.when(ctx == 0)
        def _():
            share_block(s, 2).start()
            share_block(s, 1).start()

        @pl.when(ctx == 1)
        def _():
            share_block(s, 3).start()

        spec = mm(fh_ref[...], carried) + mm(fl_ref[...], carried)
        spec_ref[8 + s, 0] = spec[:SEG]
        spec_ref[8 + s, 1] = spec[SEG:]
        return unused

    lax.fori_loop(0, blocks, mix, 0)
    for k, (src, dst) in enumerate(((proj_ref, proj_hbm), (head_ref, head_hbm), (mixed_ref, mixed_hbm))):
        saves.append(pltpu.make_async_copy(src, dst, local.at[8 + k]))
        saves[-1].start()

    def spectrum(slot, part):
        out = mm(fh_ref[...], part) + mm(fl_ref[...], part)
        spec_ref[slot, 0] = out[:SEG]
        spec_ref[slot, 1] = out[SEG:]

    spec_ref[12] = jnp.zeros(spec_ref.shape[1:], F32)

    def arrived(group, s):
        at = shared_ref.at[4 * group + s]
        return remote(at, at, s_fwd.at[s], r_car.at[group, s], spot(ctx=ctx_at(1)))

    def copy_own(group):
        def one(s, unused):
            spec_ref[4 * group + s] = spec_ref[8 + s]
            return unused

        lax.fori_loop(0, 4, one, 0)

    def receive(group):
        def one(s, unused):
            arrived(group, s).wait_recv()
            spectrum(4 * group + s, shared_ref[4 * group + s])
            return unused

        lax.fori_loop(0, 4, one, 0)

    def receive_forward(group):
        def one(s, unused):
            arrived(group, s).wait_recv()
            forward_block(s, group).start()
            spectrum(4 * group + s, shared_ref[4 * group + s])
            return unused

        lax.fori_loop(0, 4, one, 0)

    @pl.when(ctx == 0)
    def _():
        copy_own(0)

    @pl.when(ctx == 1)
    def _():
        copy_own(1)
        receive(0)

    @pl.when(ctx == 2)
    def _():
        receive_forward(0)
        receive(1)

    @pl.when(ctx == 3)
    def _():
        receive_forward(1)
        receive(0)

    saves.append(pltpu.make_async_copy(spec_ref, spec_hbm, local.at[11]))
    saves[-1].start()

    def dest(s, unused):
        above = lineage(par_ref, ctx * blocks + s)
        places = [8 + s] + [jnp.where(a >= 0, a, 12) for a in above]
        blend_all(acc_ref, [(filt_ref.at[d], spec_ref.at[places[d]]) for d in range(DEPTH)], False)
        long_out = unpack_spectrum(th, tl, acc_ref) * (1.0 / SEG)
        place = pl.ds(pl.multiple_of(s * SEG, SEG), SEG)
        convolved = long_out + skip_ref[...].reshape(1, -1) * carried_ref[place].astype(F32)
        conv_ref[place] = convolved
        gated_ref[place] = (convolved * gate_ref[place]).astype(BF16)
        return unused

    lax.fori_loop(0, blocks, dest, 0)

    for save in saves:
        save.wait()
    for i in range(1, owners):
        send_in(i).wait_send()
        send_last(i).wait_send()
        send_up(i).wait_send()
        send_down(i).wait_send()
        at = rows_of(up_hbm, owner(i), up_share)
        remote(at, at, s_up.at[i], r_up.at[owner(i)], spot(dp=owner(i))).wait_recv()
        at = down_hbm.at[owner(i)]
        remote(at, at, s_down.at[i], r_down.at[owner(i)], spot(dp=owner(i))).wait_recv()
    for i in range(1, owners * lines):
        line, own = cell(i)
        send_out(i).wait_send()
        at = out_hbm.at[line, own]
        remote(at, at, s_out.at[i], r_out.at[line, own], spot(tp=line, dp=own)).wait_recv()
    for i in range(1, 4):
        send_xt(i).wait_send()

    @pl.when(ctx == 0)
    def _():
        for s in range(blocks):
            share_block(s, 2).wait_send()
            share_block(s, 1).wait_send()

    @pl.when(ctx == 1)
    def _():
        for s in range(blocks):
            share_block(s, 3).wait_send()

    @pl.when(ctx == 2)
    def _():
        for s in range(blocks):
            forward_block(s, 0).wait_send()

    @pl.when(ctx == 3)
    def _():
        for s in range(blocks):
            forward_block(s, 1).wait_send()


class OwnerSum:
    scratch_count = 17

    @staticmethod
    def scratch(owners, shape):
        many = max(owners - 1, 1)
        return [
            pltpu.VMEM((owners,) + shape, BF16),
            pltpu.VMEM((owners,) + shape, BF16),
            pltpu.VMEM((many,) + shape, BF16),
            pltpu.VMEM(shape, BF16),
            pltpu.VMEM(shape, BF16),
            pltpu.SemaphoreType.DMA,
            pltpu.SemaphoreType.DMA,
            pltpu.SemaphoreType.DMA,
            pltpu.SemaphoreType.DMA((many,)),
            pltpu.SemaphoreType.DMA((many,)),
            pltpu.SemaphoreType.DMA,
            pltpu.SemaphoreType.DMA,
            pltpu.SemaphoreType.DMA,
            pltpu.SemaphoreType.DMA,
        ]

    def __init__(self, stage, out, scratch):
        self.stage, self.result = stage, out
        self.recv, self.keep, self.parts, self.y_own, self.y_in = scratch[:5]
        self.sems = scratch[5:]
        self.owners = stage.shape[1]
        self.dp, ctx = lax.axis_index("dp"), lax.axis_index("ctx")
        self.low = lax.rem(ctx, 2)
        self.mate = spot(ctx=ctx + 1 - 2 * self.low)
        self.across = spot(ctx=lax.rem(ctx + 2, 4))

    def load(self):
        return pltpu.make_async_copy(self.stage.at[self.low], self.keep, self.sems[0])

    def to_mate(self):
        return remote(self.stage.at[1 - self.low], self.recv, self.sems[1], self.sems[2], self.mate)

    def to_owner(self, i):
        owner = lax.rem(self.dp + i, self.owners)
        return remote(
            self.keep.at[owner], self.parts.at[self.owners - 1 - i], self.sems[3].at[i - 1],
            self.sems[4].at[self.owners - 1 - i], spot(dp=owner),
        )

    def from_owner(self, i):
        return remote(self.parts.at[i - 1], self.parts.at[i - 1], self.sems[3].at[i - 1], self.sems[4].at[i - 1], self.mate)

    def to_across(self):
        return remote(self.y_own, self.y_in, self.sems[5], self.sems[6], self.across)

    def to_back(self):
        at = self.result.at[self.low]
        return remote(at, at, self.sems[7], self.sems[8], self.mate)

    def begin(self):
        self.to_mate().start()
        self.load().start()

    def pair(self):
        self.load().wait()
        self.to_mate().wait_recv()
        for o in range(self.owners):
            self.keep[o] = (self.keep[o].astype(F32) + self.recv[o].astype(F32)).astype(BF16)
        for i in range(1, self.owners):
            self.to_owner(i).start()

    def own(self):
        total = self.keep[self.dp].astype(F32)
        for i in range(1, self.owners):
            self.from_owner(i).wait_recv()
            total = total + self.parts[i - 1].astype(F32)
        self.y_own[...] = total.astype(BF16)
        self.to_across().start()

    def cross(self):
        self.to_across().wait_recv()
        self.result[self.low] = self.y_own[...].astype(F32) + self.y_in[...].astype(F32)
        self.to_back().start()

    def finish(self):
        self.to_mate().wait_send()
        for i in range(1, self.owners):
            self.to_owner(i).wait_send()
        self.to_across().wait_send()
        self.to_back().wait_send()
        at = self.result.at[1 - self.low]
        remote(at, at, self.sems[7], self.sems[8], self.mate).wait_recv()


class SmallSum:
    @staticmethod
    def scratch(count, shape):
        return [
            pltpu.VMEM((count,) + shape, F32),
            pltpu.SemaphoreType.DMA((count,)),
            pltpu.SemaphoreType.DMA((count,)),
        ]

    def __init__(self, axis, scratch):
        self.axis = axis
        self.slots, self.send, self.recv = scratch
        self.count = self.slots.shape[0]
        self.me = lax.axis_index(axis)

    def copy(self, i):
        at = self.slots.at[self.me]
        other = lax.rem(self.me + i, self.count)
        return remote(at, at, self.send.at[i], self.recv.at[self.me], spot(**{self.axis: other}))

    def start(self, value):
        self.slots[self.me] = value
        for i in range(1, self.count):
            self.copy(i).start()

    def total(self):
        for i in range(1, self.count):
            other = lax.rem(self.me + i, self.count)
            at = self.slots.at[other]
            remote(at, at, self.send.at[i], self.recv.at[other], spot(**{self.axis: lax.rem(self.me + i, self.count)})).wait_recv()
        out = self.slots[0]
        for i in range(1, self.count):
            out = out + self.slots[i]
        return out

    def finish(self):
        for i in range(1, self.count):
            self.copy(i).wait_send()


def back_kernel(
    par_ref, dall_ref, dconv_ref, dzero_ref, mixed_ref, low_ref, w_ref, x_ref, dpart_ref,
    fh_ref, fl_ref, th_ref, tl_ref, sign_ref, sw_ref, skip_ref,
    ft_ref, f1_ref, f1b_ref, f2_ref, f2b_ref, freq_ref, last_ref, small_ref, gskip_ref,
    proj_hbm, head_hbm, spec_hbm, filt_hbm, net_hbm, sup_hbm, sdown_hbm, sout_hbm,
    dsum_ref, psum_ref, oup_ref, odown_ref, oout_ref, oin_ref, va_ref, vd_ref, vl_ref, vf_ref,
    yown_ref, dcar_ref, dtaps_ref, stage_in, ppart_ref, w1_ref, w2_ref, hd_ref, s_hd, r_hd, local, *rest,
):
    width = x_ref.shape[1]
    channels = dconv_ref.shape[1]
    total_rows = x_ref.shape[0]
    blocks = total_rows // SEG
    owners = sup_hbm.shape[1]
    ctx, tp, dp = lax.axis_index("ctx"), lax.axis_index("tp"), lax.axis_index("dp")
    rest = list(rest)

    def take(n):
        out = rest[:n]
        del rest[:n]
        return out

    down = LineSum(dpart_ref, dsum_ref, take(11))
    proj = LineSum(ppart_ref, psum_ref, take(11))
    early = [OwnerSum(s, o, take(14)) for s, o in ((sup_hbm, oup_ref), (sdown_hbm, odown_ref), (sout_hbm, oout_ref))]
    late = OwnerSum(stage_in, oin_ref, take(14))
    a_ctx, a_dp = SmallSum("ctx", take(3)), SmallSum("dp", take(3))
    d_ctx, d_dp, d_tp = SmallSum("ctx", take(3)), SmallSum("dp", take(3)), SmallSum("tp", take(3))
    l_ctx, l_dp = SmallSum("ctx", take(3)), SmallSum("dp", take(3))
    f_ctx, f_dp, f_tp = SmallSum("ctx", take(3)), SmallSum("dp", take(3)), SmallSum("tp", take(3))

    partners = [spot(tp=lax.rem(tp + i, 4)) for i in range(1, 4)]
    partners += [spot(ctx=lax.rem(ctx + i, 4)) for i in range(1, 4)]
    partners += [spot(dp=lax.rem(dp + i, owners)) for i in range(1, owners)]
    barrier, count = signal_all(partners)
    pl.semaphore_wait(barrier, count)
    for s in range(blocks):
        down.send_block(s)
    for job in early:
        job.begin()
    fh, fl, th, tl = fh_ref[...], fl_ref[...], th_ref, tl_ref
    skip = skip_ref[...].reshape(1, -1)
    scale = 1.0 / SEG

    def put(dst, value):
        dst[0] = value[:SEG] * scale
        dst[1] = value[SEG:] * scale

    def conv_inputs(filt_ref, more_ref, acc_ref):
        load = pltpu.make_async_copy(filt_hbm, filt_ref, local.at[0])
        load.start()

        def transform(s, unused):
            part = dall_ref[ctx * blocks + s]
            put(yown_ref.at[s], mm(fh, part) + mm(fl, part))
            return unused

        lax.fori_loop(0, blocks, transform, 0)
        load.wait()

        def leaf_sum(match):
            total = None
            for leaf in range(8, 16):
                term = jnp.where(match(leaf), 1.0, 0.0) * dall_ref[leaf].astype(F32)
                total = term if total is None else total + term
            return total

        def from_leaf(b):
            return lambda leaf: par_ref[0, leaf] == b

        def finish(s, terms):
            blend_all(acc_ref, terms, True)
            place = pl.ds(pl.multiple_of(s * SEG, SEG), SEG)
            dcar_ref[place] = unpack_spectrum(th, tl, acc_ref) + skip * dconv_ref[place]

        @pl.when(ctx == 0)
        def _():
            def gather(k, unused):
                p = k + 1
                total = None
                for b in range(4, 8):
                    term = jnp.where(par_ref[0, b] == p, 1.0, 0.0) * dall_ref[b].astype(F32)
                    total = term if total is None else total + term
                put(more_ref.at[k], mm_split(fh, fl, total))
                total = leaf_sum(lambda leaf: par_ref[0, par_ref[0, leaf]] == p)
                put(more_ref.at[3 + k], mm_split(fh, fl, total))
                return unused

            lax.fori_loop(0, 3, gather, 0)
            for a in range(4):
                terms = [(filt_ref.at[s - a], yown_ref.at[s]) for s in range(a, 4)]
                for p in range(max(a, 1), 4):
                    terms.append((filt_ref.at[p - a + 1], more_ref.at[p - 1]))
                    terms.append((filt_ref.at[p - a + 2], more_ref.at[p + 2]))
                finish(a, terms)

        @pl.when(ctx == 1)
        def _():
            def one(b, unused):
                put(more_ref.at[0], mm_split(fh, fl, leaf_sum(from_leaf(b + 4))))
                finish(b, [(filt_ref.at[0], yown_ref.at[b]), (filt_ref.at[1], more_ref.at[0])])
                return unused

            lax.fori_loop(0, 4, one, 0)

        @pl.when(ctx > 1)
        def _():
            def one(b, unused):
                finish(b, [(filt_ref.at[0], yown_ref.at[b])])
                return unused

            lax.fori_loop(0, 4, one, 0)

    pl.run_scoped(
        conv_inputs,
        pltpu.VMEM((DEPTH, 2, SEG, channels), F32),
        pltpu.VMEM((6, 2, SEG, channels), F32),
        pltpu.VMEM((2, SEG, channels), F32),
    )

    def to_ctx(i):
        at = hd_ref.at[pl.ds(ctx * blocks, blocks)]
        return remote(at, at, s_hd.at[i], r_hd.at[ctx], spot(ctx=lax.rem(ctx + i, 4)))

    for s in range(blocks):
        top = slice(s * SEG, s * SEG + HEADS)
        d_car = dcar_ref[top]
        rows = [dzero_ref[top], d_car * mixed_ref[1, top], d_car * mixed_ref[0, top]]
        for g in range(3):
            hd_ref[ctx * blocks + s, 2 * g : 2 * g + 2] = rows[g][0:2]
        hd_ref[ctx * blocks + s, 6:8] = jnp.zeros((2, channels), F32)
    for i in range(1, 4):
        to_ctx(i).start()
    down.steps(0, 3)
    for job in early:
        job.pair()

    def conv_filters(spec_ref, dfilt_ref):
        load = pltpu.make_async_copy(spec_hbm, spec_ref, local.at[0])
        load.start()
        load.wait()

        @pl.when(ctx == 0)
        def _():
            for d in range(4):
                blend_all(dfilt_ref.at[d], [(spec_ref.at[8 + s - d], yown_ref.at[s]) for s in range(d, 4)], True)
            dfilt_ref[4:6] = jnp.zeros((2, 2, SEG, channels), F32)

        @pl.when(ctx > 0)
        def _():
            places = []
            for s in range(blocks):
                above = lineage(par_ref, ctx * blocks + s)
                places.append([8 + s] + [jnp.where(a >= 0, a, 12) for a in above])
            for d in range(DEPTH):
                terms = [(spec_ref.at[places[s][d]], yown_ref.at[s]) for s in range(blocks)]
                blend_all(dfilt_ref.at[d], terms, True)

        down.steps(3, 6)
        sign = sign_ref[...]
        first_row = lax.broadcasted_iota(jnp.int32, (SEG, 1), 0) == 0
        for j in range(DEPTH):
            fix = None
            if j + 1 < DEPTH:
                nr, ni = dfilt_ref[j + 1, 0], dfilt_ref[j + 1, 1]
                fix = jnp.sum(sign * ni, axis=0, keepdims=True)
                dfilt_ref[j, 0] = dfilt_ref[j, 0] + sign * ni
                dfilt_ref[j, 1] = dfilt_ref[j, 1] - sign * nr
            taps = unpack_spectrum(th, tl, dfilt_ref.at[j])
            if fix is not None:
                taps = jnp.where(first_row, taps - fix, taps)
            dtaps_ref[j * SEG : (j + 1) * SEG] = taps

    pl.run_scoped(
        conv_filters,
        pltpu.VMEM((13, 2, SEG, channels), F32),
        pltpu.VMEM((DEPTH, 2, SEG, channels), F32),
    )
    down.steps(6, 9)

    va_ref[...] = jnp.zeros(va_ref.shape, F32)
    vd_ref[...] = small_ref[...]
    va_ref[15:16] = gskip_ref[...]
    for i in range(1, 4):
        other = lax.rem(ctx + i, 4)
        at = hd_ref.at[pl.ds(other * blocks, blocks)]
        remote(at, at, s_hd.at[i], r_hd.at[other], spot(ctx=other)).wait_recv()

    def mix_back(dp_ref, ext_ref, dm_ref, pin_ref, hin_ref):
        load_heads = pltpu.make_async_copy(head_hbm, hin_ref, local.at[1])
        load_heads.start()

        def fetch(s):
            rows = pl.ds(pl.multiple_of(s * SEG, SEG), SEG)
            return pltpu.make_async_copy(proj_hbm.at[:, rows], pin_ref.at[lax.rem(s, 2)], local.at[2 + lax.rem(s, 2)])

        fetch(0).start()
        load_heads.wait()

        def one(s, unused):
            rows = pl.ds(pl.multiple_of(s * SEG, SEG), SEG)
            slot = lax.rem(s, 2)
            fetch(s).wait()

            @pl.when(s + 1 < blocks)
            def _():
                fetch(s + 1).start()

            mine = ctx * blocks + s
            child = None
            for b in range(1, 16):
                term = jnp.where(par_ref[0, b] == mine, 1.0, 0.0) * hd_ref[b]
                child = term if child is None else child + term
            part = None
            for g in range(3):
                if g == 0:
                    dm = dzero_ref[rows]
                else:
                    dm = dcar_ref[rows] * mixed_ref[2 - g, rows]
                ext_ref[0:HEADS] = hin_ref[g, s]
                ext_ref[HEADS : HEADS + SEG] = pin_ref[slot, g]
                for k in range(3):
                    piece = ext_ref[HEADS - 2 + k : HEADS - 2 + k + SEG]
                    va_ref[3 * g + k : 3 * g + k + 1] += jnp.sum(piece * dm, axis=0, keepdims=True)
                va_ref[12 + g : 13 + g] += jnp.sum(dm, axis=0, keepdims=True)
                dm_ref[0:SEG] = dm
                dm_ref[SEG : SEG + 2] = child[2 * g : 2 * g + 2]
                d_proj = (
                    sw_ref[g, 2:3] * dm
                    + sw_ref[g, 1:2] * dm_ref[1 : 1 + SEG]
                    + sw_ref[g, 0:1] * dm_ref[2 : 2 + SEG]
                ).astype(BF16)
                dp_ref[g, rows] = d_proj
                va_ref[9 + g : 10 + g] += jnp.sum(d_proj.astype(F32), axis=0, keepdims=True)
                term = mm(d_proj, w_ref[g])
                part = term if part is None else part + term
            ppart_ref[rows] = part.astype(BF16)
            proj.send_block(s)
            xhat = normalize(x_ref[rows].astype(F32))[0]
            vd_ref[4:5] += jnp.sum(part * xhat, axis=0, keepdims=True)
            vd_ref[5:6] += jnp.sum(part, axis=0, keepdims=True)
            down.steps(9 + s, 10 + s)
            return unused

        lax.fori_loop(0, blocks, one, 0)
        rows = stage_in.shape[3]
        for g in range(3):
            value = mm_tn(dp_ref[g], low_ref[...])
            for t in range(2):
                store_columns(stage_in.at[:, :, g], t, value[t * rows : (t + 1) * rows])

    pl.run_scoped(
        mix_back,
        pltpu.VMEM((3, total_rows, channels), BF16),
        pltpu.VMEM((HEADS + SEG, channels), F32),
        pltpu.VMEM((HEADS + SEG, channels), F32),
        pltpu.VMEM((2, 3, SEG, channels), F32),
        pltpu.VMEM((3, blocks, HEADS, channels), F32),
    )
    late.begin()
    for job in early:
        job.own()
    down.steps(13, 15)

    def filter_back(net_ref):
        load = pltpu.make_async_copy(net_hbm, net_ref, local.at[1])
        load.start()
        d_raw = dtaps_ref[...] * decay(DEPTH * SEG, channels, tp, width)
        extend_weights(w1_ref, f1_ref, f1b_ref)
        extend_weights(w2_ref, f2_ref, f2b_ref)
        freq = freq_ref[...].reshape(1, -1)
        load.wait()
        units = last_ref.shape[0]
        l_ctx.start(jnp.dot(net_ref[3, 0:units], d_raw, **EXACT_DOT))
        s_two = lax.dot_general(last_ref[...], d_raw, NT, **EXACT_DOT) * net_ref[2, 0:units]
        g_two = lax.dot_general(net_ref[1], s_two, NT, **EXACT_DOT)
        d_one = jnp.dot(w2_ref[...] * freq, s_two, **EXACT_DOT)[0:units]
        g_one = lax.dot_general(ft_ref[...], d_one * net_ref[0, 0:units], NT, **EXACT_DOT)
        g_freq = jnp.sum(w1_ref[...] * g_one, axis=0, keepdims=True) + jnp.sum(
            w2_ref[...] * g_two, axis=0, keepdims=True
        )
        vf_ref[...] = jnp.zeros(vf_ref.shape, F32)
        vf_ref[0, 0 : g_one.shape[0]] = g_one * freq
        vf_ref[1, 0 : g_two.shape[0]] = g_two * freq
        vf_ref[2, 0:1] = g_freq
        f_ctx.start(vf_ref[...])

    pl.run_scoped(filter_back, pltpu.VMEM(net_hbm.shape, F32))
    a_ctx.start(va_ref[...])
    d_ctx.start(vd_ref[...])
    late.pair()
    down.steps(15, 17)
    for job in early:
        job.cross()
    for one, two in ((a_ctx, a_dp), (d_ctx, d_dp), (l_ctx, l_dp), (f_ctx, f_dp)):
        two.start(one.total())
    down.steps(17, 20)
    late.own()

    proj.steps(0, 4)
    va_ref[...] = a_dp.total()
    last_sum = l_dp.total()
    for o in range(owners):
        held = vl_ref.shape[1]
        vl_ref[o] = last_sum[o * held : (o + 1) * held]
    sums = d_dp.total()
    vd_ref[...] = sums
    d_tp.start(sums)
    f_tp.start(f_dp.total())
    proj.steps(4, 8)
    late.cross()
    proj.steps(8, proj.pairs + 2 * LAG)
    for s in range(blocks):
        down.wait_block(s)
        proj.wait_block(s)
    vd_ref[4:6] = d_tp.total()[4:6]
    vf_ref[...] = f_tp.total()
    for job in (a_ctx, a_dp, d_ctx, d_dp, d_tp, l_ctx, l_dp, f_ctx, f_dp, f_tp):
        job.finish()
    for job in early + [late]:
        job.finish()
    for i in range(1, 4):
        to_ctx(i).wait_send()
    down.drain()
    proj.drain()


def final_kernel(
    resid_ref, dsum_ref, dres_ref, psum_ref, x_ref, gain_ref, bias_ref, va_ref, vd_ref, vl_ref, vf_ref,
    oup_ref, odown_ref, oout_ref, oin_ref,
    result_ref, gradx_ref, up_ref, down_ref, out_ref, in_ref,
    mgain_ref, mshift_ref, inb_ref, sw_ref, sb_ref, f1_ref, f1b_ref, f2_ref, f2b_ref, freq_ref, last_ref,
    skip_ref, ob_ref, fgain_ref, fshift_ref, ub_ref, db_ref,
):
    step = pl.program_id(0)

    @pl.when(step == 0)
    def _():
        up_ref[...] = oup_ref[...]
        down_ref[...] = odown_ref[...]
        out_ref[...] = oout_ref[...]
        rows = oin_ref.shape[2]
        for h in range(2):
            in_ref[:, h * rows : (h + 1) * rows] = oin_ref[h]
        mgain_ref[...] = vd_ref[4]
        mshift_ref[...] = vd_ref[5]
        db_ref[...] = vd_ref[0]
        ob_ref[...] = vd_ref[1]
        fgain_ref[...] = vd_ref[2]
        fshift_ref[...] = vd_ref[3]
        ub_ref[...] = vd_ref[6]
        for g in range(3):
            sw_ref[g] = va_ref[3 * g : 3 * g + 3]
        inb_ref[...] = va_ref[9:12]
        sb_ref[...] = va_ref[12:15]
        skip_ref[...] = va_ref[15]
        units = f1_ref.shape[1]
        rows_one, rows_two = f1_ref.shape[0], f2_ref.shape[0]
        f1_ref[...] = vf_ref[0, 0:rows_one]
        f1b_ref[...] = vf_ref[0, rows_one]
        f2_ref[...] = vf_ref[1, 0:rows_two]
        f2b_ref[...] = vf_ref[1, rows_two]
        freq_ref[...] = vf_ref[2, 0]
        last_ref[...] = vl_ref[lax.axis_index("dp")]

    result_ref[...] = resid_ref[...] + dsum_ref[...].astype(F32) + bias_ref[...].reshape(1, -1)
    xhat, spread = normalize(x_ref[...].astype(F32))
    e = psum_ref[...].astype(F32) * gain_ref[...].reshape(1, -1)
    gradx_ref[...] = dres_ref[...] + spread * (
        e - jnp.mean(e, axis=-1, keepdims=True) - xhat * jnp.mean(e * xhat, axis=-1, keepdims=True)
    )


def body(
    block_in, out_grad, parents, mixer_gain, mixer_shift, in_proj, in_bias, short_weight, short_bias,
    filter_one, filter_one_bias, filter_two, filter_two_bias, filter_freq, filter_out, skip_gain,
    out_proj, out_bias, feed_gain, feed_shift, feed_up, feed_up_bias, feed_down, feed_down_bias,
):
    x = block_in[0]
    g = out_grad[0]
    total_rows, width = x.shape
    channels = skip_gain.shape[0]
    blocks = total_rows // SEG
    hidden = feed_up.shape[1]
    tp_count = lax.axis_size("tp")
    tp_index = lax.axis_index("tp")
    owners = lax.axis_size("dp")
    first = lax.axis_index("ctx") * blocks
    all_blocks = parents.shape[1]

    half = hidden // 2
    share = width // owners
    units, features = filter_one.shape[1], filter_one.shape[0]
    feat_rows, mid_rows = 40, units + 8
    length = DEPTH * SEG
    ft = jnp.asarray(filter_features(length, (features - 1) // 2, feat_rows))
    fh, fl, th, tl, sign = (jnp.asarray(t) for t in spectral_constants(SEG))
    dma = pltpu.SemaphoreType.DMA
    front_out = (
        sds((total_rows, width), BF16),
        sds((3, total_rows, channels), F32),
        sds((3, blocks, HEADS, channels), F32),
        sds((2, total_rows, channels), F32),
        sds((13, 2, SEG, channels), F32),
        sds((DEPTH, 2, SEG, channels), F32),
        sds((4, mid_rows, length), F32),
        sds((3, channels, width), BF16),
        sds((tp_count, owners, channels, share), BF16),
        sds((width, hidden), BF16),
        sds((owners, hidden, share), BF16),
        sds((units, channels), F32),
        sds((total_rows, channels), F32),
        sds((total_rows, channels), F32),
        sds((total_rows, channels), BF16),
        sds((total_rows, channels), BF16),
    )
    low, proj, head, mixed, spec, filt, net, in_all, out_all, up_all, down_all, last, gate, conv, gated, carried = call(
        front_kernel,
        front_out,
        [SM] + [VM] * 23,
        [
            pltpu.VMEM((3, channels, width), BF16),
            pltpu.VMEM((total_rows, width), BF16),
            pltpu.VMEM((3, total_rows, channels), F32),
            pltpu.VMEM((3, blocks, HEADS, channels), F32),
            pltpu.VMEM((2, total_rows, channels), F32),
            pltpu.VMEM((13, 2, SEG, channels), F32),
            pltpu.VMEM((DEPTH, 2, SEG, channels), F32),
            pltpu.VMEM((4, mid_rows, length), F32),
            pltpu.VMEM((length, channels), F32),
            pltpu.VMEM((8, SEG, channels), BF16),
            pltpu.VMEM((4, 2 * blocks, width), F32),
            pltpu.VMEM((3, 9, HEADS, channels), F32),
            pltpu.VMEM((3, HEADS + SEG, channels), F32),
            pltpu.VMEM((feat_rows, units), F32),
            pltpu.VMEM((mid_rows, units), F32),
            pltpu.VMEM((2, SEG, channels), F32),
            pltpu.VMEM((owners,) + filter_out.shape, BF16),
            pltpu.VMEM((owners, 3, channels, share), BF16),
            dma((owners,)), dma((owners,)), dma((owners,)), dma((owners,)),
            dma((owners * tp_count,)), dma((tp_count, owners)),
            dma((owners,)), dma((owners,)), dma((owners,)), dma((owners,)),
            dma((4,)), dma((4,)), dma((4, 4)), dma((4, 4)), dma((4,)), dma((12,)),
        ],
        1,
        out_specs=(HB,) * 11 + (VM,) * 5,
    )(
        parents, x, jnp.transpose(in_proj, (1, 2, 0)), filter_out, out_proj, feed_up, feed_down, ft,
        filter_one, filter_one_bias, filter_two, filter_two_bias, filter_freq, mixer_gain, mixer_shift,
        in_bias, short_weight, short_bias, skip_gain, fh, fl, th, tl, sign,
    )

    piece = share // 2
    residual, down_part, d_res, d_conv, d_zero, d_all, stage_up, stage_down, stage_out, small, grad_skip = call(
        feed_kernel,
        (
            sds((total_rows, width), F32),
            sds((total_rows, width), BF16),
            sds((total_rows, width), F32),
            sds((total_rows, channels), F32),
            sds((total_rows, channels), F32),
            sds((all_blocks, SEG, channels), BF16),
            sds((2, owners, piece, hidden), BF16),
            sds((2, owners, half, share), BF16),
            sds((2, owners, channels // 2, share), BF16),
            sds((8, width), F32),
            sds((1, channels), F32),
        ),
        [VM] * 13,
        [
            pltpu.VMEM((total_rows, width), BF16),
            pltpu.VMEM((total_rows, hidden), BF16),
            pltpu.VMEM((total_rows, hidden), BF16),
            pltpu.VMEM((total_rows, width), BF16),
            pltpu.VMEM((total_rows, width), BF16),
            pltpu.VMEM((total_rows, width), BF16),
            pltpu.VMEM((blocks, SEG, channels), BF16),
            pltpu.VMEM((tp_count, total_rows, channels), BF16),
            pltpu.VMEM((tp_count, channels, width), BF16),
            pltpu.VMEM((hidden, width), BF16),
            dma((tp_count, blocks)), dma((tp_count, blocks)), dma((4, blocks)), dma((4, blocks)),
        ]
        + LineSum.scratch(total_rows, width),
        2,
    )(
        gated, out_all, x, g, out_bias, feed_gain, feed_shift, up_all, feed_up_bias, down_all, gate, conv, carried
    )

    shapes = [(piece, hidden), (half, share), (channels // 2, share), (3, channels // 2, share)]
    scratch = [
        pltpu.VMEM((blocks, 2, SEG, channels), F32),
        pltpu.VMEM((total_rows, channels), F32),
        pltpu.VMEM((length, channels), F32),
        pltpu.VMEM((2, owners) + shapes[3], BF16),
        pltpu.VMEM((total_rows, width), BF16),
        pltpu.VMEM((feat_rows, units), F32),
        pltpu.VMEM((mid_rows, units), F32),
        pltpu.VMEM((all_blocks, HEADS, channels), F32),
        dma((4,)), dma((4,)), dma((8,)),
    ]
    scratch += LineSum.scratch(total_rows, width) * 2
    for shape in shapes:
        scratch += OwnerSum.scratch(owners, shape)
    smalls = ((16, channels), (8, width), (units, channels), (3, mid_rows, units))
    for shape, axes in zip(smalls, (2, 3, 2, 3)):
        for count in (4, owners, tp_count)[:axes]:
            scratch += SmallSum.scratch(count, shape)
    down_sum, proj_sum, own_up, own_down, own_out, own_in, va, vd, vl, vf = call(
        back_kernel,
        (
            sds((total_rows, width), BF16),
            sds((total_rows, width), BF16),
        )
        + tuple(sds((2,) + shape, F32) for shape in shapes)
        + (
            sds(smalls[0], F32),
            sds(smalls[1], F32),
            sds((owners,) + filter_out.shape, F32),
            sds(smalls[3], F32),
        ),
        [SM] + [VM] * 24 + [HB] * 8,
        scratch,
        3,
    )(
        parents, d_all, d_conv, d_zero, mixed, low, in_all, x, down_part, fh, fl, th, tl, sign, short_weight,
        skip_gain, ft, filter_one, filter_one_bias, filter_two, filter_two_bias, filter_freq, last, small, grad_skip,
        proj, head, spec, filt, net, stage_up, stage_down, stage_out,
    )

    def by_block(*shape):
        return pl.BlockSpec((SEG,) + shape, lambda i: (i,) + (0,) * len(shape))

    def whole(v):
        return pl.BlockSpec(v.shape, lambda i: (0,) * len(v.shape))

    wide = by_block(width)
    vectors = [
        sds(v.shape, F32)
        for v in (
            mixer_gain, mixer_shift, in_bias, short_weight, short_bias, filter_one, filter_one_bias, filter_two,
            filter_two_bias, filter_freq, filter_out, skip_gain, out_bias, feed_gain, feed_shift, feed_up_bias,
            feed_down_bias,
        )
    ]
    out = pl.pallas_call(
        final_kernel,
        grid=(blocks,),
        out_shape=[
            sds((total_rows, width), F32), sds((total_rows, width), F32), own_up, own_down, own_out,
            sds((3, channels, share), F32),
        ]
        + vectors,
        in_specs=[wide] * 5 + [whole(v) for v in (mixer_gain, feed_down_bias, va, vd, vl, vf, own_up, own_down, own_out, own_in)],
        out_specs=[wide, wide]
        + [whole(v) for v in (own_up, own_down, own_out, sds((3, channels, share), F32))]
        + [whole(v) for v in vectors],
        compiler_params=pltpu.CompilerParams(vmem_limit_bytes=LIMIT),
    )(
        residual, down_sum, d_res, proj_sum, x, mixer_gain, feed_down_bias, va, vd, vl, vf,
        own_up, own_down, own_out, own_in,
    )
    (result, grad_x, g_up, g_down, g_out, g_in, g_mgain, g_mshift, g_inb, g_sw, g_sb, g_f1, g_f1b, g_f2, g_f2b,
     g_freq, g_last, g_skip, g_ob, g_fgain, g_fshift, g_ub, g_db) = out
    return (
        result[None], grad_x[None], g_mgain, g_mshift, jnp.transpose(g_in, (2, 0, 1)), g_inb, g_sw, g_sb,
        g_f1, g_f1b, g_f2, g_f2b, g_freq, g_last, g_skip, g_out.reshape(channels, share), g_ob, g_fgain, g_fshift,
        g_up.reshape(share, hidden), g_ub, g_down.reshape(hidden, share), g_db,
    )


def solution(mesh):
    in_specs = (
        P("dp", "ctx", None), P("dp", "ctx", None), P("dp", None), P(), P(), P("dp", None, "tp"), P(None, "tp"),
        P(None, None, "tp"), P(None, "tp"), P(), P(), P(), P(), P(), P("dp", "tp"), P("tp"), P("tp", "dp"), P(),
        P(), P(), P("dp", "tp"), P("tp"), P("tp", "dp"), P(),
    )
    out_specs = (
        P("dp", "ctx", None), P("dp", "ctx", None), P(), P(), P("dp", None, "tp"), P(None, "tp"),
        P(None, None, "tp"), P(None, "tp"), P(), P(), P(), P(), P(), P("dp", "tp"), P("tp"), P("tp", "dp"), P(),
        P(), P(), P("dp", "tp"), P("tp"), P("tp", "dp"), P(),
    )
    return jax.shard_map(body, mesh=mesh, in_specs=in_specs, out_specs=out_specs, check_vma=False)
```

```python
import functools
import math

import jax
import jax.numpy as jnp
import numpy as np
from jax import lax
from jax.experimental import pallas as pl
from jax.experimental.pallas import tpu as pltpu
from jax.sharding import PartitionSpec as P

SEG = 256
DEPTH = 6
HEADS = 8
EXACT = lax.Precision.HIGHEST
EPSILON = 1e-05
SLOW_RATE = -math.log(0.01) / 1.5
FAST_RATE = -math.log(0.01) / 0.3
SHIFT_FLOOR = 0.05
F32 = jnp.float32
BF16 = jnp.bfloat16
MESH = pl.DeviceIdType.MESH
VM = pl.BlockSpec(memory_space=pltpu.VMEM)
SM = pl.BlockSpec(memory_space=pltpu.SMEM)
LIMIT = 62 << 20


def sds(shape, dtype):
    return jax.ShapeDtypeStruct(shape, dtype)


HB = pl.BlockSpec(memory_space=pl.ANY)


def call(kernel, out_shape, in_specs, scratch=(), collective=None, flops=0, traffic=0, out_specs=None):
    many = isinstance(out_shape, (tuple, list))
    return pl.pallas_call(
        kernel,
        out_shape=out_shape,
        in_specs=in_specs,
        out_specs=out_specs or (tuple(VM for _ in out_shape) if many else VM),
        scratch_shapes=list(scratch),
        compiler_params=pltpu.CompilerParams(
            vmem_limit_bytes=LIMIT,
            collective_id=collective,
            has_side_effects=collective is not None,
        ),
        cost_estimate=pl.CostEstimate(flops=flops, bytes_accessed=traffic, transcendentals=0),
    )


def spectral_constants(block_len):
    freq = np.arange(block_len)[:, None]
    place = np.arange(block_len)[None, :]
    angle = ((2 * freq + 1) * place % (4 * block_len)) * (2.0 * math.pi / (4 * block_len))
    table = np.concatenate([np.cos(angle), -np.sin(angle)], axis=0).astype(np.float32)
    high = table.astype(jnp.bfloat16)
    low = (table - high.astype(np.float32)).astype(jnp.bfloat16)
    sign = np.where(np.arange(block_len) % 2 == 0, 1.0, -1.0).astype(np.float32)[:, None]
    return high, low, np.ascontiguousarray(high.T), np.ascontiguousarray(low.T), sign


def normalize(values):
    mean_value = jnp.mean(values, axis=-1, keepdims=True)
    centered = values - mean_value
    variance = jnp.mean(centered * centered, axis=-1, keepdims=True)
    scale = lax.rsqrt(variance + EPSILON)
    return centered * scale, scale


def split(values):
    high = values.astype(BF16)
    return high, (values - high.astype(F32)).astype(BF16)


def mm(lhs, rhs):
    return jnp.dot(lhs, rhs, preferred_element_type=F32)


def mm_nt(lhs, rhs):
    return lax.dot_general(lhs, rhs, (((1,), (1,)), ((), ())), preferred_element_type=F32)


def mm_tn(lhs, rhs):
    return lax.dot_general(lhs, rhs, (((0,), (0,)), ((), ())), preferred_element_type=F32)


def mm_split(high, low, values):
    v_high, v_low = split(values)
    return mm(high, v_high) + (mm(low, v_high) + mm(high, v_low))


FT = 32


def lineage(par_ref, block):
    out = []
    current = block
    for _ in range(DEPTH - 1):
        parent = par_ref[0, jnp.maximum(current, 0)]
        current = jnp.where(current >= 0, parent, -1)
        out.append(current)
    return out


def blend_all(dst, terms, conj):
    def tile(t, unused):
        rows = pl.ds(pl.multiple_of(t * FT, FT), FT)
        re = im = None
        for a, b in terms:
            ar, ai = a[0, rows], a[1, rows]
            br, bi = b[0, rows], b[1, rows]
            if conj:
                pr, pi = ar * br + ai * bi, ar * bi - ai * br
            else:
                pr, pi = ar * br - ai * bi, ar * bi + ai * br
            re, im = (pr, pi) if re is None else (re + pr, im + pi)
        dst[0, rows] = re
        dst[1, rows] = im
        return unused

    lax.fori_loop(0, SEG // FT, tile, 0)


def unpack_spectrum(th, tl, ref):
    high_re, low_re = split(ref[0])
    high_im, low_im = split(ref[1])
    a, b = slice(0, SEG), slice(SEG, 2 * SEG)
    return (
        mm(th[:, a], high_re) + mm(th[:, b], high_im)
        + (mm(tl[:, a], high_re) + mm(tl[:, b], high_im))
        + (mm(th[:, a], low_re) + mm(th[:, b], low_im))
    )


def filter_features(length, bands, rows):
    positions = np.arange(length)
    time_pos = positions / (length - 1)
    freq = np.linspace(0.0001, bands - 1, bands)
    phases = (2.0 * math.pi / length * positions)[None, :] * freq[:, None]
    table = np.zeros((rows, length), np.float32)
    table[0] = time_pos
    table[1 : bands + 1] = np.cos(phases)
    table[bands + 1 : 2 * bands + 1] = -np.sin(phases)
    table[2 * bands + 1] = 1.0
    return table


def spot(**changes):
    base = {name: lax.axis_index(name) for name in ("dp", "ctx", "tp")}
    base.update(changes)
    return (base["dp"], base["ctx"], base["tp"])


def remote(src, dst, send, recv, where):
    return pltpu.make_async_remote_copy(
        src_ref=src, dst_ref=dst, send_sem=send, recv_sem=recv, device_id=where, device_id_type=MESH
    )


def greet(partners):
    barrier = pltpu.get_barrier_semaphore()
    for where in partners:
        pl.semaphore_signal(barrier, inc=1, device_id=where, device_id_type=MESH)
    pl.semaphore_wait(barrier, len(partners))


CHUNK = 32
PER = SEG // (2 * CHUNK)
LAG = 2


def chunk(c):
    return pl.ds(pl.multiple_of(c * CHUNK, CHUNK), CHUNK)


class LineSum:
    scratch_count = 11

    @staticmethod
    def scratch(rows, width):
        count = rows // CHUNK
        return [
            pltpu.VMEM((rows, width), BF16),
            pltpu.VMEM((rows // 2, width), BF16),
            pltpu.VMEM((rows // 2, width), BF16),
        ] + [pltpu.SemaphoreType.DMA((count,)) for _ in range(8)]

    def __init__(self, part, total, scratch):
        self.part, self.total = part, total
        self.end, self.mid, self.out = scratch[:3]
        self.sems = scratch[3:]
        self.pairs = part.shape[0] // (2 * CHUNK)
        tp = lax.axis_index("tp")
        self.inner = jnp.logical_and(tp > 0, tp < 3)
        self.outer = jnp.logical_not(self.inner)
        self.side = jnp.where(tp < 2, 0, 1)
        near = jnp.where(self.side == 0, 0, 3)
        far = jnp.where(self.side == 0, 1, 2)
        self.mate = spot(tp=jnp.where(self.inner, near, far))
        self.cross = spot(tp=3 - tp)

    def to_mid(self, c):
        return remote(self.part.at[chunk(c)], self.end.at[chunk(c)], self.sems[0].at[c], self.sems[1].at[c], self.mate)

    def to_cross(self, k):
        return remote(self.out.at[chunk(k)], self.mid.at[chunk(k)], self.sems[2].at[k], self.sems[3].at[k], self.cross)

    def final_end(self, c):
        at = self.total.at[chunk(c)]
        return remote(at, at, self.sems[4].at[c], self.sems[5].at[c], self.mate)

    def final_cross(self, c):
        at = self.total.at[chunk(c)]
        return remote(at, at, self.sems[6].at[c], self.sems[7].at[c], self.cross)

    def send_block(self, s):
        @pl.when(self.outer)
        def _():
            def one(i, unused):
                self.to_mid(s * 2 * PER + i).start()
                return unused

            lax.fori_loop(0, 2 * PER, one, 0)

    def step(self, k):
        pairs, side = self.pairs, self.side

        @pl.when(k < pairs)
        def _():
            other = 2 * k + 1 - side
            self.to_mid(2 * k).wait_recv()
            self.to_mid(2 * k + 1).wait_recv()
            self.out[chunk(k)] = (
                self.part[chunk(other)].astype(F32) + self.end[chunk(other)].astype(F32)
            ).astype(BF16)
            self.to_cross(k).start()

        j = k - LAG

        @pl.when(jnp.logical_and(j >= 0, j < pairs))
        def _():
            mine = 2 * j + side
            self.to_cross(j).wait_recv()
            self.total[chunk(mine)] = (
                self.part[chunk(mine)].astype(F32)
                + self.end[chunk(mine)].astype(F32)
                + self.mid[chunk(j)].astype(F32)
            ).astype(BF16)
            self.final_cross(mine).start()
            self.final_end(mine).start()

        i = k - 2 * LAG

        @pl.when(jnp.logical_and(i >= 0, i < pairs))
        def _():
            other = 2 * i + 1 - side
            self.final_cross(other).wait_recv()
            self.final_end(other).start()

    def steps(self, first, last):
        @pl.when(self.inner)
        def _():
            def one(k, unused):
                self.step(k)
                return unused

            lax.fori_loop(first, last, one, 0)

    def wait_block(self, s):
        @pl.when(self.outer)
        def _():
            def one(i, unused):
                self.final_end(s * 2 * PER + i).wait_recv()
                return unused

            lax.fori_loop(0, 2 * PER, one, 0)

    def drain(self):
        @pl.when(self.outer)
        def _():
            def one(c, unused):
                self.to_mid(c).wait_send()
                return unused

            lax.fori_loop(0, 2 * self.pairs, one, 0)

        @pl.when(self.inner)
        def _():
            def one(k, unused):
                mine, other = 2 * k + self.side, 2 * k + 1 - self.side
                self.to_cross(k).wait_send()
                self.final_cross(mine).wait_send()
                self.final_end(mine).wait_send()
                self.final_end(other).wait_send()
                return unused

            lax.fori_loop(0, self.pairs, one, 0)


def signal_all(partners):
    barrier = pltpu.get_barrier_semaphore()
    for where in partners:
        pl.semaphore_signal(barrier, inc=1, device_id=where, device_id_type=MESH)
    return barrier, len(partners)


def store_columns(stage, half, value):
    owners, share = stage.shape[1], stage.shape[-1]
    for o in range(owners):
        stage[half, o] = value[:, o * share : (o + 1) * share].astype(BF16)


def store_rows(stage, first, value):
    size = stage.shape[2]
    for q in range(value.shape[0] // size):
        owner, half = divmod(first // size + q, 2)
        stage[half, owner] = value[q * size : (q + 1) * size].astype(BF16)


def feed_kernel(
    gated_ref, ob_ref, gain_ref, shift_ref, ub_ref,
    out_hbm, x_hbm, g_hbm, up_hbm, down_hbm, mixed_hbm, conv_hbm, carried_hbm,
    resid_hbm, dpart_hbm, dres_hbm, dconv_hbm, dzero_hbm, gup_hbm, gdown_hbm,
    dall_ref, gout_ref, small_ref, gskip_ref,
    out_in, x_ref, g_ref, up_ref, down_in, mixed_ref, conv_ref, carried_ref,
    resid_ref, dpart_ref, dres_ref, dconv_ref, dzero_ref, gup_ref, gdown_ref, s_load, s_save, s_block,
    low_ref, hidden_ref, dpre_ref, npart_ref, nsum_ref, dmix_ref, own_ref, gall_ref, out_ref, down_ref,
    s_gate, r_gate, s_long, r_long, *line,
):
    groups, owners = out_in.shape[:2]
    width = x_ref.shape[1]
    blocks = x_ref.shape[0] // SEG
    share = width // owners
    tp, ctx = lax.axis_index("tp"), lax.axis_index("ctx")
    chain = LineSum(npart_ref, nsum_ref, line)
    barrier, count = signal_all(
        [spot(tp=lax.rem(tp + i, groups)) for i in range(1, groups)]
        + [spot(ctx=lax.rem(ctx + i, 4)) for i in range(1, 4)]
    )

    def gate_copy(s, i):
        rows = pl.ds(pl.multiple_of(s * SEG, SEG), SEG)
        return remote(
            gated_ref.at[rows], gall_ref.at[tp, rows], s_gate.at[i, s], r_gate.at[tp, s],
            spot(tp=lax.rem(tp + i, groups)),
        )

    loads = [
        pltpu.make_async_copy(src, dst, s_load.at[k])
        for k, (src, dst) in enumerate(
            (
                (out_hbm, out_in), (x_hbm, x_ref), (up_hbm, up_ref), (down_hbm, down_in), (g_hbm, g_ref),
                (mixed_hbm, mixed_ref), (conv_hbm, conv_ref), (carried_hbm, carried_ref),
            )
        )
    ]
    for load in loads:
        load.start()

    def save(k, src, dst, s):
        rows = pl.ds(pl.multiple_of(s * SEG, SEG), SEG)
        return pltpu.make_async_copy(src.at[rows], dst.at[rows], s_block.at[k, s])

    blockwise = ((resid_ref, resid_hbm), (dres_ref, dres_hbm), (dconv_ref, dconv_hbm), (dzero_ref, dzero_hbm))
    saves = [
        pltpu.make_async_copy(src, dst, s_save.at[k])
        for k, (src, dst) in enumerate(((dpart_ref, dpart_hbm), (gup_ref, gup_hbm), (gdown_ref, gdown_hbm)))
    ]
    gall_ref[tp] = gated_ref[...]
    pl.semaphore_wait(barrier, count)
    for s in range(blocks):
        for i in range(1, groups):
            gate_copy(s, i).start()
    for load in loads:
        load.wait()
    for o in range(owners):
        columns = slice(o * share, (o + 1) * share)
        down_ref[:, columns] = down_in[o]
        for z in range(groups):
            out_ref[z, :, columns] = out_in[z, o]
    ob, gain, shift = (ref[...].reshape(1, -1) for ref in (ob_ref, gain_ref, shift_ref))
    ub = ub_ref[...].reshape(1, -1)
    small_ref[...] = jnp.zeros(small_ref.shape, F32)
    gskip_ref[...] = jnp.zeros(gskip_ref.shape, F32)

    def core(s, unused):
        rows = pl.ds(pl.multiple_of(s * SEG, SEG), SEG)
        for i in range(1, groups):
            source = lax.rem(tp + i, groups)
            at = gall_ref.at[source, rows]
            remote(at, at, s_gate.at[i, s], r_gate.at[source, s], chain.mate).wait_recv()
        mixed = mm(gall_ref[0, rows], out_ref[0])
        for z in range(1, groups):
            mixed = mixed + mm(gall_ref[z, rows], out_ref[z])
        residual = x_ref[rows].astype(F32) + mixed + ob
        resid_ref[rows] = residual
        save(0, *blockwise[0], s).start()
        low = (normalize(residual)[0] * gain + shift).astype(BF16)
        low_ref[rows] = low
        pre = mm(low, up_ref[...]) + ub
        cdf = 0.5 * (1.0 + lax.erf(pre * math.sqrt(0.5)))
        hidden_ref[rows] = (pre * cdf).astype(BF16)
        slope = cdf + pre * (jnp.exp(-0.5 * pre * pre) * (1.0 / math.sqrt(2.0 * math.pi)))
        grad = g_ref[rows]
        d_pre = (mm_nt(grad, down_ref[...]) * slope).astype(BF16)
        dpre_ref[rows] = d_pre
        npart_ref[rows] = mm_nt(d_pre, up_ref[...]).astype(BF16)
        small_ref[0:1] += jnp.sum(grad.astype(F32), axis=0, keepdims=True)
        small_ref[6:7] += jnp.sum(d_pre.astype(F32), axis=0, keepdims=True)
        chain.send_block(s)
        return unused

    lax.fori_loop(0, blocks, core, 0)
    chain.steps(0, PER)

    def down(s, unused):
        rows = pl.ds(pl.multiple_of(s * SEG, SEG), SEG)
        dpart_ref[rows] = mm(hidden_ref[rows], down_ref[...]).astype(BF16)
        return unused

    lax.fori_loop(0, blocks, down, 0)
    for t in range(2):
        part = slice(t * width // 2, (t + 1) * width // 2)
        store_rows(gup_ref, t * width // 2, mm_tn(low_ref[:, part], dpre_ref[...]))
        units = hidden_ref.shape[1] // 2
        store_columns(gdown_ref, t, mm_tn(hidden_ref[:, t * units : (t + 1) * units], g_ref[...]))

    for job in saves:
        job.start()

    def to_ctx(s, other):
        return remote(own_ref.at[s], dall_ref.at[ctx * blocks + s], s_long.at[other, s], r_long.at[ctx, s], spot(ctx=other))

    def back(s, unused):
        chain.steps((s + 1) * PER, (s + 2) * PER)
        chain.wait_block(s)
        rows = pl.ds(pl.multiple_of(s * SEG, SEG), SEG)
        xhat, scale = normalize(resid_ref[rows])
        dn = nsum_ref[rows].astype(F32)
        e = dn * gain
        d_res = g_ref[rows].astype(F32) + scale * (
            e - jnp.mean(e, axis=-1, keepdims=True) - xhat * jnp.mean(e * xhat, axis=-1, keepdims=True)
        )
        dres_ref[rows] = d_res
        small_ref[2:3] += jnp.sum(dn * xhat, axis=0, keepdims=True)
        small_ref[3:4] += jnp.sum(dn, axis=0, keepdims=True)
        d_mix = d_res.astype(BF16)
        dmix_ref[rows] = d_mix
        small_ref[1:2] += jnp.sum(d_mix.astype(F32), axis=0, keepdims=True)
        d_gated = mm_nt(d_mix, out_ref[tp])
        d_conv = d_gated * mixed_ref[rows]
        dconv_ref[rows] = d_conv
        own_ref[s] = d_conv.astype(BF16)
        for other in range(3):
            @pl.when(other < ctx)
            def _():
                to_ctx(s, other).start()

        dzero_ref[rows] = d_gated * conv_ref[rows]
        gskip_ref[...] += jnp.sum(d_conv * carried_ref[rows].astype(F32), axis=0, keepdims=True)
        for k in (1, 2, 3):
            save(k, *blockwise[k], s).start()
        return unused

    lax.fori_loop(0, blocks, back, 0)
    for s in range(blocks):
        dall_ref[ctx * blocks + s] = own_ref[s]
    value = mm_tn(gated_ref[...], dmix_ref[...])
    for t in range(2):
        store_columns(gout_ref, t, value[t * gout_ref.shape[2] : (t + 1) * gout_ref.shape[2]])
    for s in range(blocks):
        for i in range(1, groups):
            gate_copy(s, i).wait_send()
    chain.drain()
    for job in saves:
        job.wait()
    for s in range(blocks):
        for k in range(4):
            save(k, *blockwise[k], s).wait()
    for other in range(4):
        @pl.when(other < ctx)
        def _():
            for s in range(blocks):
                to_ctx(s, other).wait_send()

        @pl.when(other > ctx)
        def _():
            for s in range(blocks):
                at = dall_ref.at[other * blocks + s]
                remote(at, at, s_long.at[other, s], r_long.at[other, s], chain.mate).wait_recv()


def extend_weights(ref, weight, bias):
    rows = weight.shape[0]
    ref[...] = jnp.zeros(ref.shape, F32)
    ref[0:rows] = weight[...]
    ref[rows : rows + 1] = bias[...].reshape(1, -1)


def decay(length, channels, tp, width):
    time_pos = lax.broadcasted_iota(jnp.int32, (length, 1), 0).astype(F32) * (1.0 / (length - 1))
    channel = (lax.broadcasted_iota(jnp.int32, (1, channels), 1) + tp * channels).astype(F32)
    rate = SLOW_RATE + (FAST_RATE - SLOW_RATE) * channel * (1.0 / (width - 1))
    return jnp.exp(-time_pos * rate) + SHIFT_FLOOR


EXACT_DOT = dict(precision=EXACT, preferred_element_type=F32)
TN = (((0,), (0,)), ((), ()))
NT = (((1,), (1,)), ((), ()))


def front_kernel(
    par_ref, x_ref, win_ref, last_ref, out_in, up_in, down_in, ft_ref, f1_ref, f1b_ref, f2_ref, f2b_ref, freq_ref,
    gain_ref, shift_ref, ib_ref, sw_ref, sb_ref, skip_ref, fh_ref, fl_ref, th_ref, tl_ref, sign_ref,
    low_hbm, proj_hbm, head_hbm, mixed_hbm, spec_hbm, filt_hbm, net_hbm, in_hbm, out_hbm, up_hbm, down_hbm,
    lasts_ref, gate_ref, conv_ref, gated_ref, carried_ref,
    w_ref, low_ref, proj_ref, head_ref, mixed_ref, spec_ref, filt_ref, net_ref, taps_ref, shared_ref,
    xt_ref, tail_ref, ext_ref, w1_ref, w2_ref, acc_ref, lastb_ref, wb_ref,
    s_in, r_in, s_last, r_last, s_out, r_out, s_up, r_up, s_down, r_down, s_line, r_line, s_swap,
    s_xt, r_xt, s_car, r_car, s_fwd, local,
):
    total_rows, width = x_ref.shape
    channels = ib_ref.shape[1]
    blocks = total_rows // SEG
    tp, ctx, dp = lax.axis_index("tp"), lax.axis_index("ctx"), lax.axis_index("dp")
    owners, lines = out_hbm.shape[1], out_hbm.shape[0]
    share = win_ref.shape[2]
    last_share = last_ref.shape[0]
    up_share = up_in.shape[0]

    def cell(i):
        flat = lax.rem(tp * owners + dp + i, owners * lines)
        return flat // owners, lax.rem(flat, owners)

    def owner(i):
        return lax.rem(dp + i, owners)

    def ctx_at(i):
        return lax.rem(ctx + i, 4)

    partners = [spot(ctx=ctx_at(i)) for i in range(1, 4)]
    for i in range(1, owners * lines):
        line, own = cell(i)
        partners.append(spot(tp=line, dp=own))
    barrier, count = signal_all(partners)

    def rows_of(ref, who, size):
        return ref.at[pl.ds(pl.multiple_of(who * size, size), size)]

    def send_in(i):
        return remote(win_ref, wb_ref.at[dp], s_in.at[i], r_in.at[dp], spot(dp=owner(i)))

    def send_last(i):
        return remote(last_ref, lastb_ref.at[dp], s_last.at[i], r_last.at[dp], spot(dp=owner(i)))

    def send_xt(i):
        at = xt_ref.at[ctx]
        return remote(at, at, s_xt.at[i], r_xt.at[ctx], spot(ctx=ctx_at(i)))

    for s in range(blocks):
        tail = x_ref[s * SEG + SEG - 16 : s * SEG + SEG].astype(F32)
        xt_ref[ctx, 2 * s : 2 * s + 2] = tail[14:16]
    pl.semaphore_wait(barrier, count)
    for i in range(1, owners):
        send_in(i).start()
        send_last(i).start()
    for i in range(1, 4):
        send_xt(i).start()
    wb_ref[dp] = win_ref[...]
    lastb_ref[dp] = last_ref[...]

    gain, shift = gain_ref[...].reshape(1, -1), shift_ref[...].reshape(1, -1)

    def norm(s, unused):
        rows = pl.ds(pl.multiple_of(s * SEG, SEG), SEG)
        low_ref[rows] = (normalize(x_ref[rows].astype(F32))[0] * gain + shift).astype(BF16)
        return unused

    lax.fori_loop(0, blocks, norm, 0)
    saves = [pltpu.make_async_copy(low_ref, low_hbm, local.at[1])]
    saves[-1].start()

    units = f1_ref.shape[1]
    length = ft_ref.shape[1]
    extend_weights(w1_ref, f1_ref, f1b_ref)
    extend_weights(w2_ref, f2_ref, f2b_ref)
    freq = freq_ref[...].reshape(1, -1)
    net_ref[...] = jnp.zeros(net_ref.shape, F32)
    angle = lax.dot_general(w1_ref[...] * freq, ft_ref[...], TN, **EXACT_DOT)
    net_ref[0, 0:units] = jnp.cos(angle)
    net_ref[1, 0:units] = jnp.sin(angle)
    pad = net_ref.shape[1] - units
    net_ref[1, units:] = jnp.where(lax.broadcasted_iota(jnp.int32, (pad, length), 0) == 0, 1.0, 0.0)
    angle = lax.dot_general(w2_ref[...] * freq, net_ref[1], TN, **EXACT_DOT)
    net_ref[2, 0:units] = jnp.cos(angle)
    second = jnp.sin(angle)
    net_ref[3, 0:units] = second
    saves.append(pltpu.make_async_copy(net_ref, net_hbm, local.at[2]))
    saves[-1].start()
    for i in range(1, owners):
        at = lastb_ref.at[owner(i)]
        remote(at, at, s_last.at[i], r_last.at[owner(i)], spot(dp=owner(i))).wait_recv()
    for o in range(owners):
        lasts_ref[o * last_share : (o + 1) * last_share] = lastb_ref[o].astype(F32)
    raw = lax.dot_general(second, lasts_ref[...], TN, **EXACT_DOT)
    taps_ref[...] = raw * decay(length, channels, tp, channels * lines)
    fh, fl, th, tl = fh_ref[...], fl_ref[...], th_ref, tl_ref
    sign = sign_ref[...]
    for j in range(DEPTH):
        part = taps_ref[j * SEG : (j + 1) * SEG]
        out = mm_split(fh, fl, part)
        re, im = out[:SEG], out[SEG:]
        filt_ref[j, 0] = re
        filt_ref[j, 1] = im
    for j in range(DEPTH - 1, 0, -1):
        first = taps_ref[(j - 1) * SEG : (j - 1) * SEG + 1]
        filt_ref[j, 0] = filt_ref[j, 0] - sign * filt_ref[j - 1, 1]
        filt_ref[j, 1] = filt_ref[j, 1] + sign * (filt_ref[j - 1, 0] - first)
    saves.append(pltpu.make_async_copy(filt_ref, filt_hbm, local.at[3]))
    saves[-1].start()

    for i in range(1, owners):
        at = wb_ref.at[owner(i)]
        remote(at, at, s_in.at[i], r_in.at[owner(i)], spot(dp=owner(i))).wait_recv()
    for o in range(owners):
        w_ref[:, :, o * share : (o + 1) * share] = wb_ref[o]
    saves.append(pltpu.make_async_copy(w_ref, in_hbm, local.at[4]))
    saves[-1].start()

    low_half = lax.rem(ctx, 2)
    mate = spot(ctx=ctx + 1 - 2 * low_half)

    def half_of(ref, half):
        size = ref.shape[0] // 2
        return ref.at[pl.ds(pl.multiple_of(half * size, 16), size)]

    def up_half(ref, half):
        size = ref.shape[1] // 2
        return ref.at[:, pl.ds(pl.multiple_of(half * size, size), size)]

    def line_out(i):
        return remote(
            out_in, out_hbm.at[tp, dp], s_line.at[i], r_line.at[tp], spot(tp=lax.rem(tp + i, lines))
        )

    def send_out(i, j):
        return remote(
            half_of(out_in, low_half), half_of(out_hbm.at[tp, dp], low_half), s_out.at[i, j], r_out.at[0, tp, dp],
            spot(dp=owner(i), tp=lax.rem(tp + j, lines)),
        )

    def swap_out(i, line):
        at = half_of(out_hbm.at[line, owner(i)], low_half)
        return remote(at, at, s_swap.at[2, i, line], r_out.at[1, line, owner(i)], mate)

    def send_up(i):
        return remote(
            up_half(up_in, low_half), up_half(rows_of(up_hbm, dp, up_share), low_half), s_up.at[i], r_up.at[0, dp],
            spot(dp=owner(i)),
        )

    def swap_up(i):
        at = up_half(rows_of(up_hbm, owner(i), up_share), low_half)
        return remote(at, at, s_swap.at[0, i, 0], r_up.at[1, owner(i)], mate)

    def send_down(i):
        return remote(
            half_of(down_in, low_half), half_of(down_hbm.at[dp], low_half), s_down.at[i], r_down.at[0, dp],
            spot(dp=owner(i)),
        )

    def swap_down(i):
        at = half_of(down_hbm.at[owner(i)], low_half)
        return remote(at, at, s_swap.at[1, i, 0], r_down.at[1, owner(i)], mate)

    for i in range(1, owners):
        for j in range(lines):
            send_out(i, j).start()
        send_up(i).start()
        send_down(i).start()
    for i in range(1, lines):
        line_out(i).start()
    for k, (src, dst) in enumerate(
        ((out_in, out_hbm.at[tp, dp]), (up_in, rows_of(up_hbm, dp, up_share)), (down_in, down_hbm.at[dp]))
    ):
        saves.append(pltpu.make_async_copy(src, dst, local.at[5 + k]))
        saves[-1].start()

    for i in range(1, 4):
        at = xt_ref.at[ctx_at(i)]
        remote(at, at, s_xt.at[i], r_xt.at[ctx_at(i)], spot(ctx=ctx_at(i))).wait_recv()
    tail_ref[...] = jnp.zeros(tail_ref.shape, F32)
    for half in range(2):
        tails = (normalize(xt_ref[half])[0] * gain + shift).astype(BF16)
        for g in range(3):
            value = mm_nt(tails, w_ref[g]) + ib_ref[g : g + 1]
            for s in range(4):
                tail_ref[g, 4 * half + s, 6:8] = value[2 * s : 2 * s + 2]

    def share_block(s, other):
        return remote(
            carried_ref.at[pl.ds(pl.multiple_of(s * SEG, SEG), SEG)], shared_ref.at[4 * ctx + s],
            s_car.at[other, s], r_car.at[ctx, s], spot(ctx=other),
        )

    def forward_block(s, group):
        at = shared_ref.at[4 * group + s]
        return remote(at, at, s_fwd.at[s], r_car.at[group, s], spot(ctx=5 - ctx))

    def mix(s, unused):
        rows = pl.ds(pl.multiple_of(s * SEG, SEG), SEG)
        parent = par_ref[0, ctx * blocks + s]
        slot = jnp.where(parent >= 0, parent, 8)
        out = []
        for g in range(3):
            projected = mm_nt(low_ref[rows], w_ref[g]) + ib_ref[g : g + 1]
            proj_ref[g, rows] = projected
            head = tail_ref[g, slot]
            head_ref[g, s] = head
            ext_ref[g, 0:HEADS] = head
            ext_ref[g, HEADS : HEADS + SEG] = projected
            mixed = (
                sw_ref[g, 0:1] * ext_ref[g, HEADS - 2 : HEADS - 2 + SEG]
                + sw_ref[g, 1:2] * ext_ref[g, HEADS - 1 : HEADS - 1 + SEG]
                + sw_ref[g, 2:3] * projected
                + sb_ref[g : g + 1]
            )
            if g == 0:
                gate_ref[rows] = mixed
            else:
                mixed_ref[g - 1, rows] = mixed
            out.append(mixed)
        carried = (out[2] * out[1]).astype(BF16)
        carried_ref[rows] = carried

        @pl.when(ctx == 0)
        def _():
            share_block(s, 2).start()
            share_block(s, 1).start()

        @pl.when(ctx == 1)
        def _():
            share_block(s, 3).start()

        spec = mm(fh_ref[...], carried) + mm(fl_ref[...], carried)
        spec_ref[8 + s, 0] = spec[:SEG]
        spec_ref[8 + s, 1] = spec[SEG:]
        return unused

    lax.fori_loop(0, blocks, mix, 0)
    for k, (src, dst) in enumerate(((proj_ref, proj_hbm), (head_ref, head_hbm), (mixed_ref, mixed_hbm))):
        saves.append(pltpu.make_async_copy(src, dst, local.at[8 + k]))
        saves[-1].start()

    def spectrum(slot, part):
        out = mm(fh_ref[...], part) + mm(fl_ref[...], part)
        spec_ref[slot, 0] = out[:SEG]
        spec_ref[slot, 1] = out[SEG:]

    spec_ref[12] = jnp.zeros(spec_ref.shape[1:], F32)

    def arrived(group, s):
        at = shared_ref.at[4 * group + s]
        return remote(at, at, s_fwd.at[s], r_car.at[group, s], spot(ctx=ctx_at(1)))

    def copy_own(group):
        def one(s, unused):
            spec_ref[4 * group + s] = spec_ref[8 + s]
            return unused

        lax.fori_loop(0, 4, one, 0)

    def receive(group):
        def one(s, unused):
            arrived(group, s).wait_recv()
            spectrum(4 * group + s, shared_ref[4 * group + s])
            return unused

        lax.fori_loop(0, 4, one, 0)

    def receive_forward(group):
        def one(s, unused):
            arrived(group, s).wait_recv()
            forward_block(s, group).start()
            spectrum(4 * group + s, shared_ref[4 * group + s])
            return unused

        lax.fori_loop(0, 4, one, 0)

    @pl.when(ctx == 0)
    def _():
        copy_own(0)

    @pl.when(ctx == 1)
    def _():
        copy_own(1)
        receive(0)

    @pl.when(ctx == 2)
    def _():
        receive_forward(0)
        receive(1)

    @pl.when(ctx == 3)
    def _():
        receive_forward(1)
        receive(0)

    saves.append(pltpu.make_async_copy(spec_ref, spec_hbm, local.at[11]))
    saves[-1].start()

    def dest(s, unused):
        above = lineage(par_ref, ctx * blocks + s)
        places = [8 + s] + [jnp.where(a >= 0, a, 12) for a in above]
        blend_all(acc_ref, [(filt_ref.at[d], spec_ref.at[places[d]]) for d in range(DEPTH)], False)
        long_out = unpack_spectrum(th, tl, acc_ref) * (1.0 / SEG)
        place = pl.ds(pl.multiple_of(s * SEG, SEG), SEG)
        convolved = long_out + skip_ref[...].reshape(1, -1) * carried_ref[place].astype(F32)
        conv_ref[place] = convolved
        gated_ref[place] = (convolved * gate_ref[place]).astype(BF16)
        return unused

    lax.fori_loop(0, blocks, dest, 0)

    def take_halves(stage, half):
        for i in range(1, owners):
            who = owner(i)
            at = up_half(rows_of(up_hbm, who, up_share), half)
            remote(at, at, s_up.at[i], r_up.at[stage, who], mate).wait_recv()
            if stage == 0:
                swap_up(i).start()
            at = half_of(down_hbm.at[who], half)
            remote(at, at, s_down.at[i], r_down.at[stage, who], mate).wait_recv()
            if stage == 0:
                swap_down(i).start()
            for line in range(lines):
                at = half_of(out_hbm.at[line, who], half)
                remote(at, at, s_out.at[i, line], r_out.at[stage, line, who], mate).wait_recv()
                if stage == 0:
                    swap_out(i, line).start()

    take_halves(0, low_half)

    for save in saves:
        save.wait()
    take_halves(1, 1 - low_half)
    for i in range(1, owners):
        send_in(i).wait_send()
        send_last(i).wait_send()
        send_up(i).wait_send()
        send_down(i).wait_send()
        swap_up(i).wait_send()
        swap_down(i).wait_send()
        for j in range(lines):
            send_out(i, j).wait_send()
            swap_out(i, j).wait_send()
    for i in range(1, lines):
        line_out(i).wait_send()
        line = lax.rem(tp + i, lines)
        at = out_hbm.at[line, dp]
        remote(at, at, s_line.at[i], r_line.at[line], mate).wait_recv()
    for i in range(1, 4):
        send_xt(i).wait_send()

    @pl.when(ctx == 0)
    def _():
        for s in range(blocks):
            share_block(s, 2).wait_send()
            share_block(s, 1).wait_send()

    @pl.when(ctx == 1)
    def _():
        for s in range(blocks):
            share_block(s, 3).wait_send()

    @pl.when(ctx == 2)
    def _():
        for s in range(blocks):
            forward_block(s, 0).wait_send()

    @pl.when(ctx == 3)
    def _():
        for s in range(blocks):
            forward_block(s, 1).wait_send()


class OwnerSum:
    scratch_count = 17

    @staticmethod
    def scratch(owners, shape):
        many = max(owners - 1, 1)
        return [
            pltpu.VMEM((owners,) + shape, BF16),
            pltpu.VMEM((owners,) + shape, BF16),
            pltpu.VMEM((many,) + shape, BF16),
            pltpu.VMEM(shape, BF16),
            pltpu.VMEM(shape, BF16),
            pltpu.SemaphoreType.DMA,
            pltpu.SemaphoreType.DMA,
            pltpu.SemaphoreType.DMA,
            pltpu.SemaphoreType.DMA((many,)),
            pltpu.SemaphoreType.DMA((many,)),
            pltpu.SemaphoreType.DMA,
            pltpu.SemaphoreType.DMA,
            pltpu.SemaphoreType.DMA,
            pltpu.SemaphoreType.DMA,
        ]

    def __init__(self, stage, out, scratch):
        self.stage, self.result = stage, out
        self.recv, self.keep, self.parts, self.y_own, self.y_in = scratch[:5]
        self.sems = scratch[5:]
        self.owners = stage.shape[1]
        self.dp, ctx = lax.axis_index("dp"), lax.axis_index("ctx")
        self.low = lax.rem(ctx, 2)
        self.mate = spot(ctx=ctx + 1 - 2 * self.low)
        self.across = spot(ctx=lax.rem(ctx + 2, 4))

    def load(self):
        return pltpu.make_async_copy(self.stage.at[self.low], self.keep, self.sems[0])

    def to_mate(self):
        return remote(self.stage.at[1 - self.low], self.recv, self.sems[1], self.sems[2], self.mate)

    def to_owner(self, i):
        owner = lax.rem(self.dp + i, self.owners)
        return remote(
            self.keep.at[owner], self.parts.at[self.owners - 1 - i], self.sems[3].at[i - 1],
            self.sems[4].at[self.owners - 1 - i], spot(dp=owner),
        )

    def from_owner(self, i):
        return remote(self.parts.at[i - 1], self.parts.at[i - 1], self.sems[3].at[i - 1], self.sems[4].at[i - 1], self.mate)

    def to_across(self):
        return remote(self.y_own, self.y_in, self.sems[5], self.sems[6], self.across)

    def to_back(self):
        at = self.result.at[self.low]
        return remote(at, at, self.sems[7], self.sems[8], self.mate)

    def begin(self):
        self.to_mate().start()
        self.load().start()

    def pair(self):
        self.load().wait()
        self.to_mate().wait_recv()
        for o in range(self.owners):
            self.keep[o] = (self.keep[o].astype(F32) + self.recv[o].astype(F32)).astype(BF16)
        for i in range(1, self.owners):
            self.to_owner(i).start()

    def own(self):
        total = self.keep[self.dp].astype(F32)
        for i in range(1, self.owners):
            self.from_owner(i).wait_recv()
            total = total + self.parts[i - 1].astype(F32)
        self.y_own[...] = total.astype(BF16)
        self.to_across().start()

    def cross(self):
        self.to_across().wait_recv()
        self.result[self.low] = self.y_own[...].astype(F32) + self.y_in[...].astype(F32)
        self.to_back().start()

    def finish(self):
        self.to_mate().wait_send()
        for i in range(1, self.owners):
            self.to_owner(i).wait_send()
        self.to_across().wait_send()
        self.to_back().wait_send()
        at = self.result.at[1 - self.low]
        remote(at, at, self.sems[7], self.sems[8], self.mate).wait_recv()


class SmallSum:
    @staticmethod
    def scratch(count, shape):
        return [
            pltpu.VMEM((count,) + shape, F32),
            pltpu.SemaphoreType.DMA((count,)),
            pltpu.SemaphoreType.DMA((count,)),
        ]

    def __init__(self, axis, scratch):
        self.axis = axis
        self.slots, self.send, self.recv = scratch
        self.count = self.slots.shape[0]
        self.me = lax.axis_index(axis)

    def copy(self, i):
        at = self.slots.at[self.me]
        other = lax.rem(self.me + i, self.count)
        return remote(at, at, self.send.at[i], self.recv.at[self.me], spot(**{self.axis: other}))

    def start(self, value):
        self.slots[self.me] = value
        for i in range(1, self.count):
            self.copy(i).start()

    def total(self):
        for i in range(1, self.count):
            other = lax.rem(self.me + i, self.count)
            at = self.slots.at[other]
            remote(at, at, self.send.at[i], self.recv.at[other], spot(**{self.axis: lax.rem(self.me + i, self.count)})).wait_recv()
        out = self.slots[0]
        for i in range(1, self.count):
            out = out + self.slots[i]
        return out

    def finish(self):
        for i in range(1, self.count):
            self.copy(i).wait_send()


def back_kernel(
    par_ref, dall_ref, dconv_ref, dzero_ref, dpart_ref,
    fh_ref, fl_ref, th_ref, tl_ref, sign_ref, sw_ref, skip_ref,
    ft_ref, f1_ref, f1b_ref, f2_ref, f2b_ref, freq_ref, last_ref, small_ref, gskip_ref,
    mixed_hbm, low_hbm, w_hbm, x_hbm, proj_hbm, head_hbm, spec_hbm, filt_hbm, net_hbm, sup_hbm, sdown_hbm, sout_hbm,
    dsum_ref, psum_ref, oup_ref, odown_ref, oout_ref, oin_ref, va_ref, vd_ref, vl_ref, vf_ref,
    yown_ref, dcar_ref, dtaps_ref, stage_in, ppart_ref, w1_ref, w2_ref,
    mixed_ref, low_ref, w_ref, x_ref, hd_ref, s_hd, r_hd, local, *rest,
):
    width = x_ref.shape[1]
    channels = dconv_ref.shape[1]
    total_rows = x_ref.shape[0]
    blocks = total_rows // SEG
    owners = sup_hbm.shape[1]
    ctx, tp, dp = lax.axis_index("ctx"), lax.axis_index("tp"), lax.axis_index("dp")
    rest = list(rest)

    def take(n):
        out = rest[:n]
        del rest[:n]
        return out

    down = LineSum(dpart_ref, dsum_ref, take(11))
    proj = LineSum(ppart_ref, psum_ref, take(11))
    early = [OwnerSum(s, o, take(14)) for s, o in ((sup_hbm, oup_ref), (sdown_hbm, odown_ref), (sout_hbm, oout_ref))]
    late = OwnerSum(stage_in, oin_ref, take(14))
    a_ctx, a_dp = SmallSum("ctx", take(3)), SmallSum("dp", take(3))
    d_ctx, d_dp, d_tp = SmallSum("ctx", take(3)), SmallSum("dp", take(3)), SmallSum("tp", take(3))
    l_ctx, l_dp = SmallSum("ctx", take(3)), SmallSum("dp", take(3))
    f_ctx, f_dp, f_tp = SmallSum("ctx", take(3)), SmallSum("dp", take(3)), SmallSum("tp", take(3))

    partners = [spot(tp=lax.rem(tp + i, 4)) for i in range(1, 4)]
    partners += [spot(ctx=lax.rem(ctx + i, 4)) for i in range(1, 4)]
    partners += [spot(dp=lax.rem(dp + i, owners)) for i in range(1, owners)]
    barrier, count = signal_all(partners)
    pl.semaphore_wait(barrier, count)
    for s in range(blocks):
        down.send_block(s)
    loads = [
        pltpu.make_async_copy(src, dst, local.at[4 + k])
        for k, (src, dst) in enumerate(((mixed_hbm, mixed_ref), (w_hbm, w_ref), (x_hbm, x_ref), (low_hbm, low_ref)))
    ]
    for load in loads:
        load.start()
    for job in early:
        job.begin()
    fh, fl, th, tl = fh_ref[...], fl_ref[...], th_ref, tl_ref
    skip = skip_ref[...].reshape(1, -1)
    scale = 1.0 / SEG

    def put(dst, value):
        dst[0] = value[:SEG] * scale
        dst[1] = value[SEG:] * scale

    def conv_inputs(filt_ref, more_ref, acc_ref):
        load = pltpu.make_async_copy(filt_hbm, filt_ref, local.at[0])
        load.start()

        def transform(s, unused):
            part = dall_ref[ctx * blocks + s]
            put(yown_ref.at[s], mm(fh, part) + mm(fl, part))
            return unused

        lax.fori_loop(0, blocks, transform, 0)
        load.wait()

        def leaf_sum(match):
            total = None
            for leaf in range(8, 16):
                term = jnp.where(match(leaf), 1.0, 0.0) * dall_ref[leaf].astype(F32)
                total = term if total is None else total + term
            return total

        def from_leaf(b):
            return lambda leaf: par_ref[0, leaf] == b

        def finish(s, terms):
            blend_all(acc_ref, terms, True)
            place = pl.ds(pl.multiple_of(s * SEG, SEG), SEG)
            dcar_ref[place] = unpack_spectrum(th, tl, acc_ref) + skip * dconv_ref[place]

        @pl.when(ctx == 0)
        def _():
            def gather(k, unused):
                p = k + 1
                total = None
                for b in range(4, 8):
                    term = jnp.where(par_ref[0, b] == p, 1.0, 0.0) * dall_ref[b].astype(F32)
                    total = term if total is None else total + term
                put(more_ref.at[k], mm_split(fh, fl, total))
                total = leaf_sum(lambda leaf: par_ref[0, par_ref[0, leaf]] == p)
                put(more_ref.at[3 + k], mm_split(fh, fl, total))
                return unused

            lax.fori_loop(0, 3, gather, 0)
            for a in range(4):
                terms = [(filt_ref.at[s - a], yown_ref.at[s]) for s in range(a, 4)]
                for p in range(max(a, 1), 4):
                    terms.append((filt_ref.at[p - a + 1], more_ref.at[p - 1]))
                    terms.append((filt_ref.at[p - a + 2], more_ref.at[p + 2]))
                finish(a, terms)

        @pl.when(ctx == 1)
        def _():
            def one(b, unused):
                put(more_ref.at[0], mm_split(fh, fl, leaf_sum(from_leaf(b + 4))))
                finish(b, [(filt_ref.at[0], yown_ref.at[b]), (filt_ref.at[1], more_ref.at[0])])
                return unused

            lax.fori_loop(0, 4, one, 0)

        @pl.when(ctx > 1)
        def _():
            def one(b, unused):
                finish(b, [(filt_ref.at[0], yown_ref.at[b])])
                return unused

            lax.fori_loop(0, 4, one, 0)

    pl.run_scoped(
        conv_inputs,
        pltpu.VMEM((DEPTH, 2, SEG, channels), F32),
        pltpu.VMEM((6, 2, SEG, channels), F32),
        pltpu.VMEM((2, SEG, channels), F32),
    )

    for load in loads:
        load.wait()

    def to_ctx(i):
        at = hd_ref.at[pl.ds(ctx * blocks, blocks)]
        return remote(at, at, s_hd.at[i], r_hd.at[ctx], spot(ctx=lax.rem(ctx + i, 4)))

    for s in range(blocks):
        top = slice(s * SEG, s * SEG + HEADS)
        d_car = dcar_ref[top]
        rows = [dzero_ref[top], d_car * mixed_ref[1, top], d_car * mixed_ref[0, top]]
        for g in range(3):
            hd_ref[ctx * blocks + s, 2 * g : 2 * g + 2] = rows[g][0:2]
        hd_ref[ctx * blocks + s, 6:8] = jnp.zeros((2, channels), F32)
    for i in range(1, 4):
        to_ctx(i).start()
    down.steps(0, 4)
    for job in early:
        job.pair()

    va_ref[...] = jnp.zeros(va_ref.shape, F32)
    vd_ref[...] = small_ref[...]
    va_ref[15:16] = gskip_ref[...]
    for i in range(1, 4):
        other = lax.rem(ctx + i, 4)
        at = hd_ref.at[pl.ds(other * blocks, blocks)]
        remote(at, at, s_hd.at[i], r_hd.at[other], spot(ctx=other)).wait_recv()

    def with_spectra(spec_ref):
        pltpu.make_async_copy(spec_hbm, spec_ref, local.at[0]).start()

        def mix_back(dp_ref, ext_ref, dm_ref, pin_ref, hin_ref):
            load_heads = pltpu.make_async_copy(head_hbm, hin_ref, local.at[1])
            load_heads.start()

            def fetch(s):
                rows = pl.ds(pl.multiple_of(s * SEG, SEG), SEG)
                return pltpu.make_async_copy(proj_hbm.at[:, rows], pin_ref.at[lax.rem(s, 2)], local.at[2 + lax.rem(s, 2)])

            fetch(0).start()
            load_heads.wait()

            def one(s, unused):
                rows = pl.ds(pl.multiple_of(s * SEG, SEG), SEG)
                slot = lax.rem(s, 2)
                fetch(s).wait()

                @pl.when(s + 1 < blocks)
                def _():
                    fetch(s + 1).start()

                mine = ctx * blocks + s
                child = None
                for b in range(1, 16):
                    term = jnp.where(par_ref[0, b] == mine, 1.0, 0.0) * hd_ref[b]
                    child = term if child is None else child + term
                part = None
                for g in range(3):
                    if g == 0:
                        dm = dzero_ref[rows]
                    else:
                        dm = dcar_ref[rows] * mixed_ref[2 - g, rows]
                    ext_ref[0:HEADS] = hin_ref[g, s]
                    ext_ref[HEADS : HEADS + SEG] = pin_ref[slot, g]
                    for k in range(3):
                        piece = ext_ref[HEADS - 2 + k : HEADS - 2 + k + SEG]
                        va_ref[3 * g + k : 3 * g + k + 1] += jnp.sum(piece * dm, axis=0, keepdims=True)
                    va_ref[12 + g : 13 + g] += jnp.sum(dm, axis=0, keepdims=True)
                    dm_ref[0:SEG] = dm
                    dm_ref[SEG : SEG + 2] = child[2 * g : 2 * g + 2]
                    d_proj = (
                        sw_ref[g, 2:3] * dm
                        + sw_ref[g, 1:2] * dm_ref[1 : 1 + SEG]
                        + sw_ref[g, 0:1] * dm_ref[2 : 2 + SEG]
                    ).astype(BF16)
                    dp_ref[g, rows] = d_proj
                    va_ref[9 + g : 10 + g] += jnp.sum(d_proj.astype(F32), axis=0, keepdims=True)
                    term = mm(d_proj, w_ref[g])
                    part = term if part is None else part + term
                ppart_ref[rows] = part.astype(BF16)
                proj.send_block(s)
                xhat = normalize(x_ref[rows].astype(F32))[0]
                vd_ref[4:5] += jnp.sum(part * xhat, axis=0, keepdims=True)
                vd_ref[5:6] += jnp.sum(part, axis=0, keepdims=True)
                down.steps(4 + s, 5 + s)
                return unused

            lax.fori_loop(0, blocks, one, 0)
            rows = stage_in.shape[3]
            for g in range(3):
                value = mm_tn(dp_ref[g], low_ref[...])
                for t in range(2):
                    store_columns(stage_in.at[:, :, g], t, value[t * rows : (t + 1) * rows])

        pl.run_scoped(
            mix_back,
            pltpu.VMEM((3, total_rows, channels), BF16),
            pltpu.VMEM((HEADS + SEG, channels), F32),
            pltpu.VMEM((HEADS + SEG, channels), F32),
            pltpu.VMEM((2, 3, SEG, channels), F32),
            pltpu.VMEM((3, blocks, HEADS, channels), F32),
        )
        a_ctx.start(va_ref[...])
        d_ctx.start(vd_ref[...])
        late.begin()
        down.steps(8, 11)

        def conv_filters(dfilt_ref):
            pltpu.make_async_copy(spec_hbm, spec_ref, local.at[0]).wait()

            @pl.when(ctx == 0)
            def _():
                for d in range(4):
                    blend_all(dfilt_ref.at[d], [(spec_ref.at[8 + s - d], yown_ref.at[s]) for s in range(d, 4)], True)
                dfilt_ref[4:6] = jnp.zeros((2, 2, SEG, channels), F32)

            @pl.when(ctx > 0)
            def _():
                places = []
                for s in range(blocks):
                    above = lineage(par_ref, ctx * blocks + s)
                    places.append([8 + s] + [jnp.where(a >= 0, a, 12) for a in above])
                for d in range(DEPTH):
                    terms = [(spec_ref.at[places[s][d]], yown_ref.at[s]) for s in range(blocks)]
                    blend_all(dfilt_ref.at[d], terms, True)

            down.steps(11, 12)
            sign = sign_ref[...]
            first_row = lax.broadcasted_iota(jnp.int32, (SEG, 1), 0) == 0
            for j in range(DEPTH):
                fix = None
                if j + 1 < DEPTH:
                    nr, ni = dfilt_ref[j + 1, 0], dfilt_ref[j + 1, 1]
                    fix = jnp.sum(sign * ni, axis=0, keepdims=True)
                    dfilt_ref[j, 0] = dfilt_ref[j, 0] + sign * ni
                    dfilt_ref[j, 1] = dfilt_ref[j, 1] - sign * nr
                taps = unpack_spectrum(th, tl, dfilt_ref.at[j])
                if fix is not None:
                    taps = jnp.where(first_row, taps - fix, taps)
                dtaps_ref[j * SEG : (j + 1) * SEG] = taps

        pl.run_scoped(conv_filters, pltpu.VMEM((DEPTH, 2, SEG, channels), F32))

    pl.run_scoped(with_spectra, pltpu.VMEM((13, 2, SEG, channels), F32))
    down.steps(12, 13)

    def filter_back(net_ref):
        load = pltpu.make_async_copy(net_hbm, net_ref, local.at[1])
        load.start()
        d_raw = dtaps_ref[...] * decay(DEPTH * SEG, channels, tp, width)
        extend_weights(w1_ref, f1_ref, f1b_ref)
        extend_weights(w2_ref, f2_ref, f2b_ref)
        freq = freq_ref[...].reshape(1, -1)
        load.wait()
        units = last_ref.shape[0]
        l_ctx.start(jnp.dot(net_ref[3, 0:units], d_raw, **EXACT_DOT))
        s_two = lax.dot_general(last_ref[...], d_raw, NT, **EXACT_DOT) * net_ref[2, 0:units]
        g_two = lax.dot_general(net_ref[1], s_two, NT, **EXACT_DOT)
        d_one = jnp.dot(w2_ref[...] * freq, s_two, **EXACT_DOT)[0:units]
        g_one = lax.dot_general(ft_ref[...], d_one * net_ref[0, 0:units], NT, **EXACT_DOT)
        g_freq = jnp.sum(w1_ref[...] * g_one, axis=0, keepdims=True) + jnp.sum(
            w2_ref[...] * g_two, axis=0, keepdims=True
        )
        vf_ref[...] = jnp.zeros(vf_ref.shape, F32)
        vf_ref[0 : g_one.shape[0], 0:units] = g_one * freq
        vf_ref[0 : g_two.shape[0], units : 2 * units] = g_two * freq
        vf_ref[g_two.shape[0] : g_two.shape[0] + 1, 0:units] = g_freq
        f_ctx.start(vf_ref[...])

    pl.run_scoped(filter_back, pltpu.VMEM(net_hbm.shape, F32))

    def early_own():
        for job in early:
            job.own()

    def early_cross():
        for job in early:
            job.cross()

    def vectors():
        a_dp.start(a_ctx.total())
        d_dp.start(d_ctx.total())

    def networks():
        l_dp.start(l_ctx.total())
        f_dp.start(f_ctx.total())
        late.own()

    def gains():
        va_ref[...] = a_dp.total()
        sums = d_dp.total()
        vd_ref[...] = sums
        d_tp.start(sums[4:6])

    def last_layer():
        f_tp.start(f_dp.total())
        last_sum = l_dp.total()
        for o in range(owners):
            held = vl_ref.shape[1]
            vl_ref[o] = last_sum[o * held : (o + 1) * held]

    jobs = (early_own, late.pair, early_cross, vectors, networks, gains, last_layer)
    for k, job in enumerate(jobs):
        down.steps(13 + k, 14 + k)
        proj.steps(2 * k, 2 * k + 2)
        job()
    proj.steps(14, 17)
    late.cross()
    proj.steps(17, proj.pairs + 2 * LAG)
    for s in range(blocks):
        down.wait_block(s)
        proj.wait_block(s)
    vd_ref[4:6] = d_tp.total()
    vf_ref[...] = f_tp.total()
    for job in (a_ctx, a_dp, d_ctx, d_dp, d_tp, l_ctx, l_dp, f_ctx, f_dp, f_tp):
        job.finish()
    for job in early + [late]:
        job.finish()
    for i in range(1, 4):
        to_ctx(i).wait_send()
    down.drain()
    proj.drain()


def final_kernel(
    resid_ref, dsum_ref, dres_ref, psum_ref, x_ref, gain_ref, bias_ref, va_ref, vd_ref, vl_ref, vf_ref,
    oup_ref, odown_ref, oout_ref, oin_ref,
    result_ref, gradx_ref, up_ref, down_ref, out_ref, in_ref,
    mgain_ref, mshift_ref, inb_ref, sw_ref, sb_ref, f1_ref, f1b_ref, f2_ref, f2b_ref, freq_ref, last_ref,
    skip_ref, ob_ref, fgain_ref, fshift_ref, ub_ref, db_ref,
):
    step = pl.program_id(0)

    @pl.when(step == 0)
    def _():
        up_ref[...] = oup_ref[...]
        down_ref[...] = odown_ref[...]
        out_ref[...] = oout_ref[...]
        rows = oin_ref.shape[2]
        for h in range(2):
            in_ref[:, h * rows : (h + 1) * rows] = oin_ref[h]
        mgain_ref[...] = vd_ref[4]
        mshift_ref[...] = vd_ref[5]
        db_ref[...] = vd_ref[0]
        ob_ref[...] = vd_ref[1]
        fgain_ref[...] = vd_ref[2]
        fshift_ref[...] = vd_ref[3]
        ub_ref[...] = vd_ref[6]
        for g in range(3):
            sw_ref[g] = va_ref[3 * g : 3 * g + 3]
        inb_ref[...] = va_ref[9:12]
        sb_ref[...] = va_ref[12:15]
        skip_ref[...] = va_ref[15]
        units = f1_ref.shape[1]
        rows_one, rows_two = f1_ref.shape[0], f2_ref.shape[0]
        f1_ref[...] = vf_ref[0:rows_one, 0:units]
        f1b_ref[...] = vf_ref[rows_one, 0:units]
        f2_ref[...] = vf_ref[0:rows_two, units : 2 * units]
        f2b_ref[...] = vf_ref[rows_two, units : 2 * units]
        freq_ref[...] = vf_ref[rows_two + 8, 0:units]
        last_ref[...] = vl_ref[lax.axis_index("dp")]

    result_ref[...] = resid_ref[...] + dsum_ref[...].astype(F32) + bias_ref[...].reshape(1, -1)
    xhat, spread = normalize(x_ref[...].astype(F32))
    e = psum_ref[...].astype(F32) * gain_ref[...].reshape(1, -1)
    gradx_ref[...] = dres_ref[...] + spread * (
        e - jnp.mean(e, axis=-1, keepdims=True) - xhat * jnp.mean(e * xhat, axis=-1, keepdims=True)
    )


def body(
    block_in, out_grad, parents, mixer_gain, mixer_shift, in_proj, in_bias, short_weight, short_bias,
    filter_one, filter_one_bias, filter_two, filter_two_bias, filter_freq, filter_out, skip_gain,
    out_proj, out_bias, feed_gain, feed_shift, feed_up, feed_up_bias, feed_down, feed_down_bias,
):
    x = block_in[0]
    g = out_grad[0]
    total_rows, width = x.shape
    channels = skip_gain.shape[0]
    blocks = total_rows // SEG
    hidden = feed_up.shape[1]
    tp_count = lax.axis_size("tp")
    tp_index = lax.axis_index("tp")
    owners = lax.axis_size("dp")
    first = lax.axis_index("ctx") * blocks
    all_blocks = parents.shape[1]

    half = hidden // 2
    share = width // owners
    units, features = filter_one.shape[1], filter_one.shape[0]
    feat_rows, mid_rows = 40, units + 8
    length = DEPTH * SEG
    ft = jnp.asarray(filter_features(length, (features - 1) // 2, feat_rows))
    fh, fl, th, tl, sign = (jnp.asarray(t) for t in spectral_constants(SEG))
    dma = pltpu.SemaphoreType.DMA
    front_out = (
        sds((total_rows, width), BF16),
        sds((3, total_rows, channels), F32),
        sds((3, blocks, HEADS, channels), F32),
        sds((2, total_rows, channels), F32),
        sds((13, 2, SEG, channels), F32),
        sds((DEPTH, 2, SEG, channels), F32),
        sds((4, mid_rows, length), F32),
        sds((3, channels, width), BF16),
        sds((tp_count, owners, channels, share), BF16),
        sds((width, hidden), BF16),
        sds((owners, hidden, share), BF16),
        sds((units, channels), F32),
        sds((total_rows, channels), F32),
        sds((total_rows, channels), F32),
        sds((total_rows, channels), BF16),
        sds((total_rows, channels), BF16),
    )
    low, proj, head, mixed, spec, filt, net, in_all, out_all, up_all, down_all, last, gate, conv, gated, carried = call(
        front_kernel,
        front_out,
        [SM] + [VM] * 23,
        [
            pltpu.VMEM((3, channels, width), BF16),
            pltpu.VMEM((total_rows, width), BF16),
            pltpu.VMEM((3, total_rows, channels), F32),
            pltpu.VMEM((3, blocks, HEADS, channels), F32),
            pltpu.VMEM((2, total_rows, channels), F32),
            pltpu.VMEM((13, 2, SEG, channels), F32),
            pltpu.VMEM((DEPTH, 2, SEG, channels), F32),
            pltpu.VMEM((4, mid_rows, length), F32),
            pltpu.VMEM((length, channels), F32),
            pltpu.VMEM((8, SEG, channels), BF16),
            pltpu.VMEM((4, 2 * blocks, width), F32),
            pltpu.VMEM((3, 9, HEADS, channels), F32),
            pltpu.VMEM((3, HEADS + SEG, channels), F32),
            pltpu.VMEM((feat_rows, units), F32),
            pltpu.VMEM((mid_rows, units), F32),
            pltpu.VMEM((2, SEG, channels), F32),
            pltpu.VMEM((owners,) + filter_out.shape, BF16),
            pltpu.VMEM((owners, 3, channels, share), BF16),
            dma((owners,)), dma((owners,)), dma((owners,)), dma((owners,)),
            dma((owners, tp_count)), dma((2, tp_count, owners)),
            dma((owners,)), dma((2, owners)), dma((owners,)), dma((2, owners)),
            dma((tp_count,)), dma((tp_count,)), dma((3, owners, tp_count)),
            dma((4,)), dma((4,)), dma((4, 4)), dma((4, 4)), dma((4,)), dma((12,)),
        ],
        1,
        out_specs=(HB,) * 11 + (VM,) * 5,
    )(
        parents, x, jnp.transpose(in_proj, (1, 2, 0)), filter_out, out_proj, feed_up, feed_down, ft,
        filter_one, filter_one_bias, filter_two, filter_two_bias, filter_freq, mixer_gain, mixer_shift,
        in_bias, short_weight, short_bias, skip_gain, fh, fl, th, tl, sign,
    )

    piece = share // 2
    feed_big = [
        sds((total_rows, width), F32),
        sds((total_rows, width), BF16),
        sds((total_rows, width), F32),
        sds((total_rows, channels), F32),
        sds((total_rows, channels), F32),
        sds((2, owners, piece, hidden), BF16),
        sds((2, owners, half, share), BF16),
    ]
    feed_in = (out_all, x, g, up_all, down_all, gate, conv, carried)

    def held(v):
        return pltpu.VMEM(v.shape, v.dtype)

    residual, down_part, d_res, d_conv, d_zero, stage_up, stage_down, d_all, stage_out, small, grad_skip = call(
        feed_kernel,
        feed_big
        + [
            sds((all_blocks, SEG, channels), BF16),
            sds((2, owners, channels // 2, share), BF16),
            sds((8, width), F32),
            sds((1, channels), F32),
        ],
        [VM] * 5 + [HB] * 8,
        [held(v) for v in feed_in]
        + [held(v) for v in feed_big]
        + [dma((8,)), dma((3,)), dma((4, blocks))]
        + [
            pltpu.VMEM((total_rows, width), BF16),
            pltpu.VMEM((total_rows, hidden), BF16),
            pltpu.VMEM((total_rows, hidden), BF16),
            pltpu.VMEM((total_rows, width), BF16),
            pltpu.VMEM((total_rows, width), BF16),
            pltpu.VMEM((total_rows, width), BF16),
            pltpu.VMEM((blocks, SEG, channels), BF16),
            pltpu.VMEM((tp_count, total_rows, channels), BF16),
            pltpu.VMEM((tp_count, channels, width), BF16),
            pltpu.VMEM((hidden, width), BF16),
            dma((tp_count, blocks)), dma((tp_count, blocks)), dma((4, blocks)), dma((4, blocks)),
        ]
        + LineSum.scratch(total_rows, width),
        2,
        out_specs=(HB,) * 7 + (VM,) * 4,
    )(gated, out_bias, feed_gain, feed_shift, feed_up_bias, *feed_in)

    shapes = [(piece, hidden), (half, share), (channels // 2, share), (3, channels // 2, share)]
    scratch = [
        pltpu.VMEM((blocks, 2, SEG, channels), F32),
        pltpu.VMEM((total_rows, channels), F32),
        pltpu.VMEM((length, channels), F32),
        pltpu.VMEM((2, owners) + shapes[3], BF16),
        pltpu.VMEM((total_rows, width), BF16),
        pltpu.VMEM((feat_rows, units), F32),
        pltpu.VMEM((mid_rows, units), F32),
        held(mixed), held(low), held(in_all), held(x),
        pltpu.VMEM((all_blocks, HEADS, channels), F32),
        dma((4,)), dma((4,)), dma((8,)),
    ]
    scratch += LineSum.scratch(total_rows, width) * 2
    for shape in shapes:
        scratch += OwnerSum.scratch(owners, shape)
    smalls = ((16, channels), (8, width), (units, channels), (mid_rows + 8, 2 * units))
    for counts, shape in (
        ((4, owners), smalls[0]), ((4, owners), smalls[1]), ((tp_count,), (2, width)), ((4, owners), smalls[2]),
        ((4, owners, tp_count), smalls[3]),
    ):
        for count in counts:
            scratch += SmallSum.scratch(count, shape)
    down_sum, proj_sum, own_up, own_down, own_out, own_in, va, vd, vl, vf = call(
        back_kernel,
        (
            sds((total_rows, width), BF16),
            sds((total_rows, width), BF16),
        )
        + tuple(sds((2,) + shape, F32) for shape in shapes)
        + (
            sds(smalls[0], F32),
            sds(smalls[1], F32),
            sds((owners,) + filter_out.shape, F32),
            sds(smalls[3], F32),
        ),
        [SM] + [VM] * 20 + [HB] * 12,
        scratch,
        3,
    )(
        parents, d_all, d_conv, d_zero, down_part, fh, fl, th, tl, sign, short_weight,
        skip_gain, ft, filter_one, filter_one_bias, filter_two, filter_two_bias, filter_freq, last, small, grad_skip,
        mixed, low, in_all, x, proj, head, spec, filt, net, stage_up, stage_down, stage_out,
    )

    def by_block(*shape):
        return pl.BlockSpec((SEG,) + shape, lambda i: (i,) + (0,) * len(shape))

    def whole(v):
        return pl.BlockSpec(v.shape, lambda i: (0,) * len(v.shape))

    wide = by_block(width)
    vectors = [
        sds(v.shape, F32)
        for v in (
            mixer_gain, mixer_shift, in_bias, short_weight, short_bias, filter_one, filter_one_bias, filter_two,
            filter_two_bias, filter_freq, filter_out, skip_gain, out_bias, feed_gain, feed_shift, feed_up_bias,
            feed_down_bias,
        )
    ]
    out = pl.pallas_call(
        final_kernel,
        grid=(blocks,),
        out_shape=[
            sds((total_rows, width), F32), sds((total_rows, width), F32), own_up, own_down, own_out,
            sds((3, channels, share), F32),
        ]
        + vectors,
        in_specs=[wide] * 5 + [whole(v) for v in (mixer_gain, feed_down_bias, va, vd, vl, vf, own_up, own_down, own_out, own_in)],
        out_specs=[wide, wide]
        + [whole(v) for v in (own_up, own_down, own_out, sds((3, channels, share), F32))]
        + [whole(v) for v in vectors],
        compiler_params=pltpu.CompilerParams(vmem_limit_bytes=LIMIT),
    )(
        residual, down_sum, d_res, proj_sum, x, mixer_gain, feed_down_bias, va, vd, vl, vf,
        own_up, own_down, own_out, own_in,
    )
    (result, grad_x, g_up, g_down, g_out, g_in, g_mgain, g_mshift, g_inb, g_sw, g_sb, g_f1, g_f1b, g_f2, g_f2b,
     g_freq, g_last, g_skip, g_ob, g_fgain, g_fshift, g_ub, g_db) = out
    return (
        result[None], grad_x[None], g_mgain, g_mshift, jnp.transpose(g_in, (2, 0, 1)), g_inb, g_sw, g_sb,
        g_f1, g_f1b, g_f2, g_f2b, g_freq, g_last, g_skip, g_out.reshape(channels, share), g_ob, g_fgain, g_fshift,
        g_up.reshape(share, hidden), g_ub, g_down.reshape(hidden, share), g_db,
    )


def solution(mesh):
    in_specs = (
        P("dp", "ctx", None), P("dp", "ctx", None), P("dp", None), P(), P(), P("dp", None, "tp"), P(None, "tp"),
        P(None, None, "tp"), P(None, "tp"), P(), P(), P(), P(), P(), P("dp", "tp"), P("tp"), P("tp", "dp"), P(),
        P(), P(), P("dp", "tp"), P("tp"), P("tp", "dp"), P(),
    )
    out_specs = (
        P("dp", "ctx", None), P("dp", "ctx", None), P(), P(), P("dp", None, "tp"), P(None, "tp"),
        P(None, None, "tp"), P(None, "tp"), P(), P(), P(), P(), P(), P("dp", "tp"), P("tp"), P("tp", "dp"), P(),
        P(), P(), P("dp", "tp"), P("tp"), P("tp", "dp"), P(),
    )
    return jax.shard_map(body, mesh=mesh, in_specs=in_specs, out_specs=out_specs, check_vma=False)
```

```python
import functools
import math

import jax
import jax.numpy as jnp
import numpy as np
from jax import lax
from jax.experimental import pallas as pl
from jax.experimental.pallas import tpu as pltpu
from jax.sharding import PartitionSpec as P

SEG = 256
DEPTH = 6
HEADS = 8
EXACT = lax.Precision.HIGHEST
EPSILON = 1e-05
SLOW_RATE = -math.log(0.01) / 1.5
FAST_RATE = -math.log(0.01) / 0.3
SHIFT_FLOOR = 0.05
F32 = jnp.float32
BF16 = jnp.bfloat16
MESH = pl.DeviceIdType.MESH
VM = pl.BlockSpec(memory_space=pltpu.VMEM)
SM = pl.BlockSpec(memory_space=pltpu.SMEM)
LIMIT = 62 << 20


def sds(shape, dtype):
    return jax.ShapeDtypeStruct(shape, dtype)


HB = pl.BlockSpec(memory_space=pl.ANY)


def call(kernel, out_shape, in_specs, scratch=(), collective=None, flops=0, traffic=0, out_specs=None):
    many = isinstance(out_shape, (tuple, list))
    return pl.pallas_call(
        kernel,
        out_shape=out_shape,
        in_specs=in_specs,
        out_specs=out_specs or (tuple(VM for _ in out_shape) if many else VM),
        scratch_shapes=list(scratch),
        compiler_params=pltpu.CompilerParams(
            vmem_limit_bytes=LIMIT,
            collective_id=collective,
            has_side_effects=collective is not None,
        ),
        cost_estimate=pl.CostEstimate(flops=flops, bytes_accessed=traffic, transcendentals=0),
    )


def spectral_constants(block_len):
    freq = np.arange(block_len)[:, None]
    place = np.arange(block_len)[None, :]
    angle = ((2 * freq + 1) * place % (4 * block_len)) * (2.0 * math.pi / (4 * block_len))
    table = np.concatenate([np.cos(angle), -np.sin(angle)], axis=0).astype(np.float32)
    high = table.astype(jnp.bfloat16)
    low = (table - high.astype(np.float32)).astype(jnp.bfloat16)
    sign = np.where(np.arange(block_len) % 2 == 0, 1.0, -1.0).astype(np.float32)[:, None]
    return high, low, np.ascontiguousarray(high.T), np.ascontiguousarray(low.T), sign


def normalize(values):
    mean_value = jnp.mean(values, axis=-1, keepdims=True)
    centered = values - mean_value
    variance = jnp.mean(centered * centered, axis=-1, keepdims=True)
    scale = lax.rsqrt(variance + EPSILON)
    return centered * scale, scale


def split(values):
    high = values.astype(BF16)
    return high, (values - high.astype(F32)).astype(BF16)


def mm(lhs, rhs):
    return jnp.dot(lhs, rhs, preferred_element_type=F32)


def mm_nt(lhs, rhs):
    return lax.dot_general(lhs, rhs, (((1,), (1,)), ((), ())), preferred_element_type=F32)


def mm_tn(lhs, rhs):
    return lax.dot_general(lhs, rhs, (((0,), (0,)), ((), ())), preferred_element_type=F32)


def mm_split(high, low, values):
    v_high, v_low = split(values)
    return mm(high, v_high) + (mm(low, v_high) + mm(high, v_low))


FT = 32


def lineage(par_ref, block):
    out = []
    current = block
    for _ in range(DEPTH - 1):
        parent = par_ref[0, jnp.maximum(current, 0)]
        current = jnp.where(current >= 0, parent, -1)
        out.append(current)
    return out


def blend_all(dst, terms, conj):
    def tile(t, unused):
        rows = pl.ds(pl.multiple_of(t * FT, FT), FT)
        re = im = None
        for a, b in terms:
            ar, ai = a[0, rows], a[1, rows]
            br, bi = b[0, rows], b[1, rows]
            if conj:
                pr, pi = ar * br + ai * bi, ar * bi - ai * br
            else:
                pr, pi = ar * br - ai * bi, ar * bi + ai * br
            re, im = (pr, pi) if re is None else (re + pr, im + pi)
        dst[0, rows] = re
        dst[1, rows] = im
        return unused

    lax.fori_loop(0, SEG // FT, tile, 0)


def unpack_spectrum(th, tl, ref):
    high_re, low_re = split(ref[0])
    high_im, low_im = split(ref[1])
    a, b = slice(0, SEG), slice(SEG, 2 * SEG)
    return (
        mm(th[:, a], high_re) + mm(th[:, b], high_im)
        + (mm(tl[:, a], high_re) + mm(tl[:, b], high_im))
        + (mm(th[:, a], low_re) + mm(th[:, b], low_im))
    )


def filter_features(length, bands, rows):
    positions = np.arange(length)
    time_pos = positions / (length - 1)
    freq = np.linspace(0.0001, bands - 1, bands)
    phases = (2.0 * math.pi / length * positions)[None, :] * freq[:, None]
    table = np.zeros((rows, length), np.float32)
    table[0] = time_pos
    table[1 : bands + 1] = np.cos(phases)
    table[bands + 1 : 2 * bands + 1] = -np.sin(phases)
    table[2 * bands + 1] = 1.0
    return table


def spot(**changes):
    base = {name: lax.axis_index(name) for name in ("dp", "ctx", "tp")}
    base.update(changes)
    return (base["dp"], base["ctx"], base["tp"])


def remote(src, dst, send, recv, where):
    return pltpu.make_async_remote_copy(
        src_ref=src, dst_ref=dst, send_sem=send, recv_sem=recv, device_id=where, device_id_type=MESH
    )


def greet(partners):
    barrier = pltpu.get_barrier_semaphore()
    for where in partners:
        pl.semaphore_signal(barrier, inc=1, device_id=where, device_id_type=MESH)
    pl.semaphore_wait(barrier, len(partners))


CHUNK = 32
PER = SEG // (2 * CHUNK)
LAG = 2


def chunk(c):
    return pl.ds(pl.multiple_of(c * CHUNK, CHUNK), CHUNK)


class LineSum:
    scratch_count = 11

    @staticmethod
    def scratch(rows, width):
        count = rows // CHUNK
        return [
            pltpu.VMEM((rows, width), BF16),
            pltpu.VMEM((rows // 2, width), BF16),
            pltpu.VMEM((rows // 2, width), BF16),
        ] + [pltpu.SemaphoreType.DMA((count,)) for _ in range(8)]

    def __init__(self, part, total, scratch):
        self.part, self.total = part, total
        self.end, self.mid, self.out = scratch[:3]
        self.sems = scratch[3:]
        self.pairs = part.shape[0] // (2 * CHUNK)
        tp = lax.axis_index("tp")
        self.inner = jnp.logical_and(tp > 0, tp < 3)
        self.outer = jnp.logical_not(self.inner)
        self.side = jnp.where(tp < 2, 0, 1)
        near = jnp.where(self.side == 0, 0, 3)
        far = jnp.where(self.side == 0, 1, 2)
        self.mate = spot(tp=jnp.where(self.inner, near, far))
        self.cross = spot(tp=3 - tp)

    def to_mid(self, c):
        return remote(self.part.at[chunk(c)], self.end.at[chunk(c)], self.sems[0].at[c], self.sems[1].at[c], self.mate)

    def to_cross(self, k):
        return remote(self.out.at[chunk(k)], self.mid.at[chunk(k)], self.sems[2].at[k], self.sems[3].at[k], self.cross)

    def final_end(self, c):
        at = self.total.at[chunk(c)]
        return remote(at, at, self.sems[4].at[c], self.sems[5].at[c], self.mate)

    def final_cross(self, c):
        at = self.total.at[chunk(c)]
        return remote(at, at, self.sems[6].at[c], self.sems[7].at[c], self.cross)

    def send_block(self, s):
        @pl.when(self.outer)
        def _():
            def one(i, unused):
                self.to_mid(s * 2 * PER + i).start()
                return unused

            lax.fori_loop(0, 2 * PER, one, 0)

    def step(self, k):
        pairs, side = self.pairs, self.side

        @pl.when(k < pairs)
        def _():
            other = 2 * k + 1 - side
            self.to_mid(2 * k).wait_recv()
            self.to_mid(2 * k + 1).wait_recv()
            self.out[chunk(k)] = (
                self.part[chunk(other)].astype(F32) + self.end[chunk(other)].astype(F32)
            ).astype(BF16)
            self.to_cross(k).start()

        j = k - LAG

        @pl.when(jnp.logical_and(j >= 0, j < pairs))
        def _():
            mine = 2 * j + side
            self.to_cross(j).wait_recv()
            self.total[chunk(mine)] = (
                self.part[chunk(mine)].astype(F32)
                + self.end[chunk(mine)].astype(F32)
                + self.mid[chunk(j)].astype(F32)
            ).astype(BF16)
            self.final_cross(mine).start()
            self.final_end(mine).start()

        i = k - 2 * LAG

        @pl.when(jnp.logical_and(i >= 0, i < pairs))
        def _():
            other = 2 * i + 1 - side
            self.final_cross(other).wait_recv()
            self.final_end(other).start()

    def steps(self, first, last):
        @pl.when(self.inner)
        def _():
            def one(k, unused):
                self.step(k)
                return unused

            lax.fori_loop(first, last, one, 0)

    def wait_block(self, s):
        @pl.when(self.outer)
        def _():
            def one(i, unused):
                self.final_end(s * 2 * PER + i).wait_recv()
                return unused

            lax.fori_loop(0, 2 * PER, one, 0)

    def drain(self):
        @pl.when(self.outer)
        def _():
            def one(c, unused):
                self.to_mid(c).wait_send()
                return unused

            lax.fori_loop(0, 2 * self.pairs, one, 0)

        @pl.when(self.inner)
        def _():
            def one(k, unused):
                mine, other = 2 * k + self.side, 2 * k + 1 - self.side
                self.to_cross(k).wait_send()
                self.final_cross(mine).wait_send()
                self.final_end(mine).wait_send()
                self.final_end(other).wait_send()
                return unused

            lax.fori_loop(0, self.pairs, one, 0)


def signal_all(partners):
    barrier = pltpu.get_barrier_semaphore()
    for where in partners:
        pl.semaphore_signal(barrier, inc=1, device_id=where, device_id_type=MESH)
    return barrier, len(partners)


def store_columns(stage, half, value):
    owners, share = stage.shape[1], stage.shape[-1]
    for o in range(owners):
        stage[half, o] = value[:, o * share : (o + 1) * share].astype(BF16)


def store_rows(stage, first, value):
    size = stage.shape[2]
    for q in range(value.shape[0] // size):
        owner, half = divmod(first // size + q, 2)
        stage[half, owner] = value[q * size : (q + 1) * size].astype(BF16)


def feed_kernel(
    gated_ref, ob_ref, gain_ref, shift_ref, ub_ref, own_down,
    out_hbm, x_hbm, g_hbm, up_hbm, mixed_hbm, conv_hbm, carried_hbm,
    resid_hbm, dpart_hbm, dres_hbm, dconv_hbm, dzero_hbm, gup_hbm, gdown_hbm,
    dall_ref, gout_ref, small_ref, gskip_ref,
    out_in, x_ref, g_ref, up_ref, mixed_ref, conv_ref, carried_ref,
    resid_ref, dpart_ref, dres_ref, dconv_ref, dzero_ref, gup_ref, gdown_ref, s_load, s_save, s_block, down_in, s_down, r_down,
    low_ref, hidden_ref, dpre_ref, npart_ref, nsum_ref, dmix_ref, own_ref, gall_ref, out_ref, down_ref,
    s_gate, r_gate, s_long, r_long, *line,
):
    groups, owners = out_in.shape[:2]
    width = x_ref.shape[1]
    blocks = x_ref.shape[0] // SEG
    share = width // owners
    tp, ctx, dp = lax.axis_index("tp"), lax.axis_index("ctx"), lax.axis_index("dp")
    chain = LineSum(npart_ref, nsum_ref, line)
    barrier, count = signal_all(
        [spot(tp=lax.rem(tp + i, groups)) for i in range(1, groups)]
        + [spot(ctx=lax.rem(ctx + i, 4)) for i in range(1, 4)]
        + [spot(dp=lax.rem(dp + i, owners)) for i in range(1, owners)]
    )

    low_half = lax.rem(ctx, 2)
    pair_mate = spot(ctx=ctx + 1 - 2 * low_half)

    def owner(i):
        return lax.rem(dp + i, owners)

    def half_of(ref, half):
        size = ref.shape[0] // 2
        return ref.at[pl.ds(pl.multiple_of(half * size, 16), size)]

    def send_down(i):
        return remote(
            half_of(own_down, low_half), half_of(down_in.at[dp], low_half), s_down.at[0, i], r_down.at[0, dp],
            spot(dp=owner(i)),
        )

    def swap_down(i):
        at = half_of(down_in.at[owner(i)], low_half)
        return remote(at, at, s_down.at[1, i], r_down.at[1, owner(i)], pair_mate)

    def got_down(stage, i, half):
        at = half_of(down_in.at[owner(i)], half)
        return remote(at, at, s_down.at[0, i], r_down.at[stage, owner(i)], pair_mate)

    far = jnp.where(tp < 2, tp + 2, tp - 2)
    beyond = jnp.where(chain.side == 0, 3, 0)
    other = jnp.where(chain.inner, 3 - tp, far)
    near = jnp.where(chain.inner, jnp.where(chain.side == 0, 0, 3), jnp.where(chain.side == 0, 1, 2))

    def gate_copy(s, i):
        rows = pl.ds(pl.multiple_of(s * SEG, SEG), SEG)
        where = chain.mate if i == 0 else spot(tp=other)
        return remote(gated_ref.at[rows], gall_ref.at[tp, rows], s_gate.at[i, s], r_gate.at[tp, s], where)

    def gate_pass(s, i, source):
        at = gall_ref.at[source, pl.ds(pl.multiple_of(s * SEG, SEG), SEG)]
        return remote(at, at, s_gate.at[2 + i, s], r_gate.at[source, s], chain.mate)

    def gate_from(s, source):
        at = gall_ref.at[source, pl.ds(pl.multiple_of(s * SEG, SEG), SEG)]
        return remote(at, at, s_gate.at[0, s], r_gate.at[source, s], chain.mate)

    loads = [
        pltpu.make_async_copy(src, dst, s_load.at[k])
        for k, (src, dst) in enumerate(
            (
                (out_hbm, out_in), (x_hbm, x_ref), (up_hbm, up_ref), (g_hbm, g_ref),
                (mixed_hbm, mixed_ref), (conv_hbm, conv_ref), (carried_hbm, carried_ref),
            )
        )
    ]
    for load in loads:
        load.start()

    def save(k, src, dst, s):
        rows = pl.ds(pl.multiple_of(s * SEG, SEG), SEG)
        return pltpu.make_async_copy(src.at[rows], dst.at[rows], s_block.at[k, s])

    blockwise = ((resid_ref, resid_hbm), (dres_ref, dres_hbm), (dconv_ref, dconv_hbm), (dzero_ref, dzero_hbm))
    saves = [
        pltpu.make_async_copy(src, dst, s_save.at[k])
        for k, (src, dst) in enumerate(((dpart_ref, dpart_hbm), (gup_ref, gup_hbm), (gdown_ref, gdown_hbm)))
    ]
    gall_ref[tp] = gated_ref[...]
    pl.semaphore_wait(barrier, count)
    for s in range(blocks):
        for i in range(2):
            gate_copy(s, 1 - i).start()
    for i in range(1, owners):
        send_down(i).start()
    down_in[dp] = own_down[...]
    for load in loads:
        load.wait()
    for o in range(owners):
        columns = slice(o * share, (o + 1) * share)
        for z in range(groups):
            out_ref[z, :, columns] = out_in[z, o]
    ob, gain, shift = (ref[...].reshape(1, -1) for ref in (ob_ref, gain_ref, shift_ref))
    ub = ub_ref[...].reshape(1, -1)
    small_ref[...] = jnp.zeros(small_ref.shape, F32)
    gskip_ref[...] = jnp.zeros(gskip_ref.shape, F32)

    def core(s, unused):
        rows = pl.ds(pl.multiple_of(s * SEG, SEG), SEG)

        @pl.when(chain.inner)
        def _():
            for i, source in enumerate((3 - tp, beyond)):
                gate_from(s, source).wait_recv()
                gate_pass(s, i, source).start()
            gate_from(s, near).wait_recv()

        @pl.when(chain.outer)
        def _():
            gate_from(s, near).wait_recv()
            gate_from(s, 3 - near).wait_recv()
            gate_from(s, 3 - tp).wait_recv()

        mixed = mm(gall_ref[0, rows], out_ref[0])
        for z in range(1, groups):
            mixed = mixed + mm(gall_ref[z, rows], out_ref[z])
        residual = x_ref[rows].astype(F32) + mixed + ob
        resid_ref[rows] = residual
        save(0, *blockwise[0], s).start()
        low = (normalize(residual)[0] * gain + shift).astype(BF16)
        low_ref[rows] = low
        pre = mm(low, up_ref[...]) + ub
        cdf = 0.5 * (1.0 + lax.erf(pre * math.sqrt(0.5)))
        hidden_ref[rows] = (pre * cdf).astype(BF16)
        slope = cdf + pre * (jnp.exp(-0.5 * pre * pre) * (1.0 / math.sqrt(2.0 * math.pi)))

        @pl.when(s == 0)
        def _():
            for i in range(1, owners):
                got_down(0, i, low_half).wait_recv()
                swap_down(i).start()
            for i in range(1, owners):
                got_down(1, i, 1 - low_half).wait_recv()
            for o in range(owners):
                down_ref[:, o * share : (o + 1) * share] = down_in[o]

        grad = g_ref[rows]
        d_pre = (mm_nt(grad, down_ref[...]) * slope).astype(BF16)
        dpre_ref[rows] = d_pre
        npart_ref[rows] = mm_nt(d_pre, up_ref[...]).astype(BF16)
        small_ref[0:1] += jnp.sum(grad.astype(F32), axis=0, keepdims=True)
        small_ref[6:7] += jnp.sum(d_pre.astype(F32), axis=0, keepdims=True)
        chain.send_block(s)
        return unused

    lax.fori_loop(0, blocks, core, 0)
    chain.steps(0, PER)

    def down(s, unused):
        rows = pl.ds(pl.multiple_of(s * SEG, SEG), SEG)
        dpart_ref[rows] = mm(hidden_ref[rows], down_ref[...]).astype(BF16)
        return unused

    lax.fori_loop(0, blocks, down, 0)
    for t in range(2):
        part = slice(t * width // 2, (t + 1) * width // 2)
        store_rows(gup_ref, t * width // 2, mm_tn(low_ref[:, part], dpre_ref[...]))
        units = hidden_ref.shape[1] // 2
        store_columns(gdown_ref, t, mm_tn(hidden_ref[:, t * units : (t + 1) * units], g_ref[...]))

    for job in saves:
        job.start()

    def to_ctx(s, other):
        return remote(own_ref.at[s], dall_ref.at[ctx * blocks + s], s_long.at[other, s], r_long.at[ctx, s], spot(ctx=other))

    def back(s, unused):
        chain.steps((s + 1) * PER, (s + 2) * PER)
        chain.wait_block(s)
        rows = pl.ds(pl.multiple_of(s * SEG, SEG), SEG)
        xhat, scale = normalize(resid_ref[rows])
        dn = nsum_ref[rows].astype(F32)
        e = dn * gain
        d_res = g_ref[rows].astype(F32) + scale * (
            e - jnp.mean(e, axis=-1, keepdims=True) - xhat * jnp.mean(e * xhat, axis=-1, keepdims=True)
        )
        dres_ref[rows] = d_res
        small_ref[2:3] += jnp.sum(dn * xhat, axis=0, keepdims=True)
        small_ref[3:4] += jnp.sum(dn, axis=0, keepdims=True)
        d_mix = d_res.astype(BF16)
        dmix_ref[rows] = d_mix
        small_ref[1:2] += jnp.sum(d_mix.astype(F32), axis=0, keepdims=True)
        d_gated = mm_nt(d_mix, out_ref[tp])
        d_conv = d_gated * mixed_ref[rows]
        dconv_ref[rows] = d_conv
        own_ref[s] = d_conv.astype(BF16)
        for other in range(3):
            @pl.when(other < ctx)
            def _():
                to_ctx(s, other).start()

        dzero_ref[rows] = d_gated * conv_ref[rows]
        gskip_ref[...] += jnp.sum(d_conv * carried_ref[rows].astype(F32), axis=0, keepdims=True)
        for k in (1, 2, 3):
            save(k, *blockwise[k], s).start()
        return unused

    lax.fori_loop(0, blocks, back, 0)
    for s in range(blocks):
        dall_ref[ctx * blocks + s] = own_ref[s]
    value = mm_tn(gated_ref[...], dmix_ref[...])
    for t in range(2):
        store_columns(gout_ref, t, value[t * gout_ref.shape[2] : (t + 1) * gout_ref.shape[2]])
    for i in range(1, owners):
        send_down(i).wait_send()
        swap_down(i).wait_send()
    for s in range(blocks):
        for i in range(2):
            gate_copy(s, i).wait_send()

    @pl.when(chain.inner)
    def _():
        for s in range(blocks):
            for i, source in enumerate((3 - tp, beyond)):
                gate_pass(s, i, source).wait_send()

    chain.drain()
    for job in saves:
        job.wait()
    for s in range(blocks):
        for k in range(4):
            save(k, *blockwise[k], s).wait()
    for other in range(4):
        @pl.when(other < ctx)
        def _():
            for s in range(blocks):
                to_ctx(s, other).wait_send()

        @pl.when(other > ctx)
        def _():
            for s in range(blocks):
                at = dall_ref.at[other * blocks + s]
                remote(at, at, s_long.at[other, s], r_long.at[other, s], chain.mate).wait_recv()


def sine_cosine(angle):
    turns = jnp.floor(angle * (2.0 / math.pi) + 0.5)
    rest = ((angle - turns * 1.5703125) - turns * 4.837512969970703125e-4) - turns * 7.54978995489188216e-8
    square = rest * rest
    sine = ((-1.9515295891e-4 * square + 8.3321608736e-3) * square - 1.6666654611e-1) * square * rest + rest
    cosine = ((2.443315711809948e-5 * square - 1.388731625493765e-3) * square + 4.166664568298827e-2) * (
        square * square
    ) + (1.0 - 0.5 * square)
    quarter = turns - 4.0 * jnp.floor(turns * 0.25)
    odd = jnp.logical_or(quarter == 1.0, quarter == 3.0)
    middle = jnp.logical_or(quarter == 1.0, quarter == 2.0)
    sine, cosine = jnp.where(odd, cosine, sine), jnp.where(odd, sine, cosine)
    return jnp.where(quarter >= 2.0, -sine, sine), jnp.where(middle, -cosine, cosine)


def extend_weights(ref, weight, bias):
    rows = weight.shape[0]
    ref[...] = jnp.zeros(ref.shape, F32)
    ref[0:rows] = weight[...]
    ref[rows : rows + 1] = bias[...].reshape(1, -1)


def decay(length, channels, tp, width):
    time_pos = lax.broadcasted_iota(jnp.int32, (length, 1), 0).astype(F32) * (1.0 / (length - 1))
    channel = (lax.broadcasted_iota(jnp.int32, (1, channels), 1) + tp * channels).astype(F32)
    rate = SLOW_RATE + (FAST_RATE - SLOW_RATE) * channel * (1.0 / (width - 1))
    return jnp.exp(-time_pos * rate) + SHIFT_FLOOR


EXACT_DOT = dict(precision=EXACT, preferred_element_type=F32)
TN = (((0,), (0,)), ((), ()))
NT = (((1,), (1,)), ((), ()))


def front_kernel(
    par_ref, x_ref, win_ref, last_ref, out_in, up_in, ft_ref, f1_ref, f1b_ref, f2_ref, f2b_ref, freq_ref,
    gain_ref, shift_ref, ib_ref, sw_ref, sb_ref, skip_ref, fh_ref, fl_ref, th_ref, tl_ref, sign_ref,
    low_hbm, proj_hbm, head_hbm, mixed_hbm, spec_hbm, filt_hbm, net_hbm, in_hbm, out_hbm, up_hbm,
    lasts_ref, gate_ref, conv_ref, gated_ref, carried_ref,
    w_ref, low_ref, proj_ref, head_ref, mixed_ref, spec_ref, filt_ref, net_ref, taps_ref, shared_ref,
    xt_ref, tail_ref, ext_ref, w1_ref, w2_ref, acc_ref, lastb_ref, wb_ref,
    s_in, r_in, s_last, r_last, s_out, r_out, s_up, r_up, s_line, r_line, s_swap,
    s_xt, r_xt, s_car, r_car, s_fwd, local,
):
    total_rows, width = x_ref.shape
    channels = ib_ref.shape[1]
    blocks = total_rows // SEG
    tp, ctx, dp = lax.axis_index("tp"), lax.axis_index("ctx"), lax.axis_index("dp")
    owners, lines = out_hbm.shape[1], out_hbm.shape[0]
    share = win_ref.shape[2]
    last_share = last_ref.shape[0]
    up_share = up_in.shape[0]

    def cell(i):
        flat = lax.rem(tp * owners + dp + i, owners * lines)
        return flat // owners, lax.rem(flat, owners)

    def owner(i):
        return lax.rem(dp + i, owners)

    def ctx_at(i):
        return lax.rem(ctx + i, 4)

    partners = [spot(ctx=ctx_at(i)) for i in range(1, 4)]
    for i in range(1, owners * lines):
        line, own = cell(i)
        partners.append(spot(tp=line, dp=own))
    barrier, count = signal_all(partners)

    def rows_of(ref, who, size):
        return ref.at[pl.ds(pl.multiple_of(who * size, size), size)]

    low_half = lax.rem(ctx, 2)
    mate = spot(ctx=ctx + 1 - 2 * low_half)

    def in_half(ref, half):
        size = channels // 2
        return ref.at[:, pl.ds(pl.multiple_of(half * size, 16), size)]

    def send_in(i):
        return remote(
            in_half(win_ref, low_half), in_half(wb_ref.at[dp], low_half), s_in.at[0, i], r_in.at[0, dp],
            spot(dp=owner(i)),
        )

    def swap_in(i):
        at = in_half(wb_ref.at[owner(i)], low_half)
        return remote(at, at, s_in.at[1, i], r_in.at[1, owner(i)], mate)

    def got_in(stage, i, half):
        at = in_half(wb_ref.at[owner(i)], half)
        return remote(at, at, s_in.at[0, i], r_in.at[stage, owner(i)], mate)

    def send_last(i):
        return remote(last_ref, lastb_ref.at[dp], s_last.at[i], r_last.at[dp], spot(dp=owner(i)))

    def send_xt(i):
        at = xt_ref.at[ctx]
        return remote(at, at, s_xt.at[i], r_xt.at[ctx], spot(ctx=ctx_at(i)))

    for s in range(blocks):
        tail = x_ref[s * SEG + SEG - 16 : s * SEG + SEG].astype(F32)
        xt_ref[ctx, 2 * s : 2 * s + 2] = tail[14:16]
    pl.semaphore_wait(barrier, count)
    for i in range(1, owners):
        send_in(i).start()
        send_last(i).start()
    for i in range(1, 4):
        send_xt(i).start()
    wb_ref[dp] = win_ref[...]
    lastb_ref[dp] = last_ref[...]

    gain, shift = gain_ref[...].reshape(1, -1), shift_ref[...].reshape(1, -1)

    def norm(s, unused):
        rows = pl.ds(pl.multiple_of(s * SEG, SEG), SEG)
        low_ref[rows] = (normalize(x_ref[rows].astype(F32))[0] * gain + shift).astype(BF16)
        return unused

    lax.fori_loop(0, blocks, norm, 0)
    saves = [pltpu.make_async_copy(low_ref, low_hbm, local.at[1])]
    saves[-1].start()

    units = f1_ref.shape[1]
    length = ft_ref.shape[1]
    extend_weights(w1_ref, f1_ref, f1b_ref)
    extend_weights(w2_ref, f2_ref, f2b_ref)
    freq = freq_ref[...].reshape(1, -1)
    net_ref[...] = jnp.zeros(net_ref.shape, F32)
    angle = lax.dot_general(w1_ref[...] * freq, ft_ref[...], TN, **EXACT_DOT)
    first, net_ref[0, 0:units] = sine_cosine(angle)
    net_ref[1, 0:units] = first
    pad = net_ref.shape[1] - units
    net_ref[1, units:] = jnp.where(lax.broadcasted_iota(jnp.int32, (pad, length), 0) == 0, 1.0, 0.0)
    angle = lax.dot_general(w2_ref[...] * freq, net_ref[1], TN, **EXACT_DOT)
    second, net_ref[2, 0:units] = sine_cosine(angle)
    net_ref[3, 0:units] = second
    saves.append(pltpu.make_async_copy(net_ref, net_hbm, local.at[2]))
    saves[-1].start()
    for i in range(1, owners):
        at = lastb_ref.at[owner(i)]
        remote(at, at, s_last.at[i], r_last.at[owner(i)], spot(dp=owner(i))).wait_recv()
    for o in range(owners):
        lasts_ref[o * last_share : (o + 1) * last_share] = lastb_ref[o].astype(F32)
    raw = lax.dot_general(second, lasts_ref[...], TN, **EXACT_DOT)
    taps_ref[...] = raw * decay(length, channels, tp, channels * lines)
    fh, fl, th, tl = fh_ref[...], fl_ref[...], th_ref, tl_ref
    sign = sign_ref[...]
    for j in range(DEPTH):
        part = taps_ref[j * SEG : (j + 1) * SEG]
        out = mm_split(fh, fl, part)
        re, im = out[:SEG], out[SEG:]
        filt_ref[j, 0] = re
        filt_ref[j, 1] = im
    for j in range(DEPTH - 1, 0, -1):
        first = taps_ref[(j - 1) * SEG : (j - 1) * SEG + 1]
        filt_ref[j, 0] = filt_ref[j, 0] - sign * filt_ref[j - 1, 1]
        filt_ref[j, 1] = filt_ref[j, 1] + sign * (filt_ref[j - 1, 0] - first)
    saves.append(pltpu.make_async_copy(filt_ref, filt_hbm, local.at[3]))
    saves[-1].start()

    def half_of(ref, half):
        size = ref.shape[0] // 2
        return ref.at[pl.ds(pl.multiple_of(half * size, 16), size)]

    def up_half(ref, half):
        size = ref.shape[1] // 2
        return ref.at[:, pl.ds(pl.multiple_of(half * size, size), size)]

    def line_out(i):
        return remote(
            out_in, out_hbm.at[tp, dp], s_line.at[i], r_line.at[tp], spot(tp=lax.rem(tp + i, lines))
        )

    def send_out(i, j):
        return remote(
            half_of(out_in, low_half), half_of(out_hbm.at[tp, dp], low_half), s_out.at[i, j], r_out.at[0, tp, dp],
            spot(dp=owner(i), tp=lax.rem(tp + j, lines)),
        )

    def swap_out(i, line):
        at = half_of(out_hbm.at[line, owner(i)], low_half)
        return remote(at, at, s_swap.at[2, i, line], r_out.at[1, line, owner(i)], mate)

    def send_up(i):
        return remote(
            up_half(up_in, low_half), up_half(rows_of(up_hbm, dp, up_share), low_half), s_up.at[i], r_up.at[0, dp],
            spot(dp=owner(i)),
        )

    def swap_up(i):
        at = up_half(rows_of(up_hbm, owner(i), up_share), low_half)
        return remote(at, at, s_swap.at[0, i, 0], r_up.at[1, owner(i)], mate)

    for i in range(1, owners):
        got_in(0, i, low_half).wait_recv()
        swap_in(i).start()
        send_up(i).start()
        for j in range(lines):
            send_out(i, j).start()
    for i in range(1, lines):
        line_out(i).start()
    for i in range(1, owners):
        got_in(1, i, 1 - low_half).wait_recv()
    for o in range(owners):
        w_ref[:, :, o * share : (o + 1) * share] = wb_ref[o]
    saves.append(pltpu.make_async_copy(w_ref, in_hbm, local.at[4]))
    saves[-1].start()

    for k, (src, dst) in enumerate(
        ((out_in, out_hbm.at[tp, dp]), (up_in, rows_of(up_hbm, dp, up_share)))
    ):
        saves.append(pltpu.make_async_copy(src, dst, local.at[5 + k]))
        saves[-1].start()

    for i in range(1, 4):
        at = xt_ref.at[ctx_at(i)]
        remote(at, at, s_xt.at[i], r_xt.at[ctx_at(i)], spot(ctx=ctx_at(i))).wait_recv()
    tail_ref[...] = jnp.zeros(tail_ref.shape, F32)
    for half in range(2):
        tails = (normalize(xt_ref[half])[0] * gain + shift).astype(BF16)
        for g in range(3):
            value = mm_nt(tails, w_ref[g]) + ib_ref[g : g + 1]
            for s in range(4):
                tail_ref[g, 4 * half + s, 6:8] = value[2 * s : 2 * s + 2]

    def share_block(s, other):
        return remote(
            carried_ref.at[pl.ds(pl.multiple_of(s * SEG, SEG), SEG)], shared_ref.at[4 * ctx + s],
            s_car.at[other, s], r_car.at[ctx, s], spot(ctx=other),
        )

    def forward_block(s, group):
        at = shared_ref.at[4 * group + s]
        return remote(at, at, s_fwd.at[s], r_car.at[group, s], spot(ctx=5 - ctx))

    def mix(s, unused):
        rows = pl.ds(pl.multiple_of(s * SEG, SEG), SEG)
        parent = par_ref[0, ctx * blocks + s]
        slot = jnp.where(parent >= 0, parent, 8)
        out = []
        for g in range(3):
            projected = mm_nt(low_ref[rows], w_ref[g]) + ib_ref[g : g + 1]
            proj_ref[g, rows] = projected
            head = tail_ref[g, slot]
            head_ref[g, s] = head
            ext_ref[g, 0:HEADS] = head
            ext_ref[g, HEADS : HEADS + SEG] = projected
            mixed = (
                sw_ref[g, 0:1] * ext_ref[g, HEADS - 2 : HEADS - 2 + SEG]
                + sw_ref[g, 1:2] * ext_ref[g, HEADS - 1 : HEADS - 1 + SEG]
                + sw_ref[g, 2:3] * projected
                + sb_ref[g : g + 1]
            )
            if g == 0:
                gate_ref[rows] = mixed
            else:
                mixed_ref[g - 1, rows] = mixed
            out.append(mixed)
        carried = (out[2] * out[1]).astype(BF16)
        carried_ref[rows] = carried

        @pl.when(ctx == 0)
        def _():
            share_block(s, 2).start()
            share_block(s, 1).start()

        @pl.when(ctx == 1)
        def _():
            share_block(s, 3).start()

        spec = mm(fh_ref[...], carried) + mm(fl_ref[...], carried)
        spec_ref[8 + s, 0] = spec[:SEG]
        spec_ref[8 + s, 1] = spec[SEG:]
        return unused

    lax.fori_loop(0, blocks, mix, 0)
    for k, (src, dst) in enumerate(((proj_ref, proj_hbm), (head_ref, head_hbm), (mixed_ref, mixed_hbm))):
        saves.append(pltpu.make_async_copy(src, dst, local.at[8 + k]))
        saves[-1].start()

    def spectrum(slot, part):
        out = mm(fh_ref[...], part) + mm(fl_ref[...], part)
        spec_ref[slot, 0] = out[:SEG]
        spec_ref[slot, 1] = out[SEG:]

    spec_ref[12] = jnp.zeros(spec_ref.shape[1:], F32)

    def arrived(group, s):
        at = shared_ref.at[4 * group + s]
        return remote(at, at, s_fwd.at[s], r_car.at[group, s], spot(ctx=ctx_at(1)))

    def copy_own(group):
        def one(s, unused):
            spec_ref[4 * group + s] = spec_ref[8 + s]
            return unused

        lax.fori_loop(0, 4, one, 0)

    def receive(group):
        def one(s, unused):
            arrived(group, s).wait_recv()
            spectrum(4 * group + s, shared_ref[4 * group + s])
            return unused

        lax.fori_loop(0, 4, one, 0)

    def receive_forward(group):
        def one(s, unused):
            arrived(group, s).wait_recv()
            forward_block(s, group).start()
            spectrum(4 * group + s, shared_ref[4 * group + s])
            return unused

        lax.fori_loop(0, 4, one, 0)

    @pl.when(ctx == 0)
    def _():
        copy_own(0)

    @pl.when(ctx == 1)
    def _():
        copy_own(1)
        receive(0)

    @pl.when(ctx == 2)
    def _():
        receive_forward(0)
        receive(1)

    @pl.when(ctx == 3)
    def _():
        receive_forward(1)
        receive(0)

    saves.append(pltpu.make_async_copy(spec_ref, spec_hbm, local.at[11]))
    saves[-1].start()

    def dest(s, unused):
        above = lineage(par_ref, ctx * blocks + s)
        places = [8 + s] + [jnp.where(a >= 0, a, 12) for a in above]
        blend_all(acc_ref, [(filt_ref.at[d], spec_ref.at[places[d]]) for d in range(DEPTH)], False)
        long_out = unpack_spectrum(th, tl, acc_ref) * (1.0 / SEG)
        place = pl.ds(pl.multiple_of(s * SEG, SEG), SEG)
        convolved = long_out + skip_ref[...].reshape(1, -1) * carried_ref[place].astype(F32)
        conv_ref[place] = convolved
        gated_ref[place] = (convolved * gate_ref[place]).astype(BF16)
        return unused

    lax.fori_loop(0, blocks, dest, 0)

    def take_halves(stage, half):
        for i in range(1, owners):
            who = owner(i)
            at = up_half(rows_of(up_hbm, who, up_share), half)
            remote(at, at, s_up.at[i], r_up.at[stage, who], mate).wait_recv()
            if stage == 0:
                swap_up(i).start()
            for line in range(lines):
                at = half_of(out_hbm.at[line, who], half)
                remote(at, at, s_out.at[i, line], r_out.at[stage, line, who], mate).wait_recv()
                if stage == 0:
                    swap_out(i, line).start()

    take_halves(0, low_half)

    for save in saves:
        save.wait()
    take_halves(1, 1 - low_half)
    for i in range(1, owners):
        send_in(i).wait_send()
        swap_in(i).wait_send()
        send_last(i).wait_send()
        send_up(i).wait_send()
        swap_up(i).wait_send()
        for j in range(lines):
            send_out(i, j).wait_send()
            swap_out(i, j).wait_send()
    for i in range(1, lines):
        line_out(i).wait_send()
        line = lax.rem(tp + i, lines)
        at = out_hbm.at[line, dp]
        remote(at, at, s_line.at[i], r_line.at[line], mate).wait_recv()
    for i in range(1, 4):
        send_xt(i).wait_send()

    @pl.when(ctx == 0)
    def _():
        for s in range(blocks):
            share_block(s, 2).wait_send()
            share_block(s, 1).wait_send()

    @pl.when(ctx == 1)
    def _():
        for s in range(blocks):
            share_block(s, 3).wait_send()

    @pl.when(ctx == 2)
    def _():
        for s in range(blocks):
            forward_block(s, 0).wait_send()

    @pl.when(ctx == 3)
    def _():
        for s in range(blocks):
            forward_block(s, 1).wait_send()


class OwnerSum:
    scratch_count = 17

    @staticmethod
    def scratch(owners, shape):
        many = max(owners - 1, 1)
        return [
            pltpu.VMEM((owners,) + shape, BF16),
            pltpu.VMEM((owners,) + shape, BF16),
            pltpu.VMEM((many,) + shape, BF16),
            pltpu.VMEM(shape, BF16),
            pltpu.VMEM(shape, BF16),
            pltpu.SemaphoreType.DMA,
            pltpu.SemaphoreType.DMA,
            pltpu.SemaphoreType.DMA,
            pltpu.SemaphoreType.DMA((many,)),
            pltpu.SemaphoreType.DMA((many,)),
            pltpu.SemaphoreType.DMA,
            pltpu.SemaphoreType.DMA,
            pltpu.SemaphoreType.DMA,
            pltpu.SemaphoreType.DMA,
            pltpu.SemaphoreType.DMA((2,)),
            pltpu.VMEM((2,) + shape, F32),
        ]

    def __init__(self, stage, out, scratch):
        self.stage, self.out, self.result = stage, out, scratch[-1]
        self.recv, self.keep, self.parts, self.y_own, self.y_in = scratch[:5]
        self.sems = scratch[5:-1]
        self.owners = stage.shape[1]
        self.dp, ctx = lax.axis_index("dp"), lax.axis_index("ctx")
        self.low = lax.rem(ctx, 2)
        self.mate = spot(ctx=ctx + 1 - 2 * self.low)
        self.across = spot(ctx=lax.rem(ctx + 2, 4))

    def load(self):
        return pltpu.make_async_copy(self.stage.at[self.low], self.keep, self.sems[0])

    def to_mate(self):
        return remote(self.stage.at[1 - self.low], self.recv, self.sems[1], self.sems[2], self.mate)

    def to_owner(self, i):
        owner = lax.rem(self.dp + i, self.owners)
        return remote(
            self.keep.at[owner], self.parts.at[self.owners - 1 - i], self.sems[3].at[i - 1],
            self.sems[4].at[self.owners - 1 - i], spot(dp=owner),
        )

    def from_owner(self, i):
        return remote(self.parts.at[i - 1], self.parts.at[i - 1], self.sems[3].at[i - 1], self.sems[4].at[i - 1], self.mate)

    def to_across(self):
        return remote(self.y_own, self.y_in, self.sems[5], self.sems[6], self.across)

    def to_back(self):
        at = self.result.at[self.low]
        return remote(at, at, self.sems[7], self.sems[8], self.mate)

    def save(self, half):
        return pltpu.make_async_copy(self.result.at[half], self.out.at[half], self.sems[9].at[half])

    def begin(self):
        self.to_mate().start()
        self.load().start()

    def pair(self):
        self.load().wait()
        self.to_mate().wait_recv()
        for o in range(self.owners):
            self.keep[o] = (self.keep[o].astype(F32) + self.recv[o].astype(F32)).astype(BF16)
        for i in range(1, self.owners):
            self.to_owner(i).start()

    def own(self):
        total = self.keep[self.dp].astype(F32)
        for i in range(1, self.owners):
            self.from_owner(i).wait_recv()
            total = total + self.parts[i - 1].astype(F32)
        self.y_own[...] = total.astype(BF16)
        self.to_across().start()

    def cross(self):
        self.to_across().wait_recv()
        self.result[self.low] = self.y_own[...].astype(F32) + self.y_in[...].astype(F32)
        self.to_back().start()
        self.save(self.low).start()

    def whole(self):
        at = self.result.at[1 - self.low]
        remote(at, at, self.sems[7], self.sems[8], self.mate).wait_recv()
        self.save(1 - self.low).start()

    def finish(self):
        self.to_mate().wait_send()
        for i in range(1, self.owners):
            self.to_owner(i).wait_send()
        self.to_across().wait_send()
        self.to_back().wait_send()
        self.save(self.low).wait()
        self.save(1 - self.low).wait()


class SmallSum:
    @staticmethod
    def scratch(count, shape):
        return [
            pltpu.VMEM((count,) + shape, F32),
            pltpu.SemaphoreType.DMA((count,)),
            pltpu.SemaphoreType.DMA((count,)),
        ]

    def __init__(self, axis, scratch):
        self.axis = axis
        self.slots, self.send, self.recv = scratch
        self.count = self.slots.shape[0]
        self.me = lax.axis_index(axis)

    def copy(self, i):
        at = self.slots.at[self.me]
        other = lax.rem(self.me + i, self.count)
        return remote(at, at, self.send.at[i], self.recv.at[self.me], spot(**{self.axis: other}))

    def start(self, value):
        self.slots[self.me] = value
        for i in range(1, self.count):
            self.copy(i).start()

    def total(self):
        for i in range(1, self.count):
            other = lax.rem(self.me + i, self.count)
            at = self.slots.at[other]
            remote(at, at, self.send.at[i], self.recv.at[other], spot(**{self.axis: lax.rem(self.me + i, self.count)})).wait_recv()
        out = self.slots[0]
        for i in range(1, self.count):
            out = out + self.slots[i]
        return out

    def finish(self):
        for i in range(1, self.count):
            self.copy(i).wait_send()


def back_kernel(
    par_ref, dall_ref, dconv_ref, dzero_ref, dpart_ref,
    fh_ref, fl_ref, th_ref, tl_ref, sign_ref, sw_ref, skip_ref,
    ft_ref, f1_ref, f1b_ref, f2_ref, f2b_ref, freq_ref, last_ref, small_ref, gskip_ref,
    mixed_hbm, low_hbm, w_hbm, x_hbm, proj_hbm, head_hbm, spec_hbm, filt_hbm, net_hbm, sup_hbm, sdown_hbm, sout_hbm,
    dsum_ref, psum_ref, oup_ref, odown_ref, oout_ref, oin_ref, va_ref, vd_ref, vl_ref, vf_ref,
    yown_ref, dcar_ref, dtaps_ref, stage_in, ppart_ref, w1_ref, w2_ref,
    mixed_ref, low_ref, w_ref, x_ref, hd_ref, s_hd, r_hd, local, *rest,
):
    width = x_ref.shape[1]
    channels = dconv_ref.shape[1]
    total_rows = x_ref.shape[0]
    blocks = total_rows // SEG
    owners = sup_hbm.shape[1]
    ctx, tp, dp = lax.axis_index("ctx"), lax.axis_index("tp"), lax.axis_index("dp")
    rest = list(rest)

    def take(n):
        out = rest[:n]
        del rest[:n]
        return out

    down = LineSum(dpart_ref, dsum_ref, take(11))
    proj = LineSum(ppart_ref, psum_ref, take(11))
    early = [OwnerSum(s, o, take(16)) for s, o in ((sup_hbm, oup_ref), (sdown_hbm, odown_ref), (sout_hbm, oout_ref))]
    late = OwnerSum(stage_in, oin_ref, take(16))
    a_ctx, a_dp = SmallSum("ctx", take(3)), SmallSum("dp", take(3))
    d_ctx, d_dp, d_tp = SmallSum("ctx", take(3)), SmallSum("dp", take(3)), SmallSum("tp", take(3))
    l_ctx, l_dp = SmallSum("ctx", take(3)), SmallSum("dp", take(3))
    f_ctx, f_dp, f_tp = SmallSum("ctx", take(3)), SmallSum("dp", take(3)), SmallSum("tp", take(3))

    partners = [spot(tp=lax.rem(tp + i, 4)) for i in range(1, 4)]
    partners += [spot(ctx=lax.rem(ctx + i, 4)) for i in range(1, 4)]
    partners += [spot(dp=lax.rem(dp + i, owners)) for i in range(1, owners)]
    barrier, count = signal_all(partners)
    pl.semaphore_wait(barrier, count)
    for s in range(blocks):
        down.send_block(s)
    loads = [
        pltpu.make_async_copy(src, dst, local.at[4 + k])
        for k, (src, dst) in enumerate(((mixed_hbm, mixed_ref), (w_hbm, w_ref), (x_hbm, x_ref), (low_hbm, low_ref)))
    ]
    for load in loads:
        load.start()
    for job in early:
        job.begin()
    fh, fl, th, tl = fh_ref[...], fl_ref[...], th_ref, tl_ref
    skip = skip_ref[...].reshape(1, -1)
    scale = 1.0 / SEG

    def put(dst, value):
        dst[0] = value[:SEG] * scale
        dst[1] = value[SEG:] * scale

    def conv_inputs(filt_ref, more_ref, acc_ref):
        load = pltpu.make_async_copy(filt_hbm, filt_ref, local.at[0])
        load.start()

        def transform(s, unused):
            part = dall_ref[ctx * blocks + s]
            put(yown_ref.at[s], mm(fh, part) + mm(fl, part))
            return unused

        lax.fori_loop(0, blocks, transform, 0)
        load.wait()

        def leaf_sum(match):
            total = None
            for leaf in range(8, 16):
                term = jnp.where(match(leaf), 1.0, 0.0) * dall_ref[leaf].astype(F32)
                total = term if total is None else total + term
            return total

        def from_leaf(b):
            return lambda leaf: par_ref[0, leaf] == b

        def finish(s, terms):
            blend_all(acc_ref, terms, True)
            place = pl.ds(pl.multiple_of(s * SEG, SEG), SEG)
            dcar_ref[place] = unpack_spectrum(th, tl, acc_ref) + skip * dconv_ref[place]

        @pl.when(ctx == 0)
        def _():
            def gather(k, unused):
                p = k + 1
                total = None
                for b in range(4, 8):
                    term = jnp.where(par_ref[0, b] == p, 1.0, 0.0) * dall_ref[b].astype(F32)
                    total = term if total is None else total + term
                put(more_ref.at[k], mm_split(fh, fl, total))
                total = leaf_sum(lambda leaf: par_ref[0, par_ref[0, leaf]] == p)
                put(more_ref.at[3 + k], mm_split(fh, fl, total))
                return unused

            lax.fori_loop(0, 3, gather, 0)
            for a in range(4):
                terms = [(filt_ref.at[s - a], yown_ref.at[s]) for s in range(a, 4)]
                for p in range(max(a, 1), 4):
                    terms.append((filt_ref.at[p - a + 1], more_ref.at[p - 1]))
                    terms.append((filt_ref.at[p - a + 2], more_ref.at[p + 2]))
                finish(a, terms)

        @pl.when(ctx == 1)
        def _():
            def one(b, unused):
                put(more_ref.at[0], mm_split(fh, fl, leaf_sum(from_leaf(b + 4))))
                finish(b, [(filt_ref.at[0], yown_ref.at[b]), (filt_ref.at[1], more_ref.at[0])])
                return unused

            lax.fori_loop(0, 4, one, 0)

        @pl.when(ctx > 1)
        def _():
            def one(b, unused):
                finish(b, [(filt_ref.at[0], yown_ref.at[b])])
                return unused

            lax.fori_loop(0, 4, one, 0)

    pl.run_scoped(
        conv_inputs,
        pltpu.VMEM((DEPTH, 2, SEG, channels), F32),
        pltpu.VMEM((6, 2, SEG, channels), F32),
        pltpu.VMEM((2, SEG, channels), F32),
    )

    for load in loads:
        load.wait()

    def to_ctx(i):
        at = hd_ref.at[pl.ds(ctx * blocks, blocks)]
        return remote(at, at, s_hd.at[i], r_hd.at[ctx], spot(ctx=lax.rem(ctx + i, 4)))

    for s in range(blocks):
        top = slice(s * SEG, s * SEG + HEADS)
        d_car = dcar_ref[top]
        rows = [dzero_ref[top], d_car * mixed_ref[1, top], d_car * mixed_ref[0, top]]
        for g in range(3):
            hd_ref[ctx * blocks + s, 2 * g : 2 * g + 2] = rows[g][0:2]
        hd_ref[ctx * blocks + s, 6:8] = jnp.zeros((2, channels), F32)
    for i in range(1, 4):
        to_ctx(i).start()
    down.steps(0, 4)
    for job in early:
        job.pair()

    va_ref[...] = jnp.zeros(va_ref.shape, F32)
    vd_ref[...] = small_ref[...]
    va_ref[15:16] = gskip_ref[...]
    for i in range(1, 4):
        other = lax.rem(ctx + i, 4)
        at = hd_ref.at[pl.ds(other * blocks, blocks)]
        remote(at, at, s_hd.at[i], r_hd.at[other], spot(ctx=other)).wait_recv()

    def with_spectra(spec_ref):
        pltpu.make_async_copy(spec_hbm, spec_ref, local.at[0]).start()

        def mix_back(dp_ref, ext_ref, dm_ref, pin_ref, hin_ref):
            load_heads = pltpu.make_async_copy(head_hbm, hin_ref, local.at[1])
            load_heads.start()

            def fetch(s):
                rows = pl.ds(pl.multiple_of(s * SEG, SEG), SEG)
                return pltpu.make_async_copy(proj_hbm.at[:, rows], pin_ref.at[lax.rem(s, 2)], local.at[2 + lax.rem(s, 2)])

            fetch(0).start()
            load_heads.wait()

            def one(s, unused):
                rows = pl.ds(pl.multiple_of(s * SEG, SEG), SEG)
                slot = lax.rem(s, 2)
                fetch(s).wait()

                @pl.when(s + 1 < blocks)
                def _():
                    fetch(s + 1).start()

                mine = ctx * blocks + s
                child = None
                for b in range(1, 16):
                    term = jnp.where(par_ref[0, b] == mine, 1.0, 0.0) * hd_ref[b]
                    child = term if child is None else child + term
                part = None
                for g in range(3):
                    if g == 0:
                        dm = dzero_ref[rows]
                    else:
                        dm = dcar_ref[rows] * mixed_ref[2 - g, rows]
                    ext_ref[0:HEADS] = hin_ref[g, s]
                    ext_ref[HEADS : HEADS + SEG] = pin_ref[slot, g]
                    for k in range(3):
                        piece = ext_ref[HEADS - 2 + k : HEADS - 2 + k + SEG]
                        va_ref[3 * g + k : 3 * g + k + 1] += jnp.sum(piece * dm, axis=0, keepdims=True)
                    va_ref[12 + g : 13 + g] += jnp.sum(dm, axis=0, keepdims=True)
                    dm_ref[0:SEG] = dm
                    dm_ref[SEG : SEG + 2] = child[2 * g : 2 * g + 2]
                    d_proj = (
                        sw_ref[g, 2:3] * dm
                        + sw_ref[g, 1:2] * dm_ref[1 : 1 + SEG]
                        + sw_ref[g, 0:1] * dm_ref[2 : 2 + SEG]
                    ).astype(BF16)
                    dp_ref[g, rows] = d_proj
                    va_ref[9 + g : 10 + g] += jnp.sum(d_proj.astype(F32), axis=0, keepdims=True)
                    term = mm(d_proj, w_ref[g])
                    part = term if part is None else part + term
                ppart_ref[rows] = part.astype(BF16)
                proj.send_block(s)
                xhat = normalize(x_ref[rows].astype(F32))[0]
                vd_ref[4:5] += jnp.sum(part * xhat, axis=0, keepdims=True)
                vd_ref[5:6] += jnp.sum(part, axis=0, keepdims=True)
                down.steps(4 + s, 5 + s)
                return unused

            lax.fori_loop(0, blocks, one, 0)
            rows = stage_in.shape[3]
            for g in range(3):
                value = mm_tn(dp_ref[g], low_ref[...])
                for t in range(2):
                    store_columns(stage_in.at[:, :, g], t, value[t * rows : (t + 1) * rows])

        pl.run_scoped(
            mix_back,
            pltpu.VMEM((3, total_rows, channels), BF16),
            pltpu.VMEM((HEADS + SEG, channels), F32),
            pltpu.VMEM((HEADS + SEG, channels), F32),
            pltpu.VMEM((2, 3, SEG, channels), F32),
            pltpu.VMEM((3, blocks, HEADS, channels), F32),
        )
        a_ctx.start(va_ref[...])
        d_ctx.start(vd_ref[...])
        late.begin()
        down.steps(8, 11)

        def conv_filters(dfilt_ref):
            pltpu.make_async_copy(spec_hbm, spec_ref, local.at[0]).wait()

            @pl.when(ctx == 0)
            def _():
                for d in range(4):
                    blend_all(dfilt_ref.at[d], [(spec_ref.at[8 + s - d], yown_ref.at[s]) for s in range(d, 4)], True)
                dfilt_ref[4:6] = jnp.zeros((2, 2, SEG, channels), F32)

            @pl.when(ctx > 0)
            def _():
                places = []
                for s in range(blocks):
                    above = lineage(par_ref, ctx * blocks + s)
                    places.append([8 + s] + [jnp.where(a >= 0, a, 12) for a in above])
                for d in range(DEPTH):
                    terms = [(spec_ref.at[places[s][d]], yown_ref.at[s]) for s in range(blocks)]
                    blend_all(dfilt_ref.at[d], terms, True)

            down.steps(11, 12)
            sign = sign_ref[...]
            first_row = lax.broadcasted_iota(jnp.int32, (SEG, 1), 0) == 0
            for j in range(DEPTH):
                fix = None
                if j + 1 < DEPTH:
                    nr, ni = dfilt_ref[j + 1, 0], dfilt_ref[j + 1, 1]
                    fix = jnp.sum(sign * ni, axis=0, keepdims=True)
                    dfilt_ref[j, 0] = dfilt_ref[j, 0] + sign * ni
                    dfilt_ref[j, 1] = dfilt_ref[j, 1] - sign * nr
                taps = unpack_spectrum(th, tl, dfilt_ref.at[j])
                if fix is not None:
                    taps = jnp.where(first_row, taps - fix, taps)
                dtaps_ref[j * SEG : (j + 1) * SEG] = taps

        pl.run_scoped(conv_filters, pltpu.VMEM((DEPTH, 2, SEG, channels), F32))

    pl.run_scoped(with_spectra, pltpu.VMEM((13, 2, SEG, channels), F32))
    down.steps(12, 13)

    def filter_back(net_ref):
        load = pltpu.make_async_copy(net_hbm, net_ref, local.at[1])
        load.start()
        d_raw = dtaps_ref[...] * decay(DEPTH * SEG, channels, tp, width)
        extend_weights(w1_ref, f1_ref, f1b_ref)
        extend_weights(w2_ref, f2_ref, f2b_ref)
        freq = freq_ref[...].reshape(1, -1)
        load.wait()
        units = last_ref.shape[0]
        l_ctx.start(jnp.dot(net_ref[3, 0:units], d_raw, **EXACT_DOT))
        s_two = lax.dot_general(last_ref[...], d_raw, NT, **EXACT_DOT) * net_ref[2, 0:units]
        g_two = lax.dot_general(net_ref[1], s_two, NT, **EXACT_DOT)
        d_one = jnp.dot(w2_ref[...] * freq, s_two, **EXACT_DOT)[0:units]
        g_one = lax.dot_general(ft_ref[...], d_one * net_ref[0, 0:units], NT, **EXACT_DOT)
        g_freq = jnp.sum(w1_ref[...] * g_one, axis=0, keepdims=True) + jnp.sum(
            w2_ref[...] * g_two, axis=0, keepdims=True
        )
        vf_ref[...] = jnp.zeros(vf_ref.shape, F32)
        vf_ref[0 : g_one.shape[0], 0:units] = g_one * freq
        vf_ref[0 : g_two.shape[0], units : 2 * units] = g_two * freq
        vf_ref[g_two.shape[0] : g_two.shape[0] + 1, 0:units] = g_freq
        f_ctx.start(vf_ref[...])

    pl.run_scoped(filter_back, pltpu.VMEM(net_hbm.shape, F32))

    def early_own():
        for job in early:
            job.own()

    def early_cross():
        for job in early:
            job.cross()

    def vectors():
        a_dp.start(a_ctx.total())
        d_dp.start(d_ctx.total())

    def networks():
        l_dp.start(l_ctx.total())
        f_dp.start(f_ctx.total())
        late.own()

    def gains():
        va_ref[...] = a_dp.total()
        sums = d_dp.total()
        vd_ref[...] = sums
        d_tp.start(sums[4:6])

    def last_layer():
        for job in early:
            job.whole()
        f_tp.start(f_dp.total())
        last_sum = l_dp.total()
        for o in range(owners):
            held = vl_ref.shape[1]
            vl_ref[o] = last_sum[o * held : (o + 1) * held]

    jobs = (early_own, late.pair, early_cross, vectors, networks, gains, last_layer)
    for k, job in enumerate(jobs):
        down.steps(13 + k, 14 + k)
        proj.steps(2 * k, 2 * k + 2)
        job()
    proj.steps(14, 17)
    late.cross()
    proj.steps(17, proj.pairs + 2 * LAG)
    late.whole()
    for s in range(blocks):
        down.wait_block(s)
        proj.wait_block(s)
    vd_ref[4:6] = d_tp.total()
    vf_ref[...] = f_tp.total()
    for job in (a_ctx, a_dp, d_ctx, d_dp, d_tp, l_ctx, l_dp, f_ctx, f_dp, f_tp):
        job.finish()
    for job in early + [late]:
        job.finish()
    for i in range(1, 4):
        to_ctx(i).wait_send()
    down.drain()
    proj.drain()


def final_kernel(
    resid_ref, dsum_ref, dres_ref, psum_ref, x_ref, gain_ref, bias_ref, va_ref, vd_ref, vl_ref, vf_ref,
    oup_ref, odown_ref, oout_ref, oin_ref,
    result_ref, gradx_ref, up_ref, down_ref, out_ref, in_ref,
    mgain_ref, mshift_ref, inb_ref, sw_ref, sb_ref, f1_ref, f1b_ref, f2_ref, f2b_ref, freq_ref, last_ref,
    skip_ref, ob_ref, fgain_ref, fshift_ref, ub_ref, db_ref,
):
    step = pl.program_id(0)

    @pl.when(step == 0)
    def _():
        up_ref[...] = oup_ref[...]
        down_ref[...] = odown_ref[...]
        out_ref[...] = oout_ref[...]
        rows = oin_ref.shape[2]
        for h in range(2):
            in_ref[:, h * rows : (h + 1) * rows] = oin_ref[h]
        mgain_ref[...] = vd_ref[4]
        mshift_ref[...] = vd_ref[5]
        db_ref[...] = vd_ref[0]
        ob_ref[...] = vd_ref[1]
        fgain_ref[...] = vd_ref[2]
        fshift_ref[...] = vd_ref[3]
        ub_ref[...] = vd_ref[6]
        for g in range(3):
            sw_ref[g] = va_ref[3 * g : 3 * g + 3]
        inb_ref[...] = va_ref[9:12]
        sb_ref[...] = va_ref[12:15]
        skip_ref[...] = va_ref[15]
        units = f1_ref.shape[1]
        rows_one, rows_two = f1_ref.shape[0], f2_ref.shape[0]
        f1_ref[...] = vf_ref[0:rows_one, 0:units]
        f1b_ref[...] = vf_ref[rows_one, 0:units]
        f2_ref[...] = vf_ref[0:rows_two, units : 2 * units]
        f2b_ref[...] = vf_ref[rows_two, units : 2 * units]
        freq_ref[...] = vf_ref[rows_two + 8, 0:units]
        last_ref[...] = vl_ref[lax.axis_index("dp")]

    result_ref[...] = resid_ref[...] + dsum_ref[...].astype(F32) + bias_ref[...].reshape(1, -1)
    xhat, spread = normalize(x_ref[...].astype(F32))
    e = psum_ref[...].astype(F32) * gain_ref[...].reshape(1, -1)
    gradx_ref[...] = dres_ref[...] + spread * (
        e - jnp.mean(e, axis=-1, keepdims=True) - xhat * jnp.mean(e * xhat, axis=-1, keepdims=True)
    )


def body(
    block_in, out_grad, parents, mixer_gain, mixer_shift, in_proj, in_bias, short_weight, short_bias,
    filter_one, filter_one_bias, filter_two, filter_two_bias, filter_freq, filter_out, skip_gain,
    out_proj, out_bias, feed_gain, feed_shift, feed_up, feed_up_bias, feed_down, feed_down_bias,
):
    x = block_in[0]
    g = out_grad[0]
    total_rows, width = x.shape
    channels = skip_gain.shape[0]
    blocks = total_rows // SEG
    hidden = feed_up.shape[1]
    tp_count = lax.axis_size("tp")
    tp_index = lax.axis_index("tp")
    owners = lax.axis_size("dp")
    first = lax.axis_index("ctx") * blocks
    all_blocks = parents.shape[1]

    half = hidden // 2
    share = width // owners
    units, features = filter_one.shape[1], filter_one.shape[0]
    feat_rows, mid_rows = 40, units + 8
    length = DEPTH * SEG
    ft = jnp.asarray(filter_features(length, (features - 1) // 2, feat_rows))
    fh, fl, th, tl, sign = (jnp.asarray(t) for t in spectral_constants(SEG))
    dma = pltpu.SemaphoreType.DMA
    front_out = (
        sds((total_rows, width), BF16),
        sds((3, total_rows, channels), F32),
        sds((3, blocks, HEADS, channels), F32),
        sds((2, total_rows, channels), F32),
        sds((13, 2, SEG, channels), F32),
        sds((DEPTH, 2, SEG, channels), F32),
        sds((4, mid_rows, length), F32),
        sds((3, channels, width), BF16),
        sds((tp_count, owners, channels, share), BF16),
        sds((width, hidden), BF16),
        sds((units, channels), F32),
        sds((total_rows, channels), F32),
        sds((total_rows, channels), F32),
        sds((total_rows, channels), BF16),
        sds((total_rows, channels), BF16),
    )
    low, proj, head, mixed, spec, filt, net, in_all, out_all, up_all, last, gate, conv, gated, carried = call(
        front_kernel,
        front_out,
        [SM] + [VM] * 22,
        [
            pltpu.VMEM((3, channels, width), BF16),
            pltpu.VMEM((total_rows, width), BF16),
            pltpu.VMEM((3, total_rows, channels), F32),
            pltpu.VMEM((3, blocks, HEADS, channels), F32),
            pltpu.VMEM((2, total_rows, channels), F32),
            pltpu.VMEM((13, 2, SEG, channels), F32),
            pltpu.VMEM((DEPTH, 2, SEG, channels), F32),
            pltpu.VMEM((4, mid_rows, length), F32),
            pltpu.VMEM((length, channels), F32),
            pltpu.VMEM((8, SEG, channels), BF16),
            pltpu.VMEM((4, 2 * blocks, width), F32),
            pltpu.VMEM((3, 9, HEADS, channels), F32),
            pltpu.VMEM((3, HEADS + SEG, channels), F32),
            pltpu.VMEM((feat_rows, units), F32),
            pltpu.VMEM((mid_rows, units), F32),
            pltpu.VMEM((2, SEG, channels), F32),
            pltpu.VMEM((owners,) + filter_out.shape, BF16),
            pltpu.VMEM((owners, 3, channels, share), BF16),
            dma((2, owners)), dma((2, owners)), dma((owners,)), dma((owners,)),
            dma((owners, tp_count)), dma((2, tp_count, owners)),
            dma((owners,)), dma((2, owners)),
            dma((tp_count,)), dma((tp_count,)), dma((3, owners, tp_count)),
            dma((4,)), dma((4,)), dma((4, 4)), dma((4, 4)), dma((4,)), dma((12,)),
        ],
        1,
        out_specs=(HB,) * 10 + (VM,) * 5,
    )(
        parents, x, jnp.transpose(in_proj, (1, 2, 0)), filter_out, out_proj, feed_up, ft,
        filter_one, filter_one_bias, filter_two, filter_two_bias, filter_freq, mixer_gain, mixer_shift,
        in_bias, short_weight, short_bias, skip_gain, fh, fl, th, tl, sign,
    )

    piece = share // 2
    feed_big = [
        sds((total_rows, width), F32),
        sds((total_rows, width), BF16),
        sds((total_rows, width), F32),
        sds((total_rows, channels), F32),
        sds((total_rows, channels), F32),
        sds((2, owners, piece, hidden), BF16),
        sds((2, owners, half, share), BF16),
    ]
    feed_in = (out_all, x, g, up_all, gate, conv, carried)

    def held(v):
        return pltpu.VMEM(v.shape, v.dtype)

    residual, down_part, d_res, d_conv, d_zero, stage_up, stage_down, d_all, stage_out, small, grad_skip = call(
        feed_kernel,
        feed_big
        + [
            sds((all_blocks, SEG, channels), BF16),
            sds((2, owners, channels // 2, share), BF16),
            sds((8, width), F32),
            sds((1, channels), F32),
        ],
        [VM] * 6 + [HB] * 7,
        [held(v) for v in feed_in]
        + [held(v) for v in feed_big]
        + [dma((8,)), dma((3,)), dma((4, blocks)), pltpu.VMEM((owners, hidden, share), BF16)]
        + [dma((2, owners)), dma((2, owners))]
        + [
            pltpu.VMEM((total_rows, width), BF16),
            pltpu.VMEM((total_rows, hidden), BF16),
            pltpu.VMEM((total_rows, hidden), BF16),
            pltpu.VMEM((total_rows, width), BF16),
            pltpu.VMEM((total_rows, width), BF16),
            pltpu.VMEM((total_rows, width), BF16),
            pltpu.VMEM((blocks, SEG, channels), BF16),
            pltpu.VMEM((tp_count, total_rows, channels), BF16),
            pltpu.VMEM((tp_count, channels, width), BF16),
            pltpu.VMEM((hidden, width), BF16),
            dma((tp_count, blocks)), dma((tp_count, blocks)), dma((4, blocks)), dma((4, blocks)),
        ]
        + LineSum.scratch(total_rows, width),
        2,
        out_specs=(HB,) * 7 + (VM,) * 4,
    )(gated, out_bias, feed_gain, feed_shift, feed_up_bias, feed_down, *feed_in)

    shapes = [(piece, hidden), (half, share), (channels // 2, share), (3, channels // 2, share)]
    scratch = [
        pltpu.VMEM((blocks, 2, SEG, channels), F32),
        pltpu.VMEM((total_rows, channels), F32),
        pltpu.VMEM((length, channels), F32),
        pltpu.VMEM((2, owners) + shapes[3], BF16),
        pltpu.VMEM((total_rows, width), BF16),
        pltpu.VMEM((feat_rows, units), F32),
        pltpu.VMEM((mid_rows, units), F32),
        held(mixed), held(low), held(in_all), held(x),
        pltpu.VMEM((all_blocks, HEADS, channels), F32),
        dma((4,)), dma((4,)), dma((8,)),
    ]
    scratch += LineSum.scratch(total_rows, width) * 2
    for shape in shapes:
        scratch += OwnerSum.scratch(owners, shape)
    smalls = ((16, channels), (8, width), (units, channels), (mid_rows + 8, 2 * units))
    for counts, shape in (
        ((4, owners), smalls[0]), ((4, owners), smalls[1]), ((tp_count,), (2, width)), ((4, owners), smalls[2]),
        ((4, owners, tp_count), smalls[3]),
    ):
        for count in counts:
            scratch += SmallSum.scratch(count, shape)
    down_sum, proj_sum, own_up, own_down, own_out, own_in, va, vd, vl, vf = call(
        back_kernel,
        (
            sds((total_rows, width), BF16),
            sds((total_rows, width), BF16),
        )
        + tuple(sds((2,) + shape, F32) for shape in shapes)
        + (
            sds(smalls[0], F32),
            sds(smalls[1], F32),
            sds((owners,) + filter_out.shape, F32),
            sds(smalls[3], F32),
        ),
        [SM] + [VM] * 20 + [HB] * 12,
        scratch,
        3,
        out_specs=(VM, VM, HB, HB, HB, HB, VM, VM, VM, VM),
    )(
        parents, d_all, d_conv, d_zero, down_part, fh, fl, th, tl, sign, short_weight,
        skip_gain, ft, filter_one, filter_one_bias, filter_two, filter_two_bias, filter_freq, last, small, grad_skip,
        mixed, low, in_all, x, proj, head, spec, filt, net, stage_up, stage_down, stage_out,
    )

    def by_block(*shape):
        return pl.BlockSpec((SEG,) + shape, lambda i: (i,) + (0,) * len(shape))

    def whole(v):
        return pl.BlockSpec(v.shape, lambda i: (0,) * len(v.shape))

    wide = by_block(width)
    vectors = [
        sds(v.shape, F32)
        for v in (
            mixer_gain, mixer_shift, in_bias, short_weight, short_bias, filter_one, filter_one_bias, filter_two,
            filter_two_bias, filter_freq, filter_out, skip_gain, out_bias, feed_gain, feed_shift, feed_up_bias,
            feed_down_bias,
        )
    ]
    out = pl.pallas_call(
        final_kernel,
        grid=(blocks,),
        out_shape=[
            sds((total_rows, width), F32), sds((total_rows, width), F32), own_up, own_down, own_out,
            sds((3, channels, share), F32),
        ]
        + vectors,
        in_specs=[wide] * 5 + [whole(v) for v in (mixer_gain, feed_down_bias, va, vd, vl, vf, own_up, own_down, own_out, own_in)],
        out_specs=[wide, wide]
        + [whole(v) for v in (own_up, own_down, own_out, sds((3, channels, share), F32))]
        + [whole(v) for v in vectors],
        compiler_params=pltpu.CompilerParams(vmem_limit_bytes=LIMIT),
    )(
        residual, down_sum, d_res, proj_sum, x, mixer_gain, feed_down_bias, va, vd, vl, vf,
        own_up, own_down, own_out, own_in,
    )
    (result, grad_x, g_up, g_down, g_out, g_in, g_mgain, g_mshift, g_inb, g_sw, g_sb, g_f1, g_f1b, g_f2, g_f2b,
     g_freq, g_last, g_skip, g_ob, g_fgain, g_fshift, g_ub, g_db) = out
    return (
        result[None], grad_x[None], g_mgain, g_mshift, jnp.transpose(g_in, (2, 0, 1)), g_inb, g_sw, g_sb,
        g_f1, g_f1b, g_f2, g_f2b, g_freq, g_last, g_skip, g_out.reshape(channels, share), g_ob, g_fgain, g_fshift,
        g_up.reshape(share, hidden), g_ub, g_down.reshape(hidden, share), g_db,
    )


def solution(mesh):
    in_specs = (
        P("dp", "ctx", None), P("dp", "ctx", None), P("dp", None), P(), P(), P("dp", None, "tp"), P(None, "tp"),
        P(None, None, "tp"), P(None, "tp"), P(), P(), P(), P(), P(), P("dp", "tp"), P("tp"), P("tp", "dp"), P(),
        P(), P(), P("dp", "tp"), P("tp"), P("tp", "dp"), P(),
    )
    out_specs = (
        P("dp", "ctx", None), P("dp", "ctx", None), P(), P(), P("dp", None, "tp"), P(None, "tp"),
        P(None, None, "tp"), P(None, "tp"), P(), P(), P(), P(), P(), P("dp", "tp"), P("tp"), P("tp", "dp"), P(),
        P(), P(), P("dp", "tp"), P("tp"), P("tp", "dp"), P(),
    )
    return jax.shard_map(body, mesh=mesh, in_specs=in_specs, out_specs=out_specs, check_vma=False)
```

```python
import functools
import math

import jax
import jax.numpy as jnp
import numpy as np
from jax import lax
from jax.experimental import pallas as pl
from jax.experimental.pallas import tpu as pltpu
from jax.sharding import PartitionSpec as P

SEG = 256
DEPTH = 6
HEADS = 8
EXACT = lax.Precision.HIGHEST
EPSILON = 1e-05
SLOW_RATE = -math.log(0.01) / 1.5
FAST_RATE = -math.log(0.01) / 0.3
SHIFT_FLOOR = 0.05
F32 = jnp.float32
BF16 = jnp.bfloat16
MESH = pl.DeviceIdType.MESH
VM = pl.BlockSpec(memory_space=pltpu.VMEM)
SM = pl.BlockSpec(memory_space=pltpu.SMEM)
LIMIT = 62 << 20


def sds(shape, dtype):
    return jax.ShapeDtypeStruct(shape, dtype)


HB = pl.BlockSpec(memory_space=pl.ANY)


def call(kernel, out_shape, in_specs, scratch=(), collective=None, flops=0, traffic=0, out_specs=None):
    many = isinstance(out_shape, (tuple, list))
    return pl.pallas_call(
        kernel,
        out_shape=out_shape,
        in_specs=in_specs,
        out_specs=out_specs or (tuple(VM for _ in out_shape) if many else VM),
        scratch_shapes=list(scratch),
        compiler_params=pltpu.CompilerParams(
            vmem_limit_bytes=LIMIT,
            collective_id=collective,
            has_side_effects=collective is not None,
        ),
        cost_estimate=pl.CostEstimate(flops=flops, bytes_accessed=traffic, transcendentals=0),
    )


def spectral_constants(block_len):
    freq = np.arange(block_len)[:, None]
    place = np.arange(block_len)[None, :]
    angle = ((2 * freq + 1) * place % (4 * block_len)) * (2.0 * math.pi / (4 * block_len))
    table = np.concatenate([np.cos(angle), -np.sin(angle)], axis=0).astype(np.float32)
    high = table.astype(jnp.bfloat16)
    low = (table - high.astype(np.float32)).astype(jnp.bfloat16)
    sign = np.where(np.arange(block_len) % 2 == 0, 1.0, -1.0).astype(np.float32)[:, None]
    return high, low, np.ascontiguousarray(high.T), np.ascontiguousarray(low.T), sign


def normalize(values):
    mean_value = jnp.mean(values, axis=-1, keepdims=True)
    centered = values - mean_value
    variance = jnp.mean(centered * centered, axis=-1, keepdims=True)
    scale = lax.rsqrt(variance + EPSILON)
    return centered * scale, scale


def split(values):
    high = values.astype(BF16)
    return high, (values - high.astype(F32)).astype(BF16)


def mm(lhs, rhs):
    return jnp.dot(lhs, rhs, preferred_element_type=F32)


def mm_nt(lhs, rhs):
    return lax.dot_general(lhs, rhs, (((1,), (1,)), ((), ())), preferred_element_type=F32)


def mm_tn(lhs, rhs):
    return lax.dot_general(lhs, rhs, (((0,), (0,)), ((), ())), preferred_element_type=F32)


def mm_split(high, low, values):
    v_high, v_low = split(values)
    return mm(high, v_high) + (mm(low, v_high) + mm(high, v_low))


FT = 32


def lineage(par_ref, block):
    out = []
    current = block
    for _ in range(DEPTH - 1):
        parent = par_ref[0, jnp.maximum(current, 0)]
        current = jnp.where(current >= 0, parent, -1)
        out.append(current)
    return out


def blend_all(dst, terms, conj):
    def tile(t, unused):
        rows = pl.ds(pl.multiple_of(t * FT, FT), FT)
        re = im = None
        for a, b in terms:
            ar, ai = a[0, rows], a[1, rows]
            br, bi = b[0, rows], b[1, rows]
            if conj:
                pr, pi = ar * br + ai * bi, ar * bi - ai * br
            else:
                pr, pi = ar * br - ai * bi, ar * bi + ai * br
            re, im = (pr, pi) if re is None else (re + pr, im + pi)
        dst[0, rows] = re
        dst[1, rows] = im
        return unused

    lax.fori_loop(0, SEG // FT, tile, 0)


def unpack_spectrum(th, tl, ref):
    high_re, low_re = split(ref[0])
    high_im, low_im = split(ref[1])
    a, b = slice(0, SEG), slice(SEG, 2 * SEG)
    return (
        mm(th[:, a], high_re) + mm(th[:, b], high_im)
        + (mm(tl[:, a], high_re) + mm(tl[:, b], high_im))
        + (mm(th[:, a], low_re) + mm(th[:, b], low_im))
    )


def filter_features(length, bands, rows):
    positions = np.arange(length)
    time_pos = positions / (length - 1)
    freq = np.linspace(0.0001, bands - 1, bands)
    phases = (2.0 * math.pi / length * positions)[None, :] * freq[:, None]
    table = np.zeros((rows, length), np.float32)
    table[0] = time_pos
    table[1 : bands + 1] = np.cos(phases)
    table[bands + 1 : 2 * bands + 1] = -np.sin(phases)
    table[2 * bands + 1] = 1.0
    return table


def spot(**changes):
    base = {name: lax.axis_index(name) for name in ("dp", "ctx", "tp")}
    base.update(changes)
    return (base["dp"], base["ctx"], base["tp"])


def remote(src, dst, send, recv, where):
    return pltpu.make_async_remote_copy(
        src_ref=src, dst_ref=dst, send_sem=send, recv_sem=recv, device_id=where, device_id_type=MESH
    )


def greet(partners):
    barrier = pltpu.get_barrier_semaphore()
    for where in partners:
        pl.semaphore_signal(barrier, inc=1, device_id=where, device_id_type=MESH)
    pl.semaphore_wait(barrier, len(partners))


CHUNK = 32
HALF = SEG // 2
PER = SEG // (2 * CHUNK)
LAG = 2


def chunk(c):
    return pl.ds(pl.multiple_of(c * CHUNK, CHUNK), CHUNK)


class LineRole:
    def __init__(self):
        tp = lax.axis_index("tp")
        self.inner = jnp.logical_and(tp > 0, tp < 3)
        self.outer = jnp.logical_not(self.inner)
        self.side = jnp.where(tp < 2, 0, 1)
        near = jnp.where(self.side == 0, 0, 3)
        far = jnp.where(self.side == 0, 1, 2)
        self.mate = spot(tp=jnp.where(self.inner, near, far))
        self.cross = spot(tp=3 - tp)


class LineSum(LineRole):
    scratch_count = 11

    @staticmethod
    def scratch(rows, width):
        count = rows // CHUNK
        return [
            pltpu.VMEM((rows, width), BF16),
            pltpu.VMEM((rows // 2, width), BF16),
            pltpu.VMEM((rows // 2, width), BF16),
        ] + [pltpu.SemaphoreType.DMA((count,)) for _ in range(8)]

    def __init__(self, part, total, scratch):
        super().__init__()
        self.part, self.total = part, total
        self.end, self.mid, self.out = scratch[:3]
        self.sems = scratch[3:]
        self.pairs = part.shape[0] // (2 * CHUNK)

    def to_mid(self, c):
        return remote(self.part.at[chunk(c)], self.end.at[chunk(c)], self.sems[0].at[c], self.sems[1].at[c], self.mate)

    def to_cross(self, k):
        return remote(self.out.at[chunk(k)], self.mid.at[chunk(k)], self.sems[2].at[k], self.sems[3].at[k], self.cross)

    def final_end(self, c):
        at = self.total.at[chunk(c)]
        return remote(at, at, self.sems[4].at[c], self.sems[5].at[c], self.mate)

    def final_cross(self, c):
        at = self.total.at[chunk(c)]
        return remote(at, at, self.sems[6].at[c], self.sems[7].at[c], self.cross)

    def send_block(self, s):
        @pl.when(self.outer)
        def _():
            def one(i, unused):
                self.to_mid(s * 2 * PER + i).start()
                return unused

            lax.fori_loop(0, 2 * PER, one, 0)

    def step(self, k):
        pairs, side = self.pairs, self.side

        @pl.when(k < pairs)
        def _():
            other = 2 * k + 1 - side
            self.to_mid(2 * k).wait_recv()
            self.to_mid(2 * k + 1).wait_recv()
            self.out[chunk(k)] = (
                self.part[chunk(other)].astype(F32) + self.end[chunk(other)].astype(F32)
            ).astype(BF16)
            self.to_cross(k).start()

        j = k - LAG

        @pl.when(jnp.logical_and(j >= 0, j < pairs))
        def _():
            mine = 2 * j + side
            self.to_cross(j).wait_recv()
            self.total[chunk(mine)] = (
                self.part[chunk(mine)].astype(F32)
                + self.end[chunk(mine)].astype(F32)
                + self.mid[chunk(j)].astype(F32)
            ).astype(BF16)
            self.final_cross(mine).start()
            self.final_end(mine).start()

        i = k - 2 * LAG

        @pl.when(jnp.logical_and(i >= 0, i < pairs))
        def _():
            other = 2 * i + 1 - side
            self.final_cross(other).wait_recv()
            self.final_end(other).start()

    def steps(self, first, last):
        @pl.when(self.inner)
        def _():
            def one(k, unused):
                self.step(k)
                return unused

            lax.fori_loop(first, last, one, 0)

    def wait_block(self, s):
        @pl.when(self.outer)
        def _():
            def one(i, unused):
                self.final_end(s * 2 * PER + i).wait_recv()
                return unused

            lax.fori_loop(0, 2 * PER, one, 0)

    def wait_half(self, h):
        @pl.when(self.outer)
        def _():
            def one(i, unused):
                self.final_end(h * PER + i).wait_recv()
                return unused

            lax.fori_loop(0, PER, one, 0)

    def drain(self):
        @pl.when(self.outer)
        def _():
            def one(c, unused):
                self.to_mid(c).wait_send()
                return unused

            lax.fori_loop(0, 2 * self.pairs, one, 0)

        @pl.when(self.inner)
        def _():
            def one(k, unused):
                mine, other = 2 * k + self.side, 2 * k + 1 - self.side
                self.to_cross(k).wait_send()
                self.final_cross(mine).wait_send()
                self.final_end(mine).wait_send()
                self.final_end(other).wait_send()
                return unused

            lax.fori_loop(0, self.pairs, one, 0)


def signal_all(partners):
    barrier = pltpu.get_barrier_semaphore()
    for where in partners:
        pl.semaphore_signal(barrier, inc=1, device_id=where, device_id_type=MESH)
    return barrier, len(partners)


def store_columns(stage, half, value):
    owners, share = stage.shape[1], stage.shape[-1]
    for o in range(owners):
        stage[half, o] = value[:, o * share : (o + 1) * share].astype(BF16)


def store_rows(stage, first, value):
    size = stage.shape[2]
    for q in range(value.shape[0] // size):
        owner, half = divmod(first // size + q, 2)
        stage[half, owner] = value[q * size : (q + 1) * size].astype(BF16)


def feed_kernel(
    gated_ref, ob_ref, gain_ref, shift_ref, ub_ref, own_down,
    out_hbm, x_hbm, g_hbm, up_hbm,
    resid_hbm, npart_hbm, dpart_hbm, gup_hbm, gdown_hbm, small_ref,
    out_in, x_ref, g_ref, up_ref,
    resid_ref, npart_ref, dpart_ref, gup_ref, gdown_ref, s_load, s_save, s_block, down_in, s_down, r_down,
    up_acc, down_acc, gall_ref, out_ref, down_ref, s_gate, r_gate,
):
    groups, owners = out_in.shape[:2]
    width = x_ref.shape[1]
    blocks = x_ref.shape[0] // SEG
    share = width // owners
    tp, ctx, dp = lax.axis_index("tp"), lax.axis_index("ctx"), lax.axis_index("dp")
    chain = LineRole()
    barrier, count = signal_all(
        [spot(tp=lax.rem(tp + i, groups)) for i in range(1, groups)]
        + [spot(ctx=lax.rem(ctx + i, 4)) for i in range(1, 4)]
        + [spot(dp=lax.rem(dp + i, owners)) for i in range(1, owners)]
    )

    low_half = lax.rem(ctx, 2)
    pair_mate = spot(ctx=ctx + 1 - 2 * low_half)

    def owner(i):
        return lax.rem(dp + i, owners)

    def half_of(ref, half):
        size = ref.shape[0] // 2
        return ref.at[pl.ds(pl.multiple_of(half * size, 16), size)]

    def send_down(i):
        return remote(
            half_of(own_down, low_half), half_of(down_in.at[dp], low_half), s_down.at[0, i], r_down.at[0, dp],
            spot(dp=owner(i)),
        )

    def swap_down(i):
        at = half_of(down_in.at[owner(i)], low_half)
        return remote(at, at, s_down.at[1, i], r_down.at[1, owner(i)], pair_mate)

    def got_down(stage, i, half):
        at = half_of(down_in.at[owner(i)], half)
        return remote(at, at, s_down.at[0, i], r_down.at[stage, owner(i)], pair_mate)

    far = jnp.where(tp < 2, tp + 2, tp - 2)
    beyond = jnp.where(chain.side == 0, 3, 0)
    other = jnp.where(chain.inner, 3 - tp, far)
    near = jnp.where(chain.inner, jnp.where(chain.side == 0, 0, 3), jnp.where(chain.side == 0, 1, 2))

    def gate_copy(s, i):
        rows = pl.ds(pl.multiple_of(s * SEG, SEG), SEG)
        where = chain.mate if i == 0 else spot(tp=other)
        return remote(gated_ref.at[rows], gall_ref.at[tp, rows], s_gate.at[i, s], r_gate.at[tp, s], where)

    def gate_pass(s, i, source):
        at = gall_ref.at[source, pl.ds(pl.multiple_of(s * SEG, SEG), SEG)]
        return remote(at, at, s_gate.at[2 + i, s], r_gate.at[source, s], chain.mate)

    def gate_from(s, source):
        at = gall_ref.at[source, pl.ds(pl.multiple_of(s * SEG, SEG), SEG)]
        return remote(at, at, s_gate.at[0, s], r_gate.at[source, s], chain.mate)

    loads = [
        pltpu.make_async_copy(src, dst, s_load.at[k])
        for k, (src, dst) in enumerate(
            (
                (out_hbm, out_in), (x_hbm, x_ref), (up_hbm, up_ref), (g_hbm, g_ref),
            )
        )
    ]
    for load in loads:
        load.start()

    def save(k, src, dst, s):
        rows = pl.ds(pl.multiple_of(s * SEG, SEG), SEG)
        return pltpu.make_async_copy(src.at[rows], dst.at[rows], s_block.at[k, s])

    blockwise = ((resid_ref, resid_hbm), (npart_ref, npart_hbm), (dpart_ref, dpart_hbm))
    saves = [
        pltpu.make_async_copy(src, dst, s_save.at[k])
        for k, (src, dst) in enumerate(((gup_ref, gup_hbm), (gdown_ref, gdown_hbm)))
    ]
    gall_ref[tp] = gated_ref[...]
    pl.semaphore_wait(barrier, count)
    for s in range(blocks):
        for i in range(2):
            gate_copy(s, 1 - i).start()
    for i in range(1, owners):
        send_down(i).start()
    down_in[dp] = own_down[...]
    for load in loads:
        load.wait()
    for o in range(owners):
        columns = slice(o * share, (o + 1) * share)
        for z in range(groups):
            out_ref[z, :, columns] = out_in[z, o]
    ob, gain, shift = (ref[...].reshape(1, -1) for ref in (ob_ref, gain_ref, shift_ref))
    ub = ub_ref[...].reshape(1, -1)
    for ref in (small_ref, up_acc, down_acc):
        ref[...] = jnp.zeros(ref.shape, F32)

    def core(s, unused):
        rows = pl.ds(pl.multiple_of(s * SEG, SEG), SEG)

        @pl.when(chain.inner)
        def _():
            for i, source in enumerate((3 - tp, beyond)):
                gate_from(s, source).wait_recv()
                gate_pass(s, i, source).start()
            gate_from(s, near).wait_recv()

        @pl.when(chain.outer)
        def _():
            gate_from(s, near).wait_recv()
            gate_from(s, 3 - near).wait_recv()
            gate_from(s, 3 - tp).wait_recv()

        mixed = mm(gall_ref[0, rows], out_ref[0])
        for z in range(1, groups):
            mixed = mixed + mm(gall_ref[z, rows], out_ref[z])
        residual = x_ref[rows].astype(F32) + mixed + ob
        resid_ref[rows] = residual
        save(0, *blockwise[0], s).start()
        low = (normalize(residual)[0] * gain + shift).astype(BF16)
        pre = mm(low, up_ref[...]) + ub
        cdf = 0.5 * (1.0 + lax.erf(pre * math.sqrt(0.5)))
        hidden = (pre * cdf).astype(BF16)
        slope = cdf + pre * (jnp.exp(-0.5 * pre * pre) * (1.0 / math.sqrt(2.0 * math.pi)))

        @pl.when(s == 0)
        def _():
            for i in range(1, owners):
                got_down(0, i, low_half).wait_recv()
                swap_down(i).start()
            for i in range(1, owners):
                got_down(1, i, 1 - low_half).wait_recv()
            for o in range(owners):
                down_ref[:, o * share : (o + 1) * share] = down_in[o]

        grad = g_ref[rows]
        d_pre = (mm_nt(grad, down_ref[...]) * slope).astype(BF16)
        npart_ref[rows] = mm_nt(d_pre, up_ref[...]).astype(BF16)
        dpart_ref[rows] = mm(hidden, down_ref[...]).astype(BF16)
        for k in (1, 2):
            save(k, *blockwise[k], s).start()
        up_acc[...] += mm_tn(low, d_pre)
        down_acc[...] += mm_tn(hidden, grad)
        small_ref[0:1] += jnp.sum(grad.astype(F32), axis=0, keepdims=True)
        small_ref[6:7] += jnp.sum(d_pre.astype(F32), axis=0, keepdims=True)
        return unused

    lax.fori_loop(0, blocks, core, 0)
    for t in range(2):
        part = slice(t * width // 2, (t + 1) * width // 2)
        store_rows(gup_ref, t * width // 2, up_acc[part])
        units = down_acc.shape[0] // 2
        store_columns(gdown_ref, t, down_acc[t * units : (t + 1) * units])
    for job in saves:
        job.start()
    for i in range(1, owners):
        send_down(i).wait_send()
        swap_down(i).wait_send()
    for s in range(blocks):
        for i in range(2):
            gate_copy(s, i).wait_send()

    @pl.when(chain.inner)
    def _():
        for s in range(blocks):
            for i, source in enumerate((3 - tp, beyond)):
                gate_pass(s, i, source).wait_send()

    for job in saves:
        job.wait()
    for s in range(blocks):
        for k in range(3):
            save(k, *blockwise[k], s).wait()


def sine_cosine(angle):
    turns = jnp.floor(angle * (2.0 / math.pi) + 0.5)
    rest = ((angle - turns * 1.5703125) - turns * 4.837512969970703125e-4) - turns * 7.54978995489188216e-8
    square = rest * rest
    sine = ((-1.9515295891e-4 * square + 8.3321608736e-3) * square - 1.6666654611e-1) * square * rest + rest
    cosine = ((2.443315711809948e-5 * square - 1.388731625493765e-3) * square + 4.166664568298827e-2) * (
        square * square
    ) + (1.0 - 0.5 * square)
    quarter = turns - 4.0 * jnp.floor(turns * 0.25)
    odd = jnp.logical_or(quarter == 1.0, quarter == 3.0)
    middle = jnp.logical_or(quarter == 1.0, quarter == 2.0)
    sine, cosine = jnp.where(odd, cosine, sine), jnp.where(odd, sine, cosine)
    return jnp.where(quarter >= 2.0, -sine, sine), jnp.where(middle, -cosine, cosine)


def extend_weights(ref, weight, bias):
    rows = weight.shape[0]
    ref[...] = jnp.zeros(ref.shape, F32)
    ref[0:rows] = weight[...]
    ref[rows : rows + 1] = bias[...].reshape(1, -1)


def decay(length, channels, tp, width):
    time_pos = lax.broadcasted_iota(jnp.int32, (length, 1), 0).astype(F32) * (1.0 / (length - 1))
    channel = (lax.broadcasted_iota(jnp.int32, (1, channels), 1) + tp * channels).astype(F32)
    rate = SLOW_RATE + (FAST_RATE - SLOW_RATE) * channel * (1.0 / (width - 1))
    return jnp.exp(-time_pos * rate) + SHIFT_FLOOR


EXACT_DOT = dict(precision=EXACT, preferred_element_type=F32)
TN = (((0,), (0,)), ((), ()))
NT = (((1,), (1,)), ((), ()))


def front_kernel(
    par_ref, x_ref, win_ref, last_ref, out_in, up_in, ft_ref, f1_ref, f1b_ref, f2_ref, f2b_ref, freq_ref,
    gain_ref, shift_ref, ib_ref, sw_ref, sb_ref, skip_ref, fh_ref, fl_ref, th_ref, tl_ref, sign_ref,
    low_hbm, proj_hbm, head_hbm, mixed_hbm, spec_hbm, filt_hbm, net_hbm, in_hbm, out_hbm, up_hbm,
    lasts_ref, gate_ref, conv_ref, gated_ref, carried_ref,
    w_ref, low_ref, proj_ref, head_ref, mixed_ref, spec_ref, filt_ref, net_ref, taps_ref, shared_ref,
    xt_ref, tail_ref, ext_ref, w1_ref, w2_ref, acc_ref, lastb_ref, wb_ref,
    s_in, r_in, s_last, r_last, s_out, r_out, s_up, r_up, s_line, r_line, s_swap,
    s_xt, r_xt, s_car, r_car, s_fwd, local,
):
    total_rows, width = x_ref.shape
    channels = ib_ref.shape[1]
    blocks = total_rows // SEG
    tp, ctx, dp = lax.axis_index("tp"), lax.axis_index("ctx"), lax.axis_index("dp")
    owners, lines = out_hbm.shape[1], out_hbm.shape[0]
    share = win_ref.shape[2]
    last_share = last_ref.shape[0]
    up_share = up_in.shape[0]

    def cell(i):
        flat = lax.rem(tp * owners + dp + i, owners * lines)
        return flat // owners, lax.rem(flat, owners)

    def owner(i):
        return lax.rem(dp + i, owners)

    def ctx_at(i):
        return lax.rem(ctx + i, 4)

    partners = [spot(ctx=ctx_at(i)) for i in range(1, 4)]
    for i in range(1, owners * lines):
        line, own = cell(i)
        partners.append(spot(tp=line, dp=own))
    barrier, count = signal_all(partners)

    def rows_of(ref, who, size):
        return ref.at[pl.ds(pl.multiple_of(who * size, size), size)]

    low_half = lax.rem(ctx, 2)
    mate = spot(ctx=ctx + 1 - 2 * low_half)

    def in_half(ref, half):
        size = channels // 2
        return ref.at[:, pl.ds(pl.multiple_of(half * size, 16), size)]

    def send_in(i):
        return remote(
            in_half(win_ref, low_half), in_half(wb_ref.at[dp], low_half), s_in.at[0, i], r_in.at[0, dp],
            spot(dp=owner(i)),
        )

    def swap_in(i):
        at = in_half(wb_ref.at[owner(i)], low_half)
        return remote(at, at, s_in.at[1, i], r_in.at[1, owner(i)], mate)

    def got_in(stage, i, half):
        at = in_half(wb_ref.at[owner(i)], half)
        return remote(at, at, s_in.at[0, i], r_in.at[stage, owner(i)], mate)

    def send_last(i):
        return remote(last_ref, lastb_ref.at[dp], s_last.at[i], r_last.at[dp], spot(dp=owner(i)))

    def send_xt(i):
        at = xt_ref.at[ctx]
        return remote(at, at, s_xt.at[i], r_xt.at[ctx], spot(ctx=ctx_at(i)))

    for s in range(blocks):
        tail = x_ref[s * SEG + SEG - 16 : s * SEG + SEG].astype(F32)
        xt_ref[ctx, 2 * s : 2 * s + 2] = tail[14:16]
    pl.semaphore_wait(barrier, count)
    for i in range(1, owners):
        send_in(i).start()
        send_last(i).start()
    for i in range(1, 4):
        send_xt(i).start()
    wb_ref[dp] = win_ref[...]
    lastb_ref[dp] = last_ref[...]

    gain, shift = gain_ref[...].reshape(1, -1), shift_ref[...].reshape(1, -1)

    def norm(s, unused):
        rows = pl.ds(pl.multiple_of(s * SEG, SEG), SEG)
        low_ref[rows] = (normalize(x_ref[rows].astype(F32))[0] * gain + shift).astype(BF16)
        return unused

    lax.fori_loop(0, blocks, norm, 0)
    saves = [pltpu.make_async_copy(low_ref, low_hbm, local.at[1])]
    saves[-1].start()

    units = f1_ref.shape[1]
    length = ft_ref.shape[1]
    extend_weights(w1_ref, f1_ref, f1b_ref)
    extend_weights(w2_ref, f2_ref, f2b_ref)
    freq = freq_ref[...].reshape(1, -1)
    net_ref[...] = jnp.zeros(net_ref.shape, F32)
    angle = lax.dot_general(w1_ref[...] * freq, ft_ref[...], TN, **EXACT_DOT)
    first, net_ref[0, 0:units] = sine_cosine(angle)
    net_ref[1, 0:units] = first
    pad = net_ref.shape[1] - units
    net_ref[1, units:] = jnp.where(lax.broadcasted_iota(jnp.int32, (pad, length), 0) == 0, 1.0, 0.0)
    angle = lax.dot_general(w2_ref[...] * freq, net_ref[1], TN, **EXACT_DOT)
    second, net_ref[2, 0:units] = sine_cosine(angle)
    net_ref[3, 0:units] = second
    saves.append(pltpu.make_async_copy(net_ref, net_hbm, local.at[2]))
    saves[-1].start()
    for i in range(1, owners):
        at = lastb_ref.at[owner(i)]
        remote(at, at, s_last.at[i], r_last.at[owner(i)], spot(dp=owner(i))).wait_recv()
    for o in range(owners):
        lasts_ref[o * last_share : (o + 1) * last_share] = lastb_ref[o].astype(F32)
    raw = lax.dot_general(second, lasts_ref[...], TN, **EXACT_DOT)
    taps_ref[...] = raw * decay(length, channels, tp, channels * lines)
    fh, fl, th, tl = fh_ref[...], fl_ref[...], th_ref, tl_ref
    sign = sign_ref[...]
    for j in range(DEPTH):
        part = taps_ref[j * SEG : (j + 1) * SEG]
        out = mm_split(fh, fl, part)
        re, im = out[:SEG], out[SEG:]
        filt_ref[j, 0] = re
        filt_ref[j, 1] = im
    for j in range(DEPTH - 1, 0, -1):
        first = taps_ref[(j - 1) * SEG : (j - 1) * SEG + 1]
        filt_ref[j, 0] = filt_ref[j, 0] - sign * filt_ref[j - 1, 1]
        filt_ref[j, 1] = filt_ref[j, 1] + sign * (filt_ref[j - 1, 0] - first)
    saves.append(pltpu.make_async_copy(filt_ref, filt_hbm, local.at[3]))
    saves[-1].start()

    def half_of(ref, half):
        size = ref.shape[0] // 2
        return ref.at[pl.ds(pl.multiple_of(half * size, 16), size)]

    def up_half(ref, half):
        size = ref.shape[1] // 2
        return ref.at[:, pl.ds(pl.multiple_of(half * size, size), size)]

    def line_out(i):
        return remote(
            out_in, out_hbm.at[tp, dp], s_line.at[i], r_line.at[tp], spot(tp=lax.rem(tp + i, lines))
        )

    def send_out(i, j):
        return remote(
            half_of(out_in, low_half), half_of(out_hbm.at[tp, dp], low_half), s_out.at[i, j], r_out.at[0, tp, dp],
            spot(dp=owner(i), tp=lax.rem(tp + j, lines)),
        )

    def swap_out(i, line):
        at = half_of(out_hbm.at[line, owner(i)], low_half)
        return remote(at, at, s_swap.at[2, i, line], r_out.at[1, line, owner(i)], mate)

    def send_up(i):
        return remote(
            up_half(up_in, low_half), up_half(rows_of(up_hbm, dp, up_share), low_half), s_up.at[i], r_up.at[0, dp],
            spot(dp=owner(i)),
        )

    def swap_up(i):
        at = up_half(rows_of(up_hbm, owner(i), up_share), low_half)
        return remote(at, at, s_swap.at[0, i, 0], r_up.at[1, owner(i)], mate)

    for i in range(1, owners):
        got_in(0, i, low_half).wait_recv()
        swap_in(i).start()
        send_up(i).start()
        for j in range(lines):
            send_out(i, j).start()
    for i in range(1, lines):
        line_out(i).start()
    for i in range(1, owners):
        got_in(1, i, 1 - low_half).wait_recv()
    for o in range(owners):
        w_ref[:, :, o * share : (o + 1) * share] = wb_ref[o]
    saves.append(pltpu.make_async_copy(w_ref, in_hbm, local.at[4]))
    saves[-1].start()

    for k, (src, dst) in enumerate(
        ((out_in, out_hbm.at[tp, dp]), (up_in, rows_of(up_hbm, dp, up_share)))
    ):
        saves.append(pltpu.make_async_copy(src, dst, local.at[5 + k]))
        saves[-1].start()

    for i in range(1, 4):
        at = xt_ref.at[ctx_at(i)]
        remote(at, at, s_xt.at[i], r_xt.at[ctx_at(i)], spot(ctx=ctx_at(i))).wait_recv()
    tail_ref[...] = jnp.zeros(tail_ref.shape, F32)
    for half in range(2):
        tails = (normalize(xt_ref[half])[0] * gain + shift).astype(BF16)
        for g in range(3):
            value = mm_nt(tails, w_ref[g]) + ib_ref[g : g + 1]
            for s in range(4):
                tail_ref[g, 4 * half + s, 6:8] = value[2 * s : 2 * s + 2]

    def share_block(s, other):
        return remote(
            carried_ref.at[pl.ds(pl.multiple_of(s * SEG, SEG), SEG)], shared_ref.at[4 * ctx + s],
            s_car.at[other, s], r_car.at[ctx, s], spot(ctx=other),
        )

    def forward_block(s, group):
        at = shared_ref.at[4 * group + s]
        return remote(at, at, s_fwd.at[s], r_car.at[group, s], spot(ctx=5 - ctx))

    def mix(s, unused):
        rows = pl.ds(pl.multiple_of(s * SEG, SEG), SEG)
        parent = par_ref[0, ctx * blocks + s]
        slot = jnp.where(parent >= 0, parent, 8)
        out = []
        for g in range(3):
            projected = mm_nt(low_ref[rows], w_ref[g]) + ib_ref[g : g + 1]
            proj_ref[g, rows] = projected
            head = tail_ref[g, slot]
            head_ref[g, s] = head
            ext_ref[g, 0:HEADS] = head
            ext_ref[g, HEADS : HEADS + SEG] = projected
            mixed = (
                sw_ref[g, 0:1] * ext_ref[g, HEADS - 2 : HEADS - 2 + SEG]
                + sw_ref[g, 1:2] * ext_ref[g, HEADS - 1 : HEADS - 1 + SEG]
                + sw_ref[g, 2:3] * projected
                + sb_ref[g : g + 1]
            )
            if g == 0:
                gate_ref[rows] = mixed
            else:
                mixed_ref[g - 1, rows] = mixed
            out.append(mixed)
        carried = (out[2] * out[1]).astype(BF16)
        carried_ref[rows] = carried

        @pl.when(ctx == 0)
        def _():
            share_block(s, 2).start()
            share_block(s, 1).start()

        @pl.when(ctx == 1)
        def _():
            share_block(s, 3).start()

        spec = mm(fh_ref[...], carried) + mm(fl_ref[...], carried)
        spec_ref[8 + s, 0] = spec[:SEG]
        spec_ref[8 + s, 1] = spec[SEG:]
        return unused

    lax.fori_loop(0, blocks, mix, 0)
    for k, (src, dst) in enumerate(((proj_ref, proj_hbm), (head_ref, head_hbm), (mixed_ref, mixed_hbm))):
        saves.append(pltpu.make_async_copy(src, dst, local.at[8 + k]))
        saves[-1].start()

    def spectrum(slot, part):
        out = mm(fh_ref[...], part) + mm(fl_ref[...], part)
        spec_ref[slot, 0] = out[:SEG]
        spec_ref[slot, 1] = out[SEG:]

    spec_ref[12] = jnp.zeros(spec_ref.shape[1:], F32)

    def arrived(group, s):
        at = shared_ref.at[4 * group + s]
        return remote(at, at, s_fwd.at[s], r_car.at[group, s], spot(ctx=ctx_at(1)))

    def copy_own(group):
        def one(s, unused):
            spec_ref[4 * group + s] = spec_ref[8 + s]
            return unused

        lax.fori_loop(0, 4, one, 0)

    def receive(group):
        def one(s, unused):
            arrived(group, s).wait_recv()
            spectrum(4 * group + s, shared_ref[4 * group + s])
            return unused

        lax.fori_loop(0, 4, one, 0)

    def receive_forward(group):
        def one(s, unused):
            arrived(group, s).wait_recv()
            forward_block(s, group).start()
            spectrum(4 * group + s, shared_ref[4 * group + s])
            return unused

        lax.fori_loop(0, 4, one, 0)

    @pl.when(ctx == 0)
    def _():
        copy_own(0)

    @pl.when(ctx == 1)
    def _():
        copy_own(1)
        receive(0)

    @pl.when(ctx == 2)
    def _():
        receive_forward(0)
        receive(1)

    @pl.when(ctx == 3)
    def _():
        receive_forward(1)
        receive(0)

    saves.append(pltpu.make_async_copy(spec_ref, spec_hbm, local.at[11]))
    saves[-1].start()

    def dest(s, unused):
        above = lineage(par_ref, ctx * blocks + s)
        places = [8 + s] + [jnp.where(a >= 0, a, 12) for a in above]
        blend_all(acc_ref, [(filt_ref.at[d], spec_ref.at[places[d]]) for d in range(DEPTH)], False)
        long_out = unpack_spectrum(th, tl, acc_ref) * (1.0 / SEG)
        place = pl.ds(pl.multiple_of(s * SEG, SEG), SEG)
        convolved = long_out + skip_ref[...].reshape(1, -1) * carried_ref[place].astype(F32)
        conv_ref[place] = convolved
        gated_ref[place] = (convolved * gate_ref[place]).astype(BF16)
        return unused

    lax.fori_loop(0, blocks, dest, 0)

    def take_halves(stage, half):
        for i in range(1, owners):
            who = owner(i)
            at = up_half(rows_of(up_hbm, who, up_share), half)
            remote(at, at, s_up.at[i], r_up.at[stage, who], mate).wait_recv()
            if stage == 0:
                swap_up(i).start()
            for line in range(lines):
                at = half_of(out_hbm.at[line, who], half)
                remote(at, at, s_out.at[i, line], r_out.at[stage, line, who], mate).wait_recv()
                if stage == 0:
                    swap_out(i, line).start()

    take_halves(0, low_half)

    for save in saves:
        save.wait()
    take_halves(1, 1 - low_half)
    for i in range(1, owners):
        send_in(i).wait_send()
        swap_in(i).wait_send()
        send_last(i).wait_send()
        send_up(i).wait_send()
        swap_up(i).wait_send()
        for j in range(lines):
            send_out(i, j).wait_send()
            swap_out(i, j).wait_send()
    for i in range(1, lines):
        line_out(i).wait_send()
        line = lax.rem(tp + i, lines)
        at = out_hbm.at[line, dp]
        remote(at, at, s_line.at[i], r_line.at[line], mate).wait_recv()
    for i in range(1, 4):
        send_xt(i).wait_send()

    @pl.when(ctx == 0)
    def _():
        for s in range(blocks):
            share_block(s, 2).wait_send()
            share_block(s, 1).wait_send()

    @pl.when(ctx == 1)
    def _():
        for s in range(blocks):
            share_block(s, 3).wait_send()

    @pl.when(ctx == 2)
    def _():
        for s in range(blocks):
            forward_block(s, 0).wait_send()

    @pl.when(ctx == 3)
    def _():
        for s in range(blocks):
            forward_block(s, 1).wait_send()


class OwnerSum:
    scratch_count = 17

    @staticmethod
    def scratch(owners, shape):
        many = max(owners - 1, 1)
        return [
            pltpu.VMEM((owners,) + shape, BF16),
            pltpu.VMEM((owners,) + shape, BF16),
            pltpu.VMEM((many,) + shape, BF16),
            pltpu.VMEM(shape, BF16),
            pltpu.VMEM(shape, BF16),
            pltpu.SemaphoreType.DMA,
            pltpu.SemaphoreType.DMA,
            pltpu.SemaphoreType.DMA,
            pltpu.SemaphoreType.DMA((many,)),
            pltpu.SemaphoreType.DMA((many,)),
            pltpu.SemaphoreType.DMA,
            pltpu.SemaphoreType.DMA,
            pltpu.SemaphoreType.DMA,
            pltpu.SemaphoreType.DMA,
            pltpu.SemaphoreType.DMA((2,)),
            pltpu.VMEM((2,) + shape, F32),
        ]

    def __init__(self, stage, out, scratch):
        self.stage, self.out, self.result = stage, out, scratch[-1]
        self.recv, self.keep, self.parts, self.y_own, self.y_in = scratch[:5]
        self.sems = scratch[5:-1]
        self.owners = stage.shape[1]
        self.dp, ctx = lax.axis_index("dp"), lax.axis_index("ctx")
        self.low = lax.rem(ctx, 2)
        self.mate = spot(ctx=ctx + 1 - 2 * self.low)
        self.across = spot(ctx=lax.rem(ctx + 2, 4))

    def load(self):
        return pltpu.make_async_copy(self.stage.at[self.low], self.keep, self.sems[0])

    def to_mate(self):
        return remote(self.stage.at[1 - self.low], self.recv, self.sems[1], self.sems[2], self.mate)

    def to_owner(self, i):
        owner = lax.rem(self.dp + i, self.owners)
        return remote(
            self.keep.at[owner], self.parts.at[self.owners - 1 - i], self.sems[3].at[i - 1],
            self.sems[4].at[self.owners - 1 - i], spot(dp=owner),
        )

    def from_owner(self, i):
        return remote(self.parts.at[i - 1], self.parts.at[i - 1], self.sems[3].at[i - 1], self.sems[4].at[i - 1], self.mate)

    def to_across(self):
        return remote(self.y_own, self.y_in, self.sems[5], self.sems[6], self.across)

    def to_back(self):
        at = self.result.at[self.low]
        return remote(at, at, self.sems[7], self.sems[8], self.mate)

    def save(self, half):
        return pltpu.make_async_copy(self.result.at[half], self.out.at[half], self.sems[9].at[half])

    def begin(self):
        self.to_mate().start()
        self.load().start()

    def pair(self):
        self.load().wait()
        self.to_mate().wait_recv()
        for o in range(self.owners):
            self.keep[o] = (self.keep[o].astype(F32) + self.recv[o].astype(F32)).astype(BF16)
        for i in range(1, self.owners):
            self.to_owner(i).start()

    def own(self):
        total = self.keep[self.dp].astype(F32)
        for i in range(1, self.owners):
            self.from_owner(i).wait_recv()
            total = total + self.parts[i - 1].astype(F32)
        self.y_own[...] = total.astype(BF16)
        self.to_across().start()

    def cross(self):
        self.to_across().wait_recv()
        self.result[self.low] = self.y_own[...].astype(F32) + self.y_in[...].astype(F32)
        self.to_back().start()
        self.save(self.low).start()

    def whole(self):
        at = self.result.at[1 - self.low]
        remote(at, at, self.sems[7], self.sems[8], self.mate).wait_recv()
        self.save(1 - self.low).start()

    def finish(self):
        self.to_mate().wait_send()
        for i in range(1, self.owners):
            self.to_owner(i).wait_send()
        self.to_across().wait_send()
        self.to_back().wait_send()
        self.save(self.low).wait()
        self.save(1 - self.low).wait()


class SmallSum:
    @staticmethod
    def scratch(count, shape):
        return [
            pltpu.VMEM((count,) + shape, F32),
            pltpu.SemaphoreType.DMA((count,)),
            pltpu.SemaphoreType.DMA((count,)),
        ]

    def __init__(self, axis, scratch):
        self.axis = axis
        self.slots, self.send, self.recv = scratch
        self.count = self.slots.shape[0]
        self.me = lax.axis_index(axis)

    def copy(self, i):
        at = self.slots.at[self.me]
        other = lax.rem(self.me + i, self.count)
        return remote(at, at, self.send.at[i], self.recv.at[self.me], spot(**{self.axis: other}))

    def start(self, value):
        self.slots[self.me] = value
        for i in range(1, self.count):
            self.copy(i).start()

    def total(self):
        for i in range(1, self.count):
            other = lax.rem(self.me + i, self.count)
            at = self.slots.at[other]
            remote(at, at, self.send.at[i], self.recv.at[other], spot(**{self.axis: lax.rem(self.me + i, self.count)})).wait_recv()
        out = self.slots[0]
        for i in range(1, self.count):
            out = out + self.slots[i]
        return out

    def finish(self):
        for i in range(1, self.count):
            self.copy(i).wait_send()


def back_kernel(
    par_ref, gated_ref, dpart_ref, fgain_ref,
    fh_ref, fl_ref, th_ref, tl_ref, sign_ref, sw_ref, skip_ref,
    ft_ref, f1_ref, f1b_ref, f2_ref, f2b_ref, freq_ref, last_ref, small_ref,
    npart_hbm, resid_hbm, g_hbm, gate_hbm, conv_hbm, carried_hbm, out_hbm,
    mixed_hbm, low_hbm, w_hbm, x_hbm, proj_hbm, head_hbm, spec_hbm, filt_hbm, net_hbm, sup_hbm, sdown_hbm,
    dres_hbm, dsum_ref, psum_ref, oup_ref, odown_ref, oout_ref, oin_ref, va_ref, vd_ref, vl_ref, vf_ref,
    dall_ref, dconv_ref, dzero_ref, stage_out, s_long, r_long,
    yown_ref, dcar_ref, dtaps_ref, stage_in, ppart_ref, w1_ref, w2_ref,
    mixed_ref, hd_ref, s_hd, r_hd, local, *rest,
):
    total_rows, width = ppart_ref.shape
    channels = dconv_ref.shape[1]
    blocks = total_rows // SEG
    owners = sup_hbm.shape[1]
    ctx, tp, dp = lax.axis_index("ctx"), lax.axis_index("tp"), lax.axis_index("dp")
    rest = list(rest)

    def take(n):
        out = rest[:n]
        del rest[:n]
        return out

    down = LineSum(dpart_ref, dsum_ref, take(11))
    proj = LineSum(ppart_ref, psum_ref, take(11))
    early = [OwnerSum(s, o, take(16)) for s, o in ((sup_hbm, oup_ref), (sdown_hbm, odown_ref), (stage_out, oout_ref))]
    late = OwnerSum(stage_in, oin_ref, take(16))
    a_ctx, a_dp = SmallSum("ctx", take(3)), SmallSum("dp", take(3))
    d_ctx, d_dp, d_tp = SmallSum("ctx", take(3)), SmallSum("dp", take(3)), SmallSum("tp", take(3))
    l_ctx, l_dp = SmallSum("ctx", take(3)), SmallSum("dp", take(3))
    f_ctx, f_dp, f_tp = SmallSum("ctx", take(3)), SmallSum("dp", take(3)), SmallSum("tp", take(3))

    partners = [spot(tp=lax.rem(tp + i, 4)) for i in range(1, 4)]
    partners += [spot(ctx=lax.rem(ctx + i, 4)) for i in range(1, 4)]
    partners += [spot(dp=lax.rem(dp + i, owners)) for i in range(1, owners)]
    barrier, count = signal_all(partners)
    load_part = pltpu.make_async_copy(npart_hbm, ppart_ref, local.at[10])
    load_mixed = pltpu.make_async_copy(mixed_hbm, mixed_ref, local.at[11])
    load_part.start()
    load_part.wait()
    pl.semaphore_wait(barrier, count)
    for s in range(blocks):
        proj.send_block(s)
    load_mixed.start()
    for job in early[:2]:
        job.begin()
    va_ref[...] = jnp.zeros(va_ref.shape, F32)
    vd_ref[...] = small_ref[...]
    fh, fl, th, tl = fh_ref[...], fl_ref[...], th_ref, tl_ref
    skip = skip_ref[...].reshape(1, -1)
    scale = 1.0 / SEG

    def put(dst, value):
        dst[0] = value[:SEG] * scale
        dst[1] = value[SEG:] * scale

    def half_rows(h):
        return pl.ds(pl.multiple_of(h * HALF, HALF), HALF)

    def half_of(who, h):
        return dall_ref.at[who * blocks + h // 2, half_rows(lax.rem(h, 2))]

    def long_to(h, other):
        at = half_of(ctx, h)
        return remote(at, at, s_long.at[other, h], r_long.at[ctx, h], spot(ctx=other))

    def long_from(other):
        def one(h, unused):
            at = half_of(other, h)
            remote(at, at, s_long.at[other, h], r_long.at[other, h], spot(ctx=lax.rem(ctx + 1, 4))).wait_recv()
            return unused

        lax.fori_loop(0, 2 * blocks, one, 0)

    def feed_back(in_ref, g_ref, dres_ref, gate_ref, conv_ref, carried_ref, parts_ref, out_ref, gout_ref):
        once = [
            pltpu.make_async_copy(src, dst, local.at[k])
            for k, (src, dst) in enumerate(
                ((gate_hbm, gate_ref), (conv_hbm, conv_ref), (carried_hbm, carried_ref), (out_hbm.at[tp], parts_ref))
            )
        ]
        for load in once:
            load.start()

        def fetch(h):
            slot = lax.rem(h, 2)
            return (
                pltpu.make_async_copy(resid_hbm.at[half_rows(h)], in_ref.at[slot], local.at[4 + slot]),
                pltpu.make_async_copy(g_hbm.at[half_rows(h)], g_ref.at[slot], local.at[6 + slot]),
            )

        def save(h):
            slot = lax.rem(h, 2)
            return pltpu.make_async_copy(dres_ref.at[slot], dres_hbm.at[half_rows(h)], local.at[8 + slot])

        for load in fetch(0):
            load.start()
        for load in once:
            load.wait()
        share = width // owners
        for o in range(owners):
            out_ref[:, o * share : (o + 1) * share] = parts_ref[o]
        gout_ref[...] = jnp.zeros(gout_ref.shape, F32)
        gain = fgain_ref[...].reshape(1, -1)
        proj.steps(0, PER)

        def one(h, unused):
            rows = half_rows(h)
            slot = lax.rem(h, 2)
            for load in fetch(h):
                load.wait()

            @pl.when(h + 1 < 2 * blocks)
            def _():
                for load in fetch(h + 1):
                    load.start()

            xhat, spread = normalize(in_ref[slot])
            proj.steps(PER + h * PER // 2, PER + (h + 1) * PER // 2)
            proj.wait_half(h)

            @pl.when(h == 1)
            def _():
                for job in early[:2]:
                    job.pair()

            @pl.when(h == 2 * blocks - 3)
            def _():
                for b in range(blocks):
                    down.send_block(b)

            dn = psum_ref[rows].astype(F32)
            e = dn * gain
            d_res = g_ref[slot].astype(F32) + spread * (
                e - jnp.mean(e, axis=-1, keepdims=True) - xhat * jnp.mean(e * xhat, axis=-1, keepdims=True)
            )
            d_mix = d_res.astype(BF16)
            d_gated = mm_nt(d_mix, out_ref[...])
            d_conv = d_gated * gate_ref[rows]
            dall_ref[ctx * blocks + h // 2, half_rows(lax.rem(h, 2))] = d_conv.astype(BF16)
            for other in range(2):
                @pl.when(other < ctx)
                def _():
                    long_to(h, other).start()

            @pl.when(h >= 2)
            def _():
                save(h - 2).wait()

            dres_ref[slot] = d_res
            save(h).start()
            dconv_ref[rows] = d_conv
            dzero_ref[rows] = d_gated * conv_ref[rows]

            @pl.when(lax.rem(h, 2) == 1)
            def _():
                part = dall_ref[ctx * blocks + h // 2]
                put(yown_ref.at[h // 2], mm(fh, part) + mm(fl, part))

            vd_ref[2:3] += jnp.sum(dn * xhat, axis=0, keepdims=True)
            vd_ref[3:4] += jnp.sum(dn, axis=0, keepdims=True)
            vd_ref[1:2] += jnp.sum(d_mix.astype(F32), axis=0, keepdims=True)
            va_ref[15:16] += jnp.sum(d_conv * carried_ref[rows].astype(F32), axis=0, keepdims=True)
            gout_ref[...] += mm_tn(gated_ref[rows], d_mix)
            return unused

        lax.fori_loop(0, 2 * blocks, one, 0)
        half = stage_out.shape[2]
        for t in range(2):
            store_columns(stage_out, t, gout_ref[t * half : (t + 1) * half])
        save(2 * blocks - 2).wait()
        save(2 * blocks - 1).wait()

    pl.run_scoped(
        feed_back,
        pltpu.VMEM((2, HALF, width), F32),
        pltpu.VMEM((2, HALF, width), BF16),
        pltpu.VMEM((2, HALF, width), F32),
        pltpu.VMEM((total_rows, channels), F32),
        pltpu.VMEM((total_rows, channels), F32),
        pltpu.VMEM((total_rows, channels), BF16),
        pltpu.VMEM((owners, channels, width // owners), BF16),
        pltpu.VMEM((channels, width), BF16),
        pltpu.VMEM((channels, width), F32),
    )
    early[2].begin()
    down.steps(0, 3)

    def to_ctx(i):
        at = hd_ref.at[pl.ds(ctx * blocks, blocks)]
        return remote(at, at, s_hd.at[i], r_hd.at[ctx], spot(ctx=lax.rem(ctx + i, 4)))

    def conv_inputs(filt_ref, more_ref, acc_ref):
        load = pltpu.make_async_copy(filt_hbm, filt_ref, local.at[0])
        load.start()

        load.wait()
        load_mixed.wait()

        def leaf_sum(match):
            total = None
            for leaf in range(8, 16):
                term = jnp.where(match(leaf), 1.0, 0.0) * dall_ref[leaf].astype(F32)
                total = term if total is None else total + term
            return total

        def from_leaf(b):
            return lambda leaf: par_ref[0, leaf] == b

        def finish(s, terms):
            blend_all(acc_ref.at[s], terms, True)

        @pl.when(ctx == 0)
        def _():
            for other in (1, 2, 3):
                long_from(other)

            def gather(k, unused):
                p = k + 1
                total = None
                for b in range(4, 8):
                    term = jnp.where(par_ref[0, b] == p, 1.0, 0.0) * dall_ref[b].astype(F32)
                    total = term if total is None else total + term
                put(more_ref.at[k], mm_split(fh, fl, total))
                total = leaf_sum(lambda leaf: par_ref[0, par_ref[0, leaf]] == p)
                put(more_ref.at[3 + k], mm_split(fh, fl, total))
                return unused

            lax.fori_loop(0, 3, gather, 0)
            for a in range(4):
                terms = [(filt_ref.at[s - a], yown_ref.at[s]) for s in range(a, 4)]
                for p in range(max(a, 1), 4):
                    terms.append((filt_ref.at[p - a + 1], more_ref.at[p - 1]))
                    terms.append((filt_ref.at[p - a + 2], more_ref.at[p + 2]))
                finish(a, terms)

        @pl.when(ctx == 1)
        def _():
            for other in (2, 3):
                long_from(other)

            def one(b, unused):
                put(more_ref.at[0], mm_split(fh, fl, leaf_sum(from_leaf(b + 4))))
                finish(b, [(filt_ref.at[0], yown_ref.at[b]), (filt_ref.at[1], more_ref.at[0])])
                return unused

            lax.fori_loop(0, 4, one, 0)

        @pl.when(ctx > 1)
        def _():
            def one(b, unused):
                finish(b, [(filt_ref.at[0], yown_ref.at[b])])
                return unused

            lax.fori_loop(0, 4, one, 0)

        down.steps(3, 5)
        for s in range(blocks):
            top = slice(s * SEG, s * SEG + HEADS)
            d_car = unpack_spectrum(th.at[0:16], tl.at[0:16], acc_ref.at[s])[0:HEADS] + skip * dconv_ref[top]
            rows = [dzero_ref[top], d_car * mixed_ref[1, top], d_car * mixed_ref[0, top]]
            for g in range(3):
                hd_ref[ctx * blocks + s, 2 * g : 2 * g + 2] = rows[g][0:2]
            hd_ref[ctx * blocks + s, 6:8] = jnp.zeros((2, channels), F32)
        for i in range(1, 4):
            to_ctx(i).start()

        def whole(s, unused):
            place = pl.ds(pl.multiple_of(s * SEG, SEG), SEG)
            dcar_ref[place] = unpack_spectrum(th, tl, acc_ref.at[s]) + skip * dconv_ref[place]
            return unused

        lax.fori_loop(0, blocks, whole, 0)

    def mix_stage(low_ref, w_ref, x_ref):
        loads = [
            pltpu.make_async_copy(src, dst, local.at[4 + k])
            for k, (src, dst) in enumerate(((w_hbm, w_ref), (x_hbm, x_ref), (low_hbm, low_ref)))
        ]
        for load in loads:
            load.start()
        pl.run_scoped(
            conv_inputs,
            pltpu.VMEM((DEPTH, 2, SEG, channels), F32),
            pltpu.VMEM((6, 2, SEG, channels), F32),
            pltpu.VMEM((blocks, 2, SEG, channels), F32),
        )

        down.steps(5, 7)
        proj.drain()
        for i in range(1, 4):
            other = lax.rem(ctx + i, 4)
            at = hd_ref.at[pl.ds(other * blocks, blocks)]
            remote(at, at, s_hd.at[i], r_hd.at[other], spot(ctx=other)).wait_recv()

        def mix_back(dp_ref, ext_ref, dm_ref, pin_ref, hin_ref):
            load_heads = pltpu.make_async_copy(head_hbm, hin_ref, local.at[1])
            load_heads.start()

            def fetch(s):
                rows = pl.ds(pl.multiple_of(s * SEG, SEG), SEG)
                return pltpu.make_async_copy(proj_hbm.at[:, rows], pin_ref.at[lax.rem(s, 2)], local.at[2 + lax.rem(s, 2)])

            fetch(0).start()
            load_heads.wait()
            for load in loads:
                load.wait()

            def one(s, unused):
                rows = pl.ds(pl.multiple_of(s * SEG, SEG), SEG)
                slot = lax.rem(s, 2)
                fetch(s).wait()

                @pl.when(s + 1 < blocks)
                def _():
                    fetch(s + 1).start()

                mine = ctx * blocks + s
                child = None
                for b in range(1, 16):
                    term = jnp.where(par_ref[0, b] == mine, 1.0, 0.0) * hd_ref[b]
                    child = term if child is None else child + term
                part = None
                for g in range(3):
                    if g == 0:
                        dm = dzero_ref[rows]
                    else:
                        dm = dcar_ref[rows] * mixed_ref[2 - g, rows]
                    ext_ref[0:HEADS] = hin_ref[g, s]
                    ext_ref[HEADS : HEADS + SEG] = pin_ref[slot, g]
                    for k in range(3):
                        piece = ext_ref[HEADS - 2 + k : HEADS - 2 + k + SEG]
                        va_ref[3 * g + k : 3 * g + k + 1] += jnp.sum(piece * dm, axis=0, keepdims=True)
                    va_ref[12 + g : 13 + g] += jnp.sum(dm, axis=0, keepdims=True)
                    dm_ref[0:SEG] = dm
                    dm_ref[SEG : SEG + 2] = child[2 * g : 2 * g + 2]
                    d_proj = (
                        sw_ref[g, 2:3] * dm
                        + sw_ref[g, 1:2] * dm_ref[1 : 1 + SEG]
                        + sw_ref[g, 0:1] * dm_ref[2 : 2 + SEG]
                    ).astype(BF16)
                    dp_ref[g, rows] = d_proj
                    va_ref[9 + g : 10 + g] += jnp.sum(d_proj.astype(F32), axis=0, keepdims=True)
                    term = mm(d_proj, w_ref[g])
                    part = term if part is None else part + term
                ppart_ref[rows] = part.astype(BF16)
                proj.send_block(s)
                xhat = normalize(x_ref[rows].astype(F32))[0]
                vd_ref[4:5] += jnp.sum(part * xhat, axis=0, keepdims=True)
                vd_ref[5:6] += jnp.sum(part, axis=0, keepdims=True)
                down.steps(7 + s, 8 + s)
                return unused

            lax.fori_loop(0, blocks, one, 0)
            rows = stage_in.shape[3]
            for g in range(3):
                value = mm_tn(dp_ref[g], low_ref[...])
                for t in range(2):
                    store_columns(stage_in.at[:, :, g], t, value[t * rows : (t + 1) * rows])

        pl.run_scoped(
            mix_back,
            pltpu.VMEM((3, total_rows, channels), BF16),
            pltpu.VMEM((HEADS + SEG, channels), F32),
            pltpu.VMEM((HEADS + SEG, channels), F32),
            pltpu.VMEM((2, 3, SEG, channels), F32),
            pltpu.VMEM((3, blocks, HEADS, channels), F32),
        )
    pl.run_scoped(
        mix_stage,
        pltpu.VMEM((total_rows, width), BF16),
        pltpu.VMEM((3, channels, width), BF16),
        pltpu.VMEM((total_rows, width), BF16),
    )
    a_ctx.start(va_ref[...])
    d_ctx.start(vd_ref[...])
    late.begin()
    early[2].pair()
    for job in early[:2]:
        job.own()

    def with_spectra(spec_ref):
        load_spectra = pltpu.make_async_copy(spec_hbm, spec_ref, local.at[0])
        load_spectra.start()
        down.steps(11, 13)

        def conv_filters(dfilt_ref):
            load_spectra.wait()

            @pl.when(ctx == 0)
            def _():
                for d in range(4):
                    blend_all(dfilt_ref.at[d], [(spec_ref.at[8 + s - d], yown_ref.at[s]) for s in range(d, 4)], True)
                dfilt_ref[4:6] = jnp.zeros((2, 2, SEG, channels), F32)

            @pl.when(ctx > 0)
            def _():
                places = []
                for s in range(blocks):
                    above = lineage(par_ref, ctx * blocks + s)
                    places.append([8 + s] + [jnp.where(a >= 0, a, 12) for a in above])
                for d in range(DEPTH):
                    terms = [(spec_ref.at[places[s][d]], yown_ref.at[s]) for s in range(blocks)]
                    blend_all(dfilt_ref.at[d], terms, True)

            down.steps(13, 14)
            sign = sign_ref[...]
            first_row = lax.broadcasted_iota(jnp.int32, (SEG, 1), 0) == 0
            for j in range(DEPTH):
                fix = None
                if j + 1 < DEPTH:
                    nr, ni = dfilt_ref[j + 1, 0], dfilt_ref[j + 1, 1]
                    fix = jnp.sum(sign * ni, axis=0, keepdims=True)
                    dfilt_ref[j, 0] = dfilt_ref[j, 0] + sign * ni
                    dfilt_ref[j, 1] = dfilt_ref[j, 1] - sign * nr
                taps = unpack_spectrum(th, tl, dfilt_ref.at[j])
                if fix is not None:
                    taps = jnp.where(first_row, taps - fix, taps)
                dtaps_ref[j * SEG : (j + 1) * SEG] = taps

        pl.run_scoped(conv_filters, pltpu.VMEM((DEPTH, 2, SEG, channels), F32))

    pl.run_scoped(with_spectra, pltpu.VMEM((13, 2, SEG, channels), F32))
    down.steps(14, 16)

    def filter_back(net_ref):
        load = pltpu.make_async_copy(net_hbm, net_ref, local.at[1])
        load.start()
        d_raw = dtaps_ref[...] * decay(DEPTH * SEG, channels, tp, width)
        extend_weights(w1_ref, f1_ref, f1b_ref)
        extend_weights(w2_ref, f2_ref, f2b_ref)
        freq = freq_ref[...].reshape(1, -1)
        load.wait()
        units = last_ref.shape[0]
        l_ctx.start(jnp.dot(net_ref[3, 0:units], d_raw, **EXACT_DOT))
        s_two = lax.dot_general(last_ref[...], d_raw, NT, **EXACT_DOT) * net_ref[2, 0:units]
        g_two = lax.dot_general(net_ref[1], s_two, NT, **EXACT_DOT)
        d_one = jnp.dot(w2_ref[...] * freq, s_two, **EXACT_DOT)[0:units]
        g_one = lax.dot_general(ft_ref[...], d_one * net_ref[0, 0:units], NT, **EXACT_DOT)
        g_freq = jnp.sum(w1_ref[...] * g_one, axis=0, keepdims=True) + jnp.sum(
            w2_ref[...] * g_two, axis=0, keepdims=True
        )
        vf_ref[...] = jnp.zeros(vf_ref.shape, F32)
        vf_ref[0 : g_one.shape[0], 0:units] = g_one * freq
        vf_ref[0 : g_two.shape[0], units : 2 * units] = g_two * freq
        vf_ref[g_two.shape[0] : g_two.shape[0] + 1, 0:units] = g_freq
        f_ctx.start(vf_ref[...])

    pl.run_scoped(filter_back, pltpu.VMEM(net_hbm.shape, F32))

    def first_cross():
        for job in early[:2]:
            job.cross()

    def second_own():
        early[2].own()
        late.pair()

    def second_cross():
        early[2].cross()
        late.own()

    def vectors():
        a_dp.start(a_ctx.total())
        d_dp.start(d_ctx.total())

    def networks():
        l_dp.start(l_ctx.total())
        f_dp.start(f_ctx.total())

    def gains():
        va_ref[...] = a_dp.total()
        sums = d_dp.total()
        vd_ref[...] = sums
        d_tp.start(sums[4:6])

    def last_layer():
        for job in early[:2]:
            job.whole()
        f_tp.start(f_dp.total())
        last_sum = l_dp.total()
        for o in range(owners):
            held = vl_ref.shape[1]
            vl_ref[o] = last_sum[o * held : (o + 1) * held]

    jobs = (second_own, vectors, networks, first_cross, second_cross, gains, last_layer)
    for k, job in enumerate(jobs):
        down.steps(min(16 + k, 20), min(17 + k, 20))
        proj.steps(2 * k, 2 * k + 2)
        job()
    proj.steps(14, 17)
    late.cross()
    early[2].whole()
    proj.steps(17, proj.pairs + 2 * LAG)
    late.whole()
    for s in range(blocks):
        down.wait_block(s)
        proj.wait_block(s)
    vd_ref[4:6] = d_tp.total()
    vf_ref[...] = f_tp.total()
    for job in (a_ctx, a_dp, d_ctx, d_dp, d_tp, l_ctx, l_dp, f_ctx, f_dp, f_tp):
        job.finish()
    for job in early + [late]:
        job.finish()
    for i in range(1, 4):
        to_ctx(i).wait_send()
    for other in range(2):
        @pl.when(other < ctx)
        def _():
            for h in range(2 * blocks):
                long_to(h, other).wait_send()

    down.drain()
    proj.drain()


def final_kernel(
    resid_ref, dsum_ref, dres_ref, psum_ref, x_ref, gain_ref, bias_ref, va_ref, vd_ref, vl_ref, vf_ref,
    oup_ref, odown_ref, oout_ref, oin_ref,
    result_ref, gradx_ref, up_ref, down_ref, out_ref, in_ref,
    mgain_ref, mshift_ref, inb_ref, sw_ref, sb_ref, f1_ref, f1b_ref, f2_ref, f2b_ref, freq_ref, last_ref,
    skip_ref, ob_ref, fgain_ref, fshift_ref, ub_ref, db_ref,
):
    step = pl.program_id(0)

    @pl.when(step == 0)
    def _():
        up_ref[...] = oup_ref[...]
        down_ref[...] = odown_ref[...]
        out_ref[...] = oout_ref[...]
        rows = oin_ref.shape[2]
        for h in range(2):
            in_ref[:, h * rows : (h + 1) * rows] = oin_ref[h]
        mgain_ref[...] = vd_ref[4]
        mshift_ref[...] = vd_ref[5]
        db_ref[...] = vd_ref[0]
        ob_ref[...] = vd_ref[1]
        fgain_ref[...] = vd_ref[2]
        fshift_ref[...] = vd_ref[3]
        ub_ref[...] = vd_ref[6]
        for g in range(3):
            sw_ref[g] = va_ref[3 * g : 3 * g + 3]
        inb_ref[...] = va_ref[9:12]
        sb_ref[...] = va_ref[12:15]
        skip_ref[...] = va_ref[15]
        units = f1_ref.shape[1]
        rows_one, rows_two = f1_ref.shape[0], f2_ref.shape[0]
        f1_ref[...] = vf_ref[0:rows_one, 0:units]
        f1b_ref[...] = vf_ref[rows_one, 0:units]
        f2_ref[...] = vf_ref[0:rows_two, units : 2 * units]
        f2b_ref[...] = vf_ref[rows_two, units : 2 * units]
        freq_ref[...] = vf_ref[rows_two + 8, 0:units]
        last_ref[...] = vl_ref[lax.axis_index("dp")]

    result_ref[...] = resid_ref[...] + dsum_ref[...].astype(F32) + bias_ref[...].reshape(1, -1)
    xhat, spread = normalize(x_ref[...].astype(F32))
    e = psum_ref[...].astype(F32) * gain_ref[...].reshape(1, -1)
    gradx_ref[...] = dres_ref[...] + spread * (
        e - jnp.mean(e, axis=-1, keepdims=True) - xhat * jnp.mean(e * xhat, axis=-1, keepdims=True)
    )


def body(
    block_in, out_grad, parents, mixer_gain, mixer_shift, in_proj, in_bias, short_weight, short_bias,
    filter_one, filter_one_bias, filter_two, filter_two_bias, filter_freq, filter_out, skip_gain,
    out_proj, out_bias, feed_gain, feed_shift, feed_up, feed_up_bias, feed_down, feed_down_bias,
):
    x = block_in[0]
    g = out_grad[0]
    total_rows, width = x.shape
    channels = skip_gain.shape[0]
    blocks = total_rows // SEG
    hidden = feed_up.shape[1]
    tp_count = lax.axis_size("tp")
    tp_index = lax.axis_index("tp")
    owners = lax.axis_size("dp")
    first = lax.axis_index("ctx") * blocks
    all_blocks = parents.shape[1]

    half = hidden // 2
    share = width // owners
    units, features = filter_one.shape[1], filter_one.shape[0]
    feat_rows, mid_rows = 40, units + 8
    length = DEPTH * SEG
    ft = jnp.asarray(filter_features(length, (features - 1) // 2, feat_rows))
    fh, fl, th, tl, sign = (jnp.asarray(t) for t in spectral_constants(SEG))
    dma = pltpu.SemaphoreType.DMA
    front_out = (
        sds((total_rows, width), BF16),
        sds((3, total_rows, channels), F32),
        sds((3, blocks, HEADS, channels), F32),
        sds((2, total_rows, channels), F32),
        sds((13, 2, SEG, channels), F32),
        sds((DEPTH, 2, SEG, channels), F32),
        sds((4, mid_rows, length), F32),
        sds((3, channels, width), BF16),
        sds((tp_count, owners, channels, share), BF16),
        sds((width, hidden), BF16),
        sds((units, channels), F32),
        sds((total_rows, channels), F32),
        sds((total_rows, channels), F32),
        sds((total_rows, channels), BF16),
        sds((total_rows, channels), BF16),
    )
    low, proj, head, mixed, spec, filt, net, in_all, out_all, up_all, last, gate, conv, gated, carried = call(
        front_kernel,
        front_out,
        [SM] + [VM] * 22,
        [
            pltpu.VMEM((3, channels, width), BF16),
            pltpu.VMEM((total_rows, width), BF16),
            pltpu.VMEM((3, total_rows, channels), F32),
            pltpu.VMEM((3, blocks, HEADS, channels), F32),
            pltpu.VMEM((2, total_rows, channels), F32),
            pltpu.VMEM((13, 2, SEG, channels), F32),
            pltpu.VMEM((DEPTH, 2, SEG, channels), F32),
            pltpu.VMEM((4, mid_rows, length), F32),
            pltpu.VMEM((length, channels), F32),
            pltpu.VMEM((8, SEG, channels), BF16),
            pltpu.VMEM((4, 2 * blocks, width), F32),
            pltpu.VMEM((3, 9, HEADS, channels), F32),
            pltpu.VMEM((3, HEADS + SEG, channels), F32),
            pltpu.VMEM((feat_rows, units), F32),
            pltpu.VMEM((mid_rows, units), F32),
            pltpu.VMEM((2, SEG, channels), F32),
            pltpu.VMEM((owners,) + filter_out.shape, BF16),
            pltpu.VMEM((owners, 3, channels, share), BF16),
            dma((2, owners)), dma((2, owners)), dma((owners,)), dma((owners,)),
            dma((owners, tp_count)), dma((2, tp_count, owners)),
            dma((owners,)), dma((2, owners)),
            dma((tp_count,)), dma((tp_count,)), dma((3, owners, tp_count)),
            dma((4,)), dma((4,)), dma((4, 4)), dma((4, 4)), dma((4,)), dma((12,)),
        ],
        1,
        out_specs=(HB,) * 10 + (VM,) * 5,
    )(
        parents, x, jnp.transpose(in_proj, (1, 2, 0)), filter_out, out_proj, feed_up, ft,
        filter_one, filter_one_bias, filter_two, filter_two_bias, filter_freq, mixer_gain, mixer_shift,
        in_bias, short_weight, short_bias, skip_gain, fh, fl, th, tl, sign,
    )

    piece = share // 2
    feed_big = [
        sds((total_rows, width), F32),
        sds((total_rows, width), BF16),
        sds((total_rows, width), BF16),
        sds((2, owners, piece, hidden), BF16),
        sds((2, owners, half, share), BF16),
    ]
    feed_in = (out_all, x, g, up_all)

    def held(v):
        return pltpu.VMEM(v.shape, v.dtype)

    residual, norm_part, down_part, stage_up, stage_down, small = call(
        feed_kernel,
        feed_big + [sds((8, width), F32)],
        [VM] * 6 + [HB] * 4,
        [held(v) for v in feed_in]
        + [held(v) for v in feed_big]
        + [dma((4,)), dma((2,)), dma((3, blocks)), pltpu.VMEM((owners, hidden, share), BF16)]
        + [dma((2, owners)), dma((2, owners))]
        + [
            pltpu.VMEM((width, hidden), F32),
            pltpu.VMEM((hidden, width), F32),
            pltpu.VMEM((tp_count, total_rows, channels), BF16),
            pltpu.VMEM((tp_count, channels, width), BF16),
            pltpu.VMEM((hidden, width), BF16),
            dma((tp_count, blocks)), dma((tp_count, blocks)),
        ],
        2,
        out_specs=(HB,) * 5 + (VM,),
    )(gated, out_bias, feed_gain, feed_shift, feed_up_bias, feed_down, *feed_in)

    shapes = [(piece, hidden), (half, share), (channels // 2, share), (3, channels // 2, share)]
    scratch = [
        pltpu.VMEM((all_blocks, SEG, channels), BF16),
        pltpu.VMEM((total_rows, channels), F32),
        pltpu.VMEM((total_rows, channels), F32),
        pltpu.VMEM((2, owners) + shapes[2], BF16),
        dma((4, 2 * blocks)), dma((4, 2 * blocks)),
        pltpu.VMEM((blocks, 2, SEG, channels), F32),
        pltpu.VMEM((total_rows, channels), F32),
        pltpu.VMEM((length, channels), F32),
        pltpu.VMEM((2, owners) + shapes[3], BF16),
        pltpu.VMEM((total_rows, width), BF16),
        pltpu.VMEM((feat_rows, units), F32),
        pltpu.VMEM((mid_rows, units), F32),
        held(mixed),
        pltpu.VMEM((all_blocks, HEADS, channels), F32),
        dma((4,)), dma((4,)), dma((12,)),
    ]
    scratch += LineSum.scratch(total_rows, width) * 2
    for shape in shapes:
        scratch += OwnerSum.scratch(owners, shape)
    smalls = ((16, channels), (8, width), (units, channels), (mid_rows + 8, 2 * units))
    for counts, shape in (
        ((4, owners), smalls[0]), ((4, owners), smalls[1]), ((tp_count,), (2, width)), ((4, owners), smalls[2]),
        ((4, owners, tp_count), smalls[3]),
    ):
        for count in counts:
            scratch += SmallSum.scratch(count, shape)
    d_res, down_sum, proj_sum, own_up, own_down, own_out, own_in, va, vd, vl, vf = call(
        back_kernel,
        (
            sds((total_rows, width), F32),
            sds((total_rows, width), BF16),
            sds((total_rows, width), BF16),
        )
        + tuple(sds((2,) + shape, F32) for shape in shapes)
        + (
            sds(smalls[0], F32),
            sds(smalls[1], F32),
            sds((owners,) + filter_out.shape, F32),
            sds(smalls[3], F32),
        ),
        [SM] + [VM] * 18 + [HB] * 18,
        scratch,
        3,
        out_specs=(HB, VM, VM, HB, HB, HB, HB, VM, VM, VM, VM),
    )(
        parents, gated, down_part, feed_gain, fh, fl, th, tl, sign, short_weight,
        skip_gain, ft, filter_one, filter_one_bias, filter_two, filter_two_bias, filter_freq, last, small,
        norm_part, residual, g, gate, conv, carried, out_all, mixed, low, in_all, x, proj, head, spec, filt, net, stage_up, stage_down,
    )

    def by_block(*shape):
        return pl.BlockSpec((SEG,) + shape, lambda i: (i,) + (0,) * len(shape))

    def whole(v):
        return pl.BlockSpec(v.shape, lambda i: (0,) * len(v.shape))

    wide = by_block(width)
    vectors = [
        sds(v.shape, F32)
        for v in (
            mixer_gain, mixer_shift, in_bias, short_weight, short_bias, filter_one, filter_one_bias, filter_two,
            filter_two_bias, filter_freq, filter_out, skip_gain, out_bias, feed_gain, feed_shift, feed_up_bias,
            feed_down_bias,
        )
    ]
    out = pl.pallas_call(
        final_kernel,
        grid=(blocks,),
        out_shape=[
            sds((total_rows, width), F32), sds((total_rows, width), F32), own_up, own_down, own_out,
            sds((3, channels, share), F32),
        ]
        + vectors,
        in_specs=[wide] * 5 + [whole(v) for v in (mixer_gain, feed_down_bias, va, vd, vl, vf, own_up, own_down, own_out, own_in)],
        out_specs=[wide, wide]
        + [whole(v) for v in (own_up, own_down, own_out, sds((3, channels, share), F32))]
        + [whole(v) for v in vectors],
        compiler_params=pltpu.CompilerParams(vmem_limit_bytes=LIMIT),
    )(
        residual, down_sum, d_res, proj_sum, x, mixer_gain, feed_down_bias, va, vd, vl, vf,
        own_up, own_down, own_out, own_in,
    )
    (result, grad_x, g_up, g_down, g_out, g_in, g_mgain, g_mshift, g_inb, g_sw, g_sb, g_f1, g_f1b, g_f2, g_f2b,
     g_freq, g_last, g_skip, g_ob, g_fgain, g_fshift, g_ub, g_db) = out
    return (
        result[None], grad_x[None], g_mgain, g_mshift, jnp.transpose(g_in, (2, 0, 1)), g_inb, g_sw, g_sb,
        g_f1, g_f1b, g_f2, g_f2b, g_freq, g_last, g_skip, g_out.reshape(channels, share), g_ob, g_fgain, g_fshift,
        g_up.reshape(share, hidden), g_ub, g_down.reshape(hidden, share), g_db,
    )


def solution(mesh):
    in_specs = (
        P("dp", "ctx", None), P("dp", "ctx", None), P("dp", None), P(), P(), P("dp", None, "tp"), P(None, "tp"),
        P(None, None, "tp"), P(None, "tp"), P(), P(), P(), P(), P(), P("dp", "tp"), P("tp"), P("tp", "dp"), P(),
        P(), P(), P("dp", "tp"), P("tp"), P("tp", "dp"), P(),
    )
    out_specs = (
        P("dp", "ctx", None), P("dp", "ctx", None), P(), P(), P("dp", None, "tp"), P(None, "tp"),
        P(None, None, "tp"), P(None, "tp"), P(), P(), P(), P(), P(), P("dp", "tp"), P("tp"), P("tp", "dp"), P(),
        P(), P(), P("dp", "tp"), P("tp"), P("tp", "dp"), P(),
    )
    return jax.shard_map(body, mesh=mesh, in_specs=in_specs, out_specs=out_specs, check_vma=False)
```

```python
import functools
import math

import jax
import jax.numpy as jnp
import numpy as np
from jax import lax
from jax.experimental import pallas as pl
from jax.experimental.pallas import tpu as pltpu
from jax.sharding import PartitionSpec as P

SEG = 256
DEPTH = 6
HEADS = 8
EXACT = lax.Precision.HIGHEST
EPSILON = 1e-05
SLOW_RATE = -math.log(0.01) / 1.5
FAST_RATE = -math.log(0.01) / 0.3
SHIFT_FLOOR = 0.05
F32 = jnp.float32
BF16 = jnp.bfloat16
MESH = pl.DeviceIdType.MESH
VM = pl.BlockSpec(memory_space=pltpu.VMEM)
SM = pl.BlockSpec(memory_space=pltpu.SMEM)
LIMIT = 62 << 20


def sds(shape, dtype):
    return jax.ShapeDtypeStruct(shape, dtype)


HB = pl.BlockSpec(memory_space=pl.ANY)


def call(kernel, out_shape, in_specs, scratch=(), collective=None, flops=0, traffic=0, out_specs=None):
    many = isinstance(out_shape, (tuple, list))
    return pl.pallas_call(
        kernel,
        out_shape=out_shape,
        in_specs=in_specs,
        out_specs=out_specs or (tuple(VM for _ in out_shape) if many else VM),
        scratch_shapes=list(scratch),
        compiler_params=pltpu.CompilerParams(
            vmem_limit_bytes=LIMIT,
            collective_id=collective,
            has_side_effects=collective is not None,
        ),
        cost_estimate=pl.CostEstimate(flops=flops, bytes_accessed=traffic, transcendentals=0),
    )


def spectral_constants(block_len):
    freq = np.arange(block_len)[:, None]
    place = np.arange(block_len)[None, :]
    angle = ((2 * freq + 1) * place % (4 * block_len)) * (2.0 * math.pi / (4 * block_len))
    table = np.concatenate([np.cos(angle), -np.sin(angle)], axis=0).astype(np.float32)
    high = table.astype(jnp.bfloat16)
    low = (table - high.astype(np.float32)).astype(jnp.bfloat16)
    sign = np.where(np.arange(block_len) % 2 == 0, 1.0, -1.0).astype(np.float32)[:, None]
    return high, low, np.ascontiguousarray(high.T), np.ascontiguousarray(low.T), sign


def normalize(values):
    mean_value = jnp.mean(values, axis=-1, keepdims=True)
    centered = values - mean_value
    variance = jnp.mean(centered * centered, axis=-1, keepdims=True)
    scale = lax.rsqrt(variance + EPSILON)
    return centered * scale, scale


def split(values):
    high = values.astype(BF16)
    return high, (values - high.astype(F32)).astype(BF16)


def mm(lhs, rhs):
    return jnp.dot(lhs, rhs, preferred_element_type=F32)


def mm_nt(lhs, rhs):
    return lax.dot_general(lhs, rhs, (((1,), (1,)), ((), ())), preferred_element_type=F32)


def mm_tn(lhs, rhs):
    return lax.dot_general(lhs, rhs, (((0,), (0,)), ((), ())), preferred_element_type=F32)


def mm_split(high, low, values):
    v_high, v_low = split(values)
    return mm(high, v_high) + (mm(low, v_high) + mm(high, v_low))


FT = 32


def lineage(par_ref, block):
    out = []
    current = block
    for _ in range(DEPTH - 1):
        parent = par_ref[0, jnp.maximum(current, 0)]
        current = jnp.where(current >= 0, parent, -1)
        out.append(current)
    return out


def blend_all(dst, terms, conj):
    def tile(t, unused):
        rows = pl.ds(pl.multiple_of(t * FT, FT), FT)
        re = im = None
        for a, b in terms:
            ar, ai = a[0, rows], a[1, rows]
            br, bi = b[0, rows], b[1, rows]
            if conj:
                pr, pi = ar * br + ai * bi, ar * bi - ai * br
            else:
                pr, pi = ar * br - ai * bi, ar * bi + ai * br
            re, im = (pr, pi) if re is None else (re + pr, im + pi)
        dst[0, rows] = re
        dst[1, rows] = im
        return unused

    lax.fori_loop(0, SEG // FT, tile, 0)


def unpack_spectrum(th, tl, ref):
    high_re, low_re = split(ref[0])
    high_im, low_im = split(ref[1])
    a, b = slice(0, SEG), slice(SEG, 2 * SEG)
    return (
        mm(th[:, a], high_re) + mm(th[:, b], high_im)
        + (mm(tl[:, a], high_re) + mm(tl[:, b], high_im))
        + (mm(th[:, a], low_re) + mm(th[:, b], low_im))
    )


def filter_features(length, bands, rows):
    positions = np.arange(length)
    time_pos = positions / (length - 1)
    freq = np.linspace(0.0001, bands - 1, bands)
    phases = (2.0 * math.pi / length * positions)[None, :] * freq[:, None]
    table = np.zeros((rows, length), np.float32)
    table[0] = time_pos
    table[1 : bands + 1] = np.cos(phases)
    table[bands + 1 : 2 * bands + 1] = -np.sin(phases)
    table[2 * bands + 1] = 1.0
    return table


def spot(**changes):
    base = {name: lax.axis_index(name) for name in ("dp", "ctx", "tp")}
    base.update(changes)
    return (base["dp"], base["ctx"], base["tp"])


def remote(src, dst, send, recv, where):
    return pltpu.make_async_remote_copy(
        src_ref=src, dst_ref=dst, send_sem=send, recv_sem=recv, device_id=where, device_id_type=MESH
    )


def greet(partners):
    barrier = pltpu.get_barrier_semaphore()
    for where in partners:
        pl.semaphore_signal(barrier, inc=1, device_id=where, device_id_type=MESH)
    pl.semaphore_wait(barrier, len(partners))


CHUNK = 32
HALF = SEG // 2
PER = SEG // (2 * CHUNK)
LAG = 2


def chunk(c):
    return pl.ds(pl.multiple_of(c * CHUNK, CHUNK), CHUNK)


class LineRole:
    def __init__(self):
        tp = lax.axis_index("tp")
        self.inner = jnp.logical_and(tp > 0, tp < 3)
        self.outer = jnp.logical_not(self.inner)
        self.side = jnp.where(tp < 2, 0, 1)
        near = jnp.where(self.side == 0, 0, 3)
        far = jnp.where(self.side == 0, 1, 2)
        self.mate = spot(tp=jnp.where(self.inner, near, far))
        self.cross = spot(tp=3 - tp)


class LineSum(LineRole):
    scratch_count = 11

    @staticmethod
    def scratch(rows, width):
        count = rows // CHUNK
        return [
            pltpu.VMEM((rows, width), BF16),
            pltpu.VMEM((rows // 2, width), BF16),
            pltpu.VMEM((rows // 2, width), BF16),
        ] + [pltpu.SemaphoreType.DMA((count,)) for _ in range(8)]

    def __init__(self, part, total, scratch):
        super().__init__()
        self.part, self.total = part, total
        self.end, self.mid, self.out = scratch[:3]
        self.sems = scratch[3:]
        self.pairs = part.shape[0] // (2 * CHUNK)

    def to_mid(self, c):
        return remote(self.part.at[chunk(c)], self.end.at[chunk(c)], self.sems[0].at[c], self.sems[1].at[c], self.mate)

    def to_cross(self, k):
        return remote(self.out.at[chunk(k)], self.mid.at[chunk(k)], self.sems[2].at[k], self.sems[3].at[k], self.cross)

    def final_end(self, c):
        at = self.total.at[chunk(c)]
        return remote(at, at, self.sems[4].at[c], self.sems[5].at[c], self.mate)

    def final_cross(self, c):
        at = self.total.at[chunk(c)]
        return remote(at, at, self.sems[6].at[c], self.sems[7].at[c], self.cross)

    def send_block(self, s):
        @pl.when(self.outer)
        def _():
            def one(i, unused):
                self.to_mid(s * 2 * PER + i).start()
                return unused

            lax.fori_loop(0, 2 * PER, one, 0)

    def step(self, k):
        pairs, side = self.pairs, self.side

        @pl.when(k < pairs)
        def _():
            other = 2 * k + 1 - side
            self.to_mid(2 * k).wait_recv()
            self.to_mid(2 * k + 1).wait_recv()
            self.out[chunk(k)] = (
                self.part[chunk(other)].astype(F32) + self.end[chunk(other)].astype(F32)
            ).astype(BF16)
            self.to_cross(k).start()

        j = k - LAG

        @pl.when(jnp.logical_and(j >= 0, j < pairs))
        def _():
            mine = 2 * j + side
            self.to_cross(j).wait_recv()
            self.total[chunk(mine)] = (
                self.part[chunk(mine)].astype(F32)
                + self.end[chunk(mine)].astype(F32)
                + self.mid[chunk(j)].astype(F32)
            ).astype(BF16)
            self.final_cross(mine).start()
            self.final_end(mine).start()

        i = k - 2 * LAG

        @pl.when(jnp.logical_and(i >= 0, i < pairs))
        def _():
            other = 2 * i + 1 - side
            self.final_cross(other).wait_recv()
            self.final_end(other).start()

    def steps(self, first, last):
        @pl.when(self.inner)
        def _():
            def one(k, unused):
                self.step(k)
                return unused

            lax.fori_loop(first, last, one, 0)

    def wait_block(self, s):
        @pl.when(self.outer)
        def _():
            def one(i, unused):
                self.final_end(s * 2 * PER + i).wait_recv()
                return unused

            lax.fori_loop(0, 2 * PER, one, 0)

    def wait_half(self, h):
        @pl.when(self.outer)
        def _():
            def one(i, unused):
                self.final_end(h * PER + i).wait_recv()
                return unused

            lax.fori_loop(0, PER, one, 0)

    def drain(self):
        @pl.when(self.outer)
        def _():
            def one(c, unused):
                self.to_mid(c).wait_send()
                return unused

            lax.fori_loop(0, 2 * self.pairs, one, 0)

        @pl.when(self.inner)
        def _():
            def one(k, unused):
                mine, other = 2 * k + self.side, 2 * k + 1 - self.side
                self.to_cross(k).wait_send()
                self.final_cross(mine).wait_send()
                self.final_end(mine).wait_send()
                self.final_end(other).wait_send()
                return unused

            lax.fori_loop(0, self.pairs, one, 0)


def signal_all(partners):
    barrier = pltpu.get_barrier_semaphore()
    for where in partners:
        pl.semaphore_signal(barrier, inc=1, device_id=where, device_id_type=MESH)
    return barrier, len(partners)


def store_columns(stage, half, value):
    owners, share = stage.shape[1], stage.shape[-1]
    for o in range(owners):
        stage[half, o] = value[:, o * share : (o + 1) * share].astype(BF16)


def store_rows(stage, first, value):
    size = stage.shape[2]
    for q in range(value.shape[0] // size):
        owner, half = divmod(first // size + q, 2)
        stage[half, owner] = value[q * size : (q + 1) * size].astype(BF16)


def feed_kernel(
    gated_ref, ob_ref, gain_ref, shift_ref, ub_ref, own_down,
    out_hbm, x_hbm, g_hbm, up_hbm,
    resid_hbm, npart_hbm, dpart_hbm, gup_hbm, gdown_hbm, small_ref,
    out_in, x_ref, g_ref, up_ref,
    resid_ref, npart_ref, dpart_ref, gup_ref, gdown_ref, s_load, s_save, s_block, down_in, s_down, r_down,
    up_acc, down_acc, gall_ref, out_ref, down_ref, s_gate, r_gate,
):
    groups, owners = out_in.shape[:2]
    width = x_ref.shape[1]
    blocks = x_ref.shape[0] // SEG
    share = width // owners
    tp, ctx, dp = lax.axis_index("tp"), lax.axis_index("ctx"), lax.axis_index("dp")
    chain = LineRole()
    barrier, count = signal_all(
        [spot(tp=lax.rem(tp + i, groups)) for i in range(1, groups)]
        + [spot(ctx=lax.rem(ctx + i, 4)) for i in range(1, 4)]
        + [spot(dp=lax.rem(dp + i, owners)) for i in range(1, owners)]
    )

    low_half = lax.rem(ctx, 2)
    pair_mate = spot(ctx=ctx + 1 - 2 * low_half)

    def owner(i):
        return lax.rem(dp + i, owners)

    def half_of(ref, half):
        size = ref.shape[0] // 2
        return ref.at[pl.ds(pl.multiple_of(half * size, 16), size)]

    def send_down(i):
        return remote(
            half_of(own_down, low_half), half_of(down_in.at[dp], low_half), s_down.at[0, i], r_down.at[0, dp],
            spot(dp=owner(i)),
        )

    def swap_down(i):
        at = half_of(down_in.at[owner(i)], low_half)
        return remote(at, at, s_down.at[1, i], r_down.at[1, owner(i)], pair_mate)

    def got_down(stage, i, half):
        at = half_of(down_in.at[owner(i)], half)
        return remote(at, at, s_down.at[0, i], r_down.at[stage, owner(i)], pair_mate)

    far = jnp.where(tp < 2, tp + 2, tp - 2)
    beyond = jnp.where(chain.side == 0, 3, 0)
    other = jnp.where(chain.inner, 3 - tp, far)
    near = jnp.where(chain.inner, jnp.where(chain.side == 0, 0, 3), jnp.where(chain.side == 0, 1, 2))

    def gate_copy(s, i):
        rows = pl.ds(pl.multiple_of(s * SEG, SEG), SEG)
        where = chain.mate if i == 0 else spot(tp=other)
        return remote(gated_ref.at[rows], gall_ref.at[tp, rows], s_gate.at[i, s], r_gate.at[tp, s], where)

    def gate_pass(s, i, source):
        at = gall_ref.at[source, pl.ds(pl.multiple_of(s * SEG, SEG), SEG)]
        return remote(at, at, s_gate.at[2 + i, s], r_gate.at[source, s], chain.mate)

    def gate_from(s, source):
        at = gall_ref.at[source, pl.ds(pl.multiple_of(s * SEG, SEG), SEG)]
        return remote(at, at, s_gate.at[0, s], r_gate.at[source, s], chain.mate)

    loads = [
        pltpu.make_async_copy(src, dst, s_load.at[k])
        for k, (src, dst) in enumerate(
            (
                (out_hbm, out_in), (x_hbm, x_ref), (up_hbm, up_ref), (g_hbm, g_ref),
            )
        )
    ]
    for load in loads:
        load.start()

    def save(k, src, dst, s):
        rows = pl.ds(pl.multiple_of(s * SEG, SEG), SEG)
        return pltpu.make_async_copy(src.at[rows], dst.at[rows], s_block.at[k, s])

    blockwise = ((resid_ref, resid_hbm), (npart_ref, npart_hbm), (dpart_ref, dpart_hbm))
    saves = [
        pltpu.make_async_copy(src, dst, s_save.at[k])
        for k, (src, dst) in enumerate(((gup_ref, gup_hbm), (gdown_ref, gdown_hbm)))
    ]
    gall_ref[tp] = gated_ref[...]
    pl.semaphore_wait(barrier, count)
    for s in range(blocks):
        for i in range(2):
            gate_copy(s, 1 - i).start()
    for i in range(1, owners):
        send_down(i).start()
    down_in[dp] = own_down[...]
    for load in loads:
        load.wait()
    for o in range(owners):
        columns = slice(o * share, (o + 1) * share)
        for z in range(groups):
            out_ref[z, :, columns] = out_in[z, o]
    ob, gain, shift = (ref[...].reshape(1, -1) for ref in (ob_ref, gain_ref, shift_ref))
    ub = ub_ref[...].reshape(1, -1)
    for ref in (small_ref, up_acc, down_acc):
        ref[...] = jnp.zeros(ref.shape, F32)

    def core(s, unused):
        rows = pl.ds(pl.multiple_of(s * SEG, SEG), SEG)

        @pl.when(chain.inner)
        def _():
            for i, source in enumerate((3 - tp, beyond)):
                gate_from(s, source).wait_recv()
                gate_pass(s, i, source).start()
            gate_from(s, near).wait_recv()

        @pl.when(chain.outer)
        def _():
            gate_from(s, near).wait_recv()
            gate_from(s, 3 - near).wait_recv()
            gate_from(s, 3 - tp).wait_recv()

        mixed = mm(gall_ref[0, rows], out_ref[0])
        for z in range(1, groups):
            mixed = mixed + mm(gall_ref[z, rows], out_ref[z])
        residual = x_ref[rows].astype(F32) + mixed + ob
        resid_ref[rows] = residual
        save(0, *blockwise[0], s).start()
        low = (normalize(residual)[0] * gain + shift).astype(BF16)
        pre = mm(low, up_ref[...]) + ub
        cdf = 0.5 * (1.0 + lax.erf(pre * math.sqrt(0.5)))
        hidden = (pre * cdf).astype(BF16)
        slope = cdf + pre * (jnp.exp(-0.5 * pre * pre) * (1.0 / math.sqrt(2.0 * math.pi)))

        @pl.when(s == 0)
        def _():
            for i in range(1, owners):
                got_down(0, i, low_half).wait_recv()
                swap_down(i).start()
            for i in range(1, owners):
                got_down(1, i, 1 - low_half).wait_recv()
            for o in range(owners):
                down_ref[:, o * share : (o + 1) * share] = down_in[o]

        grad = g_ref[rows]
        d_pre = (mm_nt(grad, down_ref[...]) * slope).astype(BF16)
        npart_ref[rows] = mm_nt(d_pre, up_ref[...]).astype(BF16)
        dpart_ref[rows] = mm(hidden, down_ref[...]).astype(BF16)
        for k in (1, 2):
            save(k, *blockwise[k], s).start()
        up_acc[...] += mm_tn(low, d_pre)
        down_acc[...] += mm_tn(hidden, grad)
        small_ref[0:1] += jnp.sum(grad.astype(F32), axis=0, keepdims=True)
        small_ref[6:7] += jnp.sum(d_pre.astype(F32), axis=0, keepdims=True)
        return unused

    lax.fori_loop(0, blocks, core, 0)
    for t in range(2):
        part = slice(t * width // 2, (t + 1) * width // 2)
        store_rows(gup_ref, t * width // 2, up_acc[part])
        units = down_acc.shape[0] // 2
        store_columns(gdown_ref, t, down_acc[t * units : (t + 1) * units])
    for job in saves:
        job.start()
    for i in range(1, owners):
        send_down(i).wait_send()
        swap_down(i).wait_send()
    for s in range(blocks):
        for i in range(2):
            gate_copy(s, i).wait_send()

    @pl.when(chain.inner)
    def _():
        for s in range(blocks):
            for i, source in enumerate((3 - tp, beyond)):
                gate_pass(s, i, source).wait_send()

    for job in saves:
        job.wait()
    for s in range(blocks):
        for k in range(3):
            save(k, *blockwise[k], s).wait()


def sine_cosine(angle):
    turns = jnp.floor(angle * (2.0 / math.pi) + 0.5)
    rest = ((angle - turns * 1.5703125) - turns * 4.837512969970703125e-4) - turns * 7.54978995489188216e-8
    square = rest * rest
    sine = ((-1.9515295891e-4 * square + 8.3321608736e-3) * square - 1.6666654611e-1) * square * rest + rest
    cosine = ((2.443315711809948e-5 * square - 1.388731625493765e-3) * square + 4.166664568298827e-2) * (
        square * square
    ) + (1.0 - 0.5 * square)
    quarter = turns - 4.0 * jnp.floor(turns * 0.25)
    odd = jnp.logical_or(quarter == 1.0, quarter == 3.0)
    middle = jnp.logical_or(quarter == 1.0, quarter == 2.0)
    sine, cosine = jnp.where(odd, cosine, sine), jnp.where(odd, sine, cosine)
    return jnp.where(quarter >= 2.0, -sine, sine), jnp.where(middle, -cosine, cosine)


def extend_weights(ref, weight, bias):
    rows = weight.shape[0]
    ref[...] = jnp.zeros(ref.shape, F32)
    ref[0:rows] = weight[...]
    ref[rows : rows + 1] = bias[...].reshape(1, -1)


def decay(length, channels, tp, width):
    time_pos = lax.broadcasted_iota(jnp.int32, (length, 1), 0).astype(F32) * (1.0 / (length - 1))
    channel = (lax.broadcasted_iota(jnp.int32, (1, channels), 1) + tp * channels).astype(F32)
    rate = SLOW_RATE + (FAST_RATE - SLOW_RATE) * channel * (1.0 / (width - 1))
    return jnp.exp(-time_pos * rate) + SHIFT_FLOOR


EXACT_DOT = dict(precision=EXACT, preferred_element_type=F32)
TN = (((0,), (0,)), ((), ()))
NT = (((1,), (1,)), ((), ()))


def front_kernel(
    par_ref, x_ref, win_ref, last_ref, out_in, up_in, ft_ref, f1_ref, f1b_ref, f2_ref, f2b_ref, freq_ref,
    gain_ref, shift_ref, ib_ref, sw_ref, sb_ref, skip_ref, fh_ref, fl_ref, th_ref, tl_ref, sign_ref,
    low_hbm, proj_hbm, head_hbm, mixed_hbm, spec_hbm, filt_hbm, net_hbm, in_hbm, out_hbm, up_hbm,
    lasts_ref, gate_ref, conv_ref, gated_ref, carried_ref,
    w_ref, low_ref, proj_ref, head_ref, mixed_ref, spec_ref, filt_ref, net_ref, taps_ref, shared_ref,
    xt_ref, tail_ref, ext_ref, w1_ref, w2_ref, acc_ref, lastb_ref, wb_ref,
    s_in, r_in, s_last, r_last, s_out, r_out, s_up, r_up, s_line, r_line, s_swap,
    s_xt, r_xt, s_car, r_car, s_fwd, local,
):
    total_rows, width = x_ref.shape
    channels = ib_ref.shape[1]
    blocks = total_rows // SEG
    tp, ctx, dp = lax.axis_index("tp"), lax.axis_index("ctx"), lax.axis_index("dp")
    owners, lines = out_hbm.shape[1], out_hbm.shape[0]
    share = win_ref.shape[2]
    last_share = last_ref.shape[0]
    up_share = up_in.shape[0]

    def cell(i):
        flat = lax.rem(tp * owners + dp + i, owners * lines)
        return flat // owners, lax.rem(flat, owners)

    def owner(i):
        return lax.rem(dp + i, owners)

    def ctx_at(i):
        return lax.rem(ctx + i, 4)

    partners = [spot(ctx=ctx_at(i)) for i in range(1, 4)]
    for i in range(1, owners * lines):
        line, own = cell(i)
        partners.append(spot(tp=line, dp=own))
    barrier, count = signal_all(partners)

    def rows_of(ref, who, size):
        return ref.at[pl.ds(pl.multiple_of(who * size, size), size)]

    low_half = lax.rem(ctx, 2)
    mate = spot(ctx=ctx + 1 - 2 * low_half)

    def in_half(ref, half):
        size = channels // 2
        return ref.at[:, pl.ds(pl.multiple_of(half * size, 16), size)]

    def send_in(i):
        return remote(
            in_half(win_ref, low_half), in_half(wb_ref.at[dp], low_half), s_in.at[0, i], r_in.at[0, dp],
            spot(dp=owner(i)),
        )

    def swap_in(i):
        at = in_half(wb_ref.at[owner(i)], low_half)
        return remote(at, at, s_in.at[1, i], r_in.at[1, owner(i)], mate)

    def got_in(stage, i, half):
        at = in_half(wb_ref.at[owner(i)], half)
        return remote(at, at, s_in.at[0, i], r_in.at[stage, owner(i)], mate)

    def send_last(i):
        return remote(last_ref, lastb_ref.at[dp], s_last.at[i], r_last.at[dp], spot(dp=owner(i)))

    def send_xt(i):
        at = xt_ref.at[ctx]
        return remote(at, at, s_xt.at[i], r_xt.at[ctx], spot(ctx=ctx_at(i)))

    for s in range(blocks):
        tail = x_ref[s * SEG + SEG - 16 : s * SEG + SEG].astype(F32)
        xt_ref[ctx, 2 * s : 2 * s + 2] = tail[14:16]
    pl.semaphore_wait(barrier, count)
    for i in range(1, owners):
        send_in(i).start()
        send_last(i).start()
    for i in range(1, 4):
        send_xt(i).start()
    wb_ref[dp] = win_ref[...]
    lastb_ref[dp] = last_ref[...]

    gain, shift = gain_ref[...].reshape(1, -1), shift_ref[...].reshape(1, -1)

    def norm(s, unused):
        rows = pl.ds(pl.multiple_of(s * SEG, SEG), SEG)
        low_ref[rows] = (normalize(x_ref[rows].astype(F32))[0] * gain + shift).astype(BF16)
        return unused

    lax.fori_loop(0, blocks, norm, 0)
    saves = [pltpu.make_async_copy(low_ref, low_hbm, local.at[1])]
    saves[-1].start()

    units = f1_ref.shape[1]
    length = ft_ref.shape[1]
    extend_weights(w1_ref, f1_ref, f1b_ref)
    extend_weights(w2_ref, f2_ref, f2b_ref)
    freq = freq_ref[...].reshape(1, -1)
    net_ref[...] = jnp.zeros(net_ref.shape, F32)
    angle = lax.dot_general(w1_ref[...] * freq, ft_ref[...], TN, **EXACT_DOT)
    first, net_ref[0, 0:units] = sine_cosine(angle)
    net_ref[1, 0:units] = first
    pad = net_ref.shape[1] - units
    net_ref[1, units:] = jnp.where(lax.broadcasted_iota(jnp.int32, (pad, length), 0) == 0, 1.0, 0.0)
    angle = lax.dot_general(w2_ref[...] * freq, net_ref[1], TN, **EXACT_DOT)
    second, net_ref[2, 0:units] = sine_cosine(angle)
    net_ref[3, 0:units] = second
    saves.append(pltpu.make_async_copy(net_ref, net_hbm, local.at[2]))
    saves[-1].start()
    for i in range(1, owners):
        at = lastb_ref.at[owner(i)]
        remote(at, at, s_last.at[i], r_last.at[owner(i)], spot(dp=owner(i))).wait_recv()
    for o in range(owners):
        lasts_ref[o * last_share : (o + 1) * last_share] = lastb_ref[o].astype(F32)
    raw = lax.dot_general(second, lasts_ref[...], TN, **EXACT_DOT)
    taps_ref[...] = raw * decay(length, channels, tp, channels * lines)
    fh, fl, th, tl = fh_ref[...], fl_ref[...], th_ref, tl_ref
    sign = sign_ref[...]
    for j in range(DEPTH):
        part = taps_ref[j * SEG : (j + 1) * SEG]
        out = mm_split(fh, fl, part)
        re, im = out[:SEG], out[SEG:]
        filt_ref[j, 0] = re
        filt_ref[j, 1] = im
    for j in range(DEPTH - 1, 0, -1):
        first = taps_ref[(j - 1) * SEG : (j - 1) * SEG + 1]
        filt_ref[j, 0] = filt_ref[j, 0] - sign * filt_ref[j - 1, 1]
        filt_ref[j, 1] = filt_ref[j, 1] + sign * (filt_ref[j - 1, 0] - first)
    saves.append(pltpu.make_async_copy(filt_ref, filt_hbm, local.at[3]))
    saves[-1].start()

    def half_of(ref, half):
        size = ref.shape[0] // 2
        return ref.at[pl.ds(pl.multiple_of(half * size, 16), size)]

    def up_half(ref, half):
        size = ref.shape[1] // 2
        return ref.at[:, pl.ds(pl.multiple_of(half * size, size), size)]

    def line_out(i):
        return remote(
            out_in, out_hbm.at[tp, dp], s_line.at[i], r_line.at[tp], spot(tp=lax.rem(tp + i, lines))
        )

    def send_out(i, j):
        return remote(
            half_of(out_in, low_half), half_of(out_hbm.at[tp, dp], low_half), s_out.at[i, j], r_out.at[0, tp, dp],
            spot(dp=owner(i), tp=lax.rem(tp + j, lines)),
        )

    def swap_out(i, line):
        at = half_of(out_hbm.at[line, owner(i)], low_half)
        return remote(at, at, s_swap.at[2, i, line], r_out.at[1, line, owner(i)], mate)

    def send_up(i):
        return remote(
            up_half(up_in, low_half), up_half(rows_of(up_hbm, dp, up_share), low_half), s_up.at[i], r_up.at[0, dp],
            spot(dp=owner(i)),
        )

    def swap_up(i):
        at = up_half(rows_of(up_hbm, owner(i), up_share), low_half)
        return remote(at, at, s_swap.at[0, i, 0], r_up.at[1, owner(i)], mate)

    for i in range(1, owners):
        got_in(0, i, low_half).wait_recv()
        swap_in(i).start()
        send_up(i).start()
        for j in range(lines):
            send_out(i, j).start()
    for i in range(1, lines):
        line_out(i).start()
    for i in range(1, owners):
        got_in(1, i, 1 - low_half).wait_recv()
    for o in range(owners):
        w_ref[:, :, o * share : (o + 1) * share] = wb_ref[o]
    saves.append(pltpu.make_async_copy(w_ref, in_hbm, local.at[4]))
    saves[-1].start()

    for k, (src, dst) in enumerate(
        ((out_in, out_hbm.at[tp, dp]), (up_in, rows_of(up_hbm, dp, up_share)))
    ):
        saves.append(pltpu.make_async_copy(src, dst, local.at[5 + k]))
        saves[-1].start()

    for i in range(1, 4):
        at = xt_ref.at[ctx_at(i)]
        remote(at, at, s_xt.at[i], r_xt.at[ctx_at(i)], spot(ctx=ctx_at(i))).wait_recv()
    tail_ref[...] = jnp.zeros(tail_ref.shape, F32)
    for half in range(2):
        tails = (normalize(xt_ref[half])[0] * gain + shift).astype(BF16)
        for g in range(3):
            value = mm_nt(tails, w_ref[g]) + ib_ref[g : g + 1]
            for s in range(4):
                tail_ref[g, 4 * half + s, 6:8] = value[2 * s : 2 * s + 2]

    def share_block(s, other):
        return remote(
            carried_ref.at[pl.ds(pl.multiple_of(s * SEG, SEG), SEG)], shared_ref.at[4 * ctx + s],
            s_car.at[other, s], r_car.at[ctx, s], spot(ctx=other),
        )

    def forward_block(s, group):
        at = shared_ref.at[4 * group + s]
        return remote(at, at, s_fwd.at[s], r_car.at[group, s], spot(ctx=5 - ctx))

    def mix(s, unused):
        rows = pl.ds(pl.multiple_of(s * SEG, SEG), SEG)
        parent = par_ref[0, ctx * blocks + s]
        slot = jnp.where(parent >= 0, parent, 8)
        out = []
        for g in range(3):
            projected = mm_nt(low_ref[rows], w_ref[g]) + ib_ref[g : g + 1]
            proj_ref[g, rows] = projected
            head = tail_ref[g, slot]
            head_ref[g, s] = head
            ext_ref[g, 0:HEADS] = head
            ext_ref[g, HEADS : HEADS + SEG] = projected
            mixed = (
                sw_ref[g, 0:1] * ext_ref[g, HEADS - 2 : HEADS - 2 + SEG]
                + sw_ref[g, 1:2] * ext_ref[g, HEADS - 1 : HEADS - 1 + SEG]
                + sw_ref[g, 2:3] * projected
                + sb_ref[g : g + 1]
            )
            if g == 0:
                gate_ref[rows] = mixed
            else:
                mixed_ref[g - 1, rows] = mixed
            out.append(mixed)
        carried = (out[2] * out[1]).astype(BF16)
        carried_ref[rows] = carried

        @pl.when(ctx == 0)
        def _():
            share_block(s, 2).start()
            share_block(s, 1).start()

        @pl.when(ctx == 1)
        def _():
            share_block(s, 3).start()

        spec = mm(fh_ref[...], carried) + mm(fl_ref[...], carried)
        spec_ref[8 + s, 0] = spec[:SEG]
        spec_ref[8 + s, 1] = spec[SEG:]
        return unused

    lax.fori_loop(0, blocks, mix, 0)
    for k, (src, dst) in enumerate(((proj_ref, proj_hbm), (head_ref, head_hbm), (mixed_ref, mixed_hbm))):
        saves.append(pltpu.make_async_copy(src, dst, local.at[8 + k]))
        saves[-1].start()

    def spectrum(slot, part):
        out = mm(fh_ref[...], part) + mm(fl_ref[...], part)
        spec_ref[slot, 0] = out[:SEG]
        spec_ref[slot, 1] = out[SEG:]

    spec_ref[12] = jnp.zeros(spec_ref.shape[1:], F32)

    def arrived(group, s):
        at = shared_ref.at[4 * group + s]
        return remote(at, at, s_fwd.at[s], r_car.at[group, s], spot(ctx=ctx_at(1)))

    def copy_own(group):
        def one(s, unused):
            spec_ref[4 * group + s] = spec_ref[8 + s]
            return unused

        lax.fori_loop(0, 4, one, 0)

    def receive(group):
        def one(s, unused):
            arrived(group, s).wait_recv()
            spectrum(4 * group + s, shared_ref[4 * group + s])
            return unused

        lax.fori_loop(0, 4, one, 0)

    def receive_forward(group):
        def one(s, unused):
            arrived(group, s).wait_recv()
            forward_block(s, group).start()
            spectrum(4 * group + s, shared_ref[4 * group + s])
            return unused

        lax.fori_loop(0, 4, one, 0)

    @pl.when(ctx == 0)
    def _():
        copy_own(0)

    @pl.when(ctx == 1)
    def _():
        copy_own(1)
        receive(0)

    @pl.when(ctx == 2)
    def _():
        receive_forward(0)
        receive(1)

    @pl.when(ctx == 3)
    def _():
        receive_forward(1)
        receive(0)

    saves.append(pltpu.make_async_copy(spec_ref, spec_hbm, local.at[11]))
    saves[-1].start()

    def dest(s, unused):
        above = lineage(par_ref, ctx * blocks + s)
        places = [8 + s] + [jnp.where(a >= 0, a, 12) for a in above]
        blend_all(acc_ref, [(filt_ref.at[d], spec_ref.at[places[d]]) for d in range(DEPTH)], False)
        long_out = unpack_spectrum(th, tl, acc_ref) * (1.0 / SEG)
        place = pl.ds(pl.multiple_of(s * SEG, SEG), SEG)
        convolved = long_out + skip_ref[...].reshape(1, -1) * carried_ref[place].astype(F32)
        conv_ref[place] = convolved
        gated_ref[place] = (convolved * gate_ref[place]).astype(BF16)
        return unused

    lax.fori_loop(0, blocks, dest, 0)

    def take_halves(stage, half):
        for i in range(1, owners):
            who = owner(i)
            at = up_half(rows_of(up_hbm, who, up_share), half)
            remote(at, at, s_up.at[i], r_up.at[stage, who], mate).wait_recv()
            if stage == 0:
                swap_up(i).start()
            for line in range(lines):
                at = half_of(out_hbm.at[line, who], half)
                remote(at, at, s_out.at[i, line], r_out.at[stage, line, who], mate).wait_recv()
                if stage == 0:
                    swap_out(i, line).start()

    take_halves(0, low_half)

    for save in saves:
        save.wait()
    take_halves(1, 1 - low_half)
    for i in range(1, owners):
        send_in(i).wait_send()
        swap_in(i).wait_send()
        send_last(i).wait_send()
        send_up(i).wait_send()
        swap_up(i).wait_send()
        for j in range(lines):
            send_out(i, j).wait_send()
            swap_out(i, j).wait_send()
    for i in range(1, lines):
        line_out(i).wait_send()
        line = lax.rem(tp + i, lines)
        at = out_hbm.at[line, dp]
        remote(at, at, s_line.at[i], r_line.at[line], mate).wait_recv()
    for i in range(1, 4):
        send_xt(i).wait_send()

    @pl.when(ctx == 0)
    def _():
        for s in range(blocks):
            share_block(s, 2).wait_send()
            share_block(s, 1).wait_send()

    @pl.when(ctx == 1)
    def _():
        for s in range(blocks):
            share_block(s, 3).wait_send()

    @pl.when(ctx == 2)
    def _():
        for s in range(blocks):
            forward_block(s, 0).wait_send()

    @pl.when(ctx == 3)
    def _():
        for s in range(blocks):
            forward_block(s, 1).wait_send()


class OwnerSum:
    scratch_count = 17

    @staticmethod
    def scratch(owners, shape):
        many = max(owners - 1, 1)
        return [
            pltpu.VMEM((owners,) + shape, BF16),
            pltpu.VMEM((owners,) + shape, BF16),
            pltpu.VMEM((many,) + shape, BF16),
            pltpu.VMEM(shape, BF16),
            pltpu.VMEM(shape, BF16),
            pltpu.SemaphoreType.DMA,
            pltpu.SemaphoreType.DMA,
            pltpu.SemaphoreType.DMA,
            pltpu.SemaphoreType.DMA((many,)),
            pltpu.SemaphoreType.DMA((many,)),
            pltpu.SemaphoreType.DMA,
            pltpu.SemaphoreType.DMA,
            pltpu.SemaphoreType.DMA,
            pltpu.SemaphoreType.DMA,
            pltpu.SemaphoreType.DMA((2,)),
            pltpu.VMEM((2,) + shape, F32),
        ]

    def __init__(self, stage, out, scratch):
        self.stage, self.out, self.result = stage, out, scratch[-1]
        self.recv, self.keep, self.parts, self.y_own, self.y_in = scratch[:5]
        self.sems = scratch[5:-1]
        self.owners = stage.shape[1]
        self.dp, ctx = lax.axis_index("dp"), lax.axis_index("ctx")
        self.low = lax.rem(ctx, 2)
        self.mate = spot(ctx=ctx + 1 - 2 * self.low)
        self.across = spot(ctx=lax.rem(ctx + 2, 4))

    def load(self):
        return pltpu.make_async_copy(self.stage.at[self.low], self.keep, self.sems[0])

    def to_mate(self):
        return remote(self.stage.at[1 - self.low], self.recv, self.sems[1], self.sems[2], self.mate)

    def to_owner(self, i):
        owner = lax.rem(self.dp + i, self.owners)
        return remote(
            self.keep.at[owner], self.parts.at[self.owners - 1 - i], self.sems[3].at[i - 1],
            self.sems[4].at[self.owners - 1 - i], spot(dp=owner),
        )

    def from_owner(self, i):
        return remote(self.parts.at[i - 1], self.parts.at[i - 1], self.sems[3].at[i - 1], self.sems[4].at[i - 1], self.mate)

    def to_across(self):
        return remote(self.y_own, self.y_in, self.sems[5], self.sems[6], self.across)

    def to_back(self):
        at = self.result.at[self.low]
        return remote(at, at, self.sems[7], self.sems[8], self.mate)

    def save(self, half):
        return pltpu.make_async_copy(self.result.at[half], self.out.at[half], self.sems[9].at[half])

    def begin(self):
        self.to_mate().start()
        self.load().start()

    def pair(self):
        self.load().wait()
        self.to_mate().wait_recv()
        for o in range(self.owners):
            self.keep[o] = (self.keep[o].astype(F32) + self.recv[o].astype(F32)).astype(BF16)
        for i in range(1, self.owners):
            self.to_owner(i).start()

    def own(self):
        total = self.keep[self.dp].astype(F32)
        for i in range(1, self.owners):
            self.from_owner(i).wait_recv()
            total = total + self.parts[i - 1].astype(F32)
        self.y_own[...] = total.astype(BF16)
        self.to_across().start()

    def cross(self):
        self.to_across().wait_recv()
        self.result[self.low] = self.y_own[...].astype(F32) + self.y_in[...].astype(F32)
        self.to_back().start()
        self.save(self.low).start()

    def whole(self):
        at = self.result.at[1 - self.low]
        remote(at, at, self.sems[7], self.sems[8], self.mate).wait_recv()
        self.save(1 - self.low).start()

    def finish(self):
        self.to_mate().wait_send()
        for i in range(1, self.owners):
            self.to_owner(i).wait_send()
        self.to_across().wait_send()
        self.to_back().wait_send()
        self.save(self.low).wait()
        self.save(1 - self.low).wait()


class SmallSum:
    @staticmethod
    def scratch(count, shape):
        return [
            pltpu.VMEM((count,) + shape, F32),
            pltpu.SemaphoreType.DMA((count,)),
            pltpu.SemaphoreType.DMA((count,)),
        ]

    def __init__(self, axis, scratch):
        self.axis = axis
        self.slots, self.send, self.recv = scratch
        self.count = self.slots.shape[0]
        self.me = lax.axis_index(axis)

    def copy(self, i):
        at = self.slots.at[self.me]
        other = lax.rem(self.me + i, self.count)
        return remote(at, at, self.send.at[i], self.recv.at[self.me], spot(**{self.axis: other}))

    def start(self, value):
        self.slots[self.me] = value
        for i in range(1, self.count):
            self.copy(i).start()

    def total(self):
        for i in range(1, self.count):
            other = lax.rem(self.me + i, self.count)
            at = self.slots.at[other]
            remote(at, at, self.send.at[i], self.recv.at[other], spot(**{self.axis: lax.rem(self.me + i, self.count)})).wait_recv()
        out = self.slots[0]
        for i in range(1, self.count):
            out = out + self.slots[i]
        return out

    def finish(self):
        for i in range(1, self.count):
            self.copy(i).wait_send()


def back_kernel(
    par_ref, gated_ref, dpart_ref, fgain_ref,
    fh_ref, fl_ref, th_ref, tl_ref, sign_ref, sw_ref, skip_ref,
    ft_ref, f1_ref, f1b_ref, f2_ref, f2b_ref, freq_ref, last_ref, small_ref,
    npart_hbm, resid_hbm, g_hbm, gate_hbm, conv_hbm, carried_hbm, out_hbm,
    mixed_hbm, low_hbm, w_hbm, x_hbm, proj_hbm, head_hbm, spec_hbm, filt_hbm, net_hbm, sup_hbm, sdown_hbm,
    dres_hbm, dsum_ref, psum_ref, oup_ref, odown_ref, oout_ref, oin_ref, va_ref, vd_ref, vl_ref, vf_ref,
    dall_ref, dconv_ref, dzero_ref, stage_out, s_long, r_long,
    yown_ref, dcar_ref, dtaps_ref, stage_in, ppart_ref, w1_ref, w2_ref,
    mixed_ref, hd_ref, s_hd, r_hd, local, *rest,
):
    total_rows, width = ppart_ref.shape
    channels = dconv_ref.shape[1]
    blocks = total_rows // SEG
    owners = sup_hbm.shape[1]
    ctx, tp, dp = lax.axis_index("ctx"), lax.axis_index("tp"), lax.axis_index("dp")
    rest = list(rest)

    def take(n):
        out = rest[:n]
        del rest[:n]
        return out

    down = LineSum(dpart_ref, dsum_ref, take(11))
    proj = LineSum(ppart_ref, psum_ref, take(11))
    early = [OwnerSum(s, o, take(16)) for s, o in ((sup_hbm, oup_ref), (sdown_hbm, odown_ref), (stage_out, oout_ref))]
    late = OwnerSum(stage_in, oin_ref, take(16))
    a_ctx, a_dp = SmallSum("ctx", take(3)), SmallSum("dp", take(3))
    d_ctx, d_dp, d_tp = SmallSum("ctx", take(3)), SmallSum("dp", take(3)), SmallSum("tp", take(3))
    l_ctx, l_dp = SmallSum("ctx", take(3)), SmallSum("dp", take(3))
    f_ctx, f_dp, f_tp = SmallSum("ctx", take(3)), SmallSum("dp", take(3)), SmallSum("tp", take(3))

    partners = [spot(tp=lax.rem(tp + i, 4)) for i in range(1, 4)]
    partners += [spot(ctx=lax.rem(ctx + i, 4)) for i in range(1, 4)]
    partners += [spot(dp=lax.rem(dp + i, owners)) for i in range(1, owners)]
    barrier, count = signal_all(partners)
    load_part = pltpu.make_async_copy(npart_hbm, ppart_ref, local.at[10])
    load_mixed = pltpu.make_async_copy(mixed_hbm, mixed_ref, local.at[11])
    load_part.start()
    load_part.wait()
    pl.semaphore_wait(barrier, count)
    for s in range(blocks):
        proj.send_block(s)
    load_mixed.start()
    for job in early[:2]:
        job.begin()
    va_ref[...] = jnp.zeros(va_ref.shape, F32)
    vd_ref[...] = small_ref[...]
    fh, fl, th, tl = fh_ref[...], fl_ref[...], th_ref, tl_ref
    skip = skip_ref[...].reshape(1, -1)
    scale = 1.0 / SEG

    def put(dst, value):
        dst[0] = value[:SEG] * scale
        dst[1] = value[SEG:] * scale

    def half_rows(h):
        return pl.ds(pl.multiple_of(h * HALF, HALF), HALF)

    def half_of(who, h):
        return dall_ref.at[who * blocks + h // 2, half_rows(lax.rem(h, 2))]

    def long_to(h, other):
        at = half_of(ctx, h)
        return remote(at, at, s_long.at[other, h], r_long.at[ctx, h], spot(ctx=other))

    def long_from(other):
        def one(h, unused):
            at = half_of(other, h)
            remote(at, at, s_long.at[other, h], r_long.at[other, h], spot(ctx=lax.rem(ctx + 1, 4))).wait_recv()
            return unused

        lax.fori_loop(0, 2 * blocks, one, 0)

    def feed_back(in_ref, g_ref, dres_ref, gate_ref, conv_ref, carried_ref, parts_ref, out_ref, gout_ref):
        once = [
            pltpu.make_async_copy(src, dst, local.at[k])
            for k, (src, dst) in enumerate(
                ((gate_hbm, gate_ref), (conv_hbm, conv_ref), (carried_hbm, carried_ref), (out_hbm.at[tp], parts_ref))
            )
        ]
        for load in once:
            load.start()

        def fetch(h):
            slot = lax.rem(h, 2)
            return (
                pltpu.make_async_copy(resid_hbm.at[half_rows(h)], in_ref.at[slot], local.at[4 + slot]),
                pltpu.make_async_copy(g_hbm.at[half_rows(h)], g_ref.at[slot], local.at[6 + slot]),
            )

        def save(h):
            slot = lax.rem(h, 2)
            return pltpu.make_async_copy(dres_ref.at[slot], dres_hbm.at[half_rows(h)], local.at[8 + slot])

        for load in fetch(0):
            load.start()
        for load in once:
            load.wait()
        share = width // owners
        for o in range(owners):
            out_ref[:, o * share : (o + 1) * share] = parts_ref[o]
        gout_ref[...] = jnp.zeros(gout_ref.shape, F32)
        gain = fgain_ref[...].reshape(1, -1)
        proj.steps(0, PER)

        def one(h, unused):
            rows = half_rows(h)
            slot = lax.rem(h, 2)
            for load in fetch(h):
                load.wait()

            @pl.when(h + 1 < 2 * blocks)
            def _():
                for load in fetch(h + 1):
                    load.start()

            xhat, spread = normalize(in_ref[slot])
            proj.steps(PER + h * PER // 2, PER + (h + 1) * PER // 2)
            proj.wait_half(h)

            @pl.when(h == 1)
            def _():
                for job in early[:2]:
                    job.pair()

            @pl.when(h == 2 * blocks - 3)
            def _():
                for b in range(blocks):
                    down.send_block(b)

            dn = psum_ref[rows].astype(F32)
            e = dn * gain
            d_res = g_ref[slot].astype(F32) + spread * (
                e - jnp.mean(e, axis=-1, keepdims=True) - xhat * jnp.mean(e * xhat, axis=-1, keepdims=True)
            )
            d_mix = d_res.astype(BF16)
            d_gated = mm_nt(d_mix, out_ref[...])
            d_conv = d_gated * gate_ref[rows]
            dall_ref[ctx * blocks + h // 2, half_rows(lax.rem(h, 2))] = d_conv.astype(BF16)
            for other in range(2):
                @pl.when(other < ctx)
                def _():
                    long_to(h, other).start()

            @pl.when(h >= 2)
            def _():
                save(h - 2).wait()

            dres_ref[slot] = d_res
            save(h).start()
            dconv_ref[rows] = d_conv
            dzero_ref[rows] = d_gated * conv_ref[rows]

            @pl.when(lax.rem(h, 2) == 1)
            def _():
                part = dall_ref[ctx * blocks + h // 2]
                put(yown_ref.at[h // 2], mm(fh, part) + mm(fl, part))

            vd_ref[2:3] += jnp.sum(dn * xhat, axis=0, keepdims=True)
            vd_ref[3:4] += jnp.sum(dn, axis=0, keepdims=True)
            vd_ref[1:2] += jnp.sum(d_mix.astype(F32), axis=0, keepdims=True)
            va_ref[15:16] += jnp.sum(d_conv * carried_ref[rows].astype(F32), axis=0, keepdims=True)
            gout_ref[...] += mm_tn(gated_ref[rows], d_mix)
            return unused

        lax.fori_loop(0, 2 * blocks, one, 0)
        half = stage_out.shape[2]
        for t in range(2):
            store_columns(stage_out, t, gout_ref[t * half : (t + 1) * half])
        save(2 * blocks - 2).wait()
        save(2 * blocks - 1).wait()

    pl.run_scoped(
        feed_back,
        pltpu.VMEM((2, HALF, width), F32),
        pltpu.VMEM((2, HALF, width), BF16),
        pltpu.VMEM((2, HALF, width), F32),
        pltpu.VMEM((total_rows, channels), F32),
        pltpu.VMEM((total_rows, channels), F32),
        pltpu.VMEM((total_rows, channels), BF16),
        pltpu.VMEM((owners, channels, width // owners), BF16),
        pltpu.VMEM((channels, width), BF16),
        pltpu.VMEM((channels, width), F32),
    )
    early[2].begin()
    down.steps(0, 3)

    def to_ctx(i):
        at = hd_ref.at[pl.ds(ctx * blocks, blocks)]
        return remote(at, at, s_hd.at[i], r_hd.at[ctx], spot(ctx=lax.rem(ctx + i, 4)))

    def conv_inputs(filt_ref, more_ref, acc_ref):
        load = pltpu.make_async_copy(filt_hbm, filt_ref, local.at[0])
        load.start()

        load.wait()
        load_mixed.wait()

        def leaf_sum(match):
            total = None
            for leaf in range(8, 16):
                term = jnp.where(match(leaf), 1.0, 0.0) * dall_ref[leaf].astype(F32)
                total = term if total is None else total + term
            return total

        def from_leaf(b):
            return lambda leaf: par_ref[0, leaf] == b

        def finish(s, terms):
            blend_all(acc_ref.at[s], terms, True)

        @pl.when(ctx == 0)
        def _():
            for other in (1, 2, 3):
                long_from(other)

            def gather(k, unused):
                p = k + 1
                total = None
                for b in range(4, 8):
                    term = jnp.where(par_ref[0, b] == p, 1.0, 0.0) * dall_ref[b].astype(F32)
                    total = term if total is None else total + term
                put(more_ref.at[k], mm_split(fh, fl, total))
                total = leaf_sum(lambda leaf: par_ref[0, par_ref[0, leaf]] == p)
                put(more_ref.at[3 + k], mm_split(fh, fl, total))
                return unused

            lax.fori_loop(0, 3, gather, 0)
            for a in range(4):
                terms = [(filt_ref.at[s - a], yown_ref.at[s]) for s in range(a, 4)]
                for p in range(max(a, 1), 4):
                    terms.append((filt_ref.at[p - a + 1], more_ref.at[p - 1]))
                    terms.append((filt_ref.at[p - a + 2], more_ref.at[p + 2]))
                finish(a, terms)

        @pl.when(ctx == 1)
        def _():
            for other in (2, 3):
                long_from(other)

            def one(b, unused):
                put(more_ref.at[0], mm_split(fh, fl, leaf_sum(from_leaf(b + 4))))
                finish(b, [(filt_ref.at[0], yown_ref.at[b]), (filt_ref.at[1], more_ref.at[0])])
                return unused

            lax.fori_loop(0, 4, one, 0)

        @pl.when(ctx > 1)
        def _():
            def one(b, unused):
                finish(b, [(filt_ref.at[0], yown_ref.at[b])])
                return unused

            lax.fori_loop(0, 4, one, 0)

        down.steps(3, 5)
        for s in range(blocks):
            top = slice(s * SEG, s * SEG + HEADS)
            d_car = unpack_spectrum(th.at[0:16], tl.at[0:16], acc_ref.at[s])[0:HEADS] + skip * dconv_ref[top]
            rows = [dzero_ref[top], d_car * mixed_ref[1, top], d_car * mixed_ref[0, top]]
            for g in range(3):
                hd_ref[ctx * blocks + s, 2 * g : 2 * g + 2] = rows[g][0:2]
            hd_ref[ctx * blocks + s, 6:8] = jnp.zeros((2, channels), F32)
        for i in range(1, 4):
            to_ctx(i).start()

        def whole(s, unused):
            place = pl.ds(pl.multiple_of(s * SEG, SEG), SEG)
            dcar_ref[place] = unpack_spectrum(th, tl, acc_ref.at[s]) + skip * dconv_ref[place]
            return unused

        lax.fori_loop(0, blocks, whole, 0)

    def mix_stage(low_ref, w_ref, x_ref):
        loads = [
            pltpu.make_async_copy(src, dst, local.at[4 + k])
            for k, (src, dst) in enumerate(((w_hbm, w_ref), (x_hbm, x_ref), (low_hbm, low_ref)))
        ]
        for load in loads:
            load.start()
        pl.run_scoped(
            conv_inputs,
            pltpu.VMEM((DEPTH, 2, SEG, channels), F32),
            pltpu.VMEM((6, 2, SEG, channels), F32),
            pltpu.VMEM((blocks, 2, SEG, channels), F32),
        )

        down.steps(5, 7)
        proj.drain()
        for i in range(1, 4):
            other = lax.rem(ctx + i, 4)
            at = hd_ref.at[pl.ds(other * blocks, blocks)]
            remote(at, at, s_hd.at[i], r_hd.at[other], spot(ctx=other)).wait_recv()

        def mix_back(dp_ref, ext_ref, dm_ref, pin_ref, hin_ref):
            load_heads = pltpu.make_async_copy(head_hbm, hin_ref, local.at[1])
            load_heads.start()

            def fetch(s):
                rows = pl.ds(pl.multiple_of(s * SEG, SEG), SEG)
                return pltpu.make_async_copy(proj_hbm.at[:, rows], pin_ref.at[lax.rem(s, 2)], local.at[2 + lax.rem(s, 2)])

            fetch(0).start()
            load_heads.wait()
            for load in loads:
                load.wait()

            def one(s, unused):
                rows = pl.ds(pl.multiple_of(s * SEG, SEG), SEG)
                slot = lax.rem(s, 2)
                fetch(s).wait()

                @pl.when(s + 1 < blocks)
                def _():
                    fetch(s + 1).start()

                mine = ctx * blocks + s
                child = None
                for b in range(1, 16):
                    term = jnp.where(par_ref[0, b] == mine, 1.0, 0.0) * hd_ref[b]
                    child = term if child is None else child + term
                part = None
                for g in range(3):
                    if g == 0:
                        dm = dzero_ref[rows]
                    else:
                        dm = dcar_ref[rows] * mixed_ref[2 - g, rows]
                    ext_ref[0:HEADS] = hin_ref[g, s]
                    ext_ref[HEADS : HEADS + SEG] = pin_ref[slot, g]
                    for k in range(3):
                        piece = ext_ref[HEADS - 2 + k : HEADS - 2 + k + SEG]
                        va_ref[3 * g + k : 3 * g + k + 1] += jnp.sum(piece * dm, axis=0, keepdims=True)
                    va_ref[12 + g : 13 + g] += jnp.sum(dm, axis=0, keepdims=True)
                    dm_ref[0:SEG] = dm
                    dm_ref[SEG : SEG + 2] = child[2 * g : 2 * g + 2]
                    d_proj = (
                        sw_ref[g, 2:3] * dm
                        + sw_ref[g, 1:2] * dm_ref[1 : 1 + SEG]
                        + sw_ref[g, 0:1] * dm_ref[2 : 2 + SEG]
                    ).astype(BF16)
                    dp_ref[g, rows] = d_proj
                    va_ref[9 + g : 10 + g] += jnp.sum(d_proj.astype(F32), axis=0, keepdims=True)
                    term = mm(d_proj, w_ref[g])
                    part = term if part is None else part + term
                ppart_ref[rows] = part.astype(BF16)
                proj.send_block(s)
                xhat = normalize(x_ref[rows].astype(F32))[0]
                vd_ref[4:5] += jnp.sum(part * xhat, axis=0, keepdims=True)
                vd_ref[5:6] += jnp.sum(part, axis=0, keepdims=True)
                down.steps(7 + s, 8 + s)
                return unused

            lax.fori_loop(0, blocks, one, 0)
            rows = stage_in.shape[3]
            for g in range(3):
                value = mm_tn(dp_ref[g], low_ref[...])
                for t in range(2):
                    store_columns(stage_in.at[:, :, g], t, value[t * rows : (t + 1) * rows])

        pl.run_scoped(
            mix_back,
            pltpu.VMEM((3, total_rows, channels), BF16),
            pltpu.VMEM((HEADS + SEG, channels), F32),
            pltpu.VMEM((HEADS + SEG, channels), F32),
            pltpu.VMEM((2, 3, SEG, channels), F32),
            pltpu.VMEM((3, blocks, HEADS, channels), F32),
        )
    pl.run_scoped(
        mix_stage,
        pltpu.VMEM((total_rows, width), BF16),
        pltpu.VMEM((3, channels, width), BF16),
        pltpu.VMEM((total_rows, width), BF16),
    )
    a_ctx.start(va_ref[...])
    d_ctx.start(vd_ref[...])
    late.begin()
    early[2].pair()
    for job in early[:2]:
        job.own()

    def with_spectra(spec_ref):
        load_spectra = pltpu.make_async_copy(spec_hbm, spec_ref, local.at[0])
        load_spectra.start()
        down.steps(11, 13)

        def conv_filters(dfilt_ref):
            load_spectra.wait()

            @pl.when(ctx == 0)
            def _():
                for d in range(4):
                    blend_all(dfilt_ref.at[d], [(spec_ref.at[8 + s - d], yown_ref.at[s]) for s in range(d, 4)], True)
                dfilt_ref[4:6] = jnp.zeros((2, 2, SEG, channels), F32)

            @pl.when(ctx > 0)
            def _():
                places = []
                for s in range(blocks):
                    above = lineage(par_ref, ctx * blocks + s)
                    places.append([8 + s] + [jnp.where(a >= 0, a, 12) for a in above])
                for d in range(DEPTH):
                    terms = [(spec_ref.at[places[s][d]], yown_ref.at[s]) for s in range(blocks)]
                    blend_all(dfilt_ref.at[d], terms, True)

            down.steps(13, 14)
            sign = sign_ref[...]
            first_row = lax.broadcasted_iota(jnp.int32, (SEG, 1), 0) == 0
            for j in range(DEPTH):
                fix = None
                if j + 1 < DEPTH:
                    nr, ni = dfilt_ref[j + 1, 0], dfilt_ref[j + 1, 1]
                    fix = jnp.sum(sign * ni, axis=0, keepdims=True)
                    dfilt_ref[j, 0] = dfilt_ref[j, 0] + sign * ni
                    dfilt_ref[j, 1] = dfilt_ref[j, 1] - sign * nr
                taps = unpack_spectrum(th, tl, dfilt_ref.at[j])
                if fix is not None:
                    taps = jnp.where(first_row, taps - fix, taps)
                dtaps_ref[j * SEG : (j + 1) * SEG] = taps

        pl.run_scoped(conv_filters, pltpu.VMEM((DEPTH, 2, SEG, channels), F32))

    pl.run_scoped(with_spectra, pltpu.VMEM((13, 2, SEG, channels), F32))
    down.steps(14, 16)

    def filter_back(net_ref):
        load = pltpu.make_async_copy(net_hbm, net_ref, local.at[1])
        load.start()
        d_raw = dtaps_ref[...] * decay(DEPTH * SEG, channels, tp, width)
        extend_weights(w1_ref, f1_ref, f1b_ref)
        extend_weights(w2_ref, f2_ref, f2b_ref)
        freq = freq_ref[...].reshape(1, -1)
        load.wait()
        units = last_ref.shape[0]
        l_ctx.start(jnp.dot(net_ref[3, 0:units], d_raw, **EXACT_DOT))
        s_two = lax.dot_general(last_ref[...], d_raw, NT, **EXACT_DOT) * net_ref[2, 0:units]
        g_two = lax.dot_general(net_ref[1], s_two, NT, **EXACT_DOT)
        d_one = jnp.dot(w2_ref[...] * freq, s_two, **EXACT_DOT)[0:units]
        g_one = lax.dot_general(ft_ref[...], d_one * net_ref[0, 0:units], NT, **EXACT_DOT)
        g_freq = jnp.sum(w1_ref[...] * g_one, axis=0, keepdims=True) + jnp.sum(
            w2_ref[...] * g_two, axis=0, keepdims=True
        )
        vf_ref[...] = jnp.zeros(vf_ref.shape, F32)
        vf_ref[0 : g_one.shape[0], 0:units] = g_one * freq
        vf_ref[0 : g_two.shape[0], units : 2 * units] = g_two * freq
        vf_ref[g_two.shape[0] : g_two.shape[0] + 1, 0:units] = g_freq
        f_ctx.start(vf_ref[...])

    pl.run_scoped(filter_back, pltpu.VMEM(net_hbm.shape, F32))

    def first_cross():
        for job in early[:2]:
            job.cross()

    def second_own():
        early[2].own()
        late.pair()

    def second_cross():
        early[2].cross()
        late.own()

    def vectors():
        a_dp.start(a_ctx.total())
        d_dp.start(d_ctx.total())

    def networks():
        l_dp.start(l_ctx.total())
        f_dp.start(f_ctx.total())

    def gains():
        va_ref[...] = a_dp.total()
        sums = d_dp.total()
        vd_ref[...] = sums
        d_tp.start(sums[4:6])

    def last_layer():
        for job in early[:2]:
            job.whole()
        f_tp.start(f_dp.total())
        last_sum = l_dp.total()
        for o in range(owners):
            held = vl_ref.shape[1]
            vl_ref[o] = last_sum[o * held : (o + 1) * held]

    jobs = (second_own, vectors, networks, first_cross, second_cross, gains, last_layer)
    for k, job in enumerate(jobs):
        down.steps(min(16 + k, 20), min(17 + k, 20))
        proj.steps(2 * k, 2 * k + 2)
        job()
    proj.steps(14, 17)
    late.cross()
    early[2].whole()
    proj.steps(17, proj.pairs + 2 * LAG)
    late.whole()
    for s in range(blocks):
        down.wait_block(s)
        proj.wait_block(s)
    vd_ref[4:6] = d_tp.total()
    vf_ref[...] = f_tp.total()
    for job in (a_ctx, a_dp, d_ctx, d_dp, d_tp, l_ctx, l_dp, f_ctx, f_dp, f_tp):
        job.finish()
    for job in early + [late]:
        job.finish()
    for i in range(1, 4):
        to_ctx(i).wait_send()
    for other in range(2):
        @pl.when(other < ctx)
        def _():
            for h in range(2 * blocks):
                long_to(h, other).wait_send()

    down.drain()
    proj.drain()


def final_kernel(
    resid_ref, dsum_ref, dres_ref, psum_ref, x_ref, gain_ref, bias_ref, va_ref, vd_ref, vl_ref, vf_ref,
    oup_ref, odown_ref, oout_ref, oin_ref,
    result_ref, gradx_ref, up_ref, down_ref, out_ref, in_ref,
    mgain_ref, mshift_ref, inb_ref, sw_ref, sb_ref, f1_ref, f1b_ref, f2_ref, f2b_ref, freq_ref, last_ref,
    skip_ref, ob_ref, fgain_ref, fshift_ref, ub_ref, db_ref,
):
    step = pl.program_id(0)

    @pl.when(step == 0)
    def _():
        up_ref[...] = oup_ref[...]
        down_ref[...] = odown_ref[...]
        out_ref[...] = oout_ref[...]
        rows = oin_ref.shape[2]
        for h in range(2):
            in_ref[:, h * rows : (h + 1) * rows] = oin_ref[h]
        mgain_ref[...] = vd_ref[4]
        mshift_ref[...] = vd_ref[5]
        db_ref[...] = vd_ref[0]
        ob_ref[...] = vd_ref[1]
        fgain_ref[...] = vd_ref[2]
        fshift_ref[...] = vd_ref[3]
        ub_ref[...] = vd_ref[6]
        for g in range(3):
            sw_ref[g] = va_ref[3 * g : 3 * g + 3]
        inb_ref[...] = va_ref[9:12]
        sb_ref[...] = va_ref[12:15]
        skip_ref[...] = va_ref[15]
        units = f1_ref.shape[1]
        rows_one, rows_two = f1_ref.shape[0], f2_ref.shape[0]
        f1_ref[...] = vf_ref[0:rows_one, 0:units]
        f1b_ref[...] = vf_ref[rows_one, 0:units]
        f2_ref[...] = vf_ref[0:rows_two, units : 2 * units]
        f2b_ref[...] = vf_ref[rows_two, units : 2 * units]
        freq_ref[...] = vf_ref[rows_two + 8, 0:units]
        last_ref[...] = vl_ref[lax.axis_index("dp")]

    result_ref[...] = resid_ref[...] + dsum_ref[...].astype(F32) + bias_ref[...].reshape(1, -1)
    xhat, spread = normalize(x_ref[...].astype(F32))
    e = psum_ref[...].astype(F32) * gain_ref[...].reshape(1, -1)
    gradx_ref[...] = dres_ref[...] + spread * (
        e - jnp.mean(e, axis=-1, keepdims=True) - xhat * jnp.mean(e * xhat, axis=-1, keepdims=True)
    )


def body(
    block_in, out_grad, parents, mixer_gain, mixer_shift, in_proj, in_bias, short_weight, short_bias,
    filter_one, filter_one_bias, filter_two, filter_two_bias, filter_freq, filter_out, skip_gain,
    out_proj, out_bias, feed_gain, feed_shift, feed_up, feed_up_bias, feed_down, feed_down_bias,
):
    x = block_in[0]
    g = out_grad[0]
    total_rows, width = x.shape
    channels = skip_gain.shape[0]
    blocks = total_rows // SEG
    hidden = feed_up.shape[1]
    tp_count = lax.axis_size("tp")
    tp_index = lax.axis_index("tp")
    owners = lax.axis_size("dp")
    first = lax.axis_index("ctx") * blocks
    all_blocks = parents.shape[1]

    half = hidden // 2
    share = width // owners
    units, features = filter_one.shape[1], filter_one.shape[0]
    feat_rows, mid_rows = 40, units + 8
    length = DEPTH * SEG
    ft = jnp.asarray(filter_features(length, (features - 1) // 2, feat_rows))
    fh, fl, th, tl, sign = (jnp.asarray(t) for t in spectral_constants(SEG))
    dma = pltpu.SemaphoreType.DMA
    front_out = (
        sds((total_rows, width), BF16),
        sds((3, total_rows, channels), F32),
        sds((3, blocks, HEADS, channels), F32),
        sds((2, total_rows, channels), F32),
        sds((13, 2, SEG, channels), F32),
        sds((DEPTH, 2, SEG, channels), F32),
        sds((4, mid_rows, length), F32),
        sds((3, channels, width), BF16),
        sds((tp_count, owners, channels, share), BF16),
        sds((width, hidden), BF16),
        sds((units, channels), F32),
        sds((total_rows, channels), F32),
        sds((total_rows, channels), F32),
        sds((total_rows, channels), BF16),
        sds((total_rows, channels), BF16),
    )
    low, proj, head, mixed, spec, filt, net, in_all, out_all, up_all, last, gate, conv, gated, carried = call(
        front_kernel,
        front_out,
        [SM] + [VM] * 22,
        [
            pltpu.VMEM((3, channels, width), BF16),
            pltpu.VMEM((total_rows, width), BF16),
            pltpu.VMEM((3, total_rows, channels), F32),
            pltpu.VMEM((3, blocks, HEADS, channels), F32),
            pltpu.VMEM((2, total_rows, channels), F32),
            pltpu.VMEM((13, 2, SEG, channels), F32),
            pltpu.VMEM((DEPTH, 2, SEG, channels), F32),
            pltpu.VMEM((4, mid_rows, length), F32),
            pltpu.VMEM((length, channels), F32),
            pltpu.VMEM((8, SEG, channels), BF16),
            pltpu.VMEM((4, 2 * blocks, width), F32),
            pltpu.VMEM((3, 9, HEADS, channels), F32),
            pltpu.VMEM((3, HEADS + SEG, channels), F32),
            pltpu.VMEM((feat_rows, units), F32),
            pltpu.VMEM((mid_rows, units), F32),
            pltpu.VMEM((2, SEG, channels), F32),
            pltpu.VMEM((owners,) + filter_out.shape, BF16),
            pltpu.VMEM((owners, 3, channels, share), BF16),
            dma((2, owners)), dma((2, owners)), dma((owners,)), dma((owners,)),
            dma((owners, tp_count)), dma((2, tp_count, owners)),
            dma((owners,)), dma((2, owners)),
            dma((tp_count,)), dma((tp_count,)), dma((3, owners, tp_count)),
            dma((4,)), dma((4,)), dma((4, 4)), dma((4, 4)), dma((4,)), dma((12,)),
        ],
        1,
        out_specs=(HB,) * 10 + (VM,) * 5,
    )(
        parents, x, jnp.transpose(in_proj, (1, 2, 0)), filter_out, out_proj, feed_up, ft,
        filter_one, filter_one_bias, filter_two, filter_two_bias, filter_freq, mixer_gain, mixer_shift,
        in_bias, short_weight, short_bias, skip_gain, fh, fl, th, tl, sign,
    )

    piece = share // 2
    feed_big = [
        sds((total_rows, width), F32),
        sds((total_rows, width), BF16),
        sds((total_rows, width), BF16),
        sds((2, owners, piece, hidden), BF16),
        sds((2, owners, half, share), BF16),
    ]
    feed_in = (out_all, x, g, up_all)

    def held(v):
        return pltpu.VMEM(v.shape, v.dtype)

    residual, norm_part, down_part, stage_up, stage_down, small = call(
        feed_kernel,
        feed_big + [sds((8, width), F32)],
        [VM] * 6 + [HB] * 4,
        [held(v) for v in feed_in]
        + [held(v) for v in feed_big]
        + [dma((4,)), dma((2,)), dma((3, blocks)), pltpu.VMEM((owners, hidden, share), BF16)]
        + [dma((2, owners)), dma((2, owners))]
        + [
            pltpu.VMEM((width, hidden), F32),
            pltpu.VMEM((hidden, width), F32),
            pltpu.VMEM((tp_count, total_rows, channels), BF16),
            pltpu.VMEM((tp_count, channels, width), BF16),
            pltpu.VMEM((hidden, width), BF16),
            dma((tp_count, blocks)), dma((tp_count, blocks)),
        ],
        2,
        out_specs=(HB,) * 5 + (VM,),
    )(gated, out_bias, feed_gain, feed_shift, feed_up_bias, feed_down, *feed_in)

    shapes = [(piece, hidden), (half, share), (channels // 2, share), (3, channels // 2, share)]
    scratch = [
        pltpu.VMEM((all_blocks, SEG, channels), BF16),
        pltpu.VMEM((total_rows, channels), F32),
        pltpu.VMEM((total_rows, channels), F32),
        pltpu.VMEM((2, owners) + shapes[2], BF16),
        dma((4, 2 * blocks)), dma((4, 2 * blocks)),
        pltpu.VMEM((blocks, 2, SEG, channels), F32),
        pltpu.VMEM((total_rows, channels), F32),
        pltpu.VMEM((length, channels), F32),
        pltpu.VMEM((2, owners) + shapes[3], BF16),
        pltpu.VMEM((total_rows, width), BF16),
        pltpu.VMEM((feat_rows, units), F32),
        pltpu.VMEM((mid_rows, units), F32),
        held(mixed),
        pltpu.VMEM((all_blocks, HEADS, channels), F32),
        dma((4,)), dma((4,)), dma((12,)),
    ]
    scratch += LineSum.scratch(total_rows, width) * 2
    for shape in shapes:
        scratch += OwnerSum.scratch(owners, shape)
    smalls = ((16, channels), (8, width), (units, channels), (mid_rows + 8, 2 * units))
    for counts, shape in (
        ((4, owners), smalls[0]), ((4, owners), smalls[1]), ((tp_count,), (2, width)), ((4, owners), smalls[2]),
        ((4, owners, tp_count), smalls[3]),
    ):
        for count in counts:
            scratch += SmallSum.scratch(count, shape)
    d_res, down_sum, proj_sum, own_up, own_down, own_out, own_in, va, vd, vl, vf = call(
        back_kernel,
        (
            sds((total_rows, width), F32),
            sds((total_rows, width), BF16),
            sds((total_rows, width), BF16),
        )
        + tuple(sds((2,) + shape, F32) for shape in shapes)
        + (
            sds(smalls[0], F32),
            sds(smalls[1], F32),
            sds((owners,) + filter_out.shape, F32),
            sds(smalls[3], F32),
        ),
        [SM] + [VM] * 18 + [HB] * 18,
        scratch,
        3,
        out_specs=(HB, VM, VM, HB, HB, HB, HB, VM, VM, VM, VM),
    )(
        parents, gated, down_part, feed_gain, fh, fl, th, tl, sign, short_weight,
        skip_gain, ft, filter_one, filter_one_bias, filter_two, filter_two_bias, filter_freq, last, small,
        norm_part, residual, g, gate, conv, carried, out_all, mixed, low, in_all, x, proj, head, spec, filt, net, stage_up, stage_down,
    )

    def by_block(*shape):
        return pl.BlockSpec((2 * SEG,) + shape, lambda i: (i,) + (0,) * len(shape))

    def whole(v):
        return pl.BlockSpec(v.shape, lambda i: (0,) * len(v.shape))

    wide = by_block(width)
    vectors = [
        sds(v.shape, F32)
        for v in (
            mixer_gain, mixer_shift, in_bias, short_weight, short_bias, filter_one, filter_one_bias, filter_two,
            filter_two_bias, filter_freq, filter_out, skip_gain, out_bias, feed_gain, feed_shift, feed_up_bias,
            feed_down_bias,
        )
    ]
    out = pl.pallas_call(
        final_kernel,
        grid=(blocks // 2,),
        out_shape=[
            sds((total_rows, width), F32), sds((total_rows, width), F32), own_up, own_down, own_out,
            sds((3, channels, share), F32),
        ]
        + vectors,
        in_specs=[wide] * 5 + [whole(v) for v in (mixer_gain, feed_down_bias, va, vd, vl, vf, own_up, own_down, own_out, own_in)],
        out_specs=[wide, wide]
        + [whole(v) for v in (own_up, own_down, own_out, sds((3, channels, share), F32))]
        + [whole(v) for v in vectors],
        compiler_params=pltpu.CompilerParams(vmem_limit_bytes=LIMIT),
    )(
        residual, down_sum, d_res, proj_sum, x, mixer_gain, feed_down_bias, va, vd, vl, vf,
        own_up, own_down, own_out, own_in,
    )
    (result, grad_x, g_up, g_down, g_out, g_in, g_mgain, g_mshift, g_inb, g_sw, g_sb, g_f1, g_f1b, g_f2, g_f2b,
     g_freq, g_last, g_skip, g_ob, g_fgain, g_fshift, g_ub, g_db) = out
    return (
        result[None], grad_x[None], g_mgain, g_mshift, jnp.transpose(g_in, (2, 0, 1)), g_inb, g_sw, g_sb,
        g_f1, g_f1b, g_f2, g_f2b, g_freq, g_last, g_skip, g_out.reshape(channels, share), g_ob, g_fgain, g_fshift,
        g_up.reshape(share, hidden), g_ub, g_down.reshape(hidden, share), g_db,
    )


def solution(mesh):
    in_specs = (
        P("dp", "ctx", None), P("dp", "ctx", None), P("dp", None), P(), P(), P("dp", None, "tp"), P(None, "tp"),
        P(None, None, "tp"), P(None, "tp"), P(), P(), P(), P(), P(), P("dp", "tp"), P("tp"), P("tp", "dp"), P(),
        P(), P(), P("dp", "tp"), P("tp"), P("tp", "dp"), P(),
    )
    out_specs = (
        P("dp", "ctx", None), P("dp", "ctx", None), P(), P(), P("dp", None, "tp"), P(None, "tp"),
        P(None, None, "tp"), P(None, "tp"), P(), P(), P(), P(), P(), P("dp", "tp"), P("tp"), P("tp", "dp"), P(),
        P(), P(), P("dp", "tp"), P("tp"), P("tp", "dp"), P(),
    )
    return jax.shard_map(body, mesh=mesh, in_specs=in_specs, out_specs=out_specs, check_vma=False)
```

```python
import functools
import math

import jax
import jax.numpy as jnp
import numpy as np
from jax import lax
from jax.experimental import pallas as pl
from jax.experimental.pallas import tpu as pltpu
from jax.sharding import PartitionSpec as P

SEG = 256
DEPTH = 6
HEADS = 8
EXACT = lax.Precision.HIGHEST
EPSILON = 1e-05
SLOW_RATE = -math.log(0.01) / 1.5
FAST_RATE = -math.log(0.01) / 0.3
SHIFT_FLOOR = 0.05
F32 = jnp.float32
BF16 = jnp.bfloat16
MESH = pl.DeviceIdType.MESH
VM = pl.BlockSpec(memory_space=pltpu.VMEM)
SM = pl.BlockSpec(memory_space=pltpu.SMEM)
LIMIT = 62 << 20


def sds(shape, dtype):
    return jax.ShapeDtypeStruct(shape, dtype)


HB = pl.BlockSpec(memory_space=pl.ANY)


def call(kernel, out_shape, in_specs, scratch=(), collective=None, flops=0, traffic=0, out_specs=None):
    many = isinstance(out_shape, (tuple, list))
    return pl.pallas_call(
        kernel,
        out_shape=out_shape,
        in_specs=in_specs,
        out_specs=out_specs or (tuple(VM for _ in out_shape) if many else VM),
        scratch_shapes=list(scratch),
        compiler_params=pltpu.CompilerParams(
            vmem_limit_bytes=LIMIT,
            collective_id=collective,
            has_side_effects=collective is not None,
        ),
        cost_estimate=pl.CostEstimate(flops=flops, bytes_accessed=traffic, transcendentals=0),
    )


def spectral_constants(block_len):
    freq = np.arange(block_len)[:, None]
    place = np.arange(block_len)[None, :]
    angle = ((2 * freq + 1) * place % (4 * block_len)) * (2.0 * math.pi / (4 * block_len))
    table = np.concatenate([np.cos(angle), -np.sin(angle)], axis=0).astype(np.float32)
    high = table.astype(jnp.bfloat16)
    low = (table - high.astype(np.float32)).astype(jnp.bfloat16)
    sign = np.where(np.arange(block_len) % 2 == 0, 1.0, -1.0).astype(np.float32)[:, None]
    return high, low, np.ascontiguousarray(high.T), np.ascontiguousarray(low.T), sign


def normalize(values):
    mean_value = jnp.mean(values, axis=-1, keepdims=True)
    centered = values - mean_value
    variance = jnp.mean(centered * centered, axis=-1, keepdims=True)
    scale = lax.rsqrt(variance + EPSILON)
    return centered * scale, scale


def split(values):
    high = values.astype(BF16)
    return high, (values - high.astype(F32)).astype(BF16)


def mm(lhs, rhs):
    return jnp.dot(lhs, rhs, preferred_element_type=F32)


def mm_nt(lhs, rhs):
    return lax.dot_general(lhs, rhs, (((1,), (1,)), ((), ())), preferred_element_type=F32)


def mm_tn(lhs, rhs):
    return lax.dot_general(lhs, rhs, (((0,), (0,)), ((), ())), preferred_element_type=F32)


def mm_split(high, low, values):
    v_high, v_low = split(values)
    return mm(high, v_high) + (mm(low, v_high) + mm(high, v_low))


FT = 32


def lineage(par_ref, block):
    out = []
    current = block
    for _ in range(DEPTH - 1):
        parent = par_ref[0, jnp.maximum(current, 0)]
        current = jnp.where(current >= 0, parent, -1)
        out.append(current)
    return out


def blend_all(dst, terms, conj):
    def tile(t, unused):
        rows = pl.ds(pl.multiple_of(t * FT, FT), FT)
        re = im = None
        for a, b in terms:
            ar, ai = a[0, rows], a[1, rows]
            br, bi = b[0, rows], b[1, rows]
            if conj:
                pr, pi = ar * br + ai * bi, ar * bi - ai * br
            else:
                pr, pi = ar * br - ai * bi, ar * bi + ai * br
            re, im = (pr, pi) if re is None else (re + pr, im + pi)
        dst[0, rows] = re
        dst[1, rows] = im
        return unused

    lax.fori_loop(0, SEG // FT, tile, 0)


def unpack_spectrum(th, tl, ref):
    high_re, low_re = split(ref[0])
    high_im, low_im = split(ref[1])
    a, b = slice(0, SEG), slice(SEG, 2 * SEG)
    return (
        mm(th[:, a], high_re) + mm(th[:, b], high_im)
        + (mm(tl[:, a], high_re) + mm(tl[:, b], high_im))
        + (mm(th[:, a], low_re) + mm(th[:, b], low_im))
    )


def filter_features(length, bands, rows):
    positions = np.arange(length)
    time_pos = positions / (length - 1)
    freq = np.linspace(0.0001, bands - 1, bands)
    phases = (2.0 * math.pi / length * positions)[None, :] * freq[:, None]
    table = np.zeros((rows, length), np.float32)
    table[0] = time_pos
    table[1 : bands + 1] = np.cos(phases)
    table[bands + 1 : 2 * bands + 1] = -np.sin(phases)
    table[2 * bands + 1] = 1.0
    return table


def spot(**changes):
    base = {name: lax.axis_index(name) for name in ("dp", "ctx", "tp")}
    base.update(changes)
    return (base["dp"], base["ctx"], base["tp"])


def remote(src, dst, send, recv, where):
    return pltpu.make_async_remote_copy(
        src_ref=src, dst_ref=dst, send_sem=send, recv_sem=recv, device_id=where, device_id_type=MESH
    )


def greet(partners):
    barrier = pltpu.get_barrier_semaphore()
    for where in partners:
        pl.semaphore_signal(barrier, inc=1, device_id=where, device_id_type=MESH)
    pl.semaphore_wait(barrier, len(partners))


CHUNK = 32
HALF = SEG // 2
PER = SEG // (2 * CHUNK)
LAG = 2


def chunk(c):
    return pl.ds(pl.multiple_of(c * CHUNK, CHUNK), CHUNK)


class LineRole:
    def __init__(self):
        tp = lax.axis_index("tp")
        self.inner = jnp.logical_and(tp > 0, tp < 3)
        self.outer = jnp.logical_not(self.inner)
        self.side = jnp.where(tp < 2, 0, 1)
        near = jnp.where(self.side == 0, 0, 3)
        far = jnp.where(self.side == 0, 1, 2)
        self.mate = spot(tp=jnp.where(self.inner, near, far))
        self.cross = spot(tp=3 - tp)


class LineSum(LineRole):
    scratch_count = 11

    @staticmethod
    def scratch(rows, width):
        count = rows // CHUNK
        return [
            pltpu.VMEM((rows, width), BF16),
            pltpu.VMEM((rows // 2, width), BF16),
            pltpu.VMEM((rows // 2, width), BF16),
        ] + [pltpu.SemaphoreType.DMA((count,)) for _ in range(8)]

    def __init__(self, part, total, scratch):
        super().__init__()
        self.part, self.total = part, total
        self.end, self.mid, self.out = scratch[:3]
        self.sems = scratch[3:]
        self.pairs = part.shape[0] // (2 * CHUNK)

    def to_mid(self, c):
        return remote(self.part.at[chunk(c)], self.end.at[chunk(c)], self.sems[0].at[c], self.sems[1].at[c], self.mate)

    def to_cross(self, k):
        return remote(self.out.at[chunk(k)], self.mid.at[chunk(k)], self.sems[2].at[k], self.sems[3].at[k], self.cross)

    def final_end(self, c):
        at = self.total.at[chunk(c)]
        return remote(at, at, self.sems[4].at[c], self.sems[5].at[c], self.mate)

    def final_cross(self, c):
        at = self.total.at[chunk(c)]
        return remote(at, at, self.sems[6].at[c], self.sems[7].at[c], self.cross)

    def send_block(self, s):
        @pl.when(self.outer)
        def _():
            def one(i, unused):
                self.to_mid(s * 2 * PER + i).start()
                return unused

            lax.fori_loop(0, 2 * PER, one, 0)

    def step(self, k):
        pairs, side = self.pairs, self.side

        @pl.when(k < pairs)
        def _():
            other = 2 * k + 1 - side
            self.to_mid(other).wait_recv()
            self.out[chunk(k)] = (
                self.part[chunk(other)].astype(F32) + self.end[chunk(other)].astype(F32)
            ).astype(BF16)
            self.to_cross(k).start()

        j = k - LAG

        @pl.when(jnp.logical_and(j >= 0, j < pairs))
        def _():
            mine = 2 * j + side
            self.to_mid(mine).wait_recv()
            self.to_cross(j).wait_recv()
            self.total[chunk(mine)] = (
                self.part[chunk(mine)].astype(F32)
                + self.end[chunk(mine)].astype(F32)
                + self.mid[chunk(j)].astype(F32)
            ).astype(BF16)
            self.final_cross(mine).start()
            self.final_end(mine).start()

        i = k - 2 * LAG

        @pl.when(jnp.logical_and(i >= 0, i < pairs))
        def _():
            other = 2 * i + 1 - side
            self.final_cross(other).wait_recv()
            self.final_end(other).start()

    def steps(self, first, last):
        @pl.when(self.inner)
        def _():
            def one(k, unused):
                self.step(k)
                return unused

            lax.fori_loop(first, last, one, 0)

    def wait_block(self, s):
        @pl.when(self.outer)
        def _():
            def one(i, unused):
                self.final_end(s * 2 * PER + i).wait_recv()
                return unused

            lax.fori_loop(0, 2 * PER, one, 0)

    def wait_half(self, h):
        @pl.when(self.outer)
        def _():
            def one(i, unused):
                self.final_end(h * PER + i).wait_recv()
                return unused

            lax.fori_loop(0, PER, one, 0)

    def drain(self):
        @pl.when(self.outer)
        def _():
            def one(c, unused):
                self.to_mid(c).wait_send()
                return unused

            lax.fori_loop(0, 2 * self.pairs, one, 0)

        @pl.when(self.inner)
        def _():
            def one(k, unused):
                mine, other = 2 * k + self.side, 2 * k + 1 - self.side
                self.to_cross(k).wait_send()
                self.final_cross(mine).wait_send()
                self.final_end(mine).wait_send()
                self.final_end(other).wait_send()
                return unused

            lax.fori_loop(0, self.pairs, one, 0)


def signal_all(partners):
    barrier = pltpu.get_barrier_semaphore()
    for where in partners:
        pl.semaphore_signal(barrier, inc=1, device_id=where, device_id_type=MESH)
    return barrier, len(partners)


def store_columns(stage, half, value):
    owners, share = stage.shape[1], stage.shape[-1]
    for o in range(owners):
        stage[half, o] = value[:, o * share : (o + 1) * share].astype(BF16)


def store_rows(stage, first, value):
    size = stage.shape[2]
    for q in range(value.shape[0] // size):
        owner, half = divmod(first // size + q, 2)
        stage[half, owner] = value[q * size : (q + 1) * size].astype(BF16)


def feed_kernel(
    gated_ref, ob_ref, gain_ref, shift_ref, ub_ref, own_down,
    out_hbm, x_hbm, g_hbm, up_hbm,
    resid_hbm, npart_hbm, dpart_hbm, gup_hbm, gdown_hbm, small_ref,
    out_in, x_ref, g_ref, up_ref,
    resid_ref, npart_ref, dpart_ref, gup_ref, gdown_ref, s_load, s_save, s_block, down_in, s_down, r_down,
    up_acc, down_acc, gall_ref, out_ref, down_ref, s_gate, r_gate,
):
    groups, owners = out_in.shape[:2]
    width = x_ref.shape[1]
    blocks = x_ref.shape[0] // SEG
    share = width // owners
    tp, ctx, dp = lax.axis_index("tp"), lax.axis_index("ctx"), lax.axis_index("dp")
    chain = LineRole()
    barrier, count = signal_all(
        [spot(tp=lax.rem(tp + i, groups)) for i in range(1, groups)]
        + [spot(ctx=lax.rem(ctx + i, 4)) for i in range(1, 4)]
        + [spot(dp=lax.rem(dp + i, owners)) for i in range(1, owners)]
    )

    low_half = lax.rem(ctx, 2)
    pair_mate = spot(ctx=ctx + 1 - 2 * low_half)

    def owner(i):
        return lax.rem(dp + i, owners)

    def half_of(ref, half):
        size = ref.shape[0] // 2
        return ref.at[pl.ds(pl.multiple_of(half * size, 16), size)]

    def send_down(i):
        return remote(
            half_of(own_down, low_half), half_of(down_in.at[dp], low_half), s_down.at[0, i], r_down.at[0, dp],
            spot(dp=owner(i)),
        )

    def swap_down(i):
        at = half_of(down_in.at[owner(i)], low_half)
        return remote(at, at, s_down.at[1, i], r_down.at[1, owner(i)], pair_mate)

    def got_down(stage, i, half):
        at = half_of(down_in.at[owner(i)], half)
        return remote(at, at, s_down.at[0, i], r_down.at[stage, owner(i)], pair_mate)

    far = jnp.where(tp < 2, tp + 2, tp - 2)
    beyond = jnp.where(chain.side == 0, 3, 0)
    other = jnp.where(chain.inner, 3 - tp, far)
    near = jnp.where(chain.inner, jnp.where(chain.side == 0, 0, 3), jnp.where(chain.side == 0, 1, 2))

    def gate_copy(s, i):
        rows = pl.ds(pl.multiple_of(s * SEG, SEG), SEG)
        where = chain.mate if i == 0 else spot(tp=other)
        return remote(gated_ref.at[rows], gall_ref.at[tp, rows], s_gate.at[i, s], r_gate.at[tp, s], where)

    def gate_pass(s, i, source):
        at = gall_ref.at[source, pl.ds(pl.multiple_of(s * SEG, SEG), SEG)]
        return remote(at, at, s_gate.at[2 + i, s], r_gate.at[source, s], chain.mate)

    def gate_from(s, source):
        at = gall_ref.at[source, pl.ds(pl.multiple_of(s * SEG, SEG), SEG)]
        return remote(at, at, s_gate.at[0, s], r_gate.at[source, s], chain.mate)

    loads = [
        pltpu.make_async_copy(src, dst, s_load.at[k])
        for k, (src, dst) in enumerate(
            (
                (out_hbm, out_in), (x_hbm, x_ref), (up_hbm, up_ref), (g_hbm, g_ref),
            )
        )
    ]
    for load in loads:
        load.start()

    def save(k, src, dst, s):
        rows = pl.ds(pl.multiple_of(s * SEG, SEG), SEG)
        return pltpu.make_async_copy(src.at[rows], dst.at[rows], s_block.at[k, s])

    blockwise = ((resid_ref, resid_hbm), (npart_ref, npart_hbm), (dpart_ref, dpart_hbm))
    saves = [
        pltpu.make_async_copy(src, dst, s_save.at[k])
        for k, (src, dst) in enumerate(((gup_ref, gup_hbm), (gdown_ref, gdown_hbm)))
    ]
    gall_ref[tp] = gated_ref[...]
    pl.semaphore_wait(barrier, count)
    for s in range(blocks):
        for i in range(2):
            gate_copy(s, 1 - i).start()
    for i in range(1, owners):
        send_down(i).start()
    down_in[dp] = own_down[...]
    for load in loads:
        load.wait()
    for o in range(owners):
        columns = slice(o * share, (o + 1) * share)
        for z in range(groups):
            out_ref[z, :, columns] = out_in[z, o]
    ob, gain, shift = (ref[...].reshape(1, -1) for ref in (ob_ref, gain_ref, shift_ref))
    ub = ub_ref[...].reshape(1, -1)
    for ref in (small_ref, up_acc, down_acc):
        ref[...] = jnp.zeros(ref.shape, F32)

    def core(s, unused):
        rows = pl.ds(pl.multiple_of(s * SEG, SEG), SEG)

        @pl.when(chain.inner)
        def _():
            for i, source in enumerate((3 - tp, beyond)):
                gate_from(s, source).wait_recv()
                gate_pass(s, i, source).start()
            gate_from(s, near).wait_recv()

        @pl.when(chain.outer)
        def _():
            gate_from(s, near).wait_recv()
            gate_from(s, 3 - near).wait_recv()
            gate_from(s, 3 - tp).wait_recv()

        mixed = mm(gall_ref[0, rows], out_ref[0])
        for z in range(1, groups):
            mixed = mixed + mm(gall_ref[z, rows], out_ref[z])
        residual = x_ref[rows].astype(F32) + mixed + ob
        resid_ref[rows] = residual
        save(0, *blockwise[0], s).start()
        low = (normalize(residual)[0] * gain + shift).astype(BF16)
        pre = mm(low, up_ref[...]) + ub
        cdf = 0.5 * (1.0 + lax.erf(pre * math.sqrt(0.5)))
        hidden = (pre * cdf).astype(BF16)
        slope = cdf + pre * (jnp.exp(-0.5 * pre * pre) * (1.0 / math.sqrt(2.0 * math.pi)))

        @pl.when(s == 0)
        def _():
            for i in range(1, owners):
                got_down(0, i, low_half).wait_recv()
                swap_down(i).start()
            for i in range(1, owners):
                got_down(1, i, 1 - low_half).wait_recv()
            for o in range(owners):
                down_ref[:, o * share : (o + 1) * share] = down_in[o]

        grad = g_ref[rows]
        d_pre = (mm_nt(grad, down_ref[...]) * slope).astype(BF16)
        npart_ref[rows] = mm_nt(d_pre, up_ref[...]).astype(BF16)
        dpart_ref[rows] = mm(hidden, down_ref[...]).astype(BF16)
        for k in (1, 2):
            save(k, *blockwise[k], s).start()
        up_acc[...] += mm_tn(low, d_pre)
        down_acc[...] += mm_tn(hidden, grad)
        small_ref[0:1] += jnp.sum(grad.astype(F32), axis=0, keepdims=True)
        small_ref[6:7] += jnp.sum(d_pre.astype(F32), axis=0, keepdims=True)
        return unused

    lax.fori_loop(0, blocks, core, 0)
    for t in range(2):
        part = slice(t * width // 2, (t + 1) * width // 2)
        store_rows(gup_ref, t * width // 2, up_acc[part])
        units = down_acc.shape[0] // 2
        store_columns(gdown_ref, t, down_acc[t * units : (t + 1) * units])
    for job in saves:
        job.start()
    for i in range(1, owners):
        send_down(i).wait_send()
        swap_down(i).wait_send()
    for s in range(blocks):
        for i in range(2):
            gate_copy(s, i).wait_send()

    @pl.when(chain.inner)
    def _():
        for s in range(blocks):
            for i, source in enumerate((3 - tp, beyond)):
                gate_pass(s, i, source).wait_send()

    for job in saves:
        job.wait()
    for s in range(blocks):
        for k in range(3):
            save(k, *blockwise[k], s).wait()


def sine_cosine(angle):
    turns = jnp.floor(angle * (2.0 / math.pi) + 0.5)
    rest = ((angle - turns * 1.5703125) - turns * 4.837512969970703125e-4) - turns * 7.54978995489188216e-8
    square = rest * rest
    sine = ((-1.9515295891e-4 * square + 8.3321608736e-3) * square - 1.6666654611e-1) * square * rest + rest
    cosine = ((2.443315711809948e-5 * square - 1.388731625493765e-3) * square + 4.166664568298827e-2) * (
        square * square
    ) + (1.0 - 0.5 * square)
    quarter = turns - 4.0 * jnp.floor(turns * 0.25)
    odd = jnp.logical_or(quarter == 1.0, quarter == 3.0)
    middle = jnp.logical_or(quarter == 1.0, quarter == 2.0)
    sine, cosine = jnp.where(odd, cosine, sine), jnp.where(odd, sine, cosine)
    return jnp.where(quarter >= 2.0, -sine, sine), jnp.where(middle, -cosine, cosine)


def extend_weights(ref, weight, bias):
    rows = weight.shape[0]
    ref[...] = jnp.zeros(ref.shape, F32)
    ref[0:rows] = weight[...]
    ref[rows : rows + 1] = bias[...].reshape(1, -1)


def decay(length, channels, tp, width):
    time_pos = lax.broadcasted_iota(jnp.int32, (length, 1), 0).astype(F32) * (1.0 / (length - 1))
    channel = (lax.broadcasted_iota(jnp.int32, (1, channels), 1) + tp * channels).astype(F32)
    rate = SLOW_RATE + (FAST_RATE - SLOW_RATE) * channel * (1.0 / (width - 1))
    return jnp.exp(-time_pos * rate) + SHIFT_FLOOR


EXACT_DOT = dict(precision=EXACT, preferred_element_type=F32)
TN = (((0,), (0,)), ((), ()))
NT = (((1,), (1,)), ((), ()))


def front_kernel(
    par_ref, x_ref, win_ref, last_ref, out_in, up_in, ft_ref, f1_ref, f1b_ref, f2_ref, f2b_ref, freq_ref,
    gain_ref, shift_ref, ib_ref, sw_ref, sb_ref, skip_ref, fh_ref, fl_ref, th_ref, tl_ref, sign_ref,
    low_hbm, proj_hbm, head_hbm, mixed_hbm, spec_hbm, filt_hbm, net_hbm, in_hbm, out_hbm, up_hbm,
    lasts_ref, gate_ref, conv_ref, gated_ref, carried_ref,
    w_ref, low_ref, proj_ref, head_ref, mixed_ref, spec_ref, filt_ref, net_ref, taps_ref, shared_ref,
    xt_ref, tail_ref, ext_ref, w1_ref, w2_ref, acc_ref, lastb_ref, wb_ref,
    s_in, r_in, s_last, r_last, s_out, r_out, s_up, r_up, s_line, r_line, s_swap,
    s_xt, r_xt, s_car, r_car, s_fwd, local,
):
    total_rows, width = x_ref.shape
    channels = ib_ref.shape[1]
    blocks = total_rows // SEG
    tp, ctx, dp = lax.axis_index("tp"), lax.axis_index("ctx"), lax.axis_index("dp")
    owners, lines = out_hbm.shape[1], out_hbm.shape[0]
    share = win_ref.shape[2]
    last_share = last_ref.shape[0]
    up_share = up_in.shape[0]

    def cell(i):
        flat = lax.rem(tp * owners + dp + i, owners * lines)
        return flat // owners, lax.rem(flat, owners)

    def owner(i):
        return lax.rem(dp + i, owners)

    def ctx_at(i):
        return lax.rem(ctx + i, 4)

    partners = [spot(ctx=ctx_at(i)) for i in range(1, 4)]
    for i in range(1, owners * lines):
        line, own = cell(i)
        partners.append(spot(tp=line, dp=own))
    barrier, count = signal_all(partners)

    def rows_of(ref, who, size):
        return ref.at[pl.ds(pl.multiple_of(who * size, size), size)]

    low_half = lax.rem(ctx, 2)
    mate = spot(ctx=ctx + 1 - 2 * low_half)

    def in_half(ref, half):
        size = channels // 2
        return ref.at[:, pl.ds(pl.multiple_of(half * size, 16), size)]

    def send_in(i):
        return remote(
            in_half(win_ref, low_half), in_half(wb_ref.at[dp], low_half), s_in.at[0, i], r_in.at[0, dp],
            spot(dp=owner(i)),
        )

    def swap_in(i):
        at = in_half(wb_ref.at[owner(i)], low_half)
        return remote(at, at, s_in.at[1, i], r_in.at[1, owner(i)], mate)

    def got_in(stage, i, half):
        at = in_half(wb_ref.at[owner(i)], half)
        return remote(at, at, s_in.at[0, i], r_in.at[stage, owner(i)], mate)

    def send_last(i):
        return remote(last_ref, lastb_ref.at[dp], s_last.at[i], r_last.at[dp], spot(dp=owner(i)))

    def send_xt(i):
        at = xt_ref.at[ctx]
        return remote(at, at, s_xt.at[i], r_xt.at[ctx], spot(ctx=ctx_at(i)))

    for s in range(blocks):
        tail = x_ref[s * SEG + SEG - 16 : s * SEG + SEG].astype(F32)
        xt_ref[ctx, 2 * s : 2 * s + 2] = tail[14:16]
    pl.semaphore_wait(barrier, count)
    for i in range(1, owners):
        send_in(i).start()
        send_last(i).start()
    for i in range(1, 4):
        send_xt(i).start()
    wb_ref[dp] = win_ref[...]
    lastb_ref[dp] = last_ref[...]

    gain, shift = gain_ref[...].reshape(1, -1), shift_ref[...].reshape(1, -1)

    def norm(s, unused):
        rows = pl.ds(pl.multiple_of(s * SEG, SEG), SEG)
        low_ref[rows] = (normalize(x_ref[rows].astype(F32))[0] * gain + shift).astype(BF16)
        return unused

    lax.fori_loop(0, blocks, norm, 0)
    saves = [pltpu.make_async_copy(low_ref, low_hbm, local.at[1])]
    saves[-1].start()

    units = f1_ref.shape[1]
    length = ft_ref.shape[1]
    extend_weights(w1_ref, f1_ref, f1b_ref)
    extend_weights(w2_ref, f2_ref, f2b_ref)
    freq = freq_ref[...].reshape(1, -1)
    net_ref[...] = jnp.zeros(net_ref.shape, F32)
    angle = lax.dot_general(w1_ref[...] * freq, ft_ref[...], TN, **EXACT_DOT)
    first, net_ref[0, 0:units] = sine_cosine(angle)
    net_ref[1, 0:units] = first
    pad = net_ref.shape[1] - units
    net_ref[1, units:] = jnp.where(lax.broadcasted_iota(jnp.int32, (pad, length), 0) == 0, 1.0, 0.0)
    angle = lax.dot_general(w2_ref[...] * freq, net_ref[1], TN, **EXACT_DOT)
    second, net_ref[2, 0:units] = sine_cosine(angle)
    net_ref[3, 0:units] = second
    saves.append(pltpu.make_async_copy(net_ref, net_hbm, local.at[2]))
    saves[-1].start()
    for i in range(1, owners):
        at = lastb_ref.at[owner(i)]
        remote(at, at, s_last.at[i], r_last.at[owner(i)], spot(dp=owner(i))).wait_recv()
    for o in range(owners):
        lasts_ref[o * last_share : (o + 1) * last_share] = lastb_ref[o].astype(F32)
    raw = lax.dot_general(second, lasts_ref[...], TN, **EXACT_DOT)
    taps_ref[...] = raw * decay(length, channels, tp, channels * lines)
    fh, fl, th, tl = fh_ref[...], fl_ref[...], th_ref, tl_ref
    sign = sign_ref[...]
    for j in range(DEPTH):
        part = taps_ref[j * SEG : (j + 1) * SEG]
        out = mm_split(fh, fl, part)
        re, im = out[:SEG], out[SEG:]
        filt_ref[j, 0] = re
        filt_ref[j, 1] = im
    for j in range(DEPTH - 1, 0, -1):
        first = taps_ref[(j - 1) * SEG : (j - 1) * SEG + 1]
        filt_ref[j, 0] = filt_ref[j, 0] - sign * filt_ref[j - 1, 1]
        filt_ref[j, 1] = filt_ref[j, 1] + sign * (filt_ref[j - 1, 0] - first)
    saves.append(pltpu.make_async_copy(filt_ref, filt_hbm, local.at[3]))
    saves[-1].start()

    def half_of(ref, half):
        size = ref.shape[0] // 2
        return ref.at[pl.ds(pl.multiple_of(half * size, 16), size)]

    def up_half(ref, half):
        size = ref.shape[1] // 2
        return ref.at[:, pl.ds(pl.multiple_of(half * size, size), size)]

    def line_out(i):
        return remote(
            out_in, out_hbm.at[tp, dp], s_line.at[i], r_line.at[tp], spot(tp=lax.rem(tp + i, lines))
        )

    def send_out(i, j):
        return remote(
            half_of(out_in, low_half), half_of(out_hbm.at[tp, dp], low_half), s_out.at[i, j], r_out.at[0, tp, dp],
            spot(dp=owner(i), tp=lax.rem(tp + j, lines)),
        )

    def swap_out(i, line):
        at = half_of(out_hbm.at[line, owner(i)], low_half)
        return remote(at, at, s_swap.at[2, i, line], r_out.at[1, line, owner(i)], mate)

    def send_up(i):
        return remote(
            up_half(up_in, low_half), up_half(rows_of(up_hbm, dp, up_share), low_half), s_up.at[i], r_up.at[0, dp],
            spot(dp=owner(i)),
        )

    def swap_up(i):
        at = up_half(rows_of(up_hbm, owner(i), up_share), low_half)
        return remote(at, at, s_swap.at[0, i, 0], r_up.at[1, owner(i)], mate)

    for i in range(1, owners):
        got_in(0, i, low_half).wait_recv()
        swap_in(i).start()
        send_up(i).start()
        for j in range(lines):
            send_out(i, j).start()
    for i in range(1, lines):
        line_out(i).start()
    for i in range(1, owners):
        got_in(1, i, 1 - low_half).wait_recv()
    for o in range(owners):
        w_ref[:, :, o * share : (o + 1) * share] = wb_ref[o]
    saves.append(pltpu.make_async_copy(w_ref, in_hbm, local.at[4]))
    saves[-1].start()

    for k, (src, dst) in enumerate(
        ((out_in, out_hbm.at[tp, dp]), (up_in, rows_of(up_hbm, dp, up_share)))
    ):
        saves.append(pltpu.make_async_copy(src, dst, local.at[5 + k]))
        saves[-1].start()

    for i in range(1, 4):
        at = xt_ref.at[ctx_at(i)]
        remote(at, at, s_xt.at[i], r_xt.at[ctx_at(i)], spot(ctx=ctx_at(i))).wait_recv()
    tail_ref[...] = jnp.zeros(tail_ref.shape, F32)
    for half in range(2):
        tails = (normalize(xt_ref[half])[0] * gain + shift).astype(BF16)
        for g in range(3):
            value = mm_nt(tails, w_ref[g]) + ib_ref[g : g + 1]
            for s in range(4):
                tail_ref[g, 4 * half + s, 6:8] = value[2 * s : 2 * s + 2]

    def share_block(s, other):
        return remote(
            carried_ref.at[pl.ds(pl.multiple_of(s * SEG, SEG), SEG)], shared_ref.at[4 * ctx + s],
            s_car.at[other, s], r_car.at[ctx, s], spot(ctx=other),
        )

    def forward_block(s, group):
        at = shared_ref.at[4 * group + s]
        return remote(at, at, s_fwd.at[s], r_car.at[group, s], spot(ctx=5 - ctx))

    def mix(s, unused):
        rows = pl.ds(pl.multiple_of(s * SEG, SEG), SEG)
        parent = par_ref[0, ctx * blocks + s]
        slot = jnp.where(parent >= 0, parent, 8)
        out = []
        for g in range(3):
            projected = mm_nt(low_ref[rows], w_ref[g]) + ib_ref[g : g + 1]
            proj_ref[g, rows] = projected
            head = tail_ref[g, slot]
            head_ref[g, s] = head
            ext_ref[g, 0:HEADS] = head
            ext_ref[g, HEADS : HEADS + SEG] = projected
            mixed = (
                sw_ref[g, 0:1] * ext_ref[g, HEADS - 2 : HEADS - 2 + SEG]
                + sw_ref[g, 1:2] * ext_ref[g, HEADS - 1 : HEADS - 1 + SEG]
                + sw_ref[g, 2:3] * projected
                + sb_ref[g : g + 1]
            )
            if g == 0:
                gate_ref[rows] = mixed
            else:
                mixed_ref[g - 1, rows] = mixed
            out.append(mixed)
        carried = (out[2] * out[1]).astype(BF16)
        carried_ref[rows] = carried

        @pl.when(ctx == 0)
        def _():
            share_block(s, 2).start()
            share_block(s, 1).start()

        @pl.when(ctx == 1)
        def _():
            share_block(s, 3).start()

        spec = mm(fh_ref[...], carried) + mm(fl_ref[...], carried)
        spec_ref[8 + s, 0] = spec[:SEG]
        spec_ref[8 + s, 1] = spec[SEG:]
        return unused

    lax.fori_loop(0, blocks, mix, 0)
    for k, (src, dst) in enumerate(((proj_ref, proj_hbm), (head_ref, head_hbm), (mixed_ref, mixed_hbm))):
        saves.append(pltpu.make_async_copy(src, dst, local.at[8 + k]))
        saves[-1].start()

    def spectrum(slot, part):
        out = mm(fh_ref[...], part) + mm(fl_ref[...], part)
        spec_ref[slot, 0] = out[:SEG]
        spec_ref[slot, 1] = out[SEG:]

    spec_ref[12] = jnp.zeros(spec_ref.shape[1:], F32)

    def arrived(group, s):
        at = shared_ref.at[4 * group + s]
        return remote(at, at, s_fwd.at[s], r_car.at[group, s], spot(ctx=ctx_at(1)))

    def copy_own(group):
        def one(s, unused):
            spec_ref[4 * group + s] = spec_ref[8 + s]
            return unused

        lax.fori_loop(0, 4, one, 0)

    def receive(group):
        def one(s, unused):
            arrived(group, s).wait_recv()
            spectrum(4 * group + s, shared_ref[4 * group + s])
            return unused

        lax.fori_loop(0, 4, one, 0)

    def receive_forward(group):
        def one(s, unused):
            arrived(group, s).wait_recv()
            forward_block(s, group).start()
            spectrum(4 * group + s, shared_ref[4 * group + s])
            return unused

        lax.fori_loop(0, 4, one, 0)

    @pl.when(ctx == 0)
    def _():
        copy_own(0)

    @pl.when(ctx == 1)
    def _():
        copy_own(1)
        receive(0)

    @pl.when(ctx == 2)
    def _():
        receive_forward(0)
        receive(1)

    @pl.when(ctx == 3)
    def _():
        receive_forward(1)
        receive(0)

    saves.append(pltpu.make_async_copy(spec_ref, spec_hbm, local.at[11]))
    saves[-1].start()

    def dest(s, unused):
        above = lineage(par_ref, ctx * blocks + s)
        places = [8 + s] + [jnp.where(a >= 0, a, 12) for a in above]
        blend_all(acc_ref, [(filt_ref.at[d], spec_ref.at[places[d]]) for d in range(DEPTH)], False)
        long_out = unpack_spectrum(th, tl, acc_ref) * (1.0 / SEG)
        place = pl.ds(pl.multiple_of(s * SEG, SEG), SEG)
        convolved = long_out + skip_ref[...].reshape(1, -1) * carried_ref[place].astype(F32)
        conv_ref[place] = convolved
        gated_ref[place] = (convolved * gate_ref[place]).astype(BF16)
        return unused

    lax.fori_loop(0, blocks, dest, 0)

    def take_halves(stage, half):
        for i in range(1, owners):
            who = owner(i)
            at = up_half(rows_of(up_hbm, who, up_share), half)
            remote(at, at, s_up.at[i], r_up.at[stage, who], mate).wait_recv()
            if stage == 0:
                swap_up(i).start()
            for line in range(lines):
                at = half_of(out_hbm.at[line, who], half)
                remote(at, at, s_out.at[i, line], r_out.at[stage, line, who], mate).wait_recv()
                if stage == 0:
                    swap_out(i, line).start()

    take_halves(0, low_half)

    for save in saves:
        save.wait()
    take_halves(1, 1 - low_half)
    for i in range(1, owners):
        send_in(i).wait_send()
        swap_in(i).wait_send()
        send_last(i).wait_send()
        send_up(i).wait_send()
        swap_up(i).wait_send()
        for j in range(lines):
            send_out(i, j).wait_send()
            swap_out(i, j).wait_send()
    for i in range(1, lines):
        line_out(i).wait_send()
        line = lax.rem(tp + i, lines)
        at = out_hbm.at[line, dp]
        remote(at, at, s_line.at[i], r_line.at[line], mate).wait_recv()
    for i in range(1, 4):
        send_xt(i).wait_send()

    @pl.when(ctx == 0)
    def _():
        for s in range(blocks):
            share_block(s, 2).wait_send()
            share_block(s, 1).wait_send()

    @pl.when(ctx == 1)
    def _():
        for s in range(blocks):
            share_block(s, 3).wait_send()

    @pl.when(ctx == 2)
    def _():
        for s in range(blocks):
            forward_block(s, 0).wait_send()

    @pl.when(ctx == 3)
    def _():
        for s in range(blocks):
            forward_block(s, 1).wait_send()


class OwnerSum:
    scratch_count = 17

    @staticmethod
    def scratch(owners, shape):
        many = max(owners - 1, 1)
        return [
            pltpu.VMEM((owners,) + shape, BF16),
            pltpu.VMEM((owners,) + shape, BF16),
            pltpu.VMEM((many,) + shape, BF16),
            pltpu.VMEM(shape, BF16),
            pltpu.VMEM(shape, BF16),
            pltpu.SemaphoreType.DMA,
            pltpu.SemaphoreType.DMA,
            pltpu.SemaphoreType.DMA,
            pltpu.SemaphoreType.DMA((many,)),
            pltpu.SemaphoreType.DMA((many,)),
            pltpu.SemaphoreType.DMA,
            pltpu.SemaphoreType.DMA,
            pltpu.SemaphoreType.DMA,
            pltpu.SemaphoreType.DMA,
            pltpu.SemaphoreType.DMA((2,)),
            pltpu.VMEM((2,) + shape, F32),
        ]

    def __init__(self, stage, out, scratch):
        self.stage, self.out, self.result = stage, out, scratch[-1]
        self.recv, self.keep, self.parts, self.y_own, self.y_in = scratch[:5]
        self.sems = scratch[5:-1]
        self.owners = stage.shape[1]
        self.dp, ctx = lax.axis_index("dp"), lax.axis_index("ctx")
        self.low = lax.rem(ctx, 2)
        self.mate = spot(ctx=ctx + 1 - 2 * self.low)
        self.across = spot(ctx=lax.rem(ctx + 2, 4))

    def load(self):
        return pltpu.make_async_copy(self.stage.at[self.low], self.keep, self.sems[0])

    def to_mate(self):
        return remote(self.stage.at[1 - self.low], self.recv, self.sems[1], self.sems[2], self.mate)

    def to_owner(self, i):
        owner = lax.rem(self.dp + i, self.owners)
        return remote(
            self.keep.at[owner], self.parts.at[self.owners - 1 - i], self.sems[3].at[i - 1],
            self.sems[4].at[self.owners - 1 - i], spot(dp=owner),
        )

    def from_owner(self, i):
        return remote(self.parts.at[i - 1], self.parts.at[i - 1], self.sems[3].at[i - 1], self.sems[4].at[i - 1], self.mate)

    def to_across(self):
        return remote(self.y_own, self.y_in, self.sems[5], self.sems[6], self.across)

    def to_back(self):
        at = self.result.at[self.low]
        return remote(at, at, self.sems[7], self.sems[8], self.mate)

    def save(self, half):
        return pltpu.make_async_copy(self.result.at[half], self.out.at[half], self.sems[9].at[half])

    def begin(self):
        self.to_mate().start()
        self.load().start()

    def pair(self):
        self.load().wait()
        self.to_mate().wait_recv()
        for o in range(self.owners):
            self.keep[o] = (self.keep[o].astype(F32) + self.recv[o].astype(F32)).astype(BF16)
        for i in range(1, self.owners):
            self.to_owner(i).start()

    def own(self):
        total = self.keep[self.dp].astype(F32)
        for i in range(1, self.owners):
            self.from_owner(i).wait_recv()
            total = total + self.parts[i - 1].astype(F32)
        self.y_own[...] = total.astype(BF16)
        self.to_across().start()

    def cross(self):
        self.to_across().wait_recv()
        self.result[self.low] = self.y_own[...].astype(F32) + self.y_in[...].astype(F32)
        self.to_back().start()
        self.save(self.low).start()

    def whole(self):
        at = self.result.at[1 - self.low]
        remote(at, at, self.sems[7], self.sems[8], self.mate).wait_recv()
        self.save(1 - self.low).start()

    def finish(self):
        self.to_mate().wait_send()
        for i in range(1, self.owners):
            self.to_owner(i).wait_send()
        self.to_across().wait_send()
        self.to_back().wait_send()
        self.save(self.low).wait()
        self.save(1 - self.low).wait()


class SmallSum:
    @staticmethod
    def scratch(count, shape):
        return [
            pltpu.VMEM((count,) + shape, F32),
            pltpu.SemaphoreType.DMA((count,)),
            pltpu.SemaphoreType.DMA((count,)),
        ]

    def __init__(self, axis, scratch):
        self.axis = axis
        self.slots, self.send, self.recv = scratch
        self.count = self.slots.shape[0]
        self.me = lax.axis_index(axis)

    def copy(self, i):
        at = self.slots.at[self.me]
        other = lax.rem(self.me + i, self.count)
        return remote(at, at, self.send.at[i], self.recv.at[self.me], spot(**{self.axis: other}))

    def start(self, value):
        self.slots[self.me] = value
        for i in range(1, self.count):
            self.copy(i).start()

    def total(self):
        for i in range(1, self.count):
            other = lax.rem(self.me + i, self.count)
            at = self.slots.at[other]
            remote(at, at, self.send.at[i], self.recv.at[other], spot(**{self.axis: lax.rem(self.me + i, self.count)})).wait_recv()
        out = self.slots[0]
        for i in range(1, self.count):
            out = out + self.slots[i]
        return out

    def finish(self):
        for i in range(1, self.count):
            self.copy(i).wait_send()


def back_kernel(
    par_ref, gated_ref, dpart_ref, fgain_ref,
    fh_ref, fl_ref, th_ref, tl_ref, sign_ref, sw_ref, skip_ref,
    ft_ref, f1_ref, f1b_ref, f2_ref, f2b_ref, freq_ref, last_ref, small_ref,
    npart_hbm, resid_hbm, g_hbm, gate_hbm, conv_hbm, carried_hbm, out_hbm,
    mixed_hbm, low_hbm, w_hbm, x_hbm, proj_hbm, head_hbm, spec_hbm, filt_hbm, net_hbm, sup_hbm, sdown_hbm,
    dres_hbm, dsum_ref, psum_ref, oup_ref, odown_ref, oout_ref, oin_ref, va_ref, vd_ref, vl_ref, vf_ref,
    dall_ref, dconv_ref, dzero_ref, stage_out, s_long, r_long,
    yown_ref, dcar_ref, dtaps_ref, stage_in, ppart_ref, w1_ref, w2_ref,
    mixed_ref, hd_ref, s_hd, r_hd, local, *rest,
):
    total_rows, width = ppart_ref.shape
    channels = dconv_ref.shape[1]
    blocks = total_rows // SEG
    owners = sup_hbm.shape[1]
    ctx, tp, dp = lax.axis_index("ctx"), lax.axis_index("tp"), lax.axis_index("dp")
    rest = list(rest)

    def take(n):
        out = rest[:n]
        del rest[:n]
        return out

    down = LineSum(dpart_ref, dsum_ref, take(11))
    proj = LineSum(ppart_ref, psum_ref, take(11))
    early = [OwnerSum(s, o, take(16)) for s, o in ((sup_hbm, oup_ref), (sdown_hbm, odown_ref), (stage_out, oout_ref))]
    late = OwnerSum(stage_in, oin_ref, take(16))
    a_ctx, a_dp = SmallSum("ctx", take(3)), SmallSum("dp", take(3))
    d_ctx, d_dp, d_tp = SmallSum("ctx", take(3)), SmallSum("dp", take(3)), SmallSum("tp", take(3))
    l_ctx, l_dp = SmallSum("ctx", take(3)), SmallSum("dp", take(3))
    f_ctx, f_dp, f_tp = SmallSum("ctx", take(3)), SmallSum("dp", take(3)), SmallSum("tp", take(3))

    partners = [spot(tp=lax.rem(tp + i, 4)) for i in range(1, 4)]
    partners += [spot(ctx=lax.rem(ctx + i, 4)) for i in range(1, 4)]
    partners += [spot(dp=lax.rem(dp + i, owners)) for i in range(1, owners)]
    barrier, count = signal_all(partners)
    load_part = pltpu.make_async_copy(npart_hbm, ppart_ref, local.at[10])
    load_mixed = pltpu.make_async_copy(mixed_hbm, mixed_ref, local.at[11])
    load_part.start()
    load_part.wait()
    pl.semaphore_wait(barrier, count)
    for s in range(blocks):
        proj.send_block(s)
    load_mixed.start()
    for job in early[:2]:
        job.begin()
    va_ref[...] = jnp.zeros(va_ref.shape, F32)
    vd_ref[...] = small_ref[...]
    fh, fl, th, tl = fh_ref[...], fl_ref[...], th_ref, tl_ref
    skip = skip_ref[...].reshape(1, -1)
    scale = 1.0 / SEG

    def put(dst, value):
        dst[0] = value[:SEG] * scale
        dst[1] = value[SEG:] * scale

    def half_rows(h):
        return pl.ds(pl.multiple_of(h * HALF, HALF), HALF)

    def half_of(who, h):
        return dall_ref.at[who * blocks + h // 2, half_rows(lax.rem(h, 2))]

    def long_to(h, other):
        at = half_of(ctx, h)
        return remote(at, at, s_long.at[other, h], r_long.at[ctx, h], spot(ctx=other))

    def long_from(other):
        def one(h, unused):
            at = half_of(other, h)
            remote(at, at, s_long.at[other, h], r_long.at[other, h], spot(ctx=lax.rem(ctx + 1, 4))).wait_recv()
            return unused

        lax.fori_loop(0, 2 * blocks, one, 0)

    def feed_back(in_ref, g_ref, dres_ref, gate_ref, conv_ref, carried_ref, parts_ref, out_ref, gout_ref):
        once = [
            pltpu.make_async_copy(src, dst, local.at[k])
            for k, (src, dst) in enumerate(
                ((gate_hbm, gate_ref), (conv_hbm, conv_ref), (carried_hbm, carried_ref), (out_hbm.at[tp], parts_ref))
            )
        ]
        for load in once:
            load.start()

        def fetch(h):
            slot = lax.rem(h, 2)
            return (
                pltpu.make_async_copy(resid_hbm.at[half_rows(h)], in_ref.at[slot], local.at[4 + slot]),
                pltpu.make_async_copy(g_hbm.at[half_rows(h)], g_ref.at[slot], local.at[6 + slot]),
            )

        def save(h):
            slot = lax.rem(h, 2)
            return pltpu.make_async_copy(dres_ref.at[slot], dres_hbm.at[half_rows(h)], local.at[8 + slot])

        for load in fetch(0):
            load.start()
        for load in once:
            load.wait()
        share = width // owners
        for o in range(owners):
            out_ref[:, o * share : (o + 1) * share] = parts_ref[o]
        gout_ref[...] = jnp.zeros(gout_ref.shape, F32)
        gain = fgain_ref[...].reshape(1, -1)
        proj.steps(0, PER)

        def one(h, unused):
            rows = half_rows(h)
            slot = lax.rem(h, 2)
            for load in fetch(h):
                load.wait()

            @pl.when(h + 1 < 2 * blocks)
            def _():
                for load in fetch(h + 1):
                    load.start()

            xhat, spread = normalize(in_ref[slot])
            proj.steps(PER + h * PER // 2, PER + (h + 1) * PER // 2)
            proj.wait_half(h)

            @pl.when(h == 1)
            def _():
                for job in early[:2]:
                    job.pair()

            @pl.when(h == 2 * blocks - 3)
            def _():
                for b in range(blocks):
                    down.send_block(b)

            dn = psum_ref[rows].astype(F32)
            e = dn * gain
            d_res = g_ref[slot].astype(F32) + spread * (
                e - jnp.mean(e, axis=-1, keepdims=True) - xhat * jnp.mean(e * xhat, axis=-1, keepdims=True)
            )
            d_mix = d_res.astype(BF16)
            d_gated = mm_nt(d_mix, out_ref[...])
            d_conv = d_gated * gate_ref[rows]
            dall_ref[ctx * blocks + h // 2, half_rows(lax.rem(h, 2))] = d_conv.astype(BF16)
            for other in range(2):
                @pl.when(other < ctx)
                def _():
                    long_to(h, other).start()

            @pl.when(h >= 2)
            def _():
                save(h - 2).wait()

            dres_ref[slot] = d_res
            save(h).start()
            dconv_ref[rows] = d_conv
            dzero_ref[rows] = d_gated * conv_ref[rows]

            @pl.when(lax.rem(h, 2) == 1)
            def _():
                part = dall_ref[ctx * blocks + h // 2]
                put(yown_ref.at[h // 2], mm(fh, part) + mm(fl, part))

            vd_ref[2:3] += jnp.sum(dn * xhat, axis=0, keepdims=True)
            vd_ref[3:4] += jnp.sum(dn, axis=0, keepdims=True)
            vd_ref[1:2] += jnp.sum(d_mix.astype(F32), axis=0, keepdims=True)
            va_ref[15:16] += jnp.sum(d_conv * carried_ref[rows].astype(F32), axis=0, keepdims=True)
            gout_ref[...] += mm_tn(gated_ref[rows], d_mix)
            return unused

        lax.fori_loop(0, 2 * blocks, one, 0)
        half = stage_out.shape[2]
        for t in range(2):
            store_columns(stage_out, t, gout_ref[t * half : (t + 1) * half])
        save(2 * blocks - 2).wait()
        save(2 * blocks - 1).wait()

    pl.run_scoped(
        feed_back,
        pltpu.VMEM((2, HALF, width), F32),
        pltpu.VMEM((2, HALF, width), BF16),
        pltpu.VMEM((2, HALF, width), F32),
        pltpu.VMEM((total_rows, channels), F32),
        pltpu.VMEM((total_rows, channels), F32),
        pltpu.VMEM((total_rows, channels), BF16),
        pltpu.VMEM((owners, channels, width // owners), BF16),
        pltpu.VMEM((channels, width), BF16),
        pltpu.VMEM((channels, width), F32),
    )
    early[2].begin()
    down.steps(0, 3)

    def to_ctx(i):
        at = hd_ref.at[pl.ds(ctx * blocks, blocks)]
        return remote(at, at, s_hd.at[i], r_hd.at[ctx], spot(ctx=lax.rem(ctx + i, 4)))

    def conv_inputs(filt_ref, more_ref, acc_ref):
        load = pltpu.make_async_copy(filt_hbm, filt_ref, local.at[0])
        load.start()

        load.wait()
        load_mixed.wait()

        def leaf_sum(match):
            total = None
            for leaf in range(8, 16):
                term = jnp.where(match(leaf), 1.0, 0.0) * dall_ref[leaf].astype(F32)
                total = term if total is None else total + term
            return total

        def from_leaf(b):
            return lambda leaf: par_ref[0, leaf] == b

        def finish(s, terms):
            blend_all(acc_ref.at[s], terms, True)

        @pl.when(ctx == 0)
        def _():
            for other in (1, 2, 3):
                long_from(other)

            def gather(k, unused):
                p = k + 1
                total = None
                for b in range(4, 8):
                    term = jnp.where(par_ref[0, b] == p, 1.0, 0.0) * dall_ref[b].astype(F32)
                    total = term if total is None else total + term
                put(more_ref.at[k], mm_split(fh, fl, total))
                total = leaf_sum(lambda leaf: par_ref[0, par_ref[0, leaf]] == p)
                put(more_ref.at[3 + k], mm_split(fh, fl, total))
                return unused

            lax.fori_loop(0, 3, gather, 0)
            for a in range(4):
                terms = [(filt_ref.at[s - a], yown_ref.at[s]) for s in range(a, 4)]
                for p in range(max(a, 1), 4):
                    terms.append((filt_ref.at[p - a + 1], more_ref.at[p - 1]))
                    terms.append((filt_ref.at[p - a + 2], more_ref.at[p + 2]))
                finish(a, terms)

        @pl.when(ctx == 1)
        def _():
            for other in (2, 3):
                long_from(other)

            def one(b, unused):
                put(more_ref.at[0], mm_split(fh, fl, leaf_sum(from_leaf(b + 4))))
                finish(b, [(filt_ref.at[0], yown_ref.at[b]), (filt_ref.at[1], more_ref.at[0])])
                return unused

            lax.fori_loop(0, 4, one, 0)

        @pl.when(ctx > 1)
        def _():
            def one(b, unused):
                finish(b, [(filt_ref.at[0], yown_ref.at[b])])
                return unused

            lax.fori_loop(0, 4, one, 0)

        down.steps(3, 5)
        for s in range(blocks):
            top = slice(s * SEG, s * SEG + HEADS)
            d_car = unpack_spectrum(th.at[0:16], tl.at[0:16], acc_ref.at[s])[0:HEADS] + skip * dconv_ref[top]
            rows = [dzero_ref[top], d_car * mixed_ref[1, top], d_car * mixed_ref[0, top]]
            for g in range(3):
                hd_ref[ctx * blocks + s, 2 * g : 2 * g + 2] = rows[g][0:2]
            hd_ref[ctx * blocks + s, 6:8] = jnp.zeros((2, channels), F32)
        for i in range(1, 4):
            to_ctx(i).start()

        def whole(s, unused):
            place = pl.ds(pl.multiple_of(s * SEG, SEG), SEG)
            dcar_ref[place] = unpack_spectrum(th, tl, acc_ref.at[s]) + skip * dconv_ref[place]
            return unused

        lax.fori_loop(0, blocks, whole, 0)

    def mix_stage(low_ref, w_ref, x_ref):
        loads = [
            pltpu.make_async_copy(src, dst, local.at[4 + k])
            for k, (src, dst) in enumerate(((w_hbm, w_ref), (x_hbm, x_ref), (low_hbm, low_ref)))
        ]
        for load in loads:
            load.start()
        pl.run_scoped(
            conv_inputs,
            pltpu.VMEM((DEPTH, 2, SEG, channels), F32),
            pltpu.VMEM((6, 2, SEG, channels), F32),
            pltpu.VMEM((blocks, 2, SEG, channels), F32),
        )

        down.steps(5, 7)
        proj.drain()
        for i in range(1, 4):
            other = lax.rem(ctx + i, 4)
            at = hd_ref.at[pl.ds(other * blocks, blocks)]
            remote(at, at, s_hd.at[i], r_hd.at[other], spot(ctx=other)).wait_recv()

        def mix_back(dp_ref, ext_ref, dm_ref, pin_ref, hin_ref):
            load_heads = pltpu.make_async_copy(head_hbm, hin_ref, local.at[1])
            load_heads.start()

            def fetch(s):
                rows = pl.ds(pl.multiple_of(s * SEG, SEG), SEG)
                return pltpu.make_async_copy(proj_hbm.at[:, rows], pin_ref.at[lax.rem(s, 2)], local.at[2 + lax.rem(s, 2)])

            fetch(0).start()
            load_heads.wait()
            for load in loads:
                load.wait()

            def one(s, unused):
                rows = pl.ds(pl.multiple_of(s * SEG, SEG), SEG)
                slot = lax.rem(s, 2)
                fetch(s).wait()

                @pl.when(s + 1 < blocks)
                def _():
                    fetch(s + 1).start()

                mine = ctx * blocks + s
                child = None
                for b in range(1, 16):
                    term = jnp.where(par_ref[0, b] == mine, 1.0, 0.0) * hd_ref[b]
                    child = term if child is None else child + term
                part = None
                for g in range(3):
                    if g == 0:
                        dm = dzero_ref[rows]
                    else:
                        dm = dcar_ref[rows] * mixed_ref[2 - g, rows]
                    ext_ref[0:HEADS] = hin_ref[g, s]
                    ext_ref[HEADS : HEADS + SEG] = pin_ref[slot, g]
                    for k in range(3):
                        piece = ext_ref[HEADS - 2 + k : HEADS - 2 + k + SEG]
                        va_ref[3 * g + k : 3 * g + k + 1] += jnp.sum(piece * dm, axis=0, keepdims=True)
                    va_ref[12 + g : 13 + g] += jnp.sum(dm, axis=0, keepdims=True)
                    dm_ref[0:SEG] = dm
                    dm_ref[SEG : SEG + 2] = child[2 * g : 2 * g + 2]
                    d_proj = (
                        sw_ref[g, 2:3] * dm
                        + sw_ref[g, 1:2] * dm_ref[1 : 1 + SEG]
                        + sw_ref[g, 0:1] * dm_ref[2 : 2 + SEG]
                    ).astype(BF16)
                    dp_ref[g, rows] = d_proj
                    va_ref[9 + g : 10 + g] += jnp.sum(d_proj.astype(F32), axis=0, keepdims=True)
                    term = mm(d_proj, w_ref[g])
                    part = term if part is None else part + term
                ppart_ref[rows] = part.astype(BF16)
                proj.send_block(s)
                xhat = normalize(x_ref[rows].astype(F32))[0]
                vd_ref[4:5] += jnp.sum(part * xhat, axis=0, keepdims=True)
                vd_ref[5:6] += jnp.sum(part, axis=0, keepdims=True)
                down.steps(7 + s, 8 + s)
                return unused

            lax.fori_loop(0, blocks, one, 0)
            rows = stage_in.shape[3]
            for g in range(3):
                value = mm_tn(dp_ref[g], low_ref[...])
                for t in range(2):
                    store_columns(stage_in.at[:, :, g], t, value[t * rows : (t + 1) * rows])

        pl.run_scoped(
            mix_back,
            pltpu.VMEM((3, total_rows, channels), BF16),
            pltpu.VMEM((HEADS + SEG, channels), F32),
            pltpu.VMEM((HEADS + SEG, channels), F32),
            pltpu.VMEM((2, 3, SEG, channels), F32),
            pltpu.VMEM((3, blocks, HEADS, channels), F32),
        )
    pl.run_scoped(
        mix_stage,
        pltpu.VMEM((total_rows, width), BF16),
        pltpu.VMEM((3, channels, width), BF16),
        pltpu.VMEM((total_rows, width), BF16),
    )
    a_ctx.start(va_ref[...])
    d_ctx.start(vd_ref[...])
    late.begin()
    early[2].pair()
    for job in early[:2]:
        job.own()

    def with_spectra(spec_ref):
        load_spectra = pltpu.make_async_copy(spec_hbm, spec_ref, local.at[0])
        load_spectra.start()
        down.steps(11, 13)

        def conv_filters(dfilt_ref):
            load_spectra.wait()

            @pl.when(ctx == 0)
            def _():
                for d in range(4):
                    blend_all(dfilt_ref.at[d], [(spec_ref.at[8 + s - d], yown_ref.at[s]) for s in range(d, 4)], True)
                dfilt_ref[4:6] = jnp.zeros((2, 2, SEG, channels), F32)

            @pl.when(ctx > 0)
            def _():
                places = []
                for s in range(blocks):
                    above = lineage(par_ref, ctx * blocks + s)
                    places.append([8 + s] + [jnp.where(a >= 0, a, 12) for a in above])
                for d in range(DEPTH):
                    terms = [(spec_ref.at[places[s][d]], yown_ref.at[s]) for s in range(blocks)]
                    blend_all(dfilt_ref.at[d], terms, True)

            down.steps(13, 14)
            sign = sign_ref[...]
            first_row = lax.broadcasted_iota(jnp.int32, (SEG, 1), 0) == 0
            for j in range(DEPTH):
                fix = None
                if j + 1 < DEPTH:
                    nr, ni = dfilt_ref[j + 1, 0], dfilt_ref[j + 1, 1]
                    fix = jnp.sum(sign * ni, axis=0, keepdims=True)
                    dfilt_ref[j, 0] = dfilt_ref[j, 0] + sign * ni
                    dfilt_ref[j, 1] = dfilt_ref[j, 1] - sign * nr
                taps = unpack_spectrum(th, tl, dfilt_ref.at[j])
                if fix is not None:
                    taps = jnp.where(first_row, taps - fix, taps)
                dtaps_ref[j * SEG : (j + 1) * SEG] = taps

        pl.run_scoped(conv_filters, pltpu.VMEM((DEPTH, 2, SEG, channels), F32))

    pl.run_scoped(with_spectra, pltpu.VMEM((13, 2, SEG, channels), F32))
    down.steps(14, 16)

    def filter_back(net_ref):
        load = pltpu.make_async_copy(net_hbm, net_ref, local.at[1])
        load.start()
        d_raw = dtaps_ref[...] * decay(DEPTH * SEG, channels, tp, width)
        extend_weights(w1_ref, f1_ref, f1b_ref)
        extend_weights(w2_ref, f2_ref, f2b_ref)
        freq = freq_ref[...].reshape(1, -1)
        load.wait()
        units = last_ref.shape[0]
        l_ctx.start(jnp.dot(net_ref[3, 0:units], d_raw, **EXACT_DOT))
        s_two = lax.dot_general(last_ref[...], d_raw, NT, **EXACT_DOT) * net_ref[2, 0:units]
        g_two = lax.dot_general(net_ref[1], s_two, NT, **EXACT_DOT)
        d_one = jnp.dot(w2_ref[...] * freq, s_two, **EXACT_DOT)[0:units]
        g_one = lax.dot_general(ft_ref[...], d_one * net_ref[0, 0:units], NT, **EXACT_DOT)
        g_freq = jnp.sum(w1_ref[...] * g_one, axis=0, keepdims=True) + jnp.sum(
            w2_ref[...] * g_two, axis=0, keepdims=True
        )
        vf_ref[...] = jnp.zeros(vf_ref.shape, F32)
        vf_ref[0 : g_one.shape[0], 0:units] = g_one * freq
        vf_ref[0 : g_two.shape[0], units : 2 * units] = g_two * freq
        vf_ref[g_two.shape[0] : g_two.shape[0] + 1, 0:units] = g_freq
        f_ctx.start(vf_ref[...])

    pl.run_scoped(filter_back, pltpu.VMEM(net_hbm.shape, F32))

    def first_cross():
        for job in early[:2]:
            job.cross()

    def second_own():
        early[2].own()
        late.pair()

    def second_cross():
        early[2].cross()
        late.own()

    def vectors():
        a_dp.start(a_ctx.total())
        d_dp.start(d_ctx.total())

    def networks():
        l_dp.start(l_ctx.total())
        f_dp.start(f_ctx.total())

    def gains():
        va_ref[...] = a_dp.total()
        sums = d_dp.total()
        vd_ref[...] = sums
        d_tp.start(sums[4:6])

    def last_layer():
        for job in early[:2]:
            job.whole()
        f_tp.start(f_dp.total())
        last_sum = l_dp.total()
        for o in range(owners):
            held = vl_ref.shape[1]
            vl_ref[o] = last_sum[o * held : (o + 1) * held]

    jobs = (second_own, vectors, networks, first_cross, second_cross, gains, last_layer)
    for k, job in enumerate(jobs):
        down.steps(min(16 + k, 20), min(17 + k, 20))
        proj.steps(2 * k, 2 * k + 2)
        job()
    proj.steps(14, 17)
    late.cross()
    early[2].whole()
    proj.steps(17, proj.pairs + 2 * LAG)
    late.whole()
    for s in range(blocks):
        down.wait_block(s)
        proj.wait_block(s)
    vd_ref[4:6] = d_tp.total()
    vf_ref[...] = f_tp.total()
    for job in (a_ctx, a_dp, d_ctx, d_dp, d_tp, l_ctx, l_dp, f_ctx, f_dp, f_tp):
        job.finish()
    for job in early + [late]:
        job.finish()
    for i in range(1, 4):
        to_ctx(i).wait_send()
    for other in range(2):
        @pl.when(other < ctx)
        def _():
            for h in range(2 * blocks):
                long_to(h, other).wait_send()

    down.drain()
    proj.drain()


def final_kernel(
    resid_ref, dsum_ref, dres_ref, psum_ref, x_ref, gain_ref, bias_ref, va_ref, vd_ref, vl_ref, vf_ref,
    oup_ref, odown_ref, oout_ref, oin_ref,
    result_ref, gradx_ref, up_ref, down_ref, out_ref, in_ref,
    mgain_ref, mshift_ref, inb_ref, sw_ref, sb_ref, f1_ref, f1b_ref, f2_ref, f2b_ref, freq_ref, last_ref,
    skip_ref, ob_ref, fgain_ref, fshift_ref, ub_ref, db_ref,
):
    step = pl.program_id(0)

    @pl.when(step == 0)
    def _():
        up_ref[...] = oup_ref[...]
        down_ref[...] = odown_ref[...]
        out_ref[...] = oout_ref[...]
        rows = oin_ref.shape[2]
        for h in range(2):
            in_ref[:, h * rows : (h + 1) * rows] = oin_ref[h]
        mgain_ref[...] = vd_ref[4]
        mshift_ref[...] = vd_ref[5]
        db_ref[...] = vd_ref[0]
        ob_ref[...] = vd_ref[1]
        fgain_ref[...] = vd_ref[2]
        fshift_ref[...] = vd_ref[3]
        ub_ref[...] = vd_ref[6]
        for g in range(3):
            sw_ref[g] = va_ref[3 * g : 3 * g + 3]
        inb_ref[...] = va_ref[9:12]
        sb_ref[...] = va_ref[12:15]
        skip_ref[...] = va_ref[15]
        units = f1_ref.shape[1]
        rows_one, rows_two = f1_ref.shape[0], f2_ref.shape[0]
        f1_ref[...] = vf_ref[0:rows_one, 0:units]
        f1b_ref[...] = vf_ref[rows_one, 0:units]
        f2_ref[...] = vf_ref[0:rows_two, units : 2 * units]
        f2b_ref[...] = vf_ref[rows_two, units : 2 * units]
        freq_ref[...] = vf_ref[rows_two + 8, 0:units]
        last_ref[...] = vl_ref[lax.axis_index("dp")]

    result_ref[...] = resid_ref[...] + dsum_ref[...].astype(F32) + bias_ref[...].reshape(1, -1)
    xhat, spread = normalize(x_ref[...].astype(F32))
    e = psum_ref[...].astype(F32) * gain_ref[...].reshape(1, -1)
    gradx_ref[...] = dres_ref[...] + spread * (
        e - jnp.mean(e, axis=-1, keepdims=True) - xhat * jnp.mean(e * xhat, axis=-1, keepdims=True)
    )


def body(
    block_in, out_grad, parents, mixer_gain, mixer_shift, in_proj, in_bias, short_weight, short_bias,
    filter_one, filter_one_bias, filter_two, filter_two_bias, filter_freq, filter_out, skip_gain,
    out_proj, out_bias, feed_gain, feed_shift, feed_up, feed_up_bias, feed_down, feed_down_bias,
):
    x = block_in[0]
    g = out_grad[0]
    total_rows, width = x.shape
    channels = skip_gain.shape[0]
    blocks = total_rows // SEG
    hidden = feed_up.shape[1]
    tp_count = lax.axis_size("tp")
    tp_index = lax.axis_index("tp")
    owners = lax.axis_size("dp")
    first = lax.axis_index("ctx") * blocks
    all_blocks = parents.shape[1]

    half = hidden // 2
    share = width // owners
    units, features = filter_one.shape[1], filter_one.shape[0]
    feat_rows, mid_rows = 40, units + 8
    length = DEPTH * SEG
    ft = jnp.asarray(filter_features(length, (features - 1) // 2, feat_rows))
    fh, fl, th, tl, sign = (jnp.asarray(t) for t in spectral_constants(SEG))
    dma = pltpu.SemaphoreType.DMA
    front_out = (
        sds((total_rows, width), BF16),
        sds((3, total_rows, channels), F32),
        sds((3, blocks, HEADS, channels), F32),
        sds((2, total_rows, channels), F32),
        sds((13, 2, SEG, channels), F32),
        sds((DEPTH, 2, SEG, channels), F32),
        sds((4, mid_rows, length), F32),
        sds((3, channels, width), BF16),
        sds((tp_count, owners, channels, share), BF16),
        sds((width, hidden), BF16),
        sds((units, channels), F32),
        sds((total_rows, channels), F32),
        sds((total_rows, channels), F32),
        sds((total_rows, channels), BF16),
        sds((total_rows, channels), BF16),
    )
    low, proj, head, mixed, spec, filt, net, in_all, out_all, up_all, last, gate, conv, gated, carried = call(
        front_kernel,
        front_out,
        [SM] + [VM] * 22,
        [
            pltpu.VMEM((3, channels, width), BF16),
            pltpu.VMEM((total_rows, width), BF16),
            pltpu.VMEM((3, total_rows, channels), F32),
            pltpu.VMEM((3, blocks, HEADS, channels), F32),
            pltpu.VMEM((2, total_rows, channels), F32),
            pltpu.VMEM((13, 2, SEG, channels), F32),
            pltpu.VMEM((DEPTH, 2, SEG, channels), F32),
            pltpu.VMEM((4, mid_rows, length), F32),
            pltpu.VMEM((length, channels), F32),
            pltpu.VMEM((8, SEG, channels), BF16),
            pltpu.VMEM((4, 2 * blocks, width), F32),
            pltpu.VMEM((3, 9, HEADS, channels), F32),
            pltpu.VMEM((3, HEADS + SEG, channels), F32),
            pltpu.VMEM((feat_rows, units), F32),
            pltpu.VMEM((mid_rows, units), F32),
            pltpu.VMEM((2, SEG, channels), F32),
            pltpu.VMEM((owners,) + filter_out.shape, BF16),
            pltpu.VMEM((owners, 3, channels, share), BF16),
            dma((2, owners)), dma((2, owners)), dma((owners,)), dma((owners,)),
            dma((owners, tp_count)), dma((2, tp_count, owners)),
            dma((owners,)), dma((2, owners)),
            dma((tp_count,)), dma((tp_count,)), dma((3, owners, tp_count)),
            dma((4,)), dma((4,)), dma((4, 4)), dma((4, 4)), dma((4,)), dma((12,)),
        ],
        1,
        out_specs=(HB,) * 10 + (VM,) * 5,
    )(
        parents, x, jnp.transpose(in_proj, (1, 2, 0)), filter_out, out_proj, feed_up, ft,
        filter_one, filter_one_bias, filter_two, filter_two_bias, filter_freq, mixer_gain, mixer_shift,
        in_bias, short_weight, short_bias, skip_gain, fh, fl, th, tl, sign,
    )

    piece = share // 2
    feed_big = [
        sds((total_rows, width), F32),
        sds((total_rows, width), BF16),
        sds((total_rows, width), BF16),
        sds((2, owners, piece, hidden), BF16),
        sds((2, owners, half, share), BF16),
    ]
    feed_in = (out_all, x, g, up_all)

    def held(v):
        return pltpu.VMEM(v.shape, v.dtype)

    residual, norm_part, down_part, stage_up, stage_down, small = call(
        feed_kernel,
        feed_big + [sds((8, width), F32)],
        [VM] * 6 + [HB] * 4,
        [held(v) for v in feed_in]
        + [held(v) for v in feed_big]
        + [dma((4,)), dma((2,)), dma((3, blocks)), pltpu.VMEM((owners, hidden, share), BF16)]
        + [dma((2, owners)), dma((2, owners))]
        + [
            pltpu.VMEM((width, hidden), F32),
            pltpu.VMEM((hidden, width), F32),
            pltpu.VMEM((tp_count, total_rows, channels), BF16),
            pltpu.VMEM((tp_count, channels, width), BF16),
            pltpu.VMEM((hidden, width), BF16),
            dma((tp_count, blocks)), dma((tp_count, blocks)),
        ],
        2,
        out_specs=(HB,) * 5 + (VM,),
    )(gated, out_bias, feed_gain, feed_shift, feed_up_bias, feed_down, *feed_in)

    shapes = [(piece, hidden), (half, share), (channels // 2, share), (3, channels // 2, share)]
    scratch = [
        pltpu.VMEM((all_blocks, SEG, channels), BF16),
        pltpu.VMEM((total_rows, channels), F32),
        pltpu.VMEM((total_rows, channels), F32),
        pltpu.VMEM((2, owners) + shapes[2], BF16),
        dma((4, 2 * blocks)), dma((4, 2 * blocks)),
        pltpu.VMEM((blocks, 2, SEG, channels), F32),
        pltpu.VMEM((total_rows, channels), F32),
        pltpu.VMEM((length, channels), F32),
        pltpu.VMEM((2, owners) + shapes[3], BF16),
        pltpu.VMEM((total_rows, width), BF16),
        pltpu.VMEM((feat_rows, units), F32),
        pltpu.VMEM((mid_rows, units), F32),
        held(mixed),
        pltpu.VMEM((all_blocks, HEADS, channels), F32),
        dma((4,)), dma((4,)), dma((12,)),
    ]
    scratch += LineSum.scratch(total_rows, width) * 2
    for shape in shapes:
        scratch += OwnerSum.scratch(owners, shape)
    smalls = ((16, channels), (8, width), (units, channels), (mid_rows + 8, 2 * units))
    for counts, shape in (
        ((4, owners), smalls[0]), ((4, owners), smalls[1]), ((tp_count,), (2, width)), ((4, owners), smalls[2]),
        ((4, owners, tp_count), smalls[3]),
    ):
        for count in counts:
            scratch += SmallSum.scratch(count, shape)
    d_res, down_sum, proj_sum, own_up, own_down, own_out, own_in, va, vd, vl, vf = call(
        back_kernel,
        (
            sds((total_rows, width), F32),
            sds((total_rows, width), BF16),
            sds((total_rows, width), BF16),
        )
        + tuple(sds((2,) + shape, F32) for shape in shapes)
        + (
            sds(smalls[0], F32),
            sds(smalls[1], F32),
            sds((owners,) + filter_out.shape, F32),
            sds(smalls[3], F32),
        ),
        [SM] + [VM] * 18 + [HB] * 18,
        scratch,
        3,
        out_specs=(HB, VM, VM, HB, HB, HB, HB, VM, VM, VM, VM),
    )(
        parents, gated, down_part, feed_gain, fh, fl, th, tl, sign, short_weight,
        skip_gain, ft, filter_one, filter_one_bias, filter_two, filter_two_bias, filter_freq, last, small,
        norm_part, residual, g, gate, conv, carried, out_all, mixed, low, in_all, x, proj, head, spec, filt, net, stage_up, stage_down,
    )

    def by_block(*shape):
        return pl.BlockSpec((2 * SEG,) + shape, lambda i: (i,) + (0,) * len(shape))

    def whole(v):
        return pl.BlockSpec(v.shape, lambda i: (0,) * len(v.shape))

    wide = by_block(width)
    vectors = [
        sds(v.shape, F32)
        for v in (
            mixer_gain, mixer_shift, in_bias, short_weight, short_bias, filter_one, filter_one_bias, filter_two,
            filter_two_bias, filter_freq, filter_out, skip_gain, out_bias, feed_gain, feed_shift, feed_up_bias,
            feed_down_bias,
        )
    ]
    out = pl.pallas_call(
        final_kernel,
        grid=(blocks // 2,),
        out_shape=[
            sds((total_rows, width), F32), sds((total_rows, width), F32), own_up, own_down, own_out,
            sds((3, channels, share), F32),
        ]
        + vectors,
        in_specs=[wide] * 5 + [whole(v) for v in (mixer_gain, feed_down_bias, va, vd, vl, vf, own_up, own_down, own_out, own_in)],
        out_specs=[wide, wide]
        + [whole(v) for v in (own_up, own_down, own_out, sds((3, channels, share), F32))]
        + [whole(v) for v in vectors],
        compiler_params=pltpu.CompilerParams(vmem_limit_bytes=LIMIT),
    )(
        residual, down_sum, d_res, proj_sum, x, mixer_gain, feed_down_bias, va, vd, vl, vf,
        own_up, own_down, own_out, own_in,
    )
    (result, grad_x, g_up, g_down, g_out, g_in, g_mgain, g_mshift, g_inb, g_sw, g_sb, g_f1, g_f1b, g_f2, g_f2b,
     g_freq, g_last, g_skip, g_ob, g_fgain, g_fshift, g_ub, g_db) = out
    return (
        result[None], grad_x[None], g_mgain, g_mshift, jnp.transpose(g_in, (2, 0, 1)), g_inb, g_sw, g_sb,
        g_f1, g_f1b, g_f2, g_f2b, g_freq, g_last, g_skip, g_out.reshape(channels, share), g_ob, g_fgain, g_fshift,
        g_up.reshape(share, hidden), g_ub, g_down.reshape(hidden, share), g_db,
    )


def solution(mesh):
    in_specs = (
        P("dp", "ctx", None), P("dp", "ctx", None), P("dp", None), P(), P(), P("dp", None, "tp"), P(None, "tp"),
        P(None, None, "tp"), P(None, "tp"), P(), P(), P(), P(), P(), P("dp", "tp"), P("tp"), P("tp", "dp"), P(),
        P(), P(), P("dp", "tp"), P("tp"), P("tp", "dp"), P(),
    )
    out_specs = (
        P("dp", "ctx", None), P("dp", "ctx", None), P(), P(), P("dp", None, "tp"), P(None, "tp"),
        P(None, None, "tp"), P(None, "tp"), P(), P(), P(), P(), P(), P("dp", "tp"), P("tp"), P("tp", "dp"), P(),
        P(), P(), P("dp", "tp"), P("tp"), P("tp", "dp"), P(),
    )
    return jax.shard_map(body, mesh=mesh, in_specs=in_specs, out_specs=out_specs, check_vma=False)
```
